512 devices in a mesh: ent: 128 (over y, z, core), rep: 4 (over x).
Axes of the slice: x: 4, y: 8, z: 8, core: 2. Of those that a mesh axis runs over, the one named last changes fastest.
Arguments:
- item_factors: bfloat16 [524288, 128], P(('ent', 'rep')), may hold values from -0.1 to 0.1
- tile_items: int32 [128, 4, 256, 32], P('ent', 'rep'), may hold values from 0 to 1023
- send_tiles: int32 [128, 4, 128], P('ent', 'rep'), may hold values from 1 to 2, as said below
- tile_users: int32 [128, 4, 256, 1], P('ent', 'rep'), may hold values from 0 to 7
- tile_counts: int32 [128, 4, 256, 32], P('ent', 'rep'), may hold values from 0 to 31
- recv_tiles: int32 [128, 4, 128], P('ent', 'rep'), may hold values from 1 to 2, as said below
Outputs:
- user_factors: float32 [1024, 128], P(('ent', 'rep'))
- item_rhs: float32 [524288, 128], P(('ent', 'rep'))
The draws below stay inside these ranges and needn't reach their ends.
Inputs may be any that keep to these rules, and one draw needn't show every extreme that they name: send_tiles[e, r, p] counts the leading tile slots p * 2 to p * 2 + 1 of device (e, r) that are live; every device sends 2 tiles to some peer and receives 2 tiles from some peer. recv_tiles[p, r, e] equals send_tiles[e, r, p].
All inputs are finite; a program needn't handle non-finite values.
Results may differ from the reference program's by a relative error of at most 0.0009.
The reference program's roundings to bfloat16 on the way count: a program that leaves them out, or rounds other values in their place, can miss the bound.
Values may be sent and summed in bfloat16 or wider, within the bound.
A program may use at most 64 MiB of HBM per device.

```python
import jax
import jax.numpy as jnp
from jax import lax

R = 128
ROWS = 32
SEG_ROWS = 32
CAP = 2
ITEM_DEV = 1024
SEGS = 1
U_ENT = 8
USERS = 1024
ITEMS = 524288
N_ENT = 128
N_REP = 4


def tile_loads(key):
    key_loads, key_shift = jax.random.split(jax.random.fold_in(key, 7))
    loads = jax.random.randint(key_loads, (N_ENT, N_REP, N_ENT), 1, CAP + 1)
    shift_by = jax.random.randint(key_shift, (), 0, N_ENT)
    ent_ids = jnp.arange(N_ENT)
    full_pair = ent_ids[None, :] == (ent_ids[:, None] + shift_by) % N_ENT
    loads = jnp.where(full_pair[:, None, :], CAP, loads)
    return loads.astype(jnp.int32)


def draw_send_tiles(key, part):
    return tile_loads(key)


def draw_recv_tiles(key, part):
    return jnp.transpose(tile_loads(key), (2, 1, 0))


def draw_item_factors(key, part):
    block_total = N_ENT * N_REP
    block_pos = (jnp.arange(ITEMS, dtype=jnp.int32) // ITEM_DEV).astype(jnp.float32)
    along = block_pos / float(max(block_total - 1, 1))
    values = jnp.clip(jax.random.normal(jax.random.fold_in(key, 11), (ITEMS, R), jnp.float32), -4.0, 4.0)
    amplitude = 0.00216 * jnp.power(10.0, along)
    return (values * amplitude[:, None]).astype(jnp.bfloat16)


def place_ends(array, rng, least, top_value):
    place = [jax.random.randint(jax.random.fold_in(rng, axis), (), 0, length) for axis, length in enumerate(array.shape)]
    main_axis = array.shape.index(max(array.shape))
    beside = place[:main_axis] + [(place[main_axis] + 1) % array.shape[main_axis]] + place[main_axis + 1:]
    return array.at[tuple(place)].set(least).at[tuple(beside)].set(top_value)


def setup_inputs(seed: int = 0) -> dict:
    seeds = jax.random.split(jax.random.key(seed), 7)
    return {
        "item_factors": draw_item_factors(jax.random.fold_in(seeds[6], 71), 0),
        "tile_items": place_ends(jax.random.randint(seeds[1], (N_ENT, N_REP, N_ENT * CAP, ROWS), 0, ITEM_DEV), jax.random.fold_in(seeds[1], 1), 0, ITEM_DEV - 1).astype(jnp.int32),
        "send_tiles": draw_send_tiles(jax.random.fold_in(seeds[6], 71), 0),
        "tile_users": place_ends(jax.random.randint(seeds[3], (N_ENT, N_REP, N_ENT * CAP, SEGS), 0, U_ENT), jax.random.fold_in(seeds[3], 1), 0, U_ENT - 1).astype(jnp.int32),
        "tile_counts": place_ends(jax.random.randint(seeds[4], (N_ENT, N_REP, N_ENT * CAP, ROWS), 0, 32), jax.random.fold_in(seeds[4], 1), 0, 31).astype(jnp.int32),
        "recv_tiles": draw_recv_tiles(jax.random.fold_in(seeds[6], 71), 0),
    }


ALPHA = 40.0
RIDGE = 1.0
RHS_SCALE = 1.0 / 640.0

def solve_users(gram, rhs):
    lower = jnp.linalg.cholesky(gram)
    halfway = lax.linalg.triangular_solve(lower, rhs[..., None], left_side=True, lower=True)
    result = lax.linalg.triangular_solve(lower, halfway, left_side=True, lower=True, transpose_a=True)
    return result[..., 0]

def reference(item_factors, tile_items, send_tiles, tile_users, tile_counts, recv_tiles):
    highest = lax.Precision.HIGHEST
    item_table = item_factors.reshape(N_ENT, N_REP, ITEM_DEV, R)
    global_gram = lax.dot_general(item_factors.astype(jnp.float32), item_factors.astype(jnp.float32), (((0,), (0,)), ((), ())), preferred_element_type=jnp.float32)
    base_gram = global_gram + RIDGE * jnp.eye(R, dtype=jnp.float32)
    slot_pos = jnp.arange(CAP, dtype=jnp.int32)

    def receiver(peer_ent):

        def one_rep(rep_idx):
            rep_table = lax.dynamic_index_in_dim(item_table, rep_idx, 1, keepdims=False)
            rep_items = lax.dynamic_index_in_dim(tile_items, rep_idx, 1, keepdims=False)
            chosen = lax.dynamic_slice_in_dim(rep_items, (peer_ent * CAP).astype(jnp.int32), CAP, 1)
            rows_y = jax.vmap(lambda table_one, index_one: jnp.take(table_one, index_one.reshape(-1), axis=0).reshape(CAP, ROWS, R))(rep_table, chosen)
            send_rep = lax.dynamic_index_in_dim(send_tiles, rep_idx, 1, keepdims=False)
            send_live = lax.dynamic_index_in_dim(send_rep, peer_ent, 1, keepdims=False)
            keep_rows = slot_pos[None, :] < send_live[:, None]
            rows_y = jnp.where(keep_rows[:, :, None, None], rows_y, jnp.zeros((), jnp.bfloat16))
            rows_y = rows_y.reshape(N_ENT * CAP, ROWS, R)
            count_peer = lax.dynamic_index_in_dim(tile_counts, peer_ent, 0, keepdims=False)
            counts = lax.dynamic_index_in_dim(count_peer, rep_idx, 0, keepdims=False)
            recv_peer = lax.dynamic_index_in_dim(recv_tiles, peer_ent, 0, keepdims=False)
            recv_live = lax.dynamic_index_in_dim(recv_peer, rep_idx, 0, keepdims=False)
            is_live = jnp.tile(slot_pos, N_ENT) < jnp.repeat(recv_live, CAP)
            counts_f = counts.astype(jnp.float32)
            gram_wts = ALPHA * counts_f
            rhs_wts = jnp.where(is_live[:, None] & (counts > 0), 1.0 + ALPHA * counts_f, jnp.float32(0.0))
            rows_f = rows_y.astype(jnp.float32)
            weighted = (gram_wts[:, :, None] * rows_f).astype(jnp.bfloat16).astype(jnp.float32)
            rows_s = rows_f.reshape(N_ENT * CAP, SEGS, SEG_ROWS, R)
            weighted_s = weighted.reshape(N_ENT * CAP, SEGS, SEG_ROWS, R)
            tile_gram = jnp.einsum('tsri,tsrj->tsij', weighted_s, rows_s, precision=highest).reshape(-1, R, R)
            tile_rhs = jnp.einsum('tsr,tsri->tsi', rhs_wts.reshape(N_ENT * CAP, SEGS, SEG_ROWS), rows_s, precision=highest).reshape(-1, R)
            owner_peer = lax.dynamic_index_in_dim(tile_users, peer_ent, 0, keepdims=False)
            run_owner = lax.dynamic_index_in_dim(owner_peer, rep_idx, 0, keepdims=False).reshape(-1)
            group_gram = jax.ops.segment_sum(tile_gram, run_owner, num_segments=U_ENT)
            group_rhs = jax.ops.segment_sum(tile_rhs, run_owner, num_segments=U_ENT)
            return (group_gram, group_rhs, rhs_wts)
        grams, rights, rhs_all = lax.map(one_rep, jnp.arange(N_REP, dtype=jnp.int32))
        solved = solve_users(jnp.sum(grams, axis=0) + base_gram, jnp.sum(rights, axis=0))
        return (solved, rhs_all)
    factors, weights = lax.map(receiver, jnp.arange(N_ENT, dtype=jnp.int32))
    sent_factors = lax.optimization_barrier(factors.astype(jnp.bfloat16)).astype(jnp.float32)

    def sender(sender_idx):
        ent_idx = (sender_idx // N_REP).astype(jnp.int32)
        rep_idx = (sender_idx % N_REP).astype(jnp.int32)
        users_rep = lax.dynamic_index_in_dim(tile_users, rep_idx, 1, keepdims=False)
        users_here = lax.dynamic_slice_in_dim(users_rep, (ent_idx * CAP).astype(jnp.int32), CAP, 1)
        factor_rows = jax.vmap(lambda table_one, index_one: jnp.take(table_one, index_one.reshape(-1), axis=0).reshape(CAP, SEGS, R))(sent_factors, users_here)
        weights_rep = lax.dynamic_index_in_dim(weights, rep_idx, 1, keepdims=False)
        weights_here = lax.dynamic_slice_in_dim(weights_rep, (ent_idx * CAP).astype(jnp.int32), CAP, 1)
        weights_here = weights_here.reshape(N_ENT, CAP, SEGS, SEG_ROWS)
        items_ent = lax.dynamic_index_in_dim(tile_items, ent_idx, 0, keepdims=False)
        items_here = lax.dynamic_index_in_dim(items_ent, rep_idx, 0, keepdims=False)
        contrib = (weights_here[..., None] * factor_rows[:, :, :, None, :]).reshape(-1, R)
        return jax.ops.segment_sum(contrib, items_here.reshape(-1), num_segments=ITEM_DEV) * RHS_SCALE
    item_rhs = lax.map(sender, jnp.arange(N_ENT * N_REP, dtype=jnp.int32)).reshape(ITEMS, R)
    return (factors.reshape(USERS, R), item_rhs)
```

```python
import jax
import jax.numpy as jnp
from jax import lax
from jax.sharding import PartitionSpec as P

U_DEV = 2


ALPHA = 40.0
RIDGE = 1.0
RHS_SCALE = 1.0 / 640.0


def solve_users(gram, rhs):
    lower = jnp.linalg.cholesky(gram)
    halfway = lax.linalg.triangular_solve(lower, rhs[..., None], left_side=True, lower=True)
    result = lax.linalg.triangular_solve(
        lower, halfway, left_side=True, lower=True, transpose_a=True
    )
    return result[..., 0]


def tree_sum(value, count):
    bits = count.bit_length() - 1
    for bit in range(bits):
        step = 1 << bit
        pairs = [(i, i ^ step) for i in range(count)]
        value = value + lax.ppermute(value, ("ent", "rep"), pairs)
    return value


def rep_scatter_sum(acc, n_rep, per_dev):
    me = lax.axis_index("rep")
    total = lax.dynamic_slice_in_dim(acc, me * per_dev, per_dev, 0)
    for shift in range(1, n_rep):
        dest = (me + shift) % n_rep
        piece = lax.dynamic_slice_in_dim(acc, dest * per_dev, per_dev, 0)
        pairs = [(i, (i + shift) % n_rep) for i in range(n_rep)]
        total = total + lax.ppermute(piece, "rep", pairs)
    width = acc.shape[1]
    return total[:, : width - 128], total[:, width - 128 :]


def rep_gather(value, n_rep):
    me = lax.axis_index("rep")
    got = [value]
    for shift in range(1, n_rep):
        pairs = [(i, (i + shift) % n_rep) for i in range(n_rep)]
        got.append(lax.ppermute(value, "rep", pairs))
    stacked = jnp.stack(got)
    order = (me - jnp.arange(n_rep)) % n_rep
    return jnp.take(stacked, order, axis=0).reshape(-1, value.shape[-1])


def shards(item_factors, tile_items, send_tiles, tile_users, tile_counts, recv_tiles):
    highest = lax.Precision.HIGHEST
    rank_width = item_factors.shape[1]
    item_count = item_factors.shape[0]
    n_ent = lax.axis_size("ent")
    n_rep = lax.axis_size("rep")
    tile_slots = tile_items.shape[2]
    tile_rows = tile_items.shape[3]
    seg_count = tile_users.shape[3]
    seg_length = tile_rows // seg_count
    slot_cap = tile_slots // n_ent
    user_block = U_DEV * lax.axis_size("rep")
    item_ids = tile_items.reshape(tile_slots, tile_rows)
    slot_pos = jnp.arange(tile_slots, dtype=jnp.int32) % slot_cap
    live_send = slot_pos < jnp.repeat(send_tiles.reshape(n_ent), slot_cap)
    live_recv = slot_pos < jnp.repeat(recv_tiles.reshape(n_ent), slot_cap)
    partial_gram = lax.dot_general(
        item_factors, item_factors, (((0,), (0,)), ((), ())), preferred_element_type=jnp.float32
    )
    picked = jnp.take(item_factors, item_ids.reshape(-1), axis=0).reshape(
        tile_slots, tile_rows, rank_width
    )
    picked = jnp.where(live_send[:, None, None], picked, jnp.zeros((), jnp.bfloat16))
    incoming = lax.all_to_all(
        picked.reshape(n_ent, slot_cap * tile_rows, rank_width),
        "ent",
        split_axis=0,
        concat_axis=0,
        tiled=True,
    )
    counts_int = tile_counts.reshape(tile_slots, tile_rows)
    counts_f = counts_int.astype(jnp.float32)
    gram_weight = ALPHA * counts_f
    rhs_weight = jnp.where(
        live_recv[:, None] & (counts_int > 0), 1.0 + ALPHA * counts_f, jnp.float32(0.0)
    )
    owners = tile_users.reshape(tile_slots * seg_count)
    selector = owners[None, :] == jnp.arange(user_block, dtype=jnp.int32)[:, None]
    selector_f = selector.astype(jnp.float32)
    src_group = 1
    while (
        src_group * 2 <= n_ent
        and n_ent % (src_group * 2) == 0
        and (src_group * 2 * slot_cap * tile_rows <= 4096)
    ):
        src_group = src_group * 2
    tiles_blk = src_group * slot_cap
    block_count = tile_slots // tiles_blk
    runs_blk = tiles_blk * seg_count

    def accumulate(state_pair, pieces):
        gram_run, rhs_run = state_pair
        rows_blk, gram_blk, rhs_blk, select_blk = pieces
        weighted = (gram_blk[:, :, None] * rows_blk).astype(jnp.bfloat16)
        rows_seg = rows_blk.reshape(tiles_blk, seg_count, seg_length, rank_width)
        weighted = weighted.reshape(tiles_blk, seg_count, seg_length, rank_width)
        run_gram = jnp.einsum(
            "tsri,tsrj->tsij", weighted, rows_seg, preferred_element_type=jnp.float32
        )
        run_gram = run_gram.reshape(runs_blk, rank_width * rank_width)
        run_rhs = jnp.einsum(
            "tsr,tsri->tsi",
            rhs_blk.reshape(tiles_blk, seg_count, seg_length),
            rows_seg.astype(jnp.float32),
            precision=highest,
        )
        run_rhs = run_rhs.reshape(runs_blk, rank_width)
        gram_run = gram_run + jnp.dot(select_blk, run_gram, precision=highest)
        rhs_run = rhs_run + jnp.dot(select_blk, run_rhs, precision=highest)
        return ((gram_run, rhs_run), None)

    block_pieces = (
        incoming.reshape(block_count, tiles_blk, tile_rows, rank_width),
        gram_weight.reshape(block_count, tiles_blk, tile_rows),
        rhs_weight.reshape(block_count, tiles_blk, tile_rows),
        jnp.transpose(selector_f.reshape(user_block, block_count, runs_blk), (1, 0, 2)),
    )
    start_pair = (
        jnp.zeros((user_block, rank_width * rank_width), jnp.float32),
        jnp.zeros((user_block, rank_width), jnp.float32),
    )
    (gram_acc, rhs_acc), _ = lax.scan(accumulate, start_pair, block_pieces)
    identity_mat = jnp.eye(rank_width, dtype=jnp.float32)
    added_term = tree_sum(partial_gram, n_ent * n_rep) + RIDGE * identity_mat
    own_gram, own_rhs = rep_scatter_sum(
        jnp.concatenate([gram_acc, rhs_acc], axis=1), n_rep, U_DEV
    )
    own_factors = solve_users(own_gram.reshape(-1, rank_width, rank_width) + added_term, own_rhs)
    solved = rep_gather(own_factors.astype(jnp.bfloat16), n_rep)
    run_factor = lax.dot_general(
        selector.astype(jnp.bfloat16),
        solved,
        (((0,), (0,)), ((), ())),
        preferred_element_type=jnp.float32,
    )
    back_factor, back_weight = (
        lax.all_to_all(
            run_factor.reshape(n_ent, slot_cap, seg_count * rank_width),
            "ent",
            split_axis=0,
            concat_axis=0,
            tiled=True,
        ),
        lax.all_to_all(
            rhs_weight.reshape(n_ent, slot_cap, tile_rows),
            "ent",
            split_axis=0,
            concat_axis=0,
            tiled=True,
        ),
    )

    def spread(running, pieces):
        factor_blk, weight_blk, item_blk = pieces
        contrib = (weight_blk[:, :, :, None] * factor_blk[:, :, None, :]).reshape(-1, rank_width)
        return (
            running + jax.ops.segment_sum(contrib, item_blk.reshape(-1), num_segments=item_count),
            None,
        )

    spread_pieces = (
        back_factor.reshape(block_count, tiles_blk, seg_count, rank_width),
        back_weight.reshape(block_count, tiles_blk, seg_count, seg_length),
        item_ids.reshape(block_count, tiles_blk, tile_rows),
    )
    item_rhs, _ = lax.scan(spread, jnp.zeros((item_count, rank_width), jnp.float32), spread_pieces)
    return (own_factors, item_rhs * RHS_SCALE)


def solution(mesh):
    in_specs = (
        P(("ent", "rep"), None),
        P("ent", "rep", None, None),
        P("ent", "rep", None),
        P("ent", "rep", None, None),
        P("ent", "rep", None, None),
        P("ent", "rep", None),
    )
    out_specs = (P(("ent", "rep"), None), P(("ent", "rep"), None))
    return jax.shard_map(shards, mesh=mesh, in_specs=in_specs, out_specs=out_specs, check_vma=False)
```

```python
import jax
import jax.numpy as jnp
from jax import lax
from jax.sharding import PartitionSpec as P

U_DEV = 2


ALPHA = 40.0
RIDGE = 1.0
RHS_SCALE = 1.0 / 640.0


def solve_users(gram, rhs):
    lower = jnp.linalg.cholesky(gram)
    halfway = lax.linalg.triangular_solve(lower, rhs[..., None], left_side=True, lower=True)
    result = lax.linalg.triangular_solve(
        lower, halfway, left_side=True, lower=True, transpose_a=True
    )
    return result[..., 0]


def tree_sum(value, count):
    bits = count.bit_length() - 1
    for bit in range(bits):
        step = 1 << bit
        pairs = [(i, i ^ step) for i in range(count)]
        value = value + lax.ppermute(value, ("ent", "rep"), pairs)
    return value


def rep_scatter_sum(acc, n_rep, per_dev):
    me = lax.axis_index("rep")
    total = lax.dynamic_slice_in_dim(acc, me * per_dev, per_dev, 0)
    for shift in range(1, n_rep):
        dest = (me + shift) % n_rep
        piece = lax.dynamic_slice_in_dim(acc, dest * per_dev, per_dev, 0)
        pairs = [(i, (i + shift) % n_rep) for i in range(n_rep)]
        total = total + lax.ppermute(piece, "rep", pairs)
    width = acc.shape[1]
    return total[:, : width - 128], total[:, width - 128 :]


def rep_gather(value, n_rep):
    me = lax.axis_index("rep")
    got = [value]
    for shift in range(1, n_rep):
        pairs = [(i, (i + shift) % n_rep) for i in range(n_rep)]
        got.append(lax.ppermute(value, "rep", pairs))
    stacked = jnp.stack(got)
    order = (me - jnp.arange(n_rep)) % n_rep
    return jnp.take(stacked, order, axis=0).reshape(-1, value.shape[-1])


def shards(item_factors, tile_items, send_tiles, tile_users, tile_counts, recv_tiles):
    highest = lax.Precision.HIGHEST
    rank_width = item_factors.shape[1]
    item_count = item_factors.shape[0]
    n_ent = lax.axis_size("ent")
    n_rep = lax.axis_size("rep")
    tile_slots = tile_items.shape[2]
    tile_rows = tile_items.shape[3]
    seg_count = tile_users.shape[3]
    seg_length = tile_rows // seg_count
    slot_cap = tile_slots // n_ent
    user_block = U_DEV * lax.axis_size("rep")
    item_ids = tile_items.reshape(tile_slots, tile_rows)
    slot_pos = jnp.arange(tile_slots, dtype=jnp.int32) % slot_cap
    live_send = slot_pos < jnp.repeat(send_tiles.reshape(n_ent), slot_cap)
    live_recv = slot_pos < jnp.repeat(recv_tiles.reshape(n_ent), slot_cap)
    partial_gram = lax.dot_general(
        item_factors, item_factors, (((0,), (0,)), ((), ())), preferred_element_type=jnp.float32
    )
    picked = jnp.take(item_factors, item_ids.reshape(-1), axis=0).reshape(
        tile_slots, tile_rows, rank_width
    )
    picked = jnp.where(live_send[:, None, None], picked, jnp.zeros((), jnp.bfloat16))
    incoming = lax.all_to_all(
        picked.reshape(n_ent, slot_cap * tile_rows, rank_width),
        "ent",
        split_axis=0,
        concat_axis=0,
        tiled=True,
    )
    counts_int = tile_counts.reshape(tile_slots, tile_rows)
    counts_f = counts_int.astype(jnp.float32)
    gram_weight = ALPHA * counts_f
    rhs_weight = jnp.where(
        live_recv[:, None] & (counts_int > 0), 1.0 + ALPHA * counts_f, jnp.float32(0.0)
    )
    owners = tile_users.reshape(tile_slots * seg_count)
    selector = owners[None, :] == jnp.arange(user_block, dtype=jnp.int32)[:, None]
    selector_f = selector.astype(jnp.float32)
    rows_all = incoming.reshape(tile_slots * tile_rows, rank_width)
    weighted = (gram_weight.reshape(-1, 1) * rows_all.astype(jnp.float32)).astype(jnp.bfloat16)
    row_owner = jnp.repeat(owners, seg_length)
    row_select = row_owner[:, None] == jnp.arange(user_block, dtype=jnp.int32)[None, :]
    masked = jnp.where(row_select[:, :, None], weighted[:, None, :], jnp.zeros((), jnp.bfloat16))
    gram_acc = lax.dot_general(
        masked.reshape(-1, user_block * rank_width),
        rows_all,
        (((0,), (0,)), ((), ())),
        preferred_element_type=jnp.float32,
    ).reshape(user_block, rank_width * rank_width)
    rhs_rows = jnp.where(row_select, rhs_weight.reshape(-1, 1), 0.0)
    rhs_acc = lax.dot_general(
        rhs_rows,
        rows_all.astype(jnp.float32),
        (((0,), (0,)), ((), ())),
        precision=highest,
        preferred_element_type=jnp.float32,
    )
    identity_mat = jnp.eye(rank_width, dtype=jnp.float32)
    added_term = tree_sum(partial_gram, n_ent * n_rep) + RIDGE * identity_mat
    own_gram, own_rhs = rep_scatter_sum(
        jnp.concatenate([gram_acc, rhs_acc], axis=1), n_rep, U_DEV
    )
    own_factors = solve_users(own_gram.reshape(-1, rank_width, rank_width) + added_term, own_rhs)
    solved = rep_gather(own_factors.astype(jnp.bfloat16), n_rep)
    run_factor = lax.dot_general(
        selector.astype(jnp.bfloat16),
        solved,
        (((0,), (0,)), ((), ())),
        preferred_element_type=jnp.float32,
    ).astype(jnp.bfloat16)
    back_factor, back_weight = (
        lax.all_to_all(
            run_factor.reshape(n_ent, slot_cap, seg_count * rank_width),
            "ent",
            split_axis=0,
            concat_axis=0,
            tiled=True,
        ),
        lax.all_to_all(
            rhs_weight.reshape(n_ent, slot_cap, tile_rows),
            "ent",
            split_axis=0,
            concat_axis=0,
            tiled=True,
        ),
    )
    item_hot = item_ids[:, :, None] == jnp.arange(item_count, dtype=jnp.int32)[None, None, :]
    run_weight = back_weight.reshape(tile_slots * seg_count, seg_length)
    hot_runs = item_hot.reshape(tile_slots * seg_count, seg_length, item_count)
    spread_mat = jnp.sum(jnp.where(hot_runs, run_weight[:, :, None], 0.0), axis=1)
    item_rhs = lax.dot_general(
        spread_mat,
        back_factor.reshape(tile_slots * seg_count, rank_width).astype(jnp.float32),
        (((0,), (0,)), ((), ())),
        precision=highest,
        preferred_element_type=jnp.float32,
    )
    return (own_factors, item_rhs * RHS_SCALE)


def solution(mesh):
    in_specs = (
        P(("ent", "rep"), None),
        P("ent", "rep", None, None),
        P("ent", "rep", None),
        P("ent", "rep", None, None),
        P("ent", "rep", None, None),
        P("ent", "rep", None),
    )
    out_specs = (P(("ent", "rep"), None), P(("ent", "rep"), None))
    return jax.shard_map(shards, mesh=mesh, in_specs=in_specs, out_specs=out_specs, check_vma=False)
```

```python
import functools

import jax
import jax.numpy as jnp
from jax import lax
from jax.experimental import pallas as pl
from jax.experimental.pallas import tpu as pltpu
from jax.sharding import PartitionSpec as P

MESH_ID = pl.DeviceIdType.MESH

U_DEV = 2


ALPHA = 40.0
RIDGE = 1.0
RHS_SCALE = 1.0 / 640.0


def solve_users(gram, rhs):
    lower = jnp.linalg.cholesky(gram)
    halfway = lax.linalg.triangular_solve(lower, rhs[..., None], left_side=True, lower=True)
    result = lax.linalg.triangular_solve(
        lower, halfway, left_side=True, lower=True, transpose_a=True
    )
    return result[..., 0]


def doubling_kernel(n_rep, rounds, x_ref, o_ref, recv, send_sem, recv_sem):
    flat = lax.axis_index("ent") * n_rep + lax.axis_index("rep")
    partners = []
    for bit in range(rounds):
        step = 1 << bit
        upper = (flat // step) % 2
        peer = flat + step - 2 * step * upper
        partners.append((peer // n_rep, peer % n_rep))
    barrier = pltpu.get_barrier_semaphore()
    for peer in partners:
        pl.semaphore_signal(barrier, inc=1, device_id=peer, device_id_type=MESH_ID)
    pl.semaphore_wait(barrier, rounds)
    o_ref[...] = x_ref[...]
    for bit in range(rounds):
        copy = pltpu.make_async_remote_copy(
            src_ref=o_ref,
            dst_ref=recv.at[bit],
            send_sem=send_sem.at[bit],
            recv_sem=recv_sem.at[bit],
            device_id=partners[bit],
            device_id_type=MESH_ID,
        )
        copy.start()
        copy.wait_recv()
        copy.wait_send()
        o_ref[...] = o_ref[...] + recv[bit]


def tree_sum(value, count):
    rounds = count.bit_length() - 1
    n_rep = lax.axis_size("rep")
    return pl.pallas_call(
        functools.partial(doubling_kernel, n_rep, rounds),
        out_shape=jax.ShapeDtypeStruct(value.shape, value.dtype),
        in_specs=[pl.BlockSpec(memory_space=pltpu.VMEM)],
        out_specs=pl.BlockSpec(memory_space=pltpu.VMEM),
        scratch_shapes=[
            pltpu.VMEM((rounds,) + value.shape, value.dtype),
            pltpu.SemaphoreType.DMA((rounds,)),
            pltpu.SemaphoreType.DMA((rounds,)),
        ],
        compiler_params=pltpu.CompilerParams(collective_id=0, has_side_effects=True),
    )(value)


def rep_scatter_sum(acc, n_rep, per_dev):
    me = lax.axis_index("rep")
    total = lax.dynamic_slice_in_dim(acc, me * per_dev, per_dev, 0)
    for shift in range(1, n_rep):
        dest = (me + shift) % n_rep
        piece = lax.dynamic_slice_in_dim(acc, dest * per_dev, per_dev, 0)
        pairs = [(i, (i + shift) % n_rep) for i in range(n_rep)]
        total = total + lax.ppermute(piece, "rep", pairs)
    width = acc.shape[1]
    return total[:, : width - 128], total[:, width - 128 :]


def rep_gather(value, n_rep):
    me = lax.axis_index("rep")
    got = [value]
    for shift in range(1, n_rep):
        pairs = [(i, (i + shift) % n_rep) for i in range(n_rep)]
        got.append(lax.ppermute(value, "rep", pairs))
    stacked = jnp.stack(got)
    order = (me - jnp.arange(n_rep)) % n_rep
    return jnp.take(stacked, order, axis=0).reshape(-1, value.shape[-1])


def shards(item_factors, tile_items, send_tiles, tile_users, tile_counts, recv_tiles):
    highest = lax.Precision.HIGHEST
    rank_width = item_factors.shape[1]
    item_count = item_factors.shape[0]
    n_ent = lax.axis_size("ent")
    n_rep = lax.axis_size("rep")
    tile_slots = tile_items.shape[2]
    tile_rows = tile_items.shape[3]
    seg_count = tile_users.shape[3]
    seg_length = tile_rows // seg_count
    slot_cap = tile_slots // n_ent
    user_block = U_DEV * lax.axis_size("rep")
    item_ids = tile_items.reshape(tile_slots, tile_rows)
    slot_pos = jnp.arange(tile_slots, dtype=jnp.int32) % slot_cap
    live_send = slot_pos < jnp.repeat(send_tiles.reshape(n_ent), slot_cap)
    live_recv = slot_pos < jnp.repeat(recv_tiles.reshape(n_ent), slot_cap)
    partial_gram = lax.dot_general(
        item_factors, item_factors, (((0,), (0,)), ((), ())), preferred_element_type=jnp.float32
    )
    picked = jnp.take(item_factors, item_ids.reshape(-1), axis=0).reshape(
        tile_slots, tile_rows, rank_width
    )
    picked = jnp.where(live_send[:, None, None], picked, jnp.zeros((), jnp.bfloat16))
    incoming = lax.all_to_all(
        picked.reshape(n_ent, slot_cap * tile_rows, rank_width),
        "ent",
        split_axis=0,
        concat_axis=0,
        tiled=True,
    )
    counts_int = tile_counts.reshape(tile_slots, tile_rows)
    counts_f = counts_int.astype(jnp.float32)
    gram_weight = ALPHA * counts_f
    rhs_weight = jnp.where(
        live_recv[:, None] & (counts_int > 0), 1.0 + ALPHA * counts_f, jnp.float32(0.0)
    )
    owners = tile_users.reshape(tile_slots * seg_count)
    selector = owners[None, :] == jnp.arange(user_block, dtype=jnp.int32)[:, None]
    selector_f = selector.astype(jnp.float32)
    rows_all = incoming.reshape(tile_slots * tile_rows, rank_width)
    weighted = (gram_weight.reshape(-1, 1) * rows_all.astype(jnp.float32)).astype(jnp.bfloat16)
    row_owner = jnp.repeat(owners, seg_length)
    row_select = row_owner[:, None] == jnp.arange(user_block, dtype=jnp.int32)[None, :]
    masked = jnp.where(row_select[:, :, None], weighted[:, None, :], jnp.zeros((), jnp.bfloat16))
    gram_acc = lax.dot_general(
        masked.reshape(-1, user_block * rank_width),
        rows_all,
        (((0,), (0,)), ((), ())),
        preferred_element_type=jnp.float32,
    ).reshape(user_block, rank_width * rank_width)
    rhs_rows = jnp.where(row_select, rhs_weight.reshape(-1, 1), 0.0)
    rhs_acc = lax.dot_general(
        rhs_rows,
        rows_all.astype(jnp.float32),
        (((0,), (0,)), ((), ())),
        precision=highest,
        preferred_element_type=jnp.float32,
    )
    identity_mat = jnp.eye(rank_width, dtype=jnp.float32)
    added_term = tree_sum(partial_gram, n_ent * n_rep) + RIDGE * identity_mat
    own_gram, own_rhs = rep_scatter_sum(
        jnp.concatenate([gram_acc, rhs_acc], axis=1), n_rep, U_DEV
    )
    own_factors = solve_users(own_gram.reshape(-1, rank_width, rank_width) + added_term, own_rhs)
    solved = rep_gather(own_factors.astype(jnp.bfloat16), n_rep)
    run_factor = lax.dot_general(
        selector.astype(jnp.bfloat16),
        solved,
        (((0,), (0,)), ((), ())),
        preferred_element_type=jnp.float32,
    ).astype(jnp.bfloat16)
    back_factor, back_weight = (
        lax.all_to_all(
            run_factor.reshape(n_ent, slot_cap, seg_count * rank_width),
            "ent",
            split_axis=0,
            concat_axis=0,
            tiled=True,
        ),
        lax.all_to_all(
            rhs_weight.reshape(n_ent, slot_cap, tile_rows),
            "ent",
            split_axis=0,
            concat_axis=0,
            tiled=True,
        ),
    )
    item_hot = item_ids[:, :, None] == jnp.arange(item_count, dtype=jnp.int32)[None, None, :]
    run_weight = back_weight.reshape(tile_slots * seg_count, seg_length)
    hot_runs = item_hot.reshape(tile_slots * seg_count, seg_length, item_count)
    spread_mat = jnp.sum(jnp.where(hot_runs, run_weight[:, :, None], 0.0), axis=1)
    item_rhs = lax.dot_general(
        spread_mat,
        back_factor.reshape(tile_slots * seg_count, rank_width).astype(jnp.float32),
        (((0,), (0,)), ((), ())),
        precision=highest,
        preferred_element_type=jnp.float32,
    )
    return (own_factors, item_rhs * RHS_SCALE)


def solution(mesh):
    in_specs = (
        P(("ent", "rep"), None),
        P("ent", "rep", None, None),
        P("ent", "rep", None),
        P("ent", "rep", None, None),
        P("ent", "rep", None, None),
        P("ent", "rep", None),
    )
    out_specs = (P(("ent", "rep"), None), P(("ent", "rep"), None))
    return jax.shard_map(shards, mesh=mesh, in_specs=in_specs, out_specs=out_specs, check_vma=False)
```

```python
import functools

import jax
import jax.numpy as jnp
from jax import lax
from jax.experimental import pallas as pl
from jax.experimental.pallas import tpu as pltpu
from jax.sharding import PartitionSpec as P

MESH_ID = pl.DeviceIdType.MESH

U_DEV = 2


ALPHA = 40.0
RIDGE = 1.0
RHS_SCALE = 1.0 / 640.0


def solve_users(gram, rhs):
    lower = jnp.linalg.cholesky(gram)
    halfway = lax.linalg.triangular_solve(lower, rhs[..., None], left_side=True, lower=True)
    result = lax.linalg.triangular_solve(
        lower, halfway, left_side=True, lower=True, transpose_a=True
    )
    return result[..., 0]


def doubling_kernel(n_rep, rounds, x_ref, o_ref, recv, send_sem, recv_sem):
    flat = lax.axis_index("ent") * n_rep + lax.axis_index("rep")
    partners = []
    for bit in range(rounds):
        step = 1 << bit
        upper = (flat // step) % 2
        peer = flat + step - 2 * step * upper
        partners.append((peer // n_rep, peer % n_rep))
    barrier = pltpu.get_barrier_semaphore()
    for peer in partners:
        pl.semaphore_signal(barrier, inc=1, device_id=peer, device_id_type=MESH_ID)
    pl.semaphore_wait(barrier, rounds)
    o_ref[...] = x_ref[...]
    for bit in range(rounds):
        copy = pltpu.make_async_remote_copy(
            src_ref=o_ref,
            dst_ref=recv.at[bit],
            send_sem=send_sem.at[bit],
            recv_sem=recv_sem.at[bit],
            device_id=partners[bit],
            device_id_type=MESH_ID,
        )
        copy.start()
        copy.wait_recv()
        copy.wait_send()
        o_ref[...] = o_ref[...] + recv[bit]


def tree_sum(value, count):
    rounds = count.bit_length() - 1
    n_rep = lax.axis_size("rep")
    return pl.pallas_call(
        functools.partial(doubling_kernel, n_rep, rounds),
        out_shape=jax.ShapeDtypeStruct(value.shape, value.dtype),
        in_specs=[pl.BlockSpec(memory_space=pltpu.VMEM)],
        out_specs=pl.BlockSpec(memory_space=pltpu.VMEM),
        scratch_shapes=[
            pltpu.VMEM((rounds,) + value.shape, value.dtype),
            pltpu.SemaphoreType.DMA((rounds,)),
            pltpu.SemaphoreType.DMA((rounds,)),
        ],
        compiler_params=pltpu.CompilerParams(collective_id=0, has_side_effects=True),
    )(value)


def rep_scatter_sum(acc, n_rep, per_dev):
    me = lax.axis_index("rep")
    total = lax.dynamic_slice_in_dim(acc, me * per_dev, per_dev, 0)
    for shift in range(1, n_rep):
        dest = (me + shift) % n_rep
        piece = lax.dynamic_slice_in_dim(acc, dest * per_dev, per_dev, 0)
        pairs = [(i, (i + shift) % n_rep) for i in range(n_rep)]
        total = total + lax.ppermute(piece, "rep", pairs)
    width = acc.shape[1]
    return total[:, : width - 128], total[:, width - 128 :]


def rep_gather(value, n_rep):
    me = lax.axis_index("rep")
    got = [value]
    for shift in range(1, n_rep):
        pairs = [(i, (i + shift) % n_rep) for i in range(n_rep)]
        got.append(lax.ppermute(value, "rep", pairs))
    stacked = jnp.stack(got)
    order = (me - jnp.arange(n_rep)) % n_rep
    return jnp.take(stacked, order, axis=0).reshape(-1, value.shape[-1])


def gather_kernel(idx_ref, table_ref, out_ref):
    picks = idx_ref[...] == lax.broadcasted_iota(jnp.int32, (idx_ref.shape[0], table_ref.shape[0]), 1)
    out_ref[...] = jnp.dot(
        picks.astype(jnp.bfloat16), table_ref[...], preferred_element_type=jnp.float32
    ).astype(out_ref.dtype)


def gather_rows(table, idx_col, chunk=512):
    count = idx_col.shape[0]
    return pl.pallas_call(
        gather_kernel,
        out_shape=jax.ShapeDtypeStruct((count, table.shape[1]), table.dtype),
        grid=(count // chunk,),
        in_specs=[
            pl.BlockSpec((chunk, 1), lambda i: (i, 0)),
            pl.BlockSpec(table.shape, lambda i: (0, 0)),
        ],
        out_specs=pl.BlockSpec((chunk, table.shape[1]), lambda i: (i, 0)),
        cost_estimate=pl.CostEstimate(
            flops=2 * count * table.shape[0] * table.shape[1],
            transcendentals=0,
            bytes_accessed=count * 4 + table.size * 2 + count * table.shape[1] * 2,
        ),
    )(idx_col, table)


def gram_kernel(n_user, rows_ref, gw_ref, user_ref, rw_ref, gram_ref, rhs_ref):
    step = pl.program_id(0)

    @pl.when(step == 0)
    def _():
        gram_ref[...] = jnp.zeros_like(gram_ref)
        rhs_ref[...] = jnp.zeros_like(rhs_ref)

    rows = rows_ref[...]
    rows_t = rows.astype(jnp.float32).T
    weights_t = (rows_t * gw_ref[pl.ds(step, 1), :]).astype(jnp.bfloat16)
    users = user_ref[pl.ds(step, 1), :]
    zero = jnp.zeros((), jnp.bfloat16)
    for user in range(n_user):
        picked = jnp.where(users == user, weights_t, zero)
        gram_ref[user] += jnp.dot(picked, rows, preferred_element_type=jnp.float32)
    slots = lax.broadcasted_iota(jnp.int32, (n_user, users.shape[1]), 0)
    per_user = jnp.where(users == slots, rw_ref[pl.ds(step, 1), :], 0.0)
    high = per_user.astype(jnp.bfloat16)
    low = (per_user - high.astype(jnp.float32)).astype(jnp.bfloat16)
    rhs_ref[...] += jnp.dot(high, rows, preferred_element_type=jnp.float32) + jnp.dot(
        low, rows, preferred_element_type=jnp.float32
    )


def user_grams(rows, gw_lanes, user_lanes, rw_lanes, n_user):
    chunks, chunk = gw_lanes.shape
    width = rows.shape[1]
    return pl.pallas_call(
        functools.partial(gram_kernel, n_user),
        out_shape=(
            jax.ShapeDtypeStruct((n_user, width, width), jnp.float32),
            jax.ShapeDtypeStruct((n_user, width), jnp.float32),
        ),
        grid=(chunks,),
        in_specs=[
            pl.BlockSpec((chunk, width), lambda i: (i, 0)),
            pl.BlockSpec((chunks, chunk), lambda i: (0, 0)),
            pl.BlockSpec((chunks, chunk), lambda i: (0, 0)),
            pl.BlockSpec((chunks, chunk), lambda i: (0, 0)),
        ],
        out_specs=(
            pl.BlockSpec((n_user, width, width), lambda i: (0, 0, 0)),
            pl.BlockSpec((n_user, width), lambda i: (0, 0)),
        ),
        cost_estimate=pl.CostEstimate(
            flops=2 * rows.shape[0] * width * width * (n_user + 2),
            transcendentals=0,
            bytes_accessed=rows.size * 2 + 12 * rows.shape[0] + n_user * width * (width + 1) * 4,
        ),
    )(rows, gw_lanes, user_lanes, rw_lanes)


def shards(item_factors, tile_items, send_tiles, tile_users, tile_counts, recv_tiles):
    highest = lax.Precision.HIGHEST
    rank_width = item_factors.shape[1]
    item_count = item_factors.shape[0]
    n_ent = lax.axis_size("ent")
    n_rep = lax.axis_size("rep")
    tile_slots = tile_items.shape[2]
    tile_rows = tile_items.shape[3]
    seg_count = tile_users.shape[3]
    seg_length = tile_rows // seg_count
    slot_cap = tile_slots // n_ent
    user_block = U_DEV * lax.axis_size("rep")
    item_ids = tile_items.reshape(tile_slots, tile_rows)
    slot_pos = jnp.arange(tile_slots, dtype=jnp.int32) % slot_cap
    live_send = slot_pos < jnp.repeat(send_tiles.reshape(n_ent), slot_cap)
    live_recv = slot_pos < jnp.repeat(recv_tiles.reshape(n_ent), slot_cap)
    partial_gram = lax.dot_general(
        item_factors, item_factors, (((0,), (0,)), ((), ())), preferred_element_type=jnp.float32
    )
    live_rows = jnp.repeat(live_send, tile_rows)
    idx_col = jnp.where(live_rows, item_ids.reshape(-1), -1).reshape(-1, 1)
    picked = gather_rows(item_factors, idx_col)
    incoming = lax.all_to_all(
        picked.reshape(n_ent, slot_cap * tile_rows, rank_width),
        "ent",
        split_axis=0,
        concat_axis=0,
        tiled=True,
    )
    counts_int = tile_counts.reshape(tile_slots, tile_rows)
    counts_f = counts_int.astype(jnp.float32)
    gram_weight = ALPHA * counts_f
    rhs_weight = jnp.where(
        live_recv[:, None] & (counts_int > 0), 1.0 + ALPHA * counts_f, jnp.float32(0.0)
    )
    owners = tile_users.reshape(tile_slots * seg_count)
    selector = owners[None, :] == jnp.arange(user_block, dtype=jnp.int32)[:, None]
    selector_f = selector.astype(jnp.float32)
    rows_all = incoming.reshape(tile_slots * tile_rows, rank_width)
    lane_chunk = 1024
    row_owner = jnp.repeat(owners, seg_length)
    gram_acc, rhs_acc = user_grams(
        rows_all,
        gram_weight.reshape(-1, lane_chunk),
        row_owner.reshape(-1, lane_chunk),
        rhs_weight.reshape(-1, lane_chunk),
        user_block,
    )
    gram_acc = gram_acc.reshape(user_block, rank_width * rank_width)
    identity_mat = jnp.eye(rank_width, dtype=jnp.float32)
    added_term = tree_sum(partial_gram, n_ent * n_rep) + RIDGE * identity_mat
    own_gram, own_rhs = rep_scatter_sum(
        jnp.concatenate([gram_acc, rhs_acc], axis=1), n_rep, U_DEV
    )
    own_factors = solve_users(own_gram.reshape(-1, rank_width, rank_width) + added_term, own_rhs)
    solved = rep_gather(own_factors.astype(jnp.bfloat16), n_rep)
    run_factor = lax.dot_general(
        selector.astype(jnp.bfloat16),
        solved,
        (((0,), (0,)), ((), ())),
        preferred_element_type=jnp.float32,
    ).astype(jnp.bfloat16)
    back_factor, back_weight = (
        lax.all_to_all(
            run_factor.reshape(n_ent, slot_cap, seg_count * rank_width),
            "ent",
            split_axis=0,
            concat_axis=0,
            tiled=True,
        ),
        lax.all_to_all(
            rhs_weight.reshape(n_ent, slot_cap, tile_rows),
            "ent",
            split_axis=0,
            concat_axis=0,
            tiled=True,
        ),
    )
    item_hot = item_ids[:, :, None] == jnp.arange(item_count, dtype=jnp.int32)[None, None, :]
    run_weight = back_weight.reshape(tile_slots * seg_count, seg_length)
    hot_runs = item_hot.reshape(tile_slots * seg_count, seg_length, item_count)
    spread_mat = jnp.sum(jnp.where(hot_runs, run_weight[:, :, None], 0.0), axis=1)
    item_rhs = lax.dot_general(
        spread_mat,
        back_factor.reshape(tile_slots * seg_count, rank_width).astype(jnp.float32),
        (((0,), (0,)), ((), ())),
        precision=highest,
        preferred_element_type=jnp.float32,
    )
    return (own_factors, item_rhs * RHS_SCALE)


def solution(mesh):
    in_specs = (
        P(("ent", "rep"), None),
        P("ent", "rep", None, None),
        P("ent", "rep", None),
        P("ent", "rep", None, None),
        P("ent", "rep", None, None),
        P("ent", "rep", None),
    )
    out_specs = (P(("ent", "rep"), None), P(("ent", "rep"), None))
    return jax.shard_map(shards, mesh=mesh, in_specs=in_specs, out_specs=out_specs, check_vma=False)
```

```python
import functools

import jax
import jax.numpy as jnp
from jax import lax
from jax.experimental import pallas as pl
from jax.experimental.pallas import tpu as pltpu
from jax.sharding import PartitionSpec as P

MESH_ID = pl.DeviceIdType.MESH

U_DEV = 2


ALPHA = 40.0
RIDGE = 1.0
RHS_SCALE = 1.0 / 640.0


def solve_users(gram, rhs):
    lower = jnp.linalg.cholesky(gram)
    halfway = lax.linalg.triangular_solve(lower, rhs[..., None], left_side=True, lower=True)
    result = lax.linalg.triangular_solve(
        lower, halfway, left_side=True, lower=True, transpose_a=True
    )
    return result[..., 0]


def flip_bits(value, mask, bits):
    out = value - value % (1 << bits)
    for bit in range(bits):
        here = (value // (1 << bit)) % 2
        out = out + (1 << bit) * ((1 - here) if (mask >> bit) & 1 else here)
    return out


def doubling_kernel(
    n_rep, low_bits, rounds, x_ref, o_ref, full_recv, piece_recv, piece, gath,
    sem_a, sem_b, sem_c, sem_d, sem_e, sem_f,
):
    flat = lax.axis_index("ent") * n_rep + lax.axis_index("rep")
    group = 1 << low_bits
    rows = x_ref.shape[0] // group
    slot = flat % group

    def place(p):
        return (p // n_rep, p % n_rep)

    def flip(bit):
        step = 1 << bit
        upper = (flat // step) % 2
        return flat + step - 2 * step * upper

    members = [flip_bits(flat, k, low_bits) for k in range(1, group)]
    outer = [flip(bit) for bit in range(low_bits, rounds)]
    barrier = pltpu.get_barrier_semaphore()
    for p in members + outer:
        pl.semaphore_signal(barrier, inc=1, device_id=place(p), device_id_type=MESH_ID)
    pl.semaphore_wait(barrier, len(members) + len(outer))

    o_ref[...] = x_ref[...]
    for bit in range(low_bits):
        copy = pltpu.make_async_remote_copy(
            src_ref=o_ref, dst_ref=full_recv.at[bit], send_sem=sem_a.at[bit],
            recv_sem=sem_b.at[bit], device_id=place(flip(bit)), device_id_type=MESH_ID,
        )
        copy.start()
        copy.wait_recv()
        copy.wait_send()
        o_ref[...] = o_ref[...] + full_recv[bit]

    piece[...] = o_ref[pl.ds(pl.multiple_of(slot * rows, rows), rows), :]
    for index, p in enumerate(outer):
        copy = pltpu.make_async_remote_copy(
            src_ref=piece, dst_ref=piece_recv.at[index], send_sem=sem_c.at[index],
            recv_sem=sem_d.at[index], device_id=place(p), device_id_type=MESH_ID,
        )
        copy.start()
        copy.wait_recv()
        copy.wait_send()
        piece[...] = piece[...] + piece_recv[index]

    gath[slot] = piece[...]
    sends = []
    for index, p in enumerate(members):
        copy = pltpu.make_async_remote_copy(
            src_ref=piece, dst_ref=gath.at[slot], send_sem=sem_e.at[index],
            recv_sem=sem_f.at[slot], device_id=place(p), device_id_type=MESH_ID,
        )
        copy.start()
        sends.append(copy)
    for k in range(1, group):
        source = flip_bits(slot, k, low_bits)
        pltpu.make_async_remote_copy(
            src_ref=piece, dst_ref=gath.at[source], send_sem=sem_e.at[k - 1],
            recv_sem=sem_f.at[source], device_id=place(members[k - 1]), device_id_type=MESH_ID,
        ).wait_recv()
    for copy in sends:
        copy.wait_send()
    for part in range(group):
        o_ref[pl.ds(part * rows, rows), :] = gath[part]


def tree_sum(value, count):
    rounds = count.bit_length() - 1
    n_rep = lax.axis_size("rep")
    low_bits = (n_rep * 2).bit_length() - 1
    group = 1 << low_bits
    rows = value.shape[0] // group
    outer = rounds - low_bits
    return pl.pallas_call(
        functools.partial(doubling_kernel, n_rep, low_bits, rounds),
        out_shape=jax.ShapeDtypeStruct(value.shape, value.dtype),
        in_specs=[pl.BlockSpec(memory_space=pltpu.VMEM)],
        out_specs=pl.BlockSpec(memory_space=pltpu.VMEM),
        scratch_shapes=[
            pltpu.VMEM((low_bits,) + value.shape, value.dtype),
            pltpu.VMEM((outer, rows, value.shape[1]), value.dtype),
            pltpu.VMEM((rows, value.shape[1]), value.dtype),
            pltpu.VMEM((group, rows, value.shape[1]), value.dtype),
            pltpu.SemaphoreType.DMA((low_bits,)),
            pltpu.SemaphoreType.DMA((low_bits,)),
            pltpu.SemaphoreType.DMA((outer,)),
            pltpu.SemaphoreType.DMA((outer,)),
            pltpu.SemaphoreType.DMA((group - 1,)),
            pltpu.SemaphoreType.DMA((group,)),
        ],
        compiler_params=pltpu.CompilerParams(collective_id=0, has_side_effects=True),
    )(value)


def rep_scatter_sum(acc, n_rep, per_dev):
    me = lax.axis_index("rep")
    total = lax.dynamic_slice_in_dim(acc, me * per_dev, per_dev, 0)
    for shift in range(1, n_rep):
        dest = (me + shift) % n_rep
        piece = lax.dynamic_slice_in_dim(acc, dest * per_dev, per_dev, 0)
        pairs = [(i, (i + shift) % n_rep) for i in range(n_rep)]
        total = total + lax.ppermute(piece, "rep", pairs)
    width = acc.shape[1]
    return total[:, : width - 128], total[:, width - 128 :]


def rep_gather(value, n_rep):
    me = lax.axis_index("rep")
    got = [value]
    for shift in range(1, n_rep):
        pairs = [(i, (i + shift) % n_rep) for i in range(n_rep)]
        got.append(lax.ppermute(value, "rep", pairs))
    stacked = jnp.stack(got)
    order = (me - jnp.arange(n_rep)) % n_rep
    return jnp.take(stacked, order, axis=0).reshape(-1, value.shape[-1])


def gather_kernel(idx_ref, table_ref, out_ref):
    picks = idx_ref[...] == lax.broadcasted_iota(jnp.int32, (idx_ref.shape[0], table_ref.shape[0]), 1)
    out_ref[...] = jnp.dot(
        picks.astype(jnp.bfloat16), table_ref[...], preferred_element_type=jnp.float32
    ).astype(out_ref.dtype)


def gather_rows(table, idx_col, chunk=512):
    count = idx_col.shape[0]
    return pl.pallas_call(
        gather_kernel,
        out_shape=jax.ShapeDtypeStruct((count, table.shape[1]), table.dtype),
        grid=(count // chunk,),
        in_specs=[
            pl.BlockSpec((chunk, 1), lambda i: (i, 0)),
            pl.BlockSpec(table.shape, lambda i: (0, 0)),
        ],
        out_specs=pl.BlockSpec((chunk, table.shape[1]), lambda i: (i, 0)),
        cost_estimate=pl.CostEstimate(
            flops=2 * count * table.shape[0] * table.shape[1],
            transcendentals=0,
            bytes_accessed=count * 4 + table.size * 2 + count * table.shape[1] * 2,
        ),
    )(idx_col, table)


def gram_kernel(n_user, rows_ref, gw_ref, user_ref, rw_ref, gram_ref, rhs_ref):
    step = pl.program_id(0)

    @pl.when(step == 0)
    def _():
        gram_ref[...] = jnp.zeros_like(gram_ref)
        rhs_ref[...] = jnp.zeros_like(rhs_ref)

    rows = rows_ref[...]
    rows_t = rows.astype(jnp.float32).T
    weights_t = (rows_t * gw_ref[pl.ds(step, 1), :]).astype(jnp.bfloat16)
    users = user_ref[pl.ds(step, 1), :]
    zero = jnp.zeros((), jnp.bfloat16)
    for user in range(n_user):
        picked = jnp.where(users == user, weights_t, zero)
        gram_ref[user] += jnp.dot(picked, rows, preferred_element_type=jnp.float32)
    slots = lax.broadcasted_iota(jnp.int32, (n_user, users.shape[1]), 0)
    per_user = jnp.where(users == slots, rw_ref[pl.ds(step, 1), :], 0.0)
    high = per_user.astype(jnp.bfloat16)
    low = (per_user - high.astype(jnp.float32)).astype(jnp.bfloat16)
    rhs_ref[...] += jnp.dot(high, rows, preferred_element_type=jnp.float32) + jnp.dot(
        low, rows, preferred_element_type=jnp.float32
    )


def user_grams(rows, gw_lanes, user_lanes, rw_lanes, n_user):
    chunks, chunk = gw_lanes.shape
    width = rows.shape[1]
    return pl.pallas_call(
        functools.partial(gram_kernel, n_user),
        out_shape=(
            jax.ShapeDtypeStruct((n_user, width, width), jnp.float32),
            jax.ShapeDtypeStruct((n_user, width), jnp.float32),
        ),
        grid=(chunks,),
        in_specs=[
            pl.BlockSpec((chunk, width), lambda i: (i, 0)),
            pl.BlockSpec((chunks, chunk), lambda i: (0, 0)),
            pl.BlockSpec((chunks, chunk), lambda i: (0, 0)),
            pl.BlockSpec((chunks, chunk), lambda i: (0, 0)),
        ],
        out_specs=(
            pl.BlockSpec((n_user, width, width), lambda i: (0, 0, 0)),
            pl.BlockSpec((n_user, width), lambda i: (0, 0)),
        ),
        cost_estimate=pl.CostEstimate(
            flops=2 * rows.shape[0] * width * width * (n_user + 2),
            transcendentals=0,
            bytes_accessed=rows.size * 2 + 12 * rows.shape[0] + n_user * width * (width + 1) * 4,
        ),
    )(rows, gw_lanes, user_lanes, rw_lanes)


def shards(item_factors, tile_items, send_tiles, tile_users, tile_counts, recv_tiles):
    highest = lax.Precision.HIGHEST
    rank_width = item_factors.shape[1]
    item_count = item_factors.shape[0]
    n_ent = lax.axis_size("ent")
    n_rep = lax.axis_size("rep")
    tile_slots = tile_items.shape[2]
    tile_rows = tile_items.shape[3]
    seg_count = tile_users.shape[3]
    seg_length = tile_rows // seg_count
    slot_cap = tile_slots // n_ent
    user_block = U_DEV * lax.axis_size("rep")
    item_ids = tile_items.reshape(tile_slots, tile_rows)
    slot_pos = jnp.arange(tile_slots, dtype=jnp.int32) % slot_cap
    live_send = slot_pos < jnp.repeat(send_tiles.reshape(n_ent), slot_cap)
    live_recv = slot_pos < jnp.repeat(recv_tiles.reshape(n_ent), slot_cap)
    partial_gram = lax.dot_general(
        item_factors, item_factors, (((0,), (0,)), ((), ())), preferred_element_type=jnp.float32
    )
    live_rows = jnp.repeat(live_send, tile_rows)
    idx_col = jnp.where(live_rows, item_ids.reshape(-1), -1).reshape(-1, 1)
    picked = gather_rows(item_factors, idx_col)
    incoming = lax.all_to_all(
        picked.reshape(n_ent, slot_cap * tile_rows, rank_width),
        "ent",
        split_axis=0,
        concat_axis=0,
        tiled=True,
    )
    counts_int = tile_counts.reshape(tile_slots, tile_rows)
    counts_f = counts_int.astype(jnp.float32)
    gram_weight = ALPHA * counts_f
    rhs_weight = jnp.where(
        live_recv[:, None] & (counts_int > 0), 1.0 + ALPHA * counts_f, jnp.float32(0.0)
    )
    owners = tile_users.reshape(tile_slots * seg_count)
    selector = owners[None, :] == jnp.arange(user_block, dtype=jnp.int32)[:, None]
    selector_f = selector.astype(jnp.float32)
    rows_all = incoming.reshape(tile_slots * tile_rows, rank_width)
    lane_chunk = 1024
    row_owner = jnp.repeat(owners, seg_length)
    gram_acc, rhs_acc = user_grams(
        rows_all,
        gram_weight.reshape(-1, lane_chunk),
        row_owner.reshape(-1, lane_chunk),
        rhs_weight.reshape(-1, lane_chunk),
        user_block,
    )
    gram_acc = gram_acc.reshape(user_block, rank_width * rank_width)
    identity_mat = jnp.eye(rank_width, dtype=jnp.float32)
    added_term = tree_sum(partial_gram, n_ent * n_rep) + RIDGE * identity_mat
    own_gram, own_rhs = rep_scatter_sum(
        jnp.concatenate([gram_acc, rhs_acc], axis=1), n_rep, U_DEV
    )
    own_factors = solve_users(own_gram.reshape(-1, rank_width, rank_width) + added_term, own_rhs)
    solved = rep_gather(own_factors.astype(jnp.bfloat16), n_rep)
    run_factor = lax.dot_general(
        selector.astype(jnp.bfloat16),
        solved,
        (((0,), (0,)), ((), ())),
        preferred_element_type=jnp.float32,
    ).astype(jnp.bfloat16)
    back_factor, back_weight = (
        lax.all_to_all(
            run_factor.reshape(n_ent, slot_cap, seg_count * rank_width),
            "ent",
            split_axis=0,
            concat_axis=0,
            tiled=True,
        ),
        lax.all_to_all(
            rhs_weight.reshape(n_ent, slot_cap, tile_rows),
            "ent",
            split_axis=0,
            concat_axis=0,
            tiled=True,
        ),
    )
    item_hot = item_ids[:, :, None] == jnp.arange(item_count, dtype=jnp.int32)[None, None, :]
    run_weight = back_weight.reshape(tile_slots * seg_count, seg_length)
    hot_runs = item_hot.reshape(tile_slots * seg_count, seg_length, item_count)
    spread_mat = jnp.sum(jnp.where(hot_runs, run_weight[:, :, None], 0.0), axis=1)
    item_rhs = lax.dot_general(
        spread_mat,
        back_factor.reshape(tile_slots * seg_count, rank_width).astype(jnp.float32),
        (((0,), (0,)), ((), ())),
        precision=highest,
        preferred_element_type=jnp.float32,
    )
    return (own_factors, item_rhs * RHS_SCALE)


def solution(mesh):
    in_specs = (
        P(("ent", "rep"), None),
        P("ent", "rep", None, None),
        P("ent", "rep", None),
        P("ent", "rep", None, None),
        P("ent", "rep", None, None),
        P("ent", "rep", None),
    )
    out_specs = (P(("ent", "rep"), None), P(("ent", "rep"), None))
    return jax.shard_map(shards, mesh=mesh, in_specs=in_specs, out_specs=out_specs, check_vma=False)
```

```python
import functools

import jax
import jax.numpy as jnp
from jax import lax
from jax.experimental import pallas as pl
from jax.experimental.pallas import tpu as pltpu
from jax.sharding import PartitionSpec as P

MESH_ID = pl.DeviceIdType.MESH

U_DEV = 2


ALPHA = 40.0
RIDGE = 1.0
RHS_SCALE = 1.0 / 640.0


def solve_users(gram, rhs):
    lower = jnp.linalg.cholesky(gram)
    halfway = lax.linalg.triangular_solve(lower, rhs[..., None], left_side=True, lower=True)
    result = lax.linalg.triangular_solve(
        lower, halfway, left_side=True, lower=True, transpose_a=True
    )
    return result[..., 0]


def flip_bits(value, mask, bits):
    out = value - value % (1 << bits)
    for bit in range(bits):
        here = (value // (1 << bit)) % 2
        out = out + (1 << bit) * ((1 - here) if (mask >> bit) & 1 else here)
    return out


def doubling_kernel(
    n_rep, low_bits, rounds, x_ref, o_ref, full_recv, piece_recv, piece, gath,
    sem_a, sem_b, sem_c, sem_d, sem_e, sem_f,
):
    flat = lax.axis_index("ent") * n_rep + lax.axis_index("rep")
    group = 1 << low_bits
    rows = x_ref.shape[0] // group
    slot = flat % group

    def place(p):
        return (p // n_rep, p % n_rep)

    def flip(bit):
        step = 1 << bit
        upper = (flat // step) % 2
        return flat + step - 2 * step * upper

    members = [flip_bits(flat, k, low_bits) for k in range(1, group)]
    outer = [flip(bit) for bit in range(low_bits, rounds)]
    barrier = pltpu.get_barrier_semaphore()
    for p in members + outer:
        pl.semaphore_signal(barrier, inc=1, device_id=place(p), device_id_type=MESH_ID)
    pl.semaphore_wait(barrier, len(members) + len(outer))

    o_ref[...] = x_ref[...]
    for bit in range(low_bits):
        copy = pltpu.make_async_remote_copy(
            src_ref=o_ref, dst_ref=full_recv.at[bit], send_sem=sem_a.at[bit],
            recv_sem=sem_b.at[bit], device_id=place(flip(bit)), device_id_type=MESH_ID,
        )
        copy.start()
        copy.wait_recv()
        copy.wait_send()
        o_ref[...] = o_ref[...] + full_recv[bit]

    piece[...] = o_ref[pl.ds(pl.multiple_of(slot * rows, rows), rows), :]
    for index, p in enumerate(outer):
        copy = pltpu.make_async_remote_copy(
            src_ref=piece, dst_ref=piece_recv.at[index], send_sem=sem_c.at[index],
            recv_sem=sem_d.at[index], device_id=place(p), device_id_type=MESH_ID,
        )
        copy.start()
        copy.wait_recv()
        copy.wait_send()
        piece[...] = piece[...] + piece_recv[index]

    gath[slot] = piece[...]
    sends = []
    for index, p in enumerate(members):
        copy = pltpu.make_async_remote_copy(
            src_ref=piece, dst_ref=gath.at[slot], send_sem=sem_e.at[index],
            recv_sem=sem_f.at[slot], device_id=place(p), device_id_type=MESH_ID,
        )
        copy.start()
        sends.append(copy)
    for k in range(1, group):
        source = flip_bits(slot, k, low_bits)
        pltpu.make_async_remote_copy(
            src_ref=piece, dst_ref=gath.at[source], send_sem=sem_e.at[k - 1],
            recv_sem=sem_f.at[source], device_id=place(members[k - 1]), device_id_type=MESH_ID,
        ).wait_recv()
    for copy in sends:
        copy.wait_send()
    for part in range(group):
        o_ref[pl.ds(part * rows, rows), :] = gath[part]


def tree_sum(value, count):
    rounds = count.bit_length() - 1
    n_rep = lax.axis_size("rep")
    low_bits = (n_rep * 2).bit_length() - 1
    group = 1 << low_bits
    rows = value.shape[0] // group
    outer = rounds - low_bits
    return pl.pallas_call(
        functools.partial(doubling_kernel, n_rep, low_bits, rounds),
        out_shape=jax.ShapeDtypeStruct(value.shape, value.dtype),
        in_specs=[pl.BlockSpec(memory_space=pltpu.VMEM)],
        out_specs=pl.BlockSpec(memory_space=pltpu.VMEM),
        scratch_shapes=[
            pltpu.VMEM((low_bits,) + value.shape, value.dtype),
            pltpu.VMEM((outer, rows, value.shape[1]), value.dtype),
            pltpu.VMEM((rows, value.shape[1]), value.dtype),
            pltpu.VMEM((group, rows, value.shape[1]), value.dtype),
            pltpu.SemaphoreType.DMA((low_bits,)),
            pltpu.SemaphoreType.DMA((low_bits,)),
            pltpu.SemaphoreType.DMA((outer,)),
            pltpu.SemaphoreType.DMA((outer,)),
            pltpu.SemaphoreType.DMA((group - 1,)),
            pltpu.SemaphoreType.DMA((group,)),
        ],
        compiler_params=pltpu.CompilerParams(collective_id=0, has_side_effects=True),
    )(value)


def rep_scatter_sum(acc, n_rep, per_dev):
    me = lax.axis_index("rep")
    total = lax.dynamic_slice_in_dim(acc, me * per_dev, per_dev, 0)
    for shift in range(1, n_rep):
        dest = (me + shift) % n_rep
        piece = lax.dynamic_slice_in_dim(acc, dest * per_dev, per_dev, 0)
        pairs = [(i, (i + shift) % n_rep) for i in range(n_rep)]
        total = total + lax.ppermute(piece, "rep", pairs)
    width = acc.shape[1]
    return total[:, : width - 128], total[:, width - 128 :]


def rep_gather(value, n_rep):
    me = lax.axis_index("rep")
    got = [value]
    for shift in range(1, n_rep):
        pairs = [(i, (i + shift) % n_rep) for i in range(n_rep)]
        got.append(lax.ppermute(value, "rep", pairs))
    stacked = jnp.stack(got)
    order = (me - jnp.arange(n_rep)) % n_rep
    return jnp.take(stacked, order, axis=0).reshape(-1, value.shape[-1])


def gather_kernel(idx_ref, table_t_ref, out_ref):
    step = pl.program_id(0)
    idx = idx_ref[pl.ds(step, 1), :]
    picks = lax.broadcasted_iota(jnp.int32, (table_t_ref.shape[1], idx.shape[1]), 0) == idx
    rows_t = jnp.dot(table_t_ref[...], picks.astype(jnp.bfloat16), preferred_element_type=jnp.float32)
    out_ref[...] = rows_t.T.astype(out_ref.dtype)


def gather_rows(table, idx, chunk=512):
    count = idx.shape[0]
    idx_lanes = idx.reshape(count // chunk, chunk)
    return pl.pallas_call(
        gather_kernel,
        out_shape=jax.ShapeDtypeStruct((count, table.shape[1]), table.dtype),
        grid=(count // chunk,),
        in_specs=[
            pl.BlockSpec(idx_lanes.shape, lambda i: (0, 0)),
            pl.BlockSpec((table.shape[1], table.shape[0]), lambda i: (0, 0)),
        ],
        out_specs=pl.BlockSpec((chunk, table.shape[1]), lambda i: (i, 0)),
        cost_estimate=pl.CostEstimate(
            flops=2 * count * table.shape[0] * table.shape[1],
            transcendentals=0,
            bytes_accessed=count * 4 + table.size * 2 + count * table.shape[1] * 2,
        ),
    )(idx_lanes, table.T)


def gram_kernel(n_user, rows_ref, gw_ref, user_ref, rw_ref, gram_ref, rhs_ref):
    step = pl.program_id(0)

    @pl.when(step == 0)
    def _():
        gram_ref[...] = jnp.zeros_like(gram_ref)
        rhs_ref[...] = jnp.zeros_like(rhs_ref)

    rows = rows_ref[...]
    rows_t = rows.astype(jnp.float32).T
    weights_t = (rows_t * gw_ref[pl.ds(step, 1), :]).astype(jnp.bfloat16)
    users = user_ref[pl.ds(step, 1), :]
    zero = jnp.zeros((), jnp.bfloat16)
    for user in range(n_user):
        picked = jnp.where(users == user, weights_t, zero)
        gram_ref[user] += jnp.dot(picked, rows, preferred_element_type=jnp.float32)
    slots = lax.broadcasted_iota(jnp.int32, (n_user, users.shape[1]), 0)
    per_user = jnp.where(users == slots, rw_ref[pl.ds(step, 1), :], 0.0)
    high = per_user.astype(jnp.bfloat16)
    low = (per_user - high.astype(jnp.float32)).astype(jnp.bfloat16)
    rhs_ref[...] += jnp.dot(high, rows, preferred_element_type=jnp.float32) + jnp.dot(
        low, rows, preferred_element_type=jnp.float32
    )


def user_grams(rows, gw_lanes, user_lanes, rw_lanes, n_user):
    chunks, chunk = gw_lanes.shape
    width = rows.shape[1]
    return pl.pallas_call(
        functools.partial(gram_kernel, n_user),
        out_shape=(
            jax.ShapeDtypeStruct((n_user, width, width), jnp.float32),
            jax.ShapeDtypeStruct((n_user, width), jnp.float32),
        ),
        grid=(chunks,),
        in_specs=[
            pl.BlockSpec((chunk, width), lambda i: (i, 0)),
            pl.BlockSpec((chunks, chunk), lambda i: (0, 0)),
            pl.BlockSpec((chunks, chunk), lambda i: (0, 0)),
            pl.BlockSpec((chunks, chunk), lambda i: (0, 0)),
        ],
        out_specs=(
            pl.BlockSpec((n_user, width, width), lambda i: (0, 0, 0)),
            pl.BlockSpec((n_user, width), lambda i: (0, 0)),
        ),
        cost_estimate=pl.CostEstimate(
            flops=2 * rows.shape[0] * width * width * (n_user + 2),
            transcendentals=0,
            bytes_accessed=rows.size * 2 + 12 * rows.shape[0] + n_user * width * (width + 1) * 4,
        ),
    )(rows, gw_lanes, user_lanes, rw_lanes)


def shards(item_factors, tile_items, send_tiles, tile_users, tile_counts, recv_tiles):
    highest = lax.Precision.HIGHEST
    rank_width = item_factors.shape[1]
    item_count = item_factors.shape[0]
    n_ent = lax.axis_size("ent")
    n_rep = lax.axis_size("rep")
    tile_slots = tile_items.shape[2]
    tile_rows = tile_items.shape[3]
    seg_count = tile_users.shape[3]
    seg_length = tile_rows // seg_count
    slot_cap = tile_slots // n_ent
    user_block = U_DEV * lax.axis_size("rep")
    item_ids = tile_items.reshape(tile_slots, tile_rows)
    slot_pos = jnp.arange(tile_slots, dtype=jnp.int32) % slot_cap
    live_send = slot_pos < jnp.repeat(send_tiles.reshape(n_ent), slot_cap)
    live_recv = slot_pos < jnp.repeat(recv_tiles.reshape(n_ent), slot_cap)
    partial_gram = lax.dot_general(
        item_factors, item_factors, (((0,), (0,)), ((), ())), preferred_element_type=jnp.float32
    )
    live_rows = jnp.repeat(live_send, tile_rows)
    picked = gather_rows(item_factors, jnp.where(live_rows, item_ids.reshape(-1), -1))
    incoming = lax.all_to_all(
        picked.reshape(n_ent, slot_cap * tile_rows, rank_width),
        "ent",
        split_axis=0,
        concat_axis=0,
        tiled=True,
    )
    counts_int = tile_counts.reshape(tile_slots, tile_rows)
    counts_f = counts_int.astype(jnp.float32)
    gram_weight = ALPHA * counts_f
    rhs_weight = jnp.where(
        live_recv[:, None] & (counts_int > 0), 1.0 + ALPHA * counts_f, jnp.float32(0.0)
    )
    owners = tile_users.reshape(tile_slots * seg_count)
    selector = owners[None, :] == jnp.arange(user_block, dtype=jnp.int32)[:, None]
    selector_f = selector.astype(jnp.float32)
    rows_all = incoming.reshape(tile_slots * tile_rows, rank_width)
    lane_chunk = 1024
    row_owner = jnp.repeat(owners, seg_length)
    gram_acc, rhs_acc = user_grams(
        rows_all,
        gram_weight.reshape(-1, lane_chunk),
        row_owner.reshape(-1, lane_chunk),
        rhs_weight.reshape(-1, lane_chunk),
        user_block,
    )
    gram_acc = gram_acc.reshape(user_block, rank_width * rank_width)
    identity_mat = jnp.eye(rank_width, dtype=jnp.float32)
    added_term = tree_sum(partial_gram, n_ent * n_rep) + RIDGE * identity_mat
    own_gram, own_rhs = rep_scatter_sum(
        jnp.concatenate([gram_acc, rhs_acc], axis=1), n_rep, U_DEV
    )
    own_factors = solve_users(own_gram.reshape(-1, rank_width, rank_width) + added_term, own_rhs)
    solved = rep_gather(own_factors.astype(jnp.bfloat16), n_rep)
    run_factor = lax.dot_general(
        selector.astype(jnp.bfloat16),
        solved,
        (((0,), (0,)), ((), ())),
        preferred_element_type=jnp.float32,
    ).astype(jnp.bfloat16)
    back_load = jnp.concatenate(
        [
            run_factor.reshape(tile_slots, seg_count * rank_width),
            counts_int.astype(jnp.bfloat16),
        ],
        axis=1,
    )
    back_load = lax.all_to_all(
        back_load.reshape(n_ent, slot_cap, -1), "ent", split_axis=0, concat_axis=0, tiled=True
    ).reshape(tile_slots, -1)
    back_factor = back_load[:, : seg_count * rank_width]
    back_counts = back_load[:, seg_count * rank_width :].astype(jnp.float32)
    back_weight = jnp.where(
        live_send[:, None] & (back_counts > 0), 1.0 + ALPHA * back_counts, jnp.float32(0.0)
    )
    item_hot = item_ids[:, :, None] == jnp.arange(item_count, dtype=jnp.int32)[None, None, :]
    run_weight = back_weight.reshape(tile_slots * seg_count, seg_length)
    hot_runs = item_hot.reshape(tile_slots * seg_count, seg_length, item_count)
    spread_mat = jnp.sum(jnp.where(hot_runs, run_weight[:, :, None], 0.0), axis=1)
    item_rhs = lax.dot_general(
        spread_mat,
        back_factor.reshape(tile_slots * seg_count, rank_width).astype(jnp.float32),
        (((0,), (0,)), ((), ())),
        precision=highest,
        preferred_element_type=jnp.float32,
    )
    return (own_factors, item_rhs * RHS_SCALE)


def solution(mesh):
    in_specs = (
        P(("ent", "rep"), None),
        P("ent", "rep", None, None),
        P("ent", "rep", None),
        P("ent", "rep", None, None),
        P("ent", "rep", None, None),
        P("ent", "rep", None),
    )
    out_specs = (P(("ent", "rep"), None), P(("ent", "rep"), None))
    return jax.shard_map(shards, mesh=mesh, in_specs=in_specs, out_specs=out_specs, check_vma=False)
```

```python
import functools

import jax
import jax.numpy as jnp
from jax import lax
from jax.experimental import pallas as pl
from jax.experimental.pallas import tpu as pltpu
from jax.sharding import PartitionSpec as P

MESH_ID = pl.DeviceIdType.MESH

U_DEV = 2


ALPHA = 40.0
RIDGE = 1.0
RHS_SCALE = 1.0 / 640.0


def solve_users(gram, rhs):
    lower = jnp.linalg.cholesky(gram)
    halfway = lax.linalg.triangular_solve(lower, rhs[..., None], left_side=True, lower=True)
    result = lax.linalg.triangular_solve(
        lower, halfway, left_side=True, lower=True, transpose_a=True
    )
    return result[..., 0]


def flip_bits(value, mask, bits):
    out = value - value % (1 << bits)
    for bit in range(bits):
        here = (value // (1 << bit)) % 2
        out = out + (1 << bit) * ((1 - here) if (mask >> bit) & 1 else here)
    return out


def doubling_kernel(
    n_rep, low_bits, rounds, x_ref, o_ref, full_recv, piece_recv, piece, gath,
    sem_a, sem_b, sem_c, sem_d, sem_e, sem_f,
):
    flat = lax.axis_index("ent") * n_rep + lax.axis_index("rep")
    group = 1 << low_bits
    rows = x_ref.shape[0] // group
    slot = flat % group

    def place(p):
        return (p // n_rep, p % n_rep)

    def flip(bit):
        step = 1 << bit
        upper = (flat // step) % 2
        return flat + step - 2 * step * upper

    members = [flip_bits(flat, k, low_bits) for k in range(1, group)]
    outer = [flip(bit) for bit in range(low_bits, rounds)]
    barrier = pltpu.get_barrier_semaphore()
    for p in members + outer:
        pl.semaphore_signal(barrier, inc=1, device_id=place(p), device_id_type=MESH_ID)
    pl.semaphore_wait(barrier, len(members) + len(outer))

    o_ref[...] = x_ref[...]
    for bit in range(low_bits):
        copy = pltpu.make_async_remote_copy(
            src_ref=o_ref, dst_ref=full_recv.at[bit], send_sem=sem_a.at[bit],
            recv_sem=sem_b.at[bit], device_id=place(flip(bit)), device_id_type=MESH_ID,
        )
        copy.start()
        copy.wait_recv()
        copy.wait_send()
        o_ref[...] = o_ref[...] + full_recv[bit]

    piece[...] = o_ref[pl.ds(pl.multiple_of(slot * rows, rows), rows), :]
    for index, p in enumerate(outer):
        copy = pltpu.make_async_remote_copy(
            src_ref=piece, dst_ref=piece_recv.at[index], send_sem=sem_c.at[index],
            recv_sem=sem_d.at[index], device_id=place(p), device_id_type=MESH_ID,
        )
        copy.start()
        copy.wait_recv()
        copy.wait_send()
        piece[...] = piece[...] + piece_recv[index]

    gath[slot] = piece[...]
    sends = []
    for index, p in enumerate(members):
        copy = pltpu.make_async_remote_copy(
            src_ref=piece, dst_ref=gath.at[slot], send_sem=sem_e.at[index],
            recv_sem=sem_f.at[slot], device_id=place(p), device_id_type=MESH_ID,
        )
        copy.start()
        sends.append(copy)
    for k in range(1, group):
        source = flip_bits(slot, k, low_bits)
        pltpu.make_async_remote_copy(
            src_ref=piece, dst_ref=gath.at[source], send_sem=sem_e.at[k - 1],
            recv_sem=sem_f.at[source], device_id=place(members[k - 1]), device_id_type=MESH_ID,
        ).wait_recv()
    for copy in sends:
        copy.wait_send()
    for part in range(group):
        o_ref[pl.ds(part * rows, rows), :] = gath[part]


def tree_sum(value, count):
    rounds = count.bit_length() - 1
    n_rep = lax.axis_size("rep")
    low_bits = (n_rep * 2).bit_length() - 1
    group = 1 << low_bits
    rows = value.shape[0] // group
    outer = rounds - low_bits
    return pl.pallas_call(
        functools.partial(doubling_kernel, n_rep, low_bits, rounds),
        out_shape=jax.ShapeDtypeStruct(value.shape, value.dtype),
        in_specs=[pl.BlockSpec(memory_space=pltpu.VMEM)],
        out_specs=pl.BlockSpec(memory_space=pltpu.VMEM),
        scratch_shapes=[
            pltpu.VMEM((low_bits,) + value.shape, value.dtype),
            pltpu.VMEM((outer, rows, value.shape[1]), value.dtype),
            pltpu.VMEM((rows, value.shape[1]), value.dtype),
            pltpu.VMEM((group, rows, value.shape[1]), value.dtype),
            pltpu.SemaphoreType.DMA((low_bits,)),
            pltpu.SemaphoreType.DMA((low_bits,)),
            pltpu.SemaphoreType.DMA((outer,)),
            pltpu.SemaphoreType.DMA((outer,)),
            pltpu.SemaphoreType.DMA((group - 1,)),
            pltpu.SemaphoreType.DMA((group,)),
        ],
        compiler_params=pltpu.CompilerParams(collective_id=0, has_side_effects=True),
    )(value)


def rep_peers(n_rep):
    me = lax.axis_index("rep")
    return me, [(me + shift) % n_rep for shift in range(1, n_rep)]


def scatter_kernel(n_rep, acc_ref, out_ref, recv, send_sem, recv_sem):
    me, peers = rep_peers(n_rep)
    ent = lax.axis_index("ent")
    barrier = pltpu.get_barrier_semaphore()
    for peer in peers:
        pl.semaphore_signal(barrier, inc=1, device_id=(ent, peer), device_id_type=MESH_ID)
    pl.semaphore_wait(barrier, n_rep - 1)
    copies = []
    for index, peer in enumerate(peers):
        copy = pltpu.make_async_remote_copy(
            src_ref=acc_ref.at[peer], dst_ref=recv.at[index], send_sem=send_sem.at[index],
            recv_sem=recv_sem.at[index], device_id=(ent, peer), device_id_type=MESH_ID,
        )
        copy.start()
        copies.append(copy)
    total = acc_ref[me]
    for index, copy in enumerate(copies):
        copy.wait_recv()
        total = total + recv[index]
    for copy in copies:
        copy.wait_send()
    out_ref[...] = total


def rep_scatter_sum(acc, n_rep, per_dev):
    blocks = acc.reshape(n_rep, per_dev, acc.shape[1])
    total = pl.pallas_call(
        functools.partial(scatter_kernel, n_rep),
        out_shape=jax.ShapeDtypeStruct(blocks.shape[1:], acc.dtype),
        in_specs=[pl.BlockSpec(memory_space=pltpu.VMEM)],
        out_specs=pl.BlockSpec(memory_space=pltpu.VMEM),
        scratch_shapes=[
            pltpu.VMEM((n_rep - 1,) + blocks.shape[1:], acc.dtype),
            pltpu.SemaphoreType.DMA((n_rep - 1,)),
            pltpu.SemaphoreType.DMA((n_rep - 1,)),
        ],
        compiler_params=pltpu.CompilerParams(collective_id=1, has_side_effects=True),
    )(blocks)
    width = acc.shape[1]
    return total[:, : width - 128], total[:, width - 128 :]


def allgather_kernel(n_rep, val_ref, out_ref, gath, send_sem, recv_sem):
    me, peers = rep_peers(n_rep)
    ent = lax.axis_index("ent")
    barrier = pltpu.get_barrier_semaphore()
    for peer in peers:
        pl.semaphore_signal(barrier, inc=1, device_id=(ent, peer), device_id_type=MESH_ID)
    pl.semaphore_wait(barrier, n_rep - 1)
    copies = []
    for index, peer in enumerate(peers):
        copy = pltpu.make_async_remote_copy(
            src_ref=val_ref, dst_ref=gath.at[me], send_sem=send_sem.at[index],
            recv_sem=recv_sem.at[me], device_id=(ent, peer), device_id_type=MESH_ID,
        )
        copy.start()
        copies.append(copy)
    gath[me] = val_ref[...]
    for index in range(n_rep - 1):
        source = peers[index]
        pltpu.make_async_remote_copy(
            src_ref=val_ref, dst_ref=gath.at[source], send_sem=send_sem.at[index],
            recv_sem=recv_sem.at[source], device_id=(ent, source), device_id_type=MESH_ID,
        ).wait_recv()
    for copy in copies:
        copy.wait_send()
    out_ref[...] = gath[...]


def rep_gather(value, n_rep):
    out = pl.pallas_call(
        functools.partial(allgather_kernel, n_rep),
        out_shape=jax.ShapeDtypeStruct((n_rep,) + value.shape, value.dtype),
        in_specs=[pl.BlockSpec(memory_space=pltpu.VMEM)],
        out_specs=pl.BlockSpec(memory_space=pltpu.VMEM),
        scratch_shapes=[
            pltpu.VMEM((n_rep,) + value.shape, value.dtype),
            pltpu.SemaphoreType.DMA((n_rep - 1,)),
            pltpu.SemaphoreType.DMA((n_rep,)),
        ],
        compiler_params=pltpu.CompilerParams(collective_id=2, has_side_effects=True),
    )(value)
    return out.reshape(-1, value.shape[-1])


def gather_kernel(idx_ref, table_t_ref, out_ref):
    step = pl.program_id(0)
    idx = idx_ref[pl.ds(step, 1), :]
    picks = lax.broadcasted_iota(jnp.int32, (table_t_ref.shape[1], idx.shape[1]), 0) == idx
    rows_t = jnp.dot(table_t_ref[...], picks.astype(jnp.bfloat16), preferred_element_type=jnp.float32)
    out_ref[...] = rows_t.T.astype(out_ref.dtype)


def gather_rows(table, idx, chunk=512):
    count = idx.shape[0]
    idx_lanes = idx.reshape(count // chunk, chunk)
    return pl.pallas_call(
        gather_kernel,
        out_shape=jax.ShapeDtypeStruct((count, table.shape[1]), table.dtype),
        grid=(count // chunk,),
        in_specs=[
            pl.BlockSpec(idx_lanes.shape, lambda i: (0, 0)),
            pl.BlockSpec((table.shape[1], table.shape[0]), lambda i: (0, 0)),
        ],
        out_specs=pl.BlockSpec((chunk, table.shape[1]), lambda i: (i, 0)),
        cost_estimate=pl.CostEstimate(
            flops=2 * count * table.shape[0] * table.shape[1],
            transcendentals=0,
            bytes_accessed=count * 4 + table.size * 2 + count * table.shape[1] * 2,
        ),
    )(idx_lanes, table.T)


def gram_kernel(n_user, rows_ref, gw_ref, user_ref, rw_ref, gram_ref, rhs_ref):
    step = pl.program_id(0)

    @pl.when(step == 0)
    def _():
        gram_ref[...] = jnp.zeros_like(gram_ref)
        rhs_ref[...] = jnp.zeros_like(rhs_ref)

    rows = rows_ref[...]
    rows_t = rows.astype(jnp.float32).T
    weights_t = (rows_t * gw_ref[pl.ds(step, 1), :]).astype(jnp.bfloat16)
    users = user_ref[pl.ds(step, 1), :]
    zero = jnp.zeros((), jnp.bfloat16)
    for user in range(n_user):
        picked = jnp.where(users == user, weights_t, zero)
        gram_ref[user] += jnp.dot(picked, rows, preferred_element_type=jnp.float32)
    slots = lax.broadcasted_iota(jnp.int32, (n_user, users.shape[1]), 0)
    per_user = jnp.where(users == slots, rw_ref[pl.ds(step, 1), :], 0.0)
    high = per_user.astype(jnp.bfloat16)
    low = (per_user - high.astype(jnp.float32)).astype(jnp.bfloat16)
    rhs_ref[...] += jnp.dot(high, rows, preferred_element_type=jnp.float32) + jnp.dot(
        low, rows, preferred_element_type=jnp.float32
    )


def user_grams(rows, gw_lanes, user_lanes, rw_lanes, n_user):
    chunks, chunk = gw_lanes.shape
    width = rows.shape[1]
    return pl.pallas_call(
        functools.partial(gram_kernel, n_user),
        out_shape=(
            jax.ShapeDtypeStruct((n_user, width, width), jnp.float32),
            jax.ShapeDtypeStruct((n_user, width), jnp.float32),
        ),
        grid=(chunks,),
        in_specs=[
            pl.BlockSpec((chunk, width), lambda i: (i, 0)),
            pl.BlockSpec((chunks, chunk), lambda i: (0, 0)),
            pl.BlockSpec((chunks, chunk), lambda i: (0, 0)),
            pl.BlockSpec((chunks, chunk), lambda i: (0, 0)),
        ],
        out_specs=(
            pl.BlockSpec((n_user, width, width), lambda i: (0, 0, 0)),
            pl.BlockSpec((n_user, width), lambda i: (0, 0)),
        ),
        cost_estimate=pl.CostEstimate(
            flops=2 * rows.shape[0] * width * width * (n_user + 2),
            transcendentals=0,
            bytes_accessed=rows.size * 2 + 12 * rows.shape[0] + n_user * width * (width + 1) * 4,
        ),
    )(rows, gw_lanes, user_lanes, rw_lanes)


def shards(item_factors, tile_items, send_tiles, tile_users, tile_counts, recv_tiles):
    highest = lax.Precision.HIGHEST
    rank_width = item_factors.shape[1]
    item_count = item_factors.shape[0]
    n_ent = lax.axis_size("ent")
    n_rep = lax.axis_size("rep")
    tile_slots = tile_items.shape[2]
    tile_rows = tile_items.shape[3]
    seg_count = tile_users.shape[3]
    seg_length = tile_rows // seg_count
    slot_cap = tile_slots // n_ent
    user_block = U_DEV * lax.axis_size("rep")
    item_ids = tile_items.reshape(tile_slots, tile_rows)
    slot_pos = jnp.arange(tile_slots, dtype=jnp.int32) % slot_cap
    live_send = slot_pos < jnp.repeat(send_tiles.reshape(n_ent), slot_cap)
    live_recv = slot_pos < jnp.repeat(recv_tiles.reshape(n_ent), slot_cap)
    partial_gram = lax.dot_general(
        item_factors, item_factors, (((0,), (0,)), ((), ())), preferred_element_type=jnp.float32
    )
    live_rows = jnp.repeat(live_send, tile_rows)
    picked = gather_rows(item_factors, jnp.where(live_rows, item_ids.reshape(-1), -1))
    incoming = lax.all_to_all(
        picked.reshape(n_ent, slot_cap * tile_rows, rank_width),
        "ent",
        split_axis=0,
        concat_axis=0,
        tiled=True,
    )
    counts_int = tile_counts.reshape(tile_slots, tile_rows)
    counts_f = counts_int.astype(jnp.float32)
    gram_weight = ALPHA * counts_f
    rhs_weight = jnp.where(
        live_recv[:, None] & (counts_int > 0), 1.0 + ALPHA * counts_f, jnp.float32(0.0)
    )
    owners = tile_users.reshape(tile_slots * seg_count)
    selector = owners[None, :] == jnp.arange(user_block, dtype=jnp.int32)[:, None]
    selector_f = selector.astype(jnp.float32)
    rows_all = incoming.reshape(tile_slots * tile_rows, rank_width)
    lane_chunk = 1024
    row_owner = jnp.repeat(owners, seg_length)
    gram_acc, rhs_acc = user_grams(
        rows_all,
        gram_weight.reshape(-1, lane_chunk),
        row_owner.reshape(-1, lane_chunk),
        rhs_weight.reshape(-1, lane_chunk),
        user_block,
    )
    gram_acc = gram_acc.reshape(user_block, rank_width * rank_width)
    identity_mat = jnp.eye(rank_width, dtype=jnp.float32)
    added_term = tree_sum(partial_gram, n_ent * n_rep) + RIDGE * identity_mat
    own_gram, own_rhs = rep_scatter_sum(
        jnp.concatenate([gram_acc, rhs_acc], axis=1), n_rep, U_DEV
    )
    own_factors = solve_users(own_gram.reshape(-1, rank_width, rank_width) + added_term, own_rhs)
    solved = rep_gather(own_factors.astype(jnp.bfloat16), n_rep)
    run_factor = lax.dot_general(
        selector.astype(jnp.bfloat16),
        solved,
        (((0,), (0,)), ((), ())),
        preferred_element_type=jnp.float32,
    ).astype(jnp.bfloat16)
    back_load = jnp.concatenate(
        [
            run_factor.reshape(tile_slots, seg_count * rank_width),
            counts_int.astype(jnp.bfloat16),
        ],
        axis=1,
    )
    back_load = lax.all_to_all(
        back_load.reshape(n_ent, slot_cap, -1), "ent", split_axis=0, concat_axis=0, tiled=True
    ).reshape(tile_slots, -1)
    back_factor = back_load[:, : seg_count * rank_width]
    back_counts = back_load[:, seg_count * rank_width :].astype(jnp.float32)
    back_weight = jnp.where(
        live_send[:, None] & (back_counts > 0), 1.0 + ALPHA * back_counts, jnp.float32(0.0)
    )
    item_hot = item_ids[:, :, None] == jnp.arange(item_count, dtype=jnp.int32)[None, None, :]
    run_weight = back_weight.reshape(tile_slots * seg_count, seg_length)
    hot_runs = item_hot.reshape(tile_slots * seg_count, seg_length, item_count)
    spread_mat = jnp.sum(jnp.where(hot_runs, run_weight[:, :, None], 0.0), axis=1)
    item_rhs = lax.dot_general(
        spread_mat,
        back_factor.reshape(tile_slots * seg_count, rank_width).astype(jnp.float32),
        (((0,), (0,)), ((), ())),
        precision=highest,
        preferred_element_type=jnp.float32,
    )
    return (own_factors, item_rhs * RHS_SCALE)


def solution(mesh):
    in_specs = (
        P(("ent", "rep"), None),
        P("ent", "rep", None, None),
        P("ent", "rep", None),
        P("ent", "rep", None, None),
        P("ent", "rep", None, None),
        P("ent", "rep", None),
    )
    out_specs = (P(("ent", "rep"), None), P(("ent", "rep"), None))
    return jax.shard_map(shards, mesh=mesh, in_specs=in_specs, out_specs=out_specs, check_vma=False)
```

```python
import functools

import jax
import jax.numpy as jnp
from jax import lax
from jax.experimental import pallas as pl
from jax.experimental.pallas import tpu as pltpu
from jax.sharding import PartitionSpec as P

MESH_ID = pl.DeviceIdType.MESH

U_DEV = 2


ALPHA = 40.0
RIDGE = 1.0
RHS_SCALE = 1.0 / 640.0


def cholesky_kernel(gram_ref, rhs_ref, out_ref, a_s, l_s, y_s):
    batch, n, _ = gram_ref.shape
    a_s[...] = gram_ref[...]
    y_s[...] = rhs_ref[...]
    out_ref[...] = jnp.zeros_like(out_ref)
    lane_m = lax.broadcasted_iota(jnp.int32, (n, n), 1)
    sub_m = lax.broadcasted_iota(jnp.int32, (n, n), 0)
    lane_v = lax.broadcasted_iota(jnp.int32, (1, n), 1)
    sub_v = lax.broadcasted_iota(jnp.int32, (n, 1), 0)

    def factor(j, carry):
        for b in range(batch):
            a = a_s[b]
            row = jnp.sum(jnp.where(sub_m == j, a, 0.0), axis=0, keepdims=True)
            col = jnp.sum(jnp.where(lane_m == j, a, 0.0), axis=1, keepdims=True)
            diag = jnp.sum(jnp.where(lane_v == j, row, 0.0), axis=1, keepdims=True)
            inv = 1.0 / jnp.sqrt(diag)
            l_row = jnp.where(lane_v >= j, row, 0.0) * inv
            l_col = jnp.where(sub_v >= j, col, 0.0) * inv
            a_s[b] = a - l_col * l_row
            l_s[b, pl.ds(j, 1), :] = l_row
            y = y_s[pl.ds(b, 1), :]
            y_j = jnp.sum(jnp.where(lane_v == j, y, 0.0), axis=1, keepdims=True) * inv
            y_s[pl.ds(b, 1), :] = jnp.where(lane_v == j, y_j, y - y_j * l_row)
        return carry

    lax.fori_loop(0, n, factor, 0)

    def back(t, carry):
        j = n - 1 - t
        for b in range(batch):
            l_j = l_s[b, pl.ds(j, 1), :]
            x = out_ref[pl.ds(b, 1), :]
            y_j = jnp.sum(jnp.where(lane_v == j, y_s[pl.ds(b, 1), :], 0.0), axis=1, keepdims=True)
            l_jj = jnp.sum(jnp.where(lane_v == j, l_j, 0.0), axis=1, keepdims=True)
            known = jnp.sum(jnp.where(lane_v > j, l_j * x, 0.0), axis=1, keepdims=True)
            out_ref[pl.ds(b, 1), :] = jnp.where(lane_v == j, (y_j - known) / l_jj, x)
        return carry

    lax.fori_loop(0, n, back, 0)


def solve_users(gram, rhs):
    gram = (gram + jnp.swapaxes(gram, -1, -2)) / 2
    batch, n, _ = gram.shape
    return pl.pallas_call(
        cholesky_kernel,
        out_shape=jax.ShapeDtypeStruct((batch, n), jnp.float32),
        in_specs=[pl.BlockSpec(memory_space=pltpu.VMEM)] * 2,
        out_specs=pl.BlockSpec(memory_space=pltpu.VMEM),
        scratch_shapes=[
            pltpu.VMEM((batch, n, n), jnp.float32),
            pltpu.VMEM((batch, n, n), jnp.float32),
            pltpu.VMEM((batch, n), jnp.float32),
        ],
    )(gram, rhs)


def flip_bits(value, mask, bits):
    out = value - value % (1 << bits)
    for bit in range(bits):
        here = (value // (1 << bit)) % 2
        out = out + (1 << bit) * ((1 - here) if (mask >> bit) & 1 else here)
    return out


def doubling_kernel(
    n_rep, low_bits, rounds, x_ref, o_ref, full_recv, piece_recv, piece, gath,
    sem_a, sem_b, sem_c, sem_d, sem_e, sem_f,
):
    flat = lax.axis_index("ent") * n_rep + lax.axis_index("rep")
    group = 1 << low_bits
    rows = x_ref.shape[0] // group
    slot = flat % group

    def place(p):
        return (p // n_rep, p % n_rep)

    def flip(bit):
        step = 1 << bit
        upper = (flat // step) % 2
        return flat + step - 2 * step * upper

    members = [flip_bits(flat, k, low_bits) for k in range(1, group)]
    outer = [flip(bit) for bit in range(low_bits, rounds)]
    barrier = pltpu.get_barrier_semaphore()
    for p in members + outer:
        pl.semaphore_signal(barrier, inc=1, device_id=place(p), device_id_type=MESH_ID)
    pl.semaphore_wait(barrier, len(members) + len(outer))

    o_ref[...] = x_ref[...]
    for bit in range(low_bits):
        copy = pltpu.make_async_remote_copy(
            src_ref=o_ref, dst_ref=full_recv.at[bit], send_sem=sem_a.at[bit],
            recv_sem=sem_b.at[bit], device_id=place(flip(bit)), device_id_type=MESH_ID,
        )
        copy.start()
        copy.wait_recv()
        copy.wait_send()
        o_ref[...] = o_ref[...] + full_recv[bit]

    piece[...] = o_ref[pl.ds(pl.multiple_of(slot * rows, rows), rows), :]
    for index, p in enumerate(outer):
        copy = pltpu.make_async_remote_copy(
            src_ref=piece, dst_ref=piece_recv.at[index], send_sem=sem_c.at[index],
            recv_sem=sem_d.at[index], device_id=place(p), device_id_type=MESH_ID,
        )
        copy.start()
        copy.wait_recv()
        copy.wait_send()
        piece[...] = piece[...] + piece_recv[index]

    gath[slot] = piece[...]
    sends = []
    for index, p in enumerate(members):
        copy = pltpu.make_async_remote_copy(
            src_ref=piece, dst_ref=gath.at[slot], send_sem=sem_e.at[index],
            recv_sem=sem_f.at[slot], device_id=place(p), device_id_type=MESH_ID,
        )
        copy.start()
        sends.append(copy)
    for k in range(1, group):
        source = flip_bits(slot, k, low_bits)
        pltpu.make_async_remote_copy(
            src_ref=piece, dst_ref=gath.at[source], send_sem=sem_e.at[k - 1],
            recv_sem=sem_f.at[source], device_id=place(members[k - 1]), device_id_type=MESH_ID,
        ).wait_recv()
    for copy in sends:
        copy.wait_send()
    for part in range(group):
        o_ref[pl.ds(part * rows, rows), :] = gath[part]


def tree_sum(value, count):
    rounds = count.bit_length() - 1
    n_rep = lax.axis_size("rep")
    low_bits = (n_rep * 2).bit_length() - 1
    group = 1 << low_bits
    rows = value.shape[0] // group
    outer = rounds - low_bits
    return pl.pallas_call(
        functools.partial(doubling_kernel, n_rep, low_bits, rounds),
        out_shape=jax.ShapeDtypeStruct(value.shape, value.dtype),
        in_specs=[pl.BlockSpec(memory_space=pltpu.VMEM)],
        out_specs=pl.BlockSpec(memory_space=pltpu.VMEM),
        scratch_shapes=[
            pltpu.VMEM((low_bits,) + value.shape, value.dtype),
            pltpu.VMEM((outer, rows, value.shape[1]), value.dtype),
            pltpu.VMEM((rows, value.shape[1]), value.dtype),
            pltpu.VMEM((group, rows, value.shape[1]), value.dtype),
            pltpu.SemaphoreType.DMA((low_bits,)),
            pltpu.SemaphoreType.DMA((low_bits,)),
            pltpu.SemaphoreType.DMA((outer,)),
            pltpu.SemaphoreType.DMA((outer,)),
            pltpu.SemaphoreType.DMA((group - 1,)),
            pltpu.SemaphoreType.DMA((group,)),
        ],
        compiler_params=pltpu.CompilerParams(collective_id=0, has_side_effects=True),
    )(value)


def rep_peers(n_rep):
    me = lax.axis_index("rep")
    return me, [(me + shift) % n_rep for shift in range(1, n_rep)]


def scatter_kernel(n_rep, acc_ref, out_ref, recv, send_sem, recv_sem):
    me, peers = rep_peers(n_rep)
    ent = lax.axis_index("ent")
    barrier = pltpu.get_barrier_semaphore()
    for peer in peers:
        pl.semaphore_signal(barrier, inc=1, device_id=(ent, peer), device_id_type=MESH_ID)
    pl.semaphore_wait(barrier, n_rep - 1)
    copies = []
    for index, peer in enumerate(peers):
        copy = pltpu.make_async_remote_copy(
            src_ref=acc_ref.at[peer], dst_ref=recv.at[index], send_sem=send_sem.at[index],
            recv_sem=recv_sem.at[index], device_id=(ent, peer), device_id_type=MESH_ID,
        )
        copy.start()
        copies.append(copy)
    total = acc_ref[me]
    for index, copy in enumerate(copies):
        copy.wait_recv()
        total = total + recv[index]
    for copy in copies:
        copy.wait_send()
    out_ref[...] = total


def rep_scatter_sum(acc, n_rep, per_dev):
    blocks = acc.reshape(n_rep, per_dev, acc.shape[1])
    total = pl.pallas_call(
        functools.partial(scatter_kernel, n_rep),
        out_shape=jax.ShapeDtypeStruct(blocks.shape[1:], acc.dtype),
        in_specs=[pl.BlockSpec(memory_space=pltpu.VMEM)],
        out_specs=pl.BlockSpec(memory_space=pltpu.VMEM),
        scratch_shapes=[
            pltpu.VMEM((n_rep - 1,) + blocks.shape[1:], acc.dtype),
            pltpu.SemaphoreType.DMA((n_rep - 1,)),
            pltpu.SemaphoreType.DMA((n_rep - 1,)),
        ],
        compiler_params=pltpu.CompilerParams(collective_id=1, has_side_effects=True),
    )(blocks)
    width = acc.shape[1]
    return total[:, : width - 128], total[:, width - 128 :]


def allgather_kernel(n_rep, val_ref, out_ref, gath, send_sem, recv_sem):
    me, peers = rep_peers(n_rep)
    ent = lax.axis_index("ent")
    barrier = pltpu.get_barrier_semaphore()
    for peer in peers:
        pl.semaphore_signal(barrier, inc=1, device_id=(ent, peer), device_id_type=MESH_ID)
    pl.semaphore_wait(barrier, n_rep - 1)
    copies = []
    for index, peer in enumerate(peers):
        copy = pltpu.make_async_remote_copy(
            src_ref=val_ref, dst_ref=gath.at[me], send_sem=send_sem.at[index],
            recv_sem=recv_sem.at[me], device_id=(ent, peer), device_id_type=MESH_ID,
        )
        copy.start()
        copies.append(copy)
    gath[me] = val_ref[...]
    for index in range(n_rep - 1):
        source = peers[index]
        pltpu.make_async_remote_copy(
            src_ref=val_ref, dst_ref=gath.at[source], send_sem=send_sem.at[index],
            recv_sem=recv_sem.at[source], device_id=(ent, source), device_id_type=MESH_ID,
        ).wait_recv()
    for copy in copies:
        copy.wait_send()
    out_ref[...] = gath[...]


def rep_gather(value, n_rep):
    out = pl.pallas_call(
        functools.partial(allgather_kernel, n_rep),
        out_shape=jax.ShapeDtypeStruct((n_rep,) + value.shape, value.dtype),
        in_specs=[pl.BlockSpec(memory_space=pltpu.VMEM)],
        out_specs=pl.BlockSpec(memory_space=pltpu.VMEM),
        scratch_shapes=[
            pltpu.VMEM((n_rep,) + value.shape, value.dtype),
            pltpu.SemaphoreType.DMA((n_rep - 1,)),
            pltpu.SemaphoreType.DMA((n_rep,)),
        ],
        compiler_params=pltpu.CompilerParams(collective_id=2, has_side_effects=True),
    )(value)
    return out.reshape(-1, value.shape[-1])


def gather_kernel(idx_ref, table_t_ref, out_ref):
    step = pl.program_id(0)
    idx = idx_ref[pl.ds(step, 1), :]
    picks = lax.broadcasted_iota(jnp.int32, (table_t_ref.shape[1], idx.shape[1]), 0) == idx
    rows_t = jnp.dot(table_t_ref[...], picks.astype(jnp.bfloat16), preferred_element_type=jnp.float32)
    out_ref[...] = rows_t.T.astype(out_ref.dtype)


def gather_rows(table, idx, chunk=512):
    count = idx.shape[0]
    idx_lanes = idx.reshape(count // chunk, chunk)
    return pl.pallas_call(
        gather_kernel,
        out_shape=jax.ShapeDtypeStruct((count, table.shape[1]), table.dtype),
        grid=(count // chunk,),
        in_specs=[
            pl.BlockSpec(idx_lanes.shape, lambda i: (0, 0)),
            pl.BlockSpec((table.shape[1], table.shape[0]), lambda i: (0, 0)),
        ],
        out_specs=pl.BlockSpec((chunk, table.shape[1]), lambda i: (i, 0)),
        cost_estimate=pl.CostEstimate(
            flops=2 * count * table.shape[0] * table.shape[1],
            transcendentals=0,
            bytes_accessed=count * 4 + table.size * 2 + count * table.shape[1] * 2,
        ),
    )(idx_lanes, table.T)


def gram_kernel(n_user, rows_ref, gw_ref, user_ref, rw_ref, gram_ref, rhs_ref):
    step = pl.program_id(0)

    @pl.when(step == 0)
    def _():
        gram_ref[...] = jnp.zeros_like(gram_ref)
        rhs_ref[...] = jnp.zeros_like(rhs_ref)

    rows = rows_ref[...]
    rows_t = rows.astype(jnp.float32).T
    weights_t = (rows_t * gw_ref[pl.ds(step, 1), :]).astype(jnp.bfloat16)
    users = user_ref[pl.ds(step, 1), :]
    zero = jnp.zeros((), jnp.bfloat16)
    for user in range(n_user):
        picked = jnp.where(users == user, weights_t, zero)
        gram_ref[user] += jnp.dot(picked, rows, preferred_element_type=jnp.float32)
    slots = lax.broadcasted_iota(jnp.int32, (n_user, users.shape[1]), 0)
    per_user = jnp.where(users == slots, rw_ref[pl.ds(step, 1), :], 0.0)
    high = per_user.astype(jnp.bfloat16)
    low = (per_user - high.astype(jnp.float32)).astype(jnp.bfloat16)
    rhs_ref[...] += jnp.dot(high, rows, preferred_element_type=jnp.float32) + jnp.dot(
        low, rows, preferred_element_type=jnp.float32
    )


def user_grams(rows, gw_lanes, user_lanes, rw_lanes, n_user):
    chunks, chunk = gw_lanes.shape
    width = rows.shape[1]
    return pl.pallas_call(
        functools.partial(gram_kernel, n_user),
        out_shape=(
            jax.ShapeDtypeStruct((n_user, width, width), jnp.float32),
            jax.ShapeDtypeStruct((n_user, width), jnp.float32),
        ),
        grid=(chunks,),
        in_specs=[
            pl.BlockSpec((chunk, width), lambda i: (i, 0)),
            pl.BlockSpec((chunks, chunk), lambda i: (0, 0)),
            pl.BlockSpec((chunks, chunk), lambda i: (0, 0)),
            pl.BlockSpec((chunks, chunk), lambda i: (0, 0)),
        ],
        out_specs=(
            pl.BlockSpec((n_user, width, width), lambda i: (0, 0, 0)),
            pl.BlockSpec((n_user, width), lambda i: (0, 0)),
        ),
        cost_estimate=pl.CostEstimate(
            flops=2 * rows.shape[0] * width * width * (n_user + 2),
            transcendentals=0,
            bytes_accessed=rows.size * 2 + 12 * rows.shape[0] + n_user * width * (width + 1) * 4,
        ),
    )(rows, gw_lanes, user_lanes, rw_lanes)


def shards(item_factors, tile_items, send_tiles, tile_users, tile_counts, recv_tiles):
    highest = lax.Precision.HIGHEST
    rank_width = item_factors.shape[1]
    item_count = item_factors.shape[0]
    n_ent = lax.axis_size("ent")
    n_rep = lax.axis_size("rep")
    tile_slots = tile_items.shape[2]
    tile_rows = tile_items.shape[3]
    seg_count = tile_users.shape[3]
    seg_length = tile_rows // seg_count
    slot_cap = tile_slots // n_ent
    user_block = U_DEV * lax.axis_size("rep")
    item_ids = tile_items.reshape(tile_slots, tile_rows)
    slot_pos = jnp.arange(tile_slots, dtype=jnp.int32) % slot_cap
    live_send = slot_pos < jnp.repeat(send_tiles.reshape(n_ent), slot_cap)
    live_recv = slot_pos < jnp.repeat(recv_tiles.reshape(n_ent), slot_cap)
    partial_gram = lax.dot_general(
        item_factors, item_factors, (((0,), (0,)), ((), ())), preferred_element_type=jnp.float32
    )
    live_rows = jnp.repeat(live_send, tile_rows)
    picked = gather_rows(item_factors, jnp.where(live_rows, item_ids.reshape(-1), -1))
    incoming = lax.all_to_all(
        picked.reshape(n_ent, slot_cap * tile_rows, rank_width),
        "ent",
        split_axis=0,
        concat_axis=0,
        tiled=True,
    )
    counts_int = tile_counts.reshape(tile_slots, tile_rows)
    counts_f = counts_int.astype(jnp.float32)
    gram_weight = ALPHA * counts_f
    rhs_weight = jnp.where(
        live_recv[:, None] & (counts_int > 0), 1.0 + ALPHA * counts_f, jnp.float32(0.0)
    )
    owners = tile_users.reshape(tile_slots * seg_count)
    selector = owners[None, :] == jnp.arange(user_block, dtype=jnp.int32)[:, None]
    selector_f = selector.astype(jnp.float32)
    rows_all = incoming.reshape(tile_slots * tile_rows, rank_width)
    lane_chunk = 1024
    row_owner = jnp.repeat(owners, seg_length)
    gram_acc, rhs_acc = user_grams(
        rows_all,
        gram_weight.reshape(-1, lane_chunk),
        row_owner.reshape(-1, lane_chunk),
        rhs_weight.reshape(-1, lane_chunk),
        user_block,
    )
    gram_acc = gram_acc.reshape(user_block, rank_width * rank_width)
    identity_mat = jnp.eye(rank_width, dtype=jnp.float32)
    added_term = tree_sum(partial_gram, n_ent * n_rep) + RIDGE * identity_mat
    own_gram, own_rhs = rep_scatter_sum(
        jnp.concatenate([gram_acc, rhs_acc], axis=1), n_rep, U_DEV
    )
    own_factors = solve_users(own_gram.reshape(-1, rank_width, rank_width) + added_term, own_rhs)
    solved = rep_gather(own_factors.astype(jnp.bfloat16), n_rep)
    run_factor = lax.dot_general(
        selector.astype(jnp.bfloat16),
        solved,
        (((0,), (0,)), ((), ())),
        preferred_element_type=jnp.float32,
    ).astype(jnp.bfloat16)
    back_load = jnp.concatenate(
        [
            run_factor.reshape(tile_slots, seg_count * rank_width),
            counts_int.astype(jnp.bfloat16),
        ],
        axis=1,
    )
    back_load = lax.all_to_all(
        back_load.reshape(n_ent, slot_cap, -1), "ent", split_axis=0, concat_axis=0, tiled=True
    ).reshape(tile_slots, -1)
    back_factor = back_load[:, : seg_count * rank_width]
    back_counts = back_load[:, seg_count * rank_width :].astype(jnp.float32)
    back_weight = jnp.where(
        live_send[:, None] & (back_counts > 0), 1.0 + ALPHA * back_counts, jnp.float32(0.0)
    )
    item_hot = item_ids[:, :, None] == jnp.arange(item_count, dtype=jnp.int32)[None, None, :]
    run_weight = back_weight.reshape(tile_slots * seg_count, seg_length)
    hot_runs = item_hot.reshape(tile_slots * seg_count, seg_length, item_count)
    spread_mat = jnp.sum(jnp.where(hot_runs, run_weight[:, :, None], 0.0), axis=1)
    item_rhs = lax.dot_general(
        spread_mat,
        back_factor.reshape(tile_slots * seg_count, rank_width).astype(jnp.float32),
        (((0,), (0,)), ((), ())),
        precision=highest,
        preferred_element_type=jnp.float32,
    )
    return (own_factors, item_rhs * RHS_SCALE)


def solution(mesh):
    in_specs = (
        P(("ent", "rep"), None),
        P("ent", "rep", None, None),
        P("ent", "rep", None),
        P("ent", "rep", None, None),
        P("ent", "rep", None, None),
        P("ent", "rep", None),
    )
    out_specs = (P(("ent", "rep"), None), P(("ent", "rep"), None))
    return jax.shard_map(shards, mesh=mesh, in_specs=in_specs, out_specs=out_specs, check_vma=False)
```

```python
import functools

import jax
import jax.numpy as jnp
from jax import lax
from jax.experimental import pallas as pl
from jax.experimental.pallas import tpu as pltpu
from jax.sharding import PartitionSpec as P

MESH_ID = pl.DeviceIdType.MESH

U_DEV = 2


ALPHA = 40.0
RIDGE = 1.0
RHS_SCALE = 1.0 / 640.0


def cholesky_kernel(gram_ref, rhs_ref, out_ref, a_s, l_s, y_s):
    batch, n, _ = gram_ref.shape
    a_s[...] = gram_ref[...]
    y_s[...] = rhs_ref[...]
    out_ref[...] = jnp.zeros_like(out_ref)
    lane_m = lax.broadcasted_iota(jnp.int32, (n, n), 1)
    sub_m = lax.broadcasted_iota(jnp.int32, (n, n), 0)
    lane_v = lax.broadcasted_iota(jnp.int32, (1, n), 1)
    sub_v = lax.broadcasted_iota(jnp.int32, (n, 1), 0)

    def factor(j, carry):
        for b in range(batch):
            a = a_s[b]
            row = jnp.sum(jnp.where(sub_m == j, a, 0.0), axis=0, keepdims=True)
            col = jnp.sum(jnp.where(lane_m == j, a, 0.0), axis=1, keepdims=True)
            diag = jnp.sum(jnp.where(lane_v == j, row, 0.0), axis=1, keepdims=True)
            inv = 1.0 / jnp.sqrt(diag)
            l_row = jnp.where(lane_v >= j, row, 0.0) * inv
            l_col = jnp.where(sub_v >= j, col, 0.0) * inv
            a_s[b] = a - l_col * l_row
            l_s[b, pl.ds(j, 1), :] = l_row
            y = y_s[pl.ds(b, 1), :]
            y_j = jnp.sum(jnp.where(lane_v == j, y, 0.0), axis=1, keepdims=True) * inv
            y_s[pl.ds(b, 1), :] = jnp.where(lane_v == j, y_j, y - y_j * l_row)
        return carry

    lax.fori_loop(0, n, factor, 0)

    def back(t, carry):
        j = n - 1 - t
        for b in range(batch):
            l_j = l_s[b, pl.ds(j, 1), :]
            x = out_ref[pl.ds(b, 1), :]
            y_j = jnp.sum(jnp.where(lane_v == j, y_s[pl.ds(b, 1), :], 0.0), axis=1, keepdims=True)
            l_jj = jnp.sum(jnp.where(lane_v == j, l_j, 0.0), axis=1, keepdims=True)
            known = jnp.sum(jnp.where(lane_v > j, l_j * x, 0.0), axis=1, keepdims=True)
            out_ref[pl.ds(b, 1), :] = jnp.where(lane_v == j, (y_j - known) / l_jj, x)
        return carry

    lax.fori_loop(0, n, back, 0)


def solve_users(gram, rhs):
    gram = (gram + jnp.swapaxes(gram, -1, -2)) / 2
    batch, n, _ = gram.shape
    return pl.pallas_call(
        cholesky_kernel,
        out_shape=jax.ShapeDtypeStruct((batch, n), jnp.float32),
        in_specs=[pl.BlockSpec(memory_space=pltpu.VMEM)] * 2,
        out_specs=pl.BlockSpec(memory_space=pltpu.VMEM),
        scratch_shapes=[
            pltpu.VMEM((batch, n, n), jnp.float32),
            pltpu.VMEM((batch, n, n), jnp.float32),
            pltpu.VMEM((batch, n), jnp.float32),
        ],
    )(gram, rhs)


def flip_bits(value, mask, bits):
    out = value - value % (1 << bits)
    for bit in range(bits):
        here = (value // (1 << bit)) % 2
        out = out + (1 << bit) * ((1 - here) if (mask >> bit) & 1 else here)
    return out


def doubling_kernel(
    n_rep, low_bits, rounds, x_ref, o_ref, full_recv, piece_recv, piece, gath,
    sem_a, sem_b, sem_c, sem_d, sem_e, sem_f,
):
    flat = lax.axis_index("ent") * n_rep + lax.axis_index("rep")
    group = 1 << low_bits
    rows = x_ref.shape[0] // group
    slot = flat % group

    def place(p):
        return (p // n_rep, p % n_rep)

    def flip(bit):
        step = 1 << bit
        upper = (flat // step) % 2
        return flat + step - 2 * step * upper

    members = [flip_bits(flat, k, low_bits) for k in range(1, group)]
    outer = [flip(bit) for bit in range(low_bits, rounds)]
    barrier = pltpu.get_barrier_semaphore()
    for p in members + outer:
        pl.semaphore_signal(barrier, inc=1, device_id=place(p), device_id_type=MESH_ID)
    pl.semaphore_wait(barrier, len(members) + len(outer))

    o_ref[...] = x_ref[...]
    for bit in range(low_bits):
        copy = pltpu.make_async_remote_copy(
            src_ref=o_ref, dst_ref=full_recv.at[bit], send_sem=sem_a.at[bit],
            recv_sem=sem_b.at[bit], device_id=place(flip(bit)), device_id_type=MESH_ID,
        )
        copy.start()
        copy.wait_recv()
        copy.wait_send()
        o_ref[...] = o_ref[...] + full_recv[bit]

    piece[...] = o_ref[pl.ds(pl.multiple_of(slot * rows, rows), rows), :]
    for index, p in enumerate(outer):
        copy = pltpu.make_async_remote_copy(
            src_ref=piece, dst_ref=piece_recv.at[index], send_sem=sem_c.at[index],
            recv_sem=sem_d.at[index], device_id=place(p), device_id_type=MESH_ID,
        )
        copy.start()
        copy.wait_recv()
        copy.wait_send()
        piece[...] = piece[...] + piece_recv[index]

    gath[slot] = piece[...]
    sends = []
    for index, p in enumerate(members):
        copy = pltpu.make_async_remote_copy(
            src_ref=piece, dst_ref=gath.at[slot], send_sem=sem_e.at[index],
            recv_sem=sem_f.at[slot], device_id=place(p), device_id_type=MESH_ID,
        )
        copy.start()
        sends.append(copy)
    for k in range(1, group):
        source = flip_bits(slot, k, low_bits)
        pltpu.make_async_remote_copy(
            src_ref=piece, dst_ref=gath.at[source], send_sem=sem_e.at[k - 1],
            recv_sem=sem_f.at[source], device_id=place(members[k - 1]), device_id_type=MESH_ID,
        ).wait_recv()
    for copy in sends:
        copy.wait_send()
    for part in range(group):
        o_ref[pl.ds(part * rows, rows), :] = gath[part]


def tree_sum(value, count):
    rounds = count.bit_length() - 1
    n_rep = lax.axis_size("rep")
    low_bits = (n_rep * 2).bit_length() - 1
    group = 1 << low_bits
    rows = value.shape[0] // group
    outer = rounds - low_bits
    return pl.pallas_call(
        functools.partial(doubling_kernel, n_rep, low_bits, rounds),
        out_shape=jax.ShapeDtypeStruct(value.shape, value.dtype),
        in_specs=[pl.BlockSpec(memory_space=pltpu.VMEM)],
        out_specs=pl.BlockSpec(memory_space=pltpu.VMEM),
        scratch_shapes=[
            pltpu.VMEM((low_bits,) + value.shape, value.dtype),
            pltpu.VMEM((outer, rows, value.shape[1]), value.dtype),
            pltpu.VMEM((rows, value.shape[1]), value.dtype),
            pltpu.VMEM((group, rows, value.shape[1]), value.dtype),
            pltpu.SemaphoreType.DMA((low_bits,)),
            pltpu.SemaphoreType.DMA((low_bits,)),
            pltpu.SemaphoreType.DMA((outer,)),
            pltpu.SemaphoreType.DMA((outer,)),
            pltpu.SemaphoreType.DMA((group - 1,)),
            pltpu.SemaphoreType.DMA((group,)),
        ],
        compiler_params=pltpu.CompilerParams(collective_id=0, has_side_effects=True),
    )(value)


def rep_peers(n_rep):
    me = lax.axis_index("rep")
    return me, [(me + shift) % n_rep for shift in range(1, n_rep)]


def scatter_kernel(n_rep, acc_ref, out_ref, recv, send_sem, recv_sem):
    me, peers = rep_peers(n_rep)
    ent = lax.axis_index("ent")
    barrier = pltpu.get_barrier_semaphore()
    for peer in peers:
        pl.semaphore_signal(barrier, inc=1, device_id=(ent, peer), device_id_type=MESH_ID)
    pl.semaphore_wait(barrier, n_rep - 1)
    copies = []
    for index, peer in enumerate(peers):
        copy = pltpu.make_async_remote_copy(
            src_ref=acc_ref.at[peer], dst_ref=recv.at[index], send_sem=send_sem.at[index],
            recv_sem=recv_sem.at[index], device_id=(ent, peer), device_id_type=MESH_ID,
        )
        copy.start()
        copies.append(copy)
    total = acc_ref[me]
    for index, copy in enumerate(copies):
        copy.wait_recv()
        total = total + recv[index]
    for copy in copies:
        copy.wait_send()
    out_ref[...] = total


def rep_scatter_sum(blocks, n_rep, per_dev):
    total = pl.pallas_call(
        functools.partial(scatter_kernel, n_rep),
        out_shape=jax.ShapeDtypeStruct(blocks.shape[1:], blocks.dtype),
        in_specs=[pl.BlockSpec(memory_space=pltpu.VMEM)],
        out_specs=pl.BlockSpec(memory_space=pltpu.VMEM),
        scratch_shapes=[
            pltpu.VMEM((n_rep - 1,) + blocks.shape[1:], blocks.dtype),
            pltpu.SemaphoreType.DMA((n_rep - 1,)),
            pltpu.SemaphoreType.DMA((n_rep - 1,)),
        ],
        compiler_params=pltpu.CompilerParams(collective_id=1, has_side_effects=True),
    )(blocks)
    width = blocks.shape[2]
    grams = total[: per_dev * width].reshape(per_dev, width, width)
    return grams, total[per_dev * width :]


def allgather_kernel(n_rep, val_ref, out_ref, gath, send_sem, recv_sem):
    me, peers = rep_peers(n_rep)
    ent = lax.axis_index("ent")
    barrier = pltpu.get_barrier_semaphore()
    for peer in peers:
        pl.semaphore_signal(barrier, inc=1, device_id=(ent, peer), device_id_type=MESH_ID)
    pl.semaphore_wait(barrier, n_rep - 1)
    copies = []
    for index, peer in enumerate(peers):
        copy = pltpu.make_async_remote_copy(
            src_ref=val_ref, dst_ref=gath.at[me], send_sem=send_sem.at[index],
            recv_sem=recv_sem.at[me], device_id=(ent, peer), device_id_type=MESH_ID,
        )
        copy.start()
        copies.append(copy)
    gath[me] = val_ref[...]
    for index in range(n_rep - 1):
        source = peers[index]
        pltpu.make_async_remote_copy(
            src_ref=val_ref, dst_ref=gath.at[source], send_sem=send_sem.at[index],
            recv_sem=recv_sem.at[source], device_id=(ent, source), device_id_type=MESH_ID,
        ).wait_recv()
    for copy in copies:
        copy.wait_send()
    out_ref[...] = gath[...]


def rep_gather(value, n_rep):
    out = pl.pallas_call(
        functools.partial(allgather_kernel, n_rep),
        out_shape=jax.ShapeDtypeStruct((n_rep,) + value.shape, value.dtype),
        in_specs=[pl.BlockSpec(memory_space=pltpu.VMEM)],
        out_specs=pl.BlockSpec(memory_space=pltpu.VMEM),
        scratch_shapes=[
            pltpu.VMEM((n_rep,) + value.shape, value.dtype),
            pltpu.SemaphoreType.DMA((n_rep - 1,)),
            pltpu.SemaphoreType.DMA((n_rep,)),
        ],
        compiler_params=pltpu.CompilerParams(collective_id=2, has_side_effects=True),
    )(value)
    return out.reshape(-1, value.shape[-1])


def gather_kernel(idx_ref, table_t_ref, out_ref):
    step = pl.program_id(0)
    idx = idx_ref[pl.ds(step, 1), :]
    picks = lax.broadcasted_iota(jnp.int32, (table_t_ref.shape[1], idx.shape[1]), 0) == idx
    rows_t = jnp.dot(table_t_ref[...], picks.astype(jnp.bfloat16), preferred_element_type=jnp.float32)
    out_ref[...] = rows_t.T.astype(out_ref.dtype)


def gather_rows(table, idx, chunk=512):
    count = idx.shape[0]
    idx_lanes = idx.reshape(count // chunk, chunk)
    return pl.pallas_call(
        gather_kernel,
        out_shape=jax.ShapeDtypeStruct((count, table.shape[1]), table.dtype),
        grid=(count // chunk,),
        in_specs=[
            pl.BlockSpec(idx_lanes.shape, lambda i: (0, 0)),
            pl.BlockSpec((table.shape[1], table.shape[0]), lambda i: (0, 0)),
        ],
        out_specs=pl.BlockSpec((chunk, table.shape[1]), lambda i: (i, 0)),
        cost_estimate=pl.CostEstimate(
            flops=2 * count * table.shape[0] * table.shape[1],
            transcendentals=0,
            bytes_accessed=count * 4 + table.size * 2 + count * table.shape[1] * 2,
        ),
    )(idx_lanes, table.T)


def gram_kernel(n_user, per_dev, rows_ref, gw_ref, user_ref, rw_ref, out_ref):
    step = pl.program_id(0)
    width = rows_ref.shape[1]

    @pl.when(step == 0)
    def _():
        out_ref[...] = jnp.zeros_like(out_ref)

    rows = rows_ref[...]
    rows_t = rows.astype(jnp.float32).T
    weights_t = (rows_t * gw_ref[pl.ds(step, 1), :]).astype(jnp.bfloat16)
    users = user_ref[pl.ds(step, 1), :]
    zero = jnp.zeros((), jnp.bfloat16)
    for user in range(n_user):
        picked = jnp.where(users == user, weights_t, zero)
        block, spot = user // per_dev, (user % per_dev) * width
        out_ref[block, spot : spot + width, :] += jnp.dot(
            picked, rows, preferred_element_type=jnp.float32
        )
    slots = lax.broadcasted_iota(jnp.int32, (n_user, users.shape[1]), 0)
    per_user = jnp.where(users == slots, rw_ref[pl.ds(step, 1), :], 0.0)
    high = per_user.astype(jnp.bfloat16)
    low = (per_user - high.astype(jnp.float32)).astype(jnp.bfloat16)
    rhs = jnp.dot(high, rows, preferred_element_type=jnp.float32) + jnp.dot(
        low, rows, preferred_element_type=jnp.float32
    )
    base = per_dev * width
    for block in range(n_user // per_dev):
        out_ref[block, base : base + per_dev, :] += rhs[block * per_dev : (block + 1) * per_dev]


def user_grams(rows, gw_lanes, user_lanes, rw_lanes, n_user, per_dev):
    chunks, chunk = gw_lanes.shape
    width = rows.shape[1]
    n_block = n_user // per_dev
    block_rows = per_dev * width + per_dev
    return pl.pallas_call(
        functools.partial(gram_kernel, n_user, per_dev),
        out_shape=jax.ShapeDtypeStruct((n_block, block_rows, width), jnp.float32),
        grid=(chunks,),
        in_specs=[
            pl.BlockSpec((chunk, width), lambda i: (i, 0)),
            pl.BlockSpec((chunks, chunk), lambda i: (0, 0)),
            pl.BlockSpec((chunks, chunk), lambda i: (0, 0)),
            pl.BlockSpec((chunks, chunk), lambda i: (0, 0)),
        ],
        out_specs=pl.BlockSpec((n_block, block_rows, width), lambda i: (0, 0, 0)),
        cost_estimate=pl.CostEstimate(
            flops=2 * rows.shape[0] * width * width * (n_user + 2),
            transcendentals=0,
            bytes_accessed=rows.size * 2 + 12 * rows.shape[0] + n_user * width * (width + 1) * 4,
        ),
    )(rows, gw_lanes, user_lanes, rw_lanes)

def shards(item_factors, tile_items, send_tiles, tile_users, tile_counts, recv_tiles):
    highest = lax.Precision.HIGHEST
    rank_width = item_factors.shape[1]
    item_count = item_factors.shape[0]
    n_ent = lax.axis_size("ent")
    n_rep = lax.axis_size("rep")
    tile_slots = tile_items.shape[2]
    tile_rows = tile_items.shape[3]
    seg_count = tile_users.shape[3]
    seg_length = tile_rows // seg_count
    slot_cap = tile_slots // n_ent
    user_block = U_DEV * lax.axis_size("rep")
    item_ids = tile_items.reshape(tile_slots, tile_rows)
    slot_pos = jnp.arange(tile_slots, dtype=jnp.int32) % slot_cap
    live_send = slot_pos < jnp.repeat(send_tiles.reshape(n_ent), slot_cap)
    live_recv = slot_pos < jnp.repeat(recv_tiles.reshape(n_ent), slot_cap)
    partial_gram = lax.dot_general(
        item_factors, item_factors, (((0,), (0,)), ((), ())), preferred_element_type=jnp.float32
    )
    live_rows = jnp.repeat(live_send, tile_rows)
    picked = gather_rows(item_factors, jnp.where(live_rows, item_ids.reshape(-1), -1))
    incoming = lax.all_to_all(
        picked.reshape(n_ent, slot_cap * tile_rows, rank_width),
        "ent",
        split_axis=0,
        concat_axis=0,
        tiled=True,
    )
    counts_int = tile_counts.reshape(tile_slots, tile_rows)
    counts_f = counts_int.astype(jnp.float32)
    gram_weight = ALPHA * counts_f
    rhs_weight = jnp.where(
        live_recv[:, None] & (counts_int > 0), 1.0 + ALPHA * counts_f, jnp.float32(0.0)
    )
    owners = tile_users.reshape(tile_slots * seg_count)
    selector = owners[None, :] == jnp.arange(user_block, dtype=jnp.int32)[:, None]
    selector_f = selector.astype(jnp.float32)
    rows_all = incoming.reshape(tile_slots * tile_rows, rank_width)
    lane_chunk = 1024
    row_owner = jnp.repeat(owners, seg_length)
    gram_blocks = user_grams(
        rows_all,
        gram_weight.reshape(-1, lane_chunk),
        row_owner.reshape(-1, lane_chunk),
        rhs_weight.reshape(-1, lane_chunk),
        user_block,
        U_DEV,
    )
    identity_mat = jnp.eye(rank_width, dtype=jnp.float32)
    added_term = tree_sum(partial_gram, n_ent * n_rep) + RIDGE * identity_mat
    own_gram, own_rhs = rep_scatter_sum(gram_blocks, n_rep, U_DEV)
    own_factors = solve_users(own_gram + added_term, own_rhs)
    solved = rep_gather(own_factors.astype(jnp.bfloat16), n_rep)
    run_factor = lax.dot_general(
        selector.astype(jnp.bfloat16),
        solved,
        (((0,), (0,)), ((), ())),
        preferred_element_type=jnp.float32,
    ).astype(jnp.bfloat16)
    back_load = jnp.concatenate(
        [
            run_factor.reshape(tile_slots, seg_count * rank_width),
            counts_int.astype(jnp.bfloat16),
        ],
        axis=1,
    )
    back_load = lax.all_to_all(
        back_load.reshape(n_ent, slot_cap, -1), "ent", split_axis=0, concat_axis=0, tiled=True
    ).reshape(tile_slots, -1)
    back_factor = back_load[:, : seg_count * rank_width]
    back_counts = back_load[:, seg_count * rank_width :].astype(jnp.float32)
    back_weight = jnp.where(
        live_send[:, None] & (back_counts > 0), 1.0 + ALPHA * back_counts, jnp.float32(0.0)
    )
    item_hot = item_ids[:, :, None] == jnp.arange(item_count, dtype=jnp.int32)[None, None, :]
    run_weight = back_weight.reshape(tile_slots * seg_count, seg_length)
    hot_runs = item_hot.reshape(tile_slots * seg_count, seg_length, item_count)
    spread_mat = jnp.sum(jnp.where(hot_runs, run_weight[:, :, None], 0.0), axis=1)
    item_rhs = lax.dot_general(
        spread_mat,
        back_factor.reshape(tile_slots * seg_count, rank_width).astype(jnp.float32),
        (((0,), (0,)), ((), ())),
        precision=highest,
        preferred_element_type=jnp.float32,
    )
    return (own_factors, item_rhs * RHS_SCALE)


def solution(mesh):
    in_specs = (
        P(("ent", "rep"), None),
        P("ent", "rep", None, None),
        P("ent", "rep", None),
        P("ent", "rep", None, None),
        P("ent", "rep", None, None),
        P("ent", "rep", None),
    )
    out_specs = (P(("ent", "rep"), None), P(("ent", "rep"), None))
    return jax.shard_map(shards, mesh=mesh, in_specs=in_specs, out_specs=out_specs, check_vma=False)
```

```python
import functools

import jax
import jax.numpy as jnp
from jax import lax
from jax.experimental import pallas as pl
from jax.experimental.pallas import tpu as pltpu
from jax.sharding import PartitionSpec as P

MESH_ID = pl.DeviceIdType.MESH

U_DEV = 2


ALPHA = 40.0
RIDGE = 1.0
RHS_SCALE = 1.0 / 640.0


def cholesky_kernel(gram_ref, rhs_ref, out_ref, a_s, l_s, y_s):
    batch, n, _ = gram_ref.shape
    a_s[...] = gram_ref[...]
    y_s[...] = rhs_ref[...]
    out_ref[...] = jnp.zeros_like(out_ref)
    lane_v = lax.broadcasted_iota(jnp.int32, (1, n), 1)

    def factor(top, j, carry):
        span = n - top
        lane_m = lax.broadcasted_iota(jnp.int32, (span, n), 1)
        sub_m = lax.broadcasted_iota(jnp.int32, (span, n), 0) + top
        sub_v = lax.broadcasted_iota(jnp.int32, (span, 1), 0) + top
        for b in range(batch):
            a = a_s[b, top:, :]
            row = jnp.sum(jnp.where(sub_m == j, a, 0.0), axis=0, keepdims=True)
            col = jnp.sum(jnp.where(lane_m == j, a, 0.0), axis=1, keepdims=True)
            diag = jnp.sum(jnp.where(lane_v == j, row, 0.0), axis=1, keepdims=True)
            inv = 1.0 / jnp.sqrt(diag)
            l_row = jnp.where(lane_v >= j, row, 0.0) * inv
            l_col = jnp.where(sub_v >= j, col, 0.0) * inv
            a_s[b, top:, :] = a - l_col * l_row
            l_s[b, pl.ds(j, 1), :] = l_row
            y = y_s[pl.ds(b, 1), :]
            y_j = jnp.sum(jnp.where(lane_v == j, y, 0.0), axis=1, keepdims=True) * inv
            y_s[pl.ds(b, 1), :] = jnp.where(lane_v == j, y_j, y - y_j * l_row)
        return carry

    quarter = n // 4
    for part in range(4):
        top = part * quarter
        lax.fori_loop(top, top + quarter, functools.partial(factor, top), 0)

    def back(t, carry):
        j = n - 1 - t
        for b in range(batch):
            l_j = l_s[b, pl.ds(j, 1), :]
            x = out_ref[pl.ds(b, 1), :]
            y_j = jnp.sum(jnp.where(lane_v == j, y_s[pl.ds(b, 1), :], 0.0), axis=1, keepdims=True)
            l_jj = jnp.sum(jnp.where(lane_v == j, l_j, 0.0), axis=1, keepdims=True)
            known = jnp.sum(jnp.where(lane_v > j, l_j * x, 0.0), axis=1, keepdims=True)
            out_ref[pl.ds(b, 1), :] = jnp.where(lane_v == j, (y_j - known) / l_jj, x)
        return carry

    lax.fori_loop(0, n, back, 0)


def solve_users(gram, rhs):
    gram = (gram + jnp.swapaxes(gram, -1, -2)) / 2
    batch, n, _ = gram.shape
    return pl.pallas_call(
        cholesky_kernel,
        out_shape=jax.ShapeDtypeStruct((batch, n), jnp.float32),
        in_specs=[pl.BlockSpec(memory_space=pltpu.VMEM)] * 2,
        out_specs=pl.BlockSpec(memory_space=pltpu.VMEM),
        scratch_shapes=[
            pltpu.VMEM((batch, n, n), jnp.float32),
            pltpu.VMEM((batch, n, n), jnp.float32),
            pltpu.VMEM((batch, n), jnp.float32),
        ],
    )(gram, rhs)


def flip_bits(value, mask, bits):
    out = value - value % (1 << bits)
    for bit in range(bits):
        here = (value // (1 << bit)) % 2
        out = out + (1 << bit) * ((1 - here) if (mask >> bit) & 1 else here)
    return out


def doubling_kernel(
    n_rep, low_bits, rounds, x_ref, o_ref, full_recv, piece_recv, piece, gath,
    sem_a, sem_b, sem_c, sem_d, sem_e, sem_f,
):
    flat = lax.axis_index("ent") * n_rep + lax.axis_index("rep")
    group = 1 << low_bits
    rows = x_ref.shape[0] // group
    slot = flat % group

    def place(p):
        return (p // n_rep, p % n_rep)

    def flip(bit):
        step = 1 << bit
        upper = (flat // step) % 2
        return flat + step - 2 * step * upper

    members = [flip_bits(flat, k, low_bits) for k in range(1, group)]
    outer = [flip(bit) for bit in range(low_bits, rounds)]
    barrier = pltpu.get_barrier_semaphore()
    for p in members + outer:
        pl.semaphore_signal(barrier, inc=1, device_id=place(p), device_id_type=MESH_ID)
    pl.semaphore_wait(barrier, len(members) + len(outer))

    o_ref[...] = x_ref[...]
    for bit in range(low_bits):
        copy = pltpu.make_async_remote_copy(
            src_ref=o_ref, dst_ref=full_recv.at[bit], send_sem=sem_a.at[bit],
            recv_sem=sem_b.at[bit], device_id=place(flip(bit)), device_id_type=MESH_ID,
        )
        copy.start()
        copy.wait_recv()
        copy.wait_send()
        o_ref[...] = o_ref[...] + full_recv[bit]

    piece[...] = o_ref[pl.ds(pl.multiple_of(slot * rows, rows), rows), :]
    for index, p in enumerate(outer):
        copy = pltpu.make_async_remote_copy(
            src_ref=piece, dst_ref=piece_recv.at[index], send_sem=sem_c.at[index],
            recv_sem=sem_d.at[index], device_id=place(p), device_id_type=MESH_ID,
        )
        copy.start()
        copy.wait_recv()
        copy.wait_send()
        piece[...] = piece[...] + piece_recv[index]

    gath[slot] = piece[...]
    sends = []
    for index, p in enumerate(members):
        copy = pltpu.make_async_remote_copy(
            src_ref=piece, dst_ref=gath.at[slot], send_sem=sem_e.at[index],
            recv_sem=sem_f.at[slot], device_id=place(p), device_id_type=MESH_ID,
        )
        copy.start()
        sends.append(copy)
    for k in range(1, group):
        source = flip_bits(slot, k, low_bits)
        pltpu.make_async_remote_copy(
            src_ref=piece, dst_ref=gath.at[source], send_sem=sem_e.at[k - 1],
            recv_sem=sem_f.at[source], device_id=place(members[k - 1]), device_id_type=MESH_ID,
        ).wait_recv()
    for copy in sends:
        copy.wait_send()
    for part in range(group):
        o_ref[pl.ds(part * rows, rows), :] = gath[part]


def tree_sum(value, count):
    rounds = count.bit_length() - 1
    n_rep = lax.axis_size("rep")
    low_bits = (n_rep * 2).bit_length() - 1
    group = 1 << low_bits
    rows = value.shape[0] // group
    outer = rounds - low_bits
    return pl.pallas_call(
        functools.partial(doubling_kernel, n_rep, low_bits, rounds),
        out_shape=jax.ShapeDtypeStruct(value.shape, value.dtype),
        in_specs=[pl.BlockSpec(memory_space=pltpu.VMEM)],
        out_specs=pl.BlockSpec(memory_space=pltpu.VMEM),
        scratch_shapes=[
            pltpu.VMEM((low_bits,) + value.shape, value.dtype),
            pltpu.VMEM((outer, rows, value.shape[1]), value.dtype),
            pltpu.VMEM((rows, value.shape[1]), value.dtype),
            pltpu.VMEM((group, rows, value.shape[1]), value.dtype),
            pltpu.SemaphoreType.DMA((low_bits,)),
            pltpu.SemaphoreType.DMA((low_bits,)),
            pltpu.SemaphoreType.DMA((outer,)),
            pltpu.SemaphoreType.DMA((outer,)),
            pltpu.SemaphoreType.DMA((group - 1,)),
            pltpu.SemaphoreType.DMA((group,)),
        ],
        compiler_params=pltpu.CompilerParams(collective_id=0, has_side_effects=True),
    )(value)


def rep_peers(n_rep):
    me = lax.axis_index("rep")
    return me, [(me + shift) % n_rep for shift in range(1, n_rep)]


def scatter_kernel(n_rep, acc_ref, out_ref, recv, send_sem, recv_sem):
    me, peers = rep_peers(n_rep)
    ent = lax.axis_index("ent")
    barrier = pltpu.get_barrier_semaphore()
    for peer in peers:
        pl.semaphore_signal(barrier, inc=1, device_id=(ent, peer), device_id_type=MESH_ID)
    pl.semaphore_wait(barrier, n_rep - 1)
    copies = []
    for index, peer in enumerate(peers):
        copy = pltpu.make_async_remote_copy(
            src_ref=acc_ref.at[peer], dst_ref=recv.at[index], send_sem=send_sem.at[index],
            recv_sem=recv_sem.at[index], device_id=(ent, peer), device_id_type=MESH_ID,
        )
        copy.start()
        copies.append(copy)
    total = acc_ref[me]
    for index, copy in enumerate(copies):
        copy.wait_recv()
        total = total + recv[index]
    for copy in copies:
        copy.wait_send()
    out_ref[...] = total


def rep_scatter_sum(blocks, n_rep, per_dev):
    total = pl.pallas_call(
        functools.partial(scatter_kernel, n_rep),
        out_shape=jax.ShapeDtypeStruct(blocks.shape[1:], blocks.dtype),
        in_specs=[pl.BlockSpec(memory_space=pltpu.VMEM)],
        out_specs=pl.BlockSpec(memory_space=pltpu.VMEM),
        scratch_shapes=[
            pltpu.VMEM((n_rep - 1,) + blocks.shape[1:], blocks.dtype),
            pltpu.SemaphoreType.DMA((n_rep - 1,)),
            pltpu.SemaphoreType.DMA((n_rep - 1,)),
        ],
        compiler_params=pltpu.CompilerParams(collective_id=1, has_side_effects=True),
    )(blocks)
    width = blocks.shape[2]
    grams = total[: per_dev * width].reshape(per_dev, width, width)
    return grams, total[per_dev * width :]


def allgather_kernel(n_rep, val_ref, out_ref, gath, send_sem, recv_sem):
    me, peers = rep_peers(n_rep)
    ent = lax.axis_index("ent")
    barrier = pltpu.get_barrier_semaphore()
    for peer in peers:
        pl.semaphore_signal(barrier, inc=1, device_id=(ent, peer), device_id_type=MESH_ID)
    pl.semaphore_wait(barrier, n_rep - 1)
    copies = []
    for index, peer in enumerate(peers):
        copy = pltpu.make_async_remote_copy(
            src_ref=val_ref, dst_ref=gath.at[me], send_sem=send_sem.at[index],
            recv_sem=recv_sem.at[me], device_id=(ent, peer), device_id_type=MESH_ID,
        )
        copy.start()
        copies.append(copy)
    gath[me] = val_ref[...]
    for index in range(n_rep - 1):
        source = peers[index]
        pltpu.make_async_remote_copy(
            src_ref=val_ref, dst_ref=gath.at[source], send_sem=send_sem.at[index],
            recv_sem=recv_sem.at[source], device_id=(ent, source), device_id_type=MESH_ID,
        ).wait_recv()
    for copy in copies:
        copy.wait_send()
    out_ref[...] = gath[...]


def rep_gather(value, n_rep):
    out = pl.pallas_call(
        functools.partial(allgather_kernel, n_rep),
        out_shape=jax.ShapeDtypeStruct((n_rep,) + value.shape, value.dtype),
        in_specs=[pl.BlockSpec(memory_space=pltpu.VMEM)],
        out_specs=pl.BlockSpec(memory_space=pltpu.VMEM),
        scratch_shapes=[
            pltpu.VMEM((n_rep,) + value.shape, value.dtype),
            pltpu.SemaphoreType.DMA((n_rep - 1,)),
            pltpu.SemaphoreType.DMA((n_rep,)),
        ],
        compiler_params=pltpu.CompilerParams(collective_id=2, has_side_effects=True),
    )(value)
    return out.reshape(-1, value.shape[-1])


def gather_kernel(idx_ref, table_t_ref, out_ref):
    step = pl.program_id(0)
    idx = idx_ref[pl.ds(step, 1), :]
    picks = lax.broadcasted_iota(jnp.int32, (table_t_ref.shape[1], idx.shape[1]), 0) == idx
    rows_t = jnp.dot(table_t_ref[...], picks.astype(jnp.bfloat16), preferred_element_type=jnp.float32)
    out_ref[...] = rows_t.T.astype(out_ref.dtype)


def gather_rows(table, idx, chunk=512):
    count = idx.shape[0]
    idx_lanes = idx.reshape(count // chunk, chunk)
    return pl.pallas_call(
        gather_kernel,
        out_shape=jax.ShapeDtypeStruct((count, table.shape[1]), table.dtype),
        grid=(count // chunk,),
        in_specs=[
            pl.BlockSpec(idx_lanes.shape, lambda i: (0, 0)),
            pl.BlockSpec((table.shape[1], table.shape[0]), lambda i: (0, 0)),
        ],
        out_specs=pl.BlockSpec((chunk, table.shape[1]), lambda i: (i, 0)),
        cost_estimate=pl.CostEstimate(
            flops=2 * count * table.shape[0] * table.shape[1],
            transcendentals=0,
            bytes_accessed=count * 4 + table.size * 2 + count * table.shape[1] * 2,
        ),
    )(idx_lanes, table.T)


def gram_kernel(n_user, per_dev, rows_ref, gw_ref, user_ref, rw_ref, out_ref):
    step = pl.program_id(0)
    width = rows_ref.shape[1]

    @pl.when(step == 0)
    def _():
        out_ref[...] = jnp.zeros_like(out_ref)

    rows = rows_ref[...]
    rows_t = rows.astype(jnp.float32).T
    weights_t = (rows_t * gw_ref[pl.ds(step, 1), :]).astype(jnp.bfloat16)
    users = user_ref[pl.ds(step, 1), :]
    zero = jnp.zeros((), jnp.bfloat16)
    for user in range(n_user):
        picked = jnp.where(users == user, weights_t, zero)
        block, spot = user // per_dev, (user % per_dev) * width
        out_ref[block, spot : spot + width, :] += jnp.dot(
            picked, rows, preferred_element_type=jnp.float32
        )
    slots = lax.broadcasted_iota(jnp.int32, (n_user, users.shape[1]), 0)
    per_user = jnp.where(users == slots, rw_ref[pl.ds(step, 1), :], 0.0)
    high = per_user.astype(jnp.bfloat16)
    low = (per_user - high.astype(jnp.float32)).astype(jnp.bfloat16)
    rhs = jnp.dot(high, rows, preferred_element_type=jnp.float32) + jnp.dot(
        low, rows, preferred_element_type=jnp.float32
    )
    base = per_dev * width
    for block in range(n_user // per_dev):
        out_ref[block, base : base + per_dev, :] += rhs[block * per_dev : (block + 1) * per_dev]


def user_grams(rows, gw_lanes, user_lanes, rw_lanes, n_user, per_dev):
    chunks, chunk = gw_lanes.shape
    width = rows.shape[1]
    n_block = n_user // per_dev
    block_rows = per_dev * width + per_dev
    return pl.pallas_call(
        functools.partial(gram_kernel, n_user, per_dev),
        out_shape=jax.ShapeDtypeStruct((n_block, block_rows, width), jnp.float32),
        grid=(chunks,),
        in_specs=[
            pl.BlockSpec((chunk, width), lambda i: (i, 0)),
            pl.BlockSpec((chunks, chunk), lambda i: (0, 0)),
            pl.BlockSpec((chunks, chunk), lambda i: (0, 0)),
            pl.BlockSpec((chunks, chunk), lambda i: (0, 0)),
        ],
        out_specs=pl.BlockSpec((n_block, block_rows, width), lambda i: (0, 0, 0)),
        cost_estimate=pl.CostEstimate(
            flops=2 * rows.shape[0] * width * width * (n_user + 2),
            transcendentals=0,
            bytes_accessed=rows.size * 2 + 12 * rows.shape[0] + n_user * width * (width + 1) * 4,
        ),
    )(rows, gw_lanes, user_lanes, rw_lanes)

def shards(item_factors, tile_items, send_tiles, tile_users, tile_counts, recv_tiles):
    highest = lax.Precision.HIGHEST
    rank_width = item_factors.shape[1]
    item_count = item_factors.shape[0]
    n_ent = lax.axis_size("ent")
    n_rep = lax.axis_size("rep")
    tile_slots = tile_items.shape[2]
    tile_rows = tile_items.shape[3]
    seg_count = tile_users.shape[3]
    seg_length = tile_rows // seg_count
    slot_cap = tile_slots // n_ent
    user_block = U_DEV * lax.axis_size("rep")
    item_ids = tile_items.reshape(tile_slots, tile_rows)
    slot_pos = jnp.arange(tile_slots, dtype=jnp.int32) % slot_cap
    live_send = slot_pos < jnp.repeat(send_tiles.reshape(n_ent), slot_cap)
    live_recv = slot_pos < jnp.repeat(recv_tiles.reshape(n_ent), slot_cap)
    partial_gram = lax.dot_general(
        item_factors, item_factors, (((0,), (0,)), ((), ())), preferred_element_type=jnp.float32
    )
    live_rows = jnp.repeat(live_send, tile_rows)
    picked = gather_rows(item_factors, jnp.where(live_rows, item_ids.reshape(-1), -1))
    incoming = lax.all_to_all(
        picked.reshape(n_ent, slot_cap * tile_rows, rank_width),
        "ent",
        split_axis=0,
        concat_axis=0,
        tiled=True,
    )
    counts_int = tile_counts.reshape(tile_slots, tile_rows)
    counts_f = counts_int.astype(jnp.float32)
    gram_weight = ALPHA * counts_f
    rhs_weight = jnp.where(
        live_recv[:, None] & (counts_int > 0), 1.0 + ALPHA * counts_f, jnp.float32(0.0)
    )
    owners = tile_users.reshape(tile_slots * seg_count)
    selector = owners[None, :] == jnp.arange(user_block, dtype=jnp.int32)[:, None]
    selector_f = selector.astype(jnp.float32)
    rows_all = incoming.reshape(tile_slots * tile_rows, rank_width)
    lane_chunk = 1024
    row_owner = jnp.repeat(owners, seg_length)
    gram_blocks = user_grams(
        rows_all,
        gram_weight.reshape(-1, lane_chunk),
        row_owner.reshape(-1, lane_chunk),
        rhs_weight.reshape(-1, lane_chunk),
        user_block,
        U_DEV,
    )
    identity_mat = jnp.eye(rank_width, dtype=jnp.float32)
    added_term = tree_sum(partial_gram, n_ent * n_rep) + RIDGE * identity_mat
    own_gram, own_rhs = rep_scatter_sum(gram_blocks, n_rep, U_DEV)
    own_factors = solve_users(own_gram + added_term, own_rhs)
    solved = rep_gather(own_factors.astype(jnp.bfloat16), n_rep)
    run_factor = lax.dot_general(
        selector.astype(jnp.bfloat16),
        solved,
        (((0,), (0,)), ((), ())),
        preferred_element_type=jnp.float32,
    ).astype(jnp.bfloat16)
    back_load = jnp.concatenate(
        [
            run_factor.reshape(tile_slots, seg_count * rank_width),
            counts_int.astype(jnp.bfloat16),
        ],
        axis=1,
    )
    back_load = lax.all_to_all(
        back_load.reshape(n_ent, slot_cap, -1), "ent", split_axis=0, concat_axis=0, tiled=True
    ).reshape(tile_slots, -1)
    back_factor = back_load[:, : seg_count * rank_width]
    back_counts = back_load[:, seg_count * rank_width :].astype(jnp.float32)
    back_weight = jnp.where(
        live_send[:, None] & (back_counts > 0), 1.0 + ALPHA * back_counts, jnp.float32(0.0)
    )
    item_hot = item_ids[:, :, None] == jnp.arange(item_count, dtype=jnp.int32)[None, None, :]
    run_weight = back_weight.reshape(tile_slots * seg_count, seg_length)
    hot_runs = item_hot.reshape(tile_slots * seg_count, seg_length, item_count)
    spread_mat = jnp.sum(jnp.where(hot_runs, run_weight[:, :, None], 0.0), axis=1)
    item_rhs = lax.dot_general(
        spread_mat,
        back_factor.reshape(tile_slots * seg_count, rank_width).astype(jnp.float32),
        (((0,), (0,)), ((), ())),
        precision=highest,
        preferred_element_type=jnp.float32,
    )
    return (own_factors, item_rhs * RHS_SCALE)


def solution(mesh):
    in_specs = (
        P(("ent", "rep"), None),
        P("ent", "rep", None, None),
        P("ent", "rep", None),
        P("ent", "rep", None, None),
        P("ent", "rep", None, None),
        P("ent", "rep", None),
    )
    out_specs = (P(("ent", "rep"), None), P(("ent", "rep"), None))
    return jax.shard_map(shards, mesh=mesh, in_specs=in_specs, out_specs=out_specs, check_vma=False)
```

```python
import functools

import jax
import jax.numpy as jnp
from jax import lax
from jax.experimental import pallas as pl
from jax.experimental.pallas import tpu as pltpu
from jax.sharding import PartitionSpec as P

MESH_ID = pl.DeviceIdType.MESH

U_DEV = 2


ALPHA = 40.0
RIDGE = 1.0
RHS_SCALE = 1.0 / 640.0


def cholesky_solve(a_s, l_s, y_s, out_ref):
    batch, n, _ = a_s.shape
    out_ref[...] = jnp.zeros_like(out_ref)
    lane_v = lax.broadcasted_iota(jnp.int32, (1, n), 1)

    def factor(top, j, carry):
        span = n - top
        lane_m = lax.broadcasted_iota(jnp.int32, (span, n), 1)
        sub_m = lax.broadcasted_iota(jnp.int32, (span, n), 0) + top
        sub_v = lax.broadcasted_iota(jnp.int32, (span, 1), 0) + top
        for b in range(batch):
            a = a_s[b, top:, :]
            row = jnp.sum(jnp.where(sub_m == j, a, 0.0), axis=0, keepdims=True)
            col = jnp.sum(jnp.where(lane_m == j, a, 0.0), axis=1, keepdims=True)
            diag = jnp.sum(jnp.where(lane_v == j, row, 0.0), axis=1, keepdims=True)
            inv = 1.0 / jnp.sqrt(diag)
            l_row = jnp.where(lane_v >= j, row, 0.0) * inv
            l_col = jnp.where(sub_v >= j, col, 0.0) * inv
            a_s[b, top:, :] = a - l_col * l_row
            l_s[b, pl.ds(j, 1), :] = l_row
            y = y_s[pl.ds(b, 1), :]
            y_j = jnp.sum(jnp.where(lane_v == j, y, 0.0), axis=1, keepdims=True) * inv
            y_s[pl.ds(b, 1), :] = jnp.where(lane_v == j, y_j, y - y_j * l_row)
        return carry

    quarter = n // 4
    for part in range(4):
        top = part * quarter
        lax.fori_loop(top, top + quarter, functools.partial(factor, top), 0)

    def back(t, carry):
        j = n - 1 - t
        for b in range(batch):
            l_j = l_s[b, pl.ds(j, 1), :]
            x = out_ref[pl.ds(b, 1), :]
            y_j = jnp.sum(jnp.where(lane_v == j, y_s[pl.ds(b, 1), :], 0.0), axis=1, keepdims=True)
            l_jj = jnp.sum(jnp.where(lane_v == j, l_j, 0.0), axis=1, keepdims=True)
            known = jnp.sum(jnp.where(lane_v > j, l_j * x, 0.0), axis=1, keepdims=True)
            out_ref[pl.ds(b, 1), :] = jnp.where(lane_v == j, (y_j - known) / l_jj, x)
        return carry

    lax.fori_loop(0, n, back, 0)


def flip_bits(value, mask, bits):
    out = value - value % (1 << bits)
    for bit in range(bits):
        here = (value // (1 << bit)) % 2
        out = out + (1 << bit) * ((1 - here) if (mask >> bit) & 1 else here)
    return out


def doubling_kernel(
    n_rep, low_bits, rounds, x_ref, o_ref, full_recv, piece_recv, piece, gath,
    sem_a, sem_b, sem_c, sem_d, sem_e, sem_f,
):
    flat = lax.axis_index("ent") * n_rep + lax.axis_index("rep")
    group = 1 << low_bits
    rows = x_ref.shape[0] // group
    slot = flat % group

    def place(p):
        return (p // n_rep, p % n_rep)

    def flip(bit):
        step = 1 << bit
        upper = (flat // step) % 2
        return flat + step - 2 * step * upper

    members = [flip_bits(flat, k, low_bits) for k in range(1, group)]
    outer = [flip(bit) for bit in range(low_bits, rounds)]
    barrier = pltpu.get_barrier_semaphore()
    for p in members + outer:
        pl.semaphore_signal(barrier, inc=1, device_id=place(p), device_id_type=MESH_ID)
    pl.semaphore_wait(barrier, len(members) + len(outer))

    o_ref[...] = x_ref[...]
    for bit in range(low_bits):
        copy = pltpu.make_async_remote_copy(
            src_ref=o_ref, dst_ref=full_recv.at[bit], send_sem=sem_a.at[bit],
            recv_sem=sem_b.at[bit], device_id=place(flip(bit)), device_id_type=MESH_ID,
        )
        copy.start()
        copy.wait_recv()
        copy.wait_send()
        o_ref[...] = o_ref[...] + full_recv[bit]

    piece[...] = o_ref[pl.ds(pl.multiple_of(slot * rows, rows), rows), :]
    for index, p in enumerate(outer):
        copy = pltpu.make_async_remote_copy(
            src_ref=piece, dst_ref=piece_recv.at[index], send_sem=sem_c.at[index],
            recv_sem=sem_d.at[index], device_id=place(p), device_id_type=MESH_ID,
        )
        copy.start()
        copy.wait_recv()
        copy.wait_send()
        piece[...] = piece[...] + piece_recv[index]

    gath[slot] = piece[...]
    sends = []
    for index, p in enumerate(members):
        copy = pltpu.make_async_remote_copy(
            src_ref=piece, dst_ref=gath.at[slot], send_sem=sem_e.at[index],
            recv_sem=sem_f.at[slot], device_id=place(p), device_id_type=MESH_ID,
        )
        copy.start()
        sends.append(copy)
    for k in range(1, group):
        source = flip_bits(slot, k, low_bits)
        pltpu.make_async_remote_copy(
            src_ref=piece, dst_ref=gath.at[source], send_sem=sem_e.at[k - 1],
            recv_sem=sem_f.at[source], device_id=place(members[k - 1]), device_id_type=MESH_ID,
        ).wait_recv()
    for copy in sends:
        copy.wait_send()
    for part in range(group):
        o_ref[pl.ds(part * rows, rows), :] = gath[part]


def tree_sum(value, count):
    rounds = count.bit_length() - 1
    n_rep = lax.axis_size("rep")
    low_bits = (n_rep * 2).bit_length() - 1
    group = 1 << low_bits
    rows = value.shape[0] // group
    outer = rounds - low_bits
    return pl.pallas_call(
        functools.partial(doubling_kernel, n_rep, low_bits, rounds),
        out_shape=jax.ShapeDtypeStruct(value.shape, value.dtype),
        in_specs=[pl.BlockSpec(memory_space=pltpu.VMEM)],
        out_specs=pl.BlockSpec(memory_space=pltpu.VMEM),
        scratch_shapes=[
            pltpu.VMEM((low_bits,) + value.shape, value.dtype),
            pltpu.VMEM((outer, rows, value.shape[1]), value.dtype),
            pltpu.VMEM((rows, value.shape[1]), value.dtype),
            pltpu.VMEM((group, rows, value.shape[1]), value.dtype),
            pltpu.SemaphoreType.DMA((low_bits,)),
            pltpu.SemaphoreType.DMA((low_bits,)),
            pltpu.SemaphoreType.DMA((outer,)),
            pltpu.SemaphoreType.DMA((outer,)),
            pltpu.SemaphoreType.DMA((group - 1,)),
            pltpu.SemaphoreType.DMA((group,)),
        ],
        compiler_params=pltpu.CompilerParams(collective_id=0, has_side_effects=True),
    )(value)


def rep_peers(n_rep):
    me = lax.axis_index("rep")
    return me, [(me + shift) % n_rep for shift in range(1, n_rep)]


def owner_kernel(n_rep, blocks_ref, base_ref, out_ref, x_s, recv, a_s, l_s, y_s, fac, gath,
                 sem_a, sem_b, sem_c, sem_d):
    me, peers = rep_peers(n_rep)
    ent = lax.axis_index("ent")
    batch, n, _ = a_s.shape
    barrier = pltpu.get_barrier_semaphore()
    for peer in peers:
        pl.semaphore_signal(barrier, inc=1, device_id=(ent, peer), device_id_type=MESH_ID)
    pl.semaphore_wait(barrier, n_rep - 1)
    copies = []
    for index, peer in enumerate(peers):
        copy = pltpu.make_async_remote_copy(
            src_ref=blocks_ref.at[peer], dst_ref=recv.at[index], send_sem=sem_a.at[index],
            recv_sem=sem_b.at[index], device_id=(ent, peer), device_id_type=MESH_ID,
        )
        copy.start()
        copies.append(copy)
    total = blocks_ref[me]
    for index, copy in enumerate(copies):
        copy.wait_recv()
        total = total + recv[index]
    for copy in copies:
        copy.wait_send()
    base = base_ref[...]
    for b in range(batch):
        gram = total[b * n : (b + 1) * n] + base
        a_s[b] = (gram + gram.T) / 2
    y_s[...] = total[batch * n : batch * n + batch]
    cholesky_solve(a_s, l_s, y_s, x_s)
    fac[...] = x_s[...].astype(fac.dtype)
    gath[me] = fac[...]
    sends = []
    for index, peer in enumerate(peers):
        copy = pltpu.make_async_remote_copy(
            src_ref=fac, dst_ref=gath.at[me], send_sem=sem_c.at[index],
            recv_sem=sem_d.at[me], device_id=(ent, peer), device_id_type=MESH_ID,
        )
        copy.start()
        sends.append(copy)
    for index, source in enumerate(peers):
        pltpu.make_async_remote_copy(
            src_ref=fac, dst_ref=gath.at[source], send_sem=sem_c.at[index],
            recv_sem=sem_d.at[source], device_id=(ent, source), device_id_type=MESH_ID,
        ).wait_recv()
    for copy in sends:
        copy.wait_send()
    out_ref[...] = gath[...]


def solve_owned(blocks, base, n_rep, per_dev):
    n = blocks.shape[2]
    return pl.pallas_call(
        functools.partial(owner_kernel, n_rep),
        out_shape=(
            jax.ShapeDtypeStruct((n_rep, per_dev, n), jnp.bfloat16),
            jax.ShapeDtypeStruct((per_dev, n), jnp.float32),
        ),
        in_specs=[pl.BlockSpec(memory_space=pltpu.VMEM)] * 2,
        out_specs=(pl.BlockSpec(memory_space=pltpu.VMEM), pl.BlockSpec(memory_space=pltpu.VMEM)),
        scratch_shapes=[
            pltpu.VMEM((n_rep - 1,) + blocks.shape[1:], jnp.float32),
            pltpu.VMEM((per_dev, n, n), jnp.float32),
            pltpu.VMEM((per_dev, n, n), jnp.float32),
            pltpu.VMEM((per_dev, n), jnp.float32),
            pltpu.VMEM((per_dev, n), jnp.bfloat16),
            pltpu.VMEM((n_rep, per_dev, n), jnp.bfloat16),
            pltpu.SemaphoreType.DMA((n_rep - 1,)),
            pltpu.SemaphoreType.DMA((n_rep - 1,)),
            pltpu.SemaphoreType.DMA((n_rep - 1,)),
            pltpu.SemaphoreType.DMA((n_rep,)),
        ],
        compiler_params=pltpu.CompilerParams(collective_id=1, has_side_effects=True),
    )(blocks, base)


def gather_kernel(idx_ref, table_t_ref, out_ref):
    step = pl.program_id(0)
    idx = idx_ref[pl.ds(step, 1), :]
    picks = lax.broadcasted_iota(jnp.int32, (table_t_ref.shape[1], idx.shape[1]), 0) == idx
    rows_t = jnp.dot(table_t_ref[...], picks.astype(jnp.bfloat16), preferred_element_type=jnp.float32)
    out_ref[...] = rows_t.T.astype(out_ref.dtype)


def gather_rows(table, idx, chunk=512):
    count = idx.shape[0]
    idx_lanes = idx.reshape(count // chunk, chunk)
    return pl.pallas_call(
        gather_kernel,
        out_shape=jax.ShapeDtypeStruct((count, table.shape[1]), table.dtype),
        grid=(count // chunk,),
        in_specs=[
            pl.BlockSpec(idx_lanes.shape, lambda i: (0, 0)),
            pl.BlockSpec((table.shape[1], table.shape[0]), lambda i: (0, 0)),
        ],
        out_specs=pl.BlockSpec((chunk, table.shape[1]), lambda i: (i, 0)),
        cost_estimate=pl.CostEstimate(
            flops=2 * count * table.shape[0] * table.shape[1],
            transcendentals=0,
            bytes_accessed=count * 4 + table.size * 2 + count * table.shape[1] * 2,
        ),
    )(idx_lanes, table.T)


def gram_kernel(n_user, per_dev, rows_ref, gw_ref, user_ref, rw_ref, out_ref):
    step = pl.program_id(0)
    width = rows_ref.shape[1]

    @pl.when(step == 0)
    def _():
        out_ref[...] = jnp.zeros_like(out_ref)

    rows = rows_ref[...]
    rows_t = rows.astype(jnp.float32).T
    weights_t = (rows_t * gw_ref[pl.ds(step, 1), :]).astype(jnp.bfloat16)
    users = user_ref[pl.ds(step, 1), :]
    zero = jnp.zeros((), jnp.bfloat16)
    for user in range(n_user):
        picked = jnp.where(users == user, weights_t, zero)
        block, spot = user // per_dev, (user % per_dev) * width
        out_ref[block, spot : spot + width, :] += jnp.dot(
            picked, rows, preferred_element_type=jnp.float32
        )
    slots = lax.broadcasted_iota(jnp.int32, (n_user, users.shape[1]), 0)
    per_user = jnp.where(users == slots, rw_ref[pl.ds(step, 1), :], 0.0)
    high = per_user.astype(jnp.bfloat16)
    low = (per_user - high.astype(jnp.float32)).astype(jnp.bfloat16)
    rhs = jnp.dot(high, rows, preferred_element_type=jnp.float32) + jnp.dot(
        low, rows, preferred_element_type=jnp.float32
    )
    base = per_dev * width
    for block in range(n_user // per_dev):
        out_ref[block, base : base + per_dev, :] += rhs[block * per_dev : (block + 1) * per_dev]


def user_grams(rows, gw_lanes, user_lanes, rw_lanes, n_user, per_dev):
    chunks, chunk = gw_lanes.shape
    width = rows.shape[1]
    n_block = n_user // per_dev
    block_rows = per_dev * width + per_dev
    return pl.pallas_call(
        functools.partial(gram_kernel, n_user, per_dev),
        out_shape=jax.ShapeDtypeStruct((n_block, block_rows, width), jnp.float32),
        grid=(chunks,),
        in_specs=[
            pl.BlockSpec((chunk, width), lambda i: (i, 0)),
            pl.BlockSpec((chunks, chunk), lambda i: (0, 0)),
            pl.BlockSpec((chunks, chunk), lambda i: (0, 0)),
            pl.BlockSpec((chunks, chunk), lambda i: (0, 0)),
        ],
        out_specs=pl.BlockSpec((n_block, block_rows, width), lambda i: (0, 0, 0)),
        cost_estimate=pl.CostEstimate(
            flops=2 * rows.shape[0] * width * width * (n_user + 2),
            transcendentals=0,
            bytes_accessed=rows.size * 2 + 12 * rows.shape[0] + n_user * width * (width + 1) * 4,
        ),
    )(rows, gw_lanes, user_lanes, rw_lanes)

def shards(item_factors, tile_items, send_tiles, tile_users, tile_counts, recv_tiles):
    highest = lax.Precision.HIGHEST
    rank_width = item_factors.shape[1]
    item_count = item_factors.shape[0]
    n_ent = lax.axis_size("ent")
    n_rep = lax.axis_size("rep")
    tile_slots = tile_items.shape[2]
    tile_rows = tile_items.shape[3]
    seg_count = tile_users.shape[3]
    seg_length = tile_rows // seg_count
    slot_cap = tile_slots // n_ent
    user_block = U_DEV * lax.axis_size("rep")
    item_ids = tile_items.reshape(tile_slots, tile_rows)
    slot_pos = jnp.arange(tile_slots, dtype=jnp.int32) % slot_cap
    live_send = slot_pos < jnp.repeat(send_tiles.reshape(n_ent), slot_cap)
    live_recv = slot_pos < jnp.repeat(recv_tiles.reshape(n_ent), slot_cap)
    partial_gram = lax.dot_general(
        item_factors, item_factors, (((0,), (0,)), ((), ())), preferred_element_type=jnp.float32
    )
    live_rows = jnp.repeat(live_send, tile_rows)
    picked = gather_rows(item_factors, jnp.where(live_rows, item_ids.reshape(-1), -1))
    incoming = lax.all_to_all(
        picked.reshape(n_ent, slot_cap * tile_rows, rank_width),
        "ent",
        split_axis=0,
        concat_axis=0,
        tiled=True,
    )
    counts_int = tile_counts.reshape(tile_slots, tile_rows)
    counts_f = counts_int.astype(jnp.float32)
    gram_weight = ALPHA * counts_f
    rhs_weight = jnp.where(
        live_recv[:, None] & (counts_int > 0), 1.0 + ALPHA * counts_f, jnp.float32(0.0)
    )
    owners = tile_users.reshape(tile_slots * seg_count)
    selector = owners[None, :] == jnp.arange(user_block, dtype=jnp.int32)[:, None]
    selector_f = selector.astype(jnp.float32)
    rows_all = incoming.reshape(tile_slots * tile_rows, rank_width)
    lane_chunk = 1024
    row_owner = jnp.repeat(owners, seg_length)
    gram_blocks = user_grams(
        rows_all,
        gram_weight.reshape(-1, lane_chunk),
        row_owner.reshape(-1, lane_chunk),
        rhs_weight.reshape(-1, lane_chunk),
        user_block,
        U_DEV,
    )
    identity_mat = jnp.eye(rank_width, dtype=jnp.float32)
    added_term = tree_sum(partial_gram, n_ent * n_rep) + RIDGE * identity_mat
    solved, own_factors = solve_owned(gram_blocks, added_term, n_rep, U_DEV)
    solved = solved.reshape(user_block, rank_width)
    run_factor = lax.dot_general(
        selector.astype(jnp.bfloat16),
        solved,
        (((0,), (0,)), ((), ())),
        preferred_element_type=jnp.float32,
    ).astype(jnp.bfloat16)
    back_load = jnp.concatenate(
        [
            run_factor.reshape(tile_slots, seg_count * rank_width),
            counts_int.astype(jnp.bfloat16),
        ],
        axis=1,
    )
    back_load = lax.all_to_all(
        back_load.reshape(n_ent, slot_cap, -1), "ent", split_axis=0, concat_axis=0, tiled=True
    ).reshape(tile_slots, -1)
    back_factor = back_load[:, : seg_count * rank_width]
    back_counts = back_load[:, seg_count * rank_width :].astype(jnp.float32)
    back_weight = jnp.where(
        live_send[:, None] & (back_counts > 0), 1.0 + ALPHA * back_counts, jnp.float32(0.0)
    )
    item_hot = item_ids[:, :, None] == jnp.arange(item_count, dtype=jnp.int32)[None, None, :]
    run_weight = back_weight.reshape(tile_slots * seg_count, seg_length)
    hot_runs = item_hot.reshape(tile_slots * seg_count, seg_length, item_count)
    spread_mat = jnp.sum(jnp.where(hot_runs, run_weight[:, :, None], 0.0), axis=1)
    item_rhs = lax.dot_general(
        spread_mat,
        back_factor.reshape(tile_slots * seg_count, rank_width).astype(jnp.float32),
        (((0,), (0,)), ((), ())),
        precision=highest,
        preferred_element_type=jnp.float32,
    )
    return (own_factors, item_rhs * RHS_SCALE)


def solution(mesh):
    in_specs = (
        P(("ent", "rep"), None),
        P("ent", "rep", None, None),
        P("ent", "rep", None),
        P("ent", "rep", None, None),
        P("ent", "rep", None, None),
        P("ent", "rep", None),
    )
    out_specs = (P(("ent", "rep"), None), P(("ent", "rep"), None))
    return jax.shard_map(shards, mesh=mesh, in_specs=in_specs, out_specs=out_specs, check_vma=False)
```

```python
import functools

import jax
import jax.numpy as jnp
from jax import lax
from jax.experimental import pallas as pl
from jax.experimental.pallas import tpu as pltpu
from jax.sharding import PartitionSpec as P

MESH_ID = pl.DeviceIdType.MESH

U_DEV = 2


ALPHA = 40.0
RIDGE = 1.0
RHS_SCALE = 1.0 / 640.0


def cholesky_solve(a_s, l_s, y_s, out_ref):
    batch, n, _ = a_s.shape
    out_ref[...] = jnp.zeros_like(out_ref)
    lane_v = lax.broadcasted_iota(jnp.int32, (1, n), 1)

    def factor(top, j, carry):
        span = n - top
        lane_m = lax.broadcasted_iota(jnp.int32, (span, n), 1)
        sub_m = lax.broadcasted_iota(jnp.int32, (span, n), 0) + top
        sub_v = lax.broadcasted_iota(jnp.int32, (span, 1), 0) + top
        for b in range(batch):
            a = a_s[b, top:, :]
            row = jnp.sum(jnp.where(sub_m == j, a, 0.0), axis=0, keepdims=True)
            col = jnp.sum(jnp.where(lane_m == j, a, 0.0), axis=1, keepdims=True)
            diag = jnp.sum(jnp.where(lane_v == j, row, 0.0), axis=1, keepdims=True)
            inv = 1.0 / jnp.sqrt(diag)
            l_row = jnp.where(lane_v >= j, row, 0.0) * inv
            l_col = jnp.where(sub_v >= j, col, 0.0) * inv
            a_s[b, top:, :] = a - l_col * l_row
            l_s[b, pl.ds(j, 1), :] = l_row
            y = y_s[pl.ds(b, 1), :]
            y_j = jnp.sum(jnp.where(lane_v == j, y, 0.0), axis=1, keepdims=True) * inv
            y_s[pl.ds(b, 1), :] = jnp.where(lane_v == j, y_j, y - y_j * l_row)
        return carry

    quarter = n // 4
    for part in range(4):
        top = part * quarter
        lax.fori_loop(top, top + quarter, functools.partial(factor, top), 0)

    def back(t, carry):
        j = n - 1 - t
        for b in range(batch):
            l_j = l_s[b, pl.ds(j, 1), :]
            x = out_ref[pl.ds(b, 1), :]
            y_j = jnp.sum(jnp.where(lane_v == j, y_s[pl.ds(b, 1), :], 0.0), axis=1, keepdims=True)
            l_jj = jnp.sum(jnp.where(lane_v == j, l_j, 0.0), axis=1, keepdims=True)
            known = jnp.sum(jnp.where(lane_v > j, l_j * x, 0.0), axis=1, keepdims=True)
            out_ref[pl.ds(b, 1), :] = jnp.where(lane_v == j, (y_j - known) / l_jj, x)
        return carry

    lax.fori_loop(0, n, back, 0)


def flip_bits(value, mask, bits):
    out = value - value % (1 << bits)
    for bit in range(bits):
        here = (value // (1 << bit)) % 2
        out = out + (1 << bit) * ((1 - here) if (mask >> bit) & 1 else here)
    return out


def doubling_kernel(
    n_rep, low_bits, rounds, x_ref, o_ref, full_recv, piece_recv, piece, gath,
    sem_a, sem_b, sem_c, sem_d, sem_e, sem_f,
):
    flat = lax.axis_index("ent") * n_rep + lax.axis_index("rep")
    group = 1 << low_bits
    rows = x_ref.shape[0] // group
    slot = flat % group

    def place(p):
        return (p // n_rep, p % n_rep)

    def flip(bit):
        step = 1 << bit
        upper = (flat // step) % 2
        return flat + step - 2 * step * upper

    members = [flip_bits(flat, k, low_bits) for k in range(1, group)]
    outer = [flip(bit) for bit in range(low_bits, rounds)]
    barrier = pltpu.get_barrier_semaphore()
    for p in members + outer:
        pl.semaphore_signal(barrier, inc=1, device_id=place(p), device_id_type=MESH_ID)
    pl.semaphore_wait(barrier, len(members) + len(outer))

    o_ref[...] = x_ref[...]
    for bit in range(low_bits):
        copy = pltpu.make_async_remote_copy(
            src_ref=o_ref, dst_ref=full_recv.at[bit], send_sem=sem_a.at[bit],
            recv_sem=sem_b.at[bit], device_id=place(flip(bit)), device_id_type=MESH_ID,
        )
        copy.start()
        copy.wait_recv()
        copy.wait_send()
        o_ref[...] = o_ref[...] + full_recv[bit]

    piece[...] = o_ref[pl.ds(pl.multiple_of(slot * rows, rows), rows), :]
    for index, p in enumerate(outer):
        copy = pltpu.make_async_remote_copy(
            src_ref=piece, dst_ref=piece_recv.at[index], send_sem=sem_c.at[index],
            recv_sem=sem_d.at[index], device_id=place(p), device_id_type=MESH_ID,
        )
        copy.start()
        copy.wait_recv()
        copy.wait_send()
        piece[...] = piece[...] + piece_recv[index]

    gath[slot] = piece[...]
    sends = []
    for index, p in enumerate(members):
        copy = pltpu.make_async_remote_copy(
            src_ref=piece, dst_ref=gath.at[slot], send_sem=sem_e.at[index],
            recv_sem=sem_f.at[slot], device_id=place(p), device_id_type=MESH_ID,
        )
        copy.start()
        sends.append(copy)
    for k in range(1, group):
        source = flip_bits(slot, k, low_bits)
        pltpu.make_async_remote_copy(
            src_ref=piece, dst_ref=gath.at[source], send_sem=sem_e.at[k - 1],
            recv_sem=sem_f.at[source], device_id=place(members[k - 1]), device_id_type=MESH_ID,
        ).wait_recv()
    for copy in sends:
        copy.wait_send()
    for part in range(group):
        o_ref[pl.ds(part * rows, rows), :] = gath[part]


def tree_sum(value, count):
    rounds = count.bit_length() - 1
    n_rep = lax.axis_size("rep")
    low_bits = (n_rep * 2).bit_length() - 1
    group = 1 << low_bits
    rows = value.shape[0] // group
    outer = rounds - low_bits
    return pl.pallas_call(
        functools.partial(doubling_kernel, n_rep, low_bits, rounds),
        out_shape=jax.ShapeDtypeStruct(value.shape, value.dtype),
        in_specs=[pl.BlockSpec(memory_space=pltpu.VMEM)],
        out_specs=pl.BlockSpec(memory_space=pltpu.VMEM),
        scratch_shapes=[
            pltpu.VMEM((low_bits,) + value.shape, value.dtype),
            pltpu.VMEM((outer, rows, value.shape[1]), value.dtype),
            pltpu.VMEM((rows, value.shape[1]), value.dtype),
            pltpu.VMEM((group, rows, value.shape[1]), value.dtype),
            pltpu.SemaphoreType.DMA((low_bits,)),
            pltpu.SemaphoreType.DMA((low_bits,)),
            pltpu.SemaphoreType.DMA((outer,)),
            pltpu.SemaphoreType.DMA((outer,)),
            pltpu.SemaphoreType.DMA((group - 1,)),
            pltpu.SemaphoreType.DMA((group,)),
        ],
        compiler_params=pltpu.CompilerParams(collective_id=0, has_side_effects=True),
    )(value)


def rep_peers(n_rep):
    me = lax.axis_index("rep")
    return me, [(me + shift) % n_rep for shift in range(1, n_rep)]


def owner_kernel(n_rep, blocks_ref, base_ref, out_ref, x_s, recv, a_s, l_s, y_s, fac, gath,
                 sem_a, sem_b, sem_c, sem_d):
    me, peers = rep_peers(n_rep)
    ent = lax.axis_index("ent")
    batch, n, _ = a_s.shape
    barrier = pltpu.get_barrier_semaphore()
    for peer in peers:
        pl.semaphore_signal(barrier, inc=1, device_id=(ent, peer), device_id_type=MESH_ID)
    pl.semaphore_wait(barrier, n_rep - 1)
    copies = []
    for index, peer in enumerate(peers):
        copy = pltpu.make_async_remote_copy(
            src_ref=blocks_ref.at[peer], dst_ref=recv.at[index], send_sem=sem_a.at[index],
            recv_sem=sem_b.at[index], device_id=(ent, peer), device_id_type=MESH_ID,
        )
        copy.start()
        copies.append(copy)
    total = blocks_ref[me]
    for index, copy in enumerate(copies):
        copy.wait_recv()
        total = total + recv[index]
    for copy in copies:
        copy.wait_send()
    base = base_ref[...]
    for b in range(batch):
        gram = total[b * n : (b + 1) * n] + base
        a_s[b] = (gram + gram.T) / 2
    y_s[...] = total[batch * n : batch * n + batch]
    cholesky_solve(a_s, l_s, y_s, x_s)
    fac[...] = x_s[...].astype(fac.dtype)
    gath[me] = fac[...]
    sends = []
    for index, peer in enumerate(peers):
        copy = pltpu.make_async_remote_copy(
            src_ref=fac, dst_ref=gath.at[me], send_sem=sem_c.at[index],
            recv_sem=sem_d.at[me], device_id=(ent, peer), device_id_type=MESH_ID,
        )
        copy.start()
        sends.append(copy)
    for index, source in enumerate(peers):
        pltpu.make_async_remote_copy(
            src_ref=fac, dst_ref=gath.at[source], send_sem=sem_c.at[index],
            recv_sem=sem_d.at[source], device_id=(ent, source), device_id_type=MESH_ID,
        ).wait_recv()
    for copy in sends:
        copy.wait_send()
    out_ref[...] = gath[...]


def solve_owned(blocks, base, n_rep, per_dev):
    n = blocks.shape[2]
    return pl.pallas_call(
        functools.partial(owner_kernel, n_rep),
        out_shape=(
            jax.ShapeDtypeStruct((n_rep, per_dev, n), jnp.bfloat16),
            jax.ShapeDtypeStruct((per_dev, n), jnp.float32),
        ),
        in_specs=[pl.BlockSpec(memory_space=pltpu.VMEM)] * 2,
        out_specs=(pl.BlockSpec(memory_space=pltpu.VMEM), pl.BlockSpec(memory_space=pltpu.VMEM)),
        scratch_shapes=[
            pltpu.VMEM((n_rep - 1,) + blocks.shape[1:], jnp.float32),
            pltpu.VMEM((per_dev, n, n), jnp.float32),
            pltpu.VMEM((per_dev, n, n), jnp.float32),
            pltpu.VMEM((per_dev, n), jnp.float32),
            pltpu.VMEM((per_dev, n), jnp.bfloat16),
            pltpu.VMEM((n_rep, per_dev, n), jnp.bfloat16),
            pltpu.SemaphoreType.DMA((n_rep - 1,)),
            pltpu.SemaphoreType.DMA((n_rep - 1,)),
            pltpu.SemaphoreType.DMA((n_rep - 1,)),
            pltpu.SemaphoreType.DMA((n_rep,)),
        ],
        compiler_params=pltpu.CompilerParams(collective_id=1, has_side_effects=True),
    )(blocks, base)


def gather_kernel(idx_ref, table_t_ref, out_ref):
    step = pl.program_id(0)
    idx = idx_ref[pl.ds(step, 1), :]
    picks = lax.broadcasted_iota(jnp.int32, (table_t_ref.shape[1], idx.shape[1]), 0) == idx
    rows_t = jnp.dot(table_t_ref[...], picks.astype(jnp.bfloat16), preferred_element_type=jnp.float32)
    out_ref[...] = rows_t.T.astype(out_ref.dtype)


def gather_rows(table, idx, chunk=512):
    count = idx.shape[0]
    idx_lanes = idx.reshape(count // chunk, chunk)
    return pl.pallas_call(
        gather_kernel,
        out_shape=jax.ShapeDtypeStruct((count, table.shape[1]), table.dtype),
        grid=(count // chunk,),
        in_specs=[
            pl.BlockSpec(idx_lanes.shape, lambda i: (0, 0)),
            pl.BlockSpec((table.shape[1], table.shape[0]), lambda i: (0, 0)),
        ],
        out_specs=pl.BlockSpec((chunk, table.shape[1]), lambda i: (i, 0)),
        cost_estimate=pl.CostEstimate(
            flops=2 * count * table.shape[0] * table.shape[1],
            transcendentals=0,
            bytes_accessed=count * 4 + table.size * 2 + count * table.shape[1] * 2,
        ),
    )(idx_lanes, table.T)


def gram_kernel(n_user, per_dev, rows_ref, gw_ref, user_ref, rw_ref, out_ref):
    step = pl.program_id(0)
    width = rows_ref.shape[1]

    @pl.when(step == 0)
    def _():
        out_ref[...] = jnp.zeros_like(out_ref)

    rows = rows_ref[...]
    rows_t = rows.astype(jnp.float32).T
    weights_t = (rows_t * gw_ref[pl.ds(step, 1), :]).astype(jnp.bfloat16)
    users = user_ref[pl.ds(step, 1), :]
    zero = jnp.zeros((), jnp.bfloat16)
    for user in range(n_user):
        picked = jnp.where(users == user, weights_t, zero)
        block, spot = user // per_dev, (user % per_dev) * width
        out_ref[block, spot : spot + width, :] += jnp.dot(
            picked, rows, preferred_element_type=jnp.float32
        )
    slots = lax.broadcasted_iota(jnp.int32, (n_user, users.shape[1]), 0)
    per_user = jnp.where(users == slots, rw_ref[pl.ds(step, 1), :], 0.0)
    high = per_user.astype(jnp.bfloat16)
    low = (per_user - high.astype(jnp.float32)).astype(jnp.bfloat16)
    rhs = jnp.dot(high, rows, preferred_element_type=jnp.float32) + jnp.dot(
        low, rows, preferred_element_type=jnp.float32
    )
    base = per_dev * width
    for block in range(n_user // per_dev):
        out_ref[block, base : base + per_dev, :] += rhs[block * per_dev : (block + 1) * per_dev]


def user_grams(rows, gw_lanes, user_lanes, rw_lanes, n_user, per_dev):
    chunks, chunk = gw_lanes.shape
    width = rows.shape[1]
    n_block = n_user // per_dev
    block_rows = per_dev * width + per_dev
    return pl.pallas_call(
        functools.partial(gram_kernel, n_user, per_dev),
        out_shape=jax.ShapeDtypeStruct((n_block, block_rows, width), jnp.float32),
        grid=(chunks,),
        in_specs=[
            pl.BlockSpec((chunk, width), lambda i: (i, 0)),
            pl.BlockSpec((chunks, chunk), lambda i: (0, 0)),
            pl.BlockSpec((chunks, chunk), lambda i: (0, 0)),
            pl.BlockSpec((chunks, chunk), lambda i: (0, 0)),
        ],
        out_specs=pl.BlockSpec((n_block, block_rows, width), lambda i: (0, 0, 0)),
        cost_estimate=pl.CostEstimate(
            flops=2 * rows.shape[0] * width * width * (n_user + 2),
            transcendentals=0,
            bytes_accessed=rows.size * 2 + 12 * rows.shape[0] + n_user * width * (width + 1) * 4,
        ),
    )(rows, gw_lanes, user_lanes, rw_lanes)

def shards(item_factors, tile_items, send_tiles, tile_users, tile_counts, recv_tiles):
    highest = lax.Precision.HIGHEST
    rank_width = item_factors.shape[1]
    item_count = item_factors.shape[0]
    n_ent = lax.axis_size("ent")
    n_rep = lax.axis_size("rep")
    tile_slots = tile_items.shape[2]
    tile_rows = tile_items.shape[3]
    seg_count = tile_users.shape[3]
    seg_length = tile_rows // seg_count
    slot_cap = tile_slots // n_ent
    user_block = U_DEV * lax.axis_size("rep")
    item_ids = tile_items.reshape(tile_slots, tile_rows)
    slot_pos = jnp.arange(tile_slots, dtype=jnp.int32) % slot_cap
    live_send = slot_pos < jnp.repeat(send_tiles.reshape(n_ent), slot_cap)
    live_recv = slot_pos < jnp.repeat(recv_tiles.reshape(n_ent), slot_cap)
    partial_gram = lax.dot_general(
        item_factors, item_factors, (((0,), (0,)), ((), ())), preferred_element_type=jnp.float32
    )
    live_rows = jnp.repeat(live_send, tile_rows)
    picked = gather_rows(item_factors, jnp.where(live_rows, item_ids.reshape(-1), -1))
    incoming = lax.all_to_all(
        picked.reshape(n_ent, slot_cap * tile_rows, rank_width),
        "ent",
        split_axis=0,
        concat_axis=0,
        tiled=True,
    )
    counts_int = tile_counts.reshape(tile_slots, tile_rows)
    counts_f = counts_int.astype(jnp.float32)
    gram_weight = ALPHA * counts_f
    rhs_weight = jnp.where(
        live_recv[:, None] & (counts_int > 0), 1.0 + ALPHA * counts_f, jnp.float32(0.0)
    )
    owners = tile_users.reshape(tile_slots * seg_count)
    selector = owners[None, :] == jnp.arange(user_block, dtype=jnp.int32)[:, None]
    selector_f = selector.astype(jnp.float32)
    rows_all = incoming.reshape(tile_slots * tile_rows, rank_width)
    lane_chunk = 1024
    row_owner = jnp.repeat(owners, seg_length)
    gram_blocks = user_grams(
        rows_all,
        gram_weight.reshape(-1, lane_chunk),
        row_owner.reshape(-1, lane_chunk),
        rhs_weight.reshape(-1, lane_chunk),
        user_block,
        U_DEV,
    )
    identity_mat = jnp.eye(rank_width, dtype=jnp.float32)
    added_term = tree_sum(partial_gram, n_ent * n_rep) + RIDGE * identity_mat
    solved, own_factors = solve_owned(gram_blocks, added_term, n_rep, U_DEV)
    solved = solved.reshape(user_block, rank_width)
    run_factor = lax.dot_general(
        selector.astype(jnp.bfloat16),
        solved,
        (((0,), (0,)), ((), ())),
        preferred_element_type=jnp.float32,
    ).astype(jnp.bfloat16)
    back_load = jnp.concatenate(
        [
            run_factor.reshape(tile_slots, seg_count * rank_width),
            counts_int.astype(jnp.bfloat16),
        ],
        axis=1,
    )
    back_load = lax.all_to_all(
        back_load.reshape(n_ent, slot_cap, -1), "ent", split_axis=0, concat_axis=0, tiled=True
    ).reshape(tile_slots, -1)
    back_factor = back_load[:, : seg_count * rank_width]
    back_counts = back_load[:, seg_count * rank_width :].astype(jnp.int32)
    back_weight = jnp.where(live_send[:, None] & (back_counts > 0), 1 + 40 * back_counts, 0)
    run_count = tile_slots * seg_count
    run_items = item_ids.reshape(run_count, seg_length)
    run_weight = back_weight.reshape(run_count, seg_length)
    minor = 32
    major = item_count // minor
    hot_major = (run_items[:, :, None] // minor == jnp.arange(major)[None, None, :]).astype(jnp.bfloat16)
    hot_minor = (run_items[:, :, None] % minor == jnp.arange(minor)[None, None, :]).astype(jnp.bfloat16)
    weight_top = (run_weight // 16) * 16
    weight_hi = weight_top.astype(jnp.bfloat16)
    weight_lo = (run_weight - weight_top).astype(jnp.bfloat16)
    weighted_minor = jnp.concatenate(
        [hot_minor * weight_hi[:, :, None], hot_minor * weight_lo[:, :, None]], axis=2
    )
    both = jnp.einsum("rla,rlc->rac", hot_major, weighted_minor, preferred_element_type=jnp.float32)
    spread_mat = (both[:, :, :minor] + both[:, :, minor:]).reshape(run_count, item_count)
    item_rhs = lax.dot_general(
        spread_mat,
        back_factor.reshape(run_count, rank_width).astype(jnp.float32),
        (((0,), (0,)), ((), ())),
        precision=highest,
        preferred_element_type=jnp.float32,
    )
    return (own_factors, item_rhs * RHS_SCALE)


def solution(mesh):
    in_specs = (
        P(("ent", "rep"), None),
        P("ent", "rep", None, None),
        P("ent", "rep", None),
        P("ent", "rep", None, None),
        P("ent", "rep", None, None),
        P("ent", "rep", None),
    )
    out_specs = (P(("ent", "rep"), None), P(("ent", "rep"), None))
    return jax.shard_map(shards, mesh=mesh, in_specs=in_specs, out_specs=out_specs, check_vma=False)
```

```python
import functools

import jax
import jax.numpy as jnp
from jax import lax
from jax.experimental import pallas as pl
from jax.experimental.pallas import tpu as pltpu
from jax.sharding import PartitionSpec as P

MESH_ID = pl.DeviceIdType.MESH

U_DEV = 2


ALPHA = 40.0
RIDGE = 1.0
RHS_SCALE = 1.0 / 640.0


def cholesky_solve(a_s, l_s, y_s, out_ref):
    batch, n, _ = a_s.shape
    out_ref[...] = jnp.zeros_like(out_ref)
    lane_v = lax.broadcasted_iota(jnp.int32, (1, n), 1)

    def factor(top, j, carry):
        span = n - top
        lane_m = lax.broadcasted_iota(jnp.int32, (span, n), 1)
        sub_m = lax.broadcasted_iota(jnp.int32, (span, n), 0) + top
        sub_v = lax.broadcasted_iota(jnp.int32, (span, 1), 0) + top
        for b in range(batch):
            a = a_s[b, top:, :]
            row = jnp.sum(jnp.where(sub_m == j, a, 0.0), axis=0, keepdims=True)
            col = jnp.sum(jnp.where(lane_m == j, a, 0.0), axis=1, keepdims=True)
            diag = jnp.sum(jnp.where(lane_v == j, row, 0.0), axis=1, keepdims=True)
            inv = 1.0 / jnp.sqrt(diag)
            l_row = jnp.where(lane_v >= j, row, 0.0) * inv
            l_col = jnp.where(sub_v >= j, col, 0.0) * inv
            a_s[b, top:, :] = a - l_col * l_row
            l_s[b, pl.ds(j, 1), :] = l_row
            y = y_s[pl.ds(b, 1), :]
            y_j = jnp.sum(jnp.where(lane_v == j, y, 0.0), axis=1, keepdims=True) * inv
            y_s[pl.ds(b, 1), :] = jnp.where(lane_v == j, y_j, y - y_j * l_row)
        return carry

    quarter = n // 4
    for part in range(4):
        top = part * quarter
        lax.fori_loop(top, top + quarter, functools.partial(factor, top), 0)

    def back(t, carry):
        j = n - 1 - t
        for b in range(batch):
            l_j = l_s[b, pl.ds(j, 1), :]
            x = out_ref[pl.ds(b, 1), :]
            y_j = jnp.sum(jnp.where(lane_v == j, y_s[pl.ds(b, 1), :], 0.0), axis=1, keepdims=True)
            l_jj = jnp.sum(jnp.where(lane_v == j, l_j, 0.0), axis=1, keepdims=True)
            known = jnp.sum(jnp.where(lane_v > j, l_j * x, 0.0), axis=1, keepdims=True)
            out_ref[pl.ds(b, 1), :] = jnp.where(lane_v == j, (y_j - known) / l_jj, x)
        return carry

    lax.fori_loop(0, n, back, 0)


def flip_bits(value, mask, bits):
    out = value - value % (1 << bits)
    for bit in range(bits):
        here = (value // (1 << bit)) % 2
        out = out + (1 << bit) * ((1 - here) if (mask >> bit) & 1 else here)
    return out


def doubling_kernel(
    n_rep, low_bits, rounds, x_ref, o_ref, full_recv, piece_recv, piece, gath,
    sem_a, sem_b, sem_c, sem_d, sem_e, sem_f,
):
    flat = lax.axis_index("ent") * n_rep + lax.axis_index("rep")
    group = 1 << low_bits
    rows = x_ref.shape[0] // group
    slot = flat % group

    def place(p):
        return (p // n_rep, p % n_rep)

    def flip(bit):
        step = 1 << bit
        upper = (flat // step) % 2
        return flat + step - 2 * step * upper

    members = [flip_bits(flat, k, low_bits) for k in range(1, group)]
    outer = [flip(bit) for bit in range(low_bits, rounds)]
    barrier = pltpu.get_barrier_semaphore()
    for p in members + outer:
        pl.semaphore_signal(barrier, inc=1, device_id=place(p), device_id_type=MESH_ID)
    pl.semaphore_wait(barrier, len(members) + len(outer))

    o_ref[...] = x_ref[...]
    for bit in range(low_bits):
        copy = pltpu.make_async_remote_copy(
            src_ref=o_ref, dst_ref=full_recv.at[bit], send_sem=sem_a.at[bit],
            recv_sem=sem_b.at[bit], device_id=place(flip(bit)), device_id_type=MESH_ID,
        )
        copy.start()
        copy.wait_recv()
        copy.wait_send()
        o_ref[...] = o_ref[...] + full_recv[bit]

    piece[...] = o_ref[pl.ds(pl.multiple_of(slot * rows, rows), rows), :]
    for index, p in enumerate(outer):
        copy = pltpu.make_async_remote_copy(
            src_ref=piece, dst_ref=piece_recv.at[index], send_sem=sem_c.at[index],
            recv_sem=sem_d.at[index], device_id=place(p), device_id_type=MESH_ID,
        )
        copy.start()
        copy.wait_recv()
        copy.wait_send()
        piece[...] = piece[...] + piece_recv[index]

    gath[slot] = piece[...]
    sends = []
    for index, p in enumerate(members):
        copy = pltpu.make_async_remote_copy(
            src_ref=piece, dst_ref=gath.at[slot], send_sem=sem_e.at[index],
            recv_sem=sem_f.at[slot], device_id=place(p), device_id_type=MESH_ID,
        )
        copy.start()
        sends.append(copy)
    for k in range(1, group):
        source = flip_bits(slot, k, low_bits)
        pltpu.make_async_remote_copy(
            src_ref=piece, dst_ref=gath.at[source], send_sem=sem_e.at[k - 1],
            recv_sem=sem_f.at[source], device_id=place(members[k - 1]), device_id_type=MESH_ID,
        ).wait_recv()
    for copy in sends:
        copy.wait_send()
    for part in range(group):
        o_ref[pl.ds(part * rows, rows), :] = gath[part]


def tree_sum(value, count):
    rounds = count.bit_length() - 1
    n_rep = lax.axis_size("rep")
    low_bits = (n_rep * 2).bit_length() - 1
    group = 1 << low_bits
    rows = value.shape[0] // group
    outer = rounds - low_bits
    return pl.pallas_call(
        functools.partial(doubling_kernel, n_rep, low_bits, rounds),
        out_shape=jax.ShapeDtypeStruct(value.shape, value.dtype),
        in_specs=[pl.BlockSpec(memory_space=pltpu.VMEM)],
        out_specs=pl.BlockSpec(memory_space=pltpu.VMEM),
        scratch_shapes=[
            pltpu.VMEM((low_bits,) + value.shape, value.dtype),
            pltpu.VMEM((outer, rows, value.shape[1]), value.dtype),
            pltpu.VMEM((rows, value.shape[1]), value.dtype),
            pltpu.VMEM((group, rows, value.shape[1]), value.dtype),
            pltpu.SemaphoreType.DMA((low_bits,)),
            pltpu.SemaphoreType.DMA((low_bits,)),
            pltpu.SemaphoreType.DMA((outer,)),
            pltpu.SemaphoreType.DMA((outer,)),
            pltpu.SemaphoreType.DMA((group - 1,)),
            pltpu.SemaphoreType.DMA((group,)),
        ],
        compiler_params=pltpu.CompilerParams(collective_id=0, has_side_effects=True),
    )(value)


def rep_peers(n_rep):
    me = lax.axis_index("rep")
    return me, [(me + shift) % n_rep for shift in range(1, n_rep)]


def owner_kernel(n_rep, blocks_ref, base_ref, out_ref, x_s, recv, a_s, l_s, y_s, fac, gath,
                 sem_a, sem_b, sem_c, sem_d):
    me, peers = rep_peers(n_rep)
    ent = lax.axis_index("ent")
    batch, n, _ = a_s.shape
    barrier = pltpu.get_barrier_semaphore()
    for peer in peers:
        pl.semaphore_signal(barrier, inc=1, device_id=(ent, peer), device_id_type=MESH_ID)
    pl.semaphore_wait(barrier, n_rep - 1)
    copies = []
    for index, peer in enumerate(peers):
        copy = pltpu.make_async_remote_copy(
            src_ref=blocks_ref.at[peer], dst_ref=recv.at[index], send_sem=sem_a.at[index],
            recv_sem=sem_b.at[index], device_id=(ent, peer), device_id_type=MESH_ID,
        )
        copy.start()
        copies.append(copy)
    total = blocks_ref[me]
    for index, copy in enumerate(copies):
        copy.wait_recv()
        total = total + recv[index]
    for copy in copies:
        copy.wait_send()
    base = base_ref[...]
    for b in range(batch):
        gram = total[b * n : (b + 1) * n] + base
        a_s[b] = (gram + gram.T) / 2
    y_s[...] = total[batch * n : batch * n + batch]
    cholesky_solve(a_s, l_s, y_s, x_s)
    fac[...] = x_s[...].astype(fac.dtype)
    gath[me] = fac[...]
    sends = []
    for index, peer in enumerate(peers):
        copy = pltpu.make_async_remote_copy(
            src_ref=fac, dst_ref=gath.at[me], send_sem=sem_c.at[index],
            recv_sem=sem_d.at[me], device_id=(ent, peer), device_id_type=MESH_ID,
        )
        copy.start()
        sends.append(copy)
    for index, source in enumerate(peers):
        pltpu.make_async_remote_copy(
            src_ref=fac, dst_ref=gath.at[source], send_sem=sem_c.at[index],
            recv_sem=sem_d.at[source], device_id=(ent, source), device_id_type=MESH_ID,
        ).wait_recv()
    for copy in sends:
        copy.wait_send()
    out_ref[...] = gath[...]


def solve_owned(blocks, base, n_rep, per_dev):
    n = blocks.shape[2]
    return pl.pallas_call(
        functools.partial(owner_kernel, n_rep),
        out_shape=(
            jax.ShapeDtypeStruct((n_rep, per_dev, n), jnp.bfloat16),
            jax.ShapeDtypeStruct((per_dev, n), jnp.float32),
        ),
        in_specs=[pl.BlockSpec(memory_space=pltpu.VMEM)] * 2,
        out_specs=(pl.BlockSpec(memory_space=pltpu.VMEM), pl.BlockSpec(memory_space=pltpu.VMEM)),
        scratch_shapes=[
            pltpu.VMEM((n_rep - 1,) + blocks.shape[1:], jnp.float32),
            pltpu.VMEM((per_dev, n, n), jnp.float32),
            pltpu.VMEM((per_dev, n, n), jnp.float32),
            pltpu.VMEM((per_dev, n), jnp.float32),
            pltpu.VMEM((per_dev, n), jnp.bfloat16),
            pltpu.VMEM((n_rep, per_dev, n), jnp.bfloat16),
            pltpu.SemaphoreType.DMA((n_rep - 1,)),
            pltpu.SemaphoreType.DMA((n_rep - 1,)),
            pltpu.SemaphoreType.DMA((n_rep - 1,)),
            pltpu.SemaphoreType.DMA((n_rep,)),
        ],
        compiler_params=pltpu.CompilerParams(collective_id=1, has_side_effects=True),
    )(blocks, base)


def gather_kernel(idx_ref, table_t_ref, out_ref):
    step = pl.program_id(0)
    idx = idx_ref[pl.ds(step, 1), :]
    picks = lax.broadcasted_iota(jnp.int32, (table_t_ref.shape[1], idx.shape[1]), 0) == idx
    rows_t = jnp.dot(table_t_ref[...], picks.astype(jnp.bfloat16), preferred_element_type=jnp.float32)
    out_ref[...] = rows_t.T.astype(out_ref.dtype)


def gather_rows(table, idx, chunk=1024):
    count = idx.shape[0]
    idx_lanes = idx.reshape(count // chunk, chunk)
    return pl.pallas_call(
        gather_kernel,
        out_shape=jax.ShapeDtypeStruct((count, table.shape[1]), table.dtype),
        grid=(count // chunk,),
        in_specs=[
            pl.BlockSpec(idx_lanes.shape, lambda i: (0, 0)),
            pl.BlockSpec((table.shape[1], table.shape[0]), lambda i: (0, 0)),
        ],
        out_specs=pl.BlockSpec((chunk, table.shape[1]), lambda i: (i, 0)),
        cost_estimate=pl.CostEstimate(
            flops=2 * count * table.shape[0] * table.shape[1],
            transcendentals=0,
            bytes_accessed=count * 4 + table.size * 2 + count * table.shape[1] * 2,
        ),
    )(idx_lanes, table.T)


def gram_kernel(n_user, per_dev, rows_ref, gw_ref, user_ref, rw_ref, out_ref):
    step = pl.program_id(0)
    width = rows_ref.shape[1]

    @pl.when(step == 0)
    def _():
        out_ref[...] = jnp.zeros_like(out_ref)

    rows = rows_ref[...]
    rows_t = rows.astype(jnp.float32).T
    weights_t = (rows_t * gw_ref[pl.ds(step, 1), :]).astype(jnp.bfloat16)
    users = user_ref[pl.ds(step, 1), :]
    zero = jnp.zeros((), jnp.bfloat16)
    for user in range(n_user):
        picked = jnp.where(users == user, weights_t, zero)
        block, spot = user // per_dev, (user % per_dev) * width
        out_ref[block, spot : spot + width, :] += jnp.dot(
            picked, rows, preferred_element_type=jnp.float32
        )
    slots = lax.broadcasted_iota(jnp.int32, (n_user, users.shape[1]), 0)
    per_user = jnp.where(users == slots, rw_ref[pl.ds(step, 1), :], 0.0)
    high = per_user.astype(jnp.bfloat16)
    low = (per_user - high.astype(jnp.float32)).astype(jnp.bfloat16)
    rhs = jnp.dot(high, rows, preferred_element_type=jnp.float32) + jnp.dot(
        low, rows, preferred_element_type=jnp.float32
    )
    base = per_dev * width
    for block in range(n_user // per_dev):
        out_ref[block, base : base + per_dev, :] += rhs[block * per_dev : (block + 1) * per_dev]


def user_grams(rows, gw_lanes, user_lanes, rw_lanes, n_user, per_dev):
    chunks, chunk = gw_lanes.shape
    width = rows.shape[1]
    n_block = n_user // per_dev
    block_rows = per_dev * width + per_dev
    return pl.pallas_call(
        functools.partial(gram_kernel, n_user, per_dev),
        out_shape=jax.ShapeDtypeStruct((n_block, block_rows, width), jnp.float32),
        grid=(chunks,),
        in_specs=[
            pl.BlockSpec((chunk, width), lambda i: (i, 0)),
            pl.BlockSpec((chunks, chunk), lambda i: (0, 0)),
            pl.BlockSpec((chunks, chunk), lambda i: (0, 0)),
            pl.BlockSpec((chunks, chunk), lambda i: (0, 0)),
        ],
        out_specs=pl.BlockSpec((n_block, block_rows, width), lambda i: (0, 0, 0)),
        cost_estimate=pl.CostEstimate(
            flops=2 * rows.shape[0] * width * width * (n_user + 2),
            transcendentals=0,
            bytes_accessed=rows.size * 2 + 12 * rows.shape[0] + n_user * width * (width + 1) * 4,
        ),
    )(rows, gw_lanes, user_lanes, rw_lanes)

def shards(item_factors, tile_items, send_tiles, tile_users, tile_counts, recv_tiles):
    highest = lax.Precision.HIGHEST
    rank_width = item_factors.shape[1]
    item_count = item_factors.shape[0]
    n_ent = lax.axis_size("ent")
    n_rep = lax.axis_size("rep")
    tile_slots = tile_items.shape[2]
    tile_rows = tile_items.shape[3]
    seg_count = tile_users.shape[3]
    seg_length = tile_rows // seg_count
    slot_cap = tile_slots // n_ent
    user_block = U_DEV * lax.axis_size("rep")
    item_ids = tile_items.reshape(tile_slots, tile_rows)
    slot_pos = jnp.arange(tile_slots, dtype=jnp.int32) % slot_cap
    live_send = slot_pos < jnp.repeat(send_tiles.reshape(n_ent), slot_cap)
    live_recv = slot_pos < jnp.repeat(recv_tiles.reshape(n_ent), slot_cap)
    partial_gram = lax.dot_general(
        item_factors, item_factors, (((0,), (0,)), ((), ())), preferred_element_type=jnp.float32
    )
    live_rows = jnp.repeat(live_send, tile_rows)
    picked = gather_rows(item_factors, jnp.where(live_rows, item_ids.reshape(-1), -1))
    incoming = lax.all_to_all(
        picked.reshape(n_ent, slot_cap * tile_rows, rank_width),
        "ent",
        split_axis=0,
        concat_axis=0,
        tiled=True,
    )
    counts_int = tile_counts.reshape(tile_slots, tile_rows)
    counts_f = counts_int.astype(jnp.float32)
    gram_weight = ALPHA * counts_f
    rhs_weight = jnp.where(
        live_recv[:, None] & (counts_int > 0), 1.0 + ALPHA * counts_f, jnp.float32(0.0)
    )
    owners = tile_users.reshape(tile_slots * seg_count)
    selector = owners[None, :] == jnp.arange(user_block, dtype=jnp.int32)[:, None]
    selector_f = selector.astype(jnp.float32)
    rows_all = incoming.reshape(tile_slots * tile_rows, rank_width)
    lane_chunk = 1024
    row_owner = jnp.repeat(owners, seg_length)
    gram_blocks = user_grams(
        rows_all,
        gram_weight.reshape(-1, lane_chunk),
        row_owner.reshape(-1, lane_chunk),
        rhs_weight.reshape(-1, lane_chunk),
        user_block,
        U_DEV,
    )
    identity_mat = jnp.eye(rank_width, dtype=jnp.float32)
    added_term = tree_sum(partial_gram, n_ent * n_rep) + RIDGE * identity_mat
    solved, own_factors = solve_owned(gram_blocks, added_term, n_rep, U_DEV)
    solved = solved.reshape(user_block, rank_width)
    run_factor = lax.dot_general(
        selector.astype(jnp.bfloat16),
        solved,
        (((0,), (0,)), ((), ())),
        preferred_element_type=jnp.float32,
    ).astype(jnp.bfloat16)
    back_load = jnp.concatenate(
        [
            run_factor.reshape(tile_slots, seg_count * rank_width),
            counts_int.astype(jnp.bfloat16),
        ],
        axis=1,
    )
    back_load = lax.all_to_all(
        back_load.reshape(n_ent, slot_cap, -1), "ent", split_axis=0, concat_axis=0, tiled=True
    ).reshape(tile_slots, -1)
    back_factor = back_load[:, : seg_count * rank_width]
    back_counts = back_load[:, seg_count * rank_width :].astype(jnp.float32)
    back_weight = jnp.where(
        live_send[:, None] & (back_counts > 0), 1.0 + ALPHA * back_counts, jnp.float32(0.0)
    )
    item_hot = item_ids[:, :, None] == jnp.arange(item_count, dtype=jnp.int32)[None, None, :]
    run_weight = back_weight.reshape(tile_slots * seg_count, seg_length)
    hot_runs = item_hot.reshape(tile_slots * seg_count, seg_length, item_count)
    spread_mat = jnp.sum(jnp.where(hot_runs, run_weight[:, :, None], 0.0), axis=1)
    item_rhs = lax.dot_general(
        spread_mat,
        back_factor.reshape(tile_slots * seg_count, rank_width).astype(jnp.float32),
        (((0,), (0,)), ((), ())),
        precision=highest,
        preferred_element_type=jnp.float32,
    )
    return (own_factors, item_rhs * RHS_SCALE)


def solution(mesh):
    in_specs = (
        P(("ent", "rep"), None),
        P("ent", "rep", None, None),
        P("ent", "rep", None),
        P("ent", "rep", None, None),
        P("ent", "rep", None, None),
        P("ent", "rep", None),
    )
    out_specs = (P(("ent", "rep"), None), P(("ent", "rep"), None))
    return jax.shard_map(shards, mesh=mesh, in_specs=in_specs, out_specs=out_specs, check_vma=False)
```

```python
import functools

import jax
import jax.numpy as jnp
from jax import lax
from jax.experimental import pallas as pl
from jax.experimental.pallas import tpu as pltpu
from jax.sharding import PartitionSpec as P

MESH_ID = pl.DeviceIdType.MESH

U_DEV = 2


ALPHA = 40.0
RIDGE = 1.0
RHS_SCALE = 1.0 / 640.0


def cholesky_solve(a_s, l_s, y_s, out_ref):
    batch, n, _ = a_s.shape
    out_ref[...] = jnp.zeros_like(out_ref)
    lane_v = lax.broadcasted_iota(jnp.int32, (1, n), 1)

    def factor(top, j, carry):
        span = n - top
        lane_m = lax.broadcasted_iota(jnp.int32, (span, n), 1)
        sub_m = lax.broadcasted_iota(jnp.int32, (span, n), 0) + top
        sub_v = lax.broadcasted_iota(jnp.int32, (span, 1), 0) + top
        for b in range(batch):
            a = a_s[b, top:, :]
            row = jnp.sum(jnp.where(sub_m == j, a, 0.0), axis=0, keepdims=True)
            col = jnp.sum(jnp.where(lane_m == j, a, 0.0), axis=1, keepdims=True)
            diag = jnp.sum(jnp.where(lane_v == j, row, 0.0), axis=1, keepdims=True)
            inv = 1.0 / jnp.sqrt(diag)
            l_row = jnp.where(lane_v >= j, row, 0.0) * inv
            l_col = jnp.where(sub_v >= j, col, 0.0) * inv
            a_s[b, top:, :] = a - l_col * l_row
            l_s[b, pl.ds(j, 1), :] = l_row
            y = y_s[pl.ds(b, 1), :]
            y_j = jnp.sum(jnp.where(lane_v == j, y, 0.0), axis=1, keepdims=True) * inv
            y_s[pl.ds(b, 1), :] = jnp.where(lane_v == j, y_j, y - y_j * l_row)
        return carry

    quarter = n // 4
    for part in range(4):
        top = part * quarter
        lax.fori_loop(top, top + quarter, functools.partial(factor, top), 0)

    def back(t, carry):
        j = n - 1 - t
        for b in range(batch):
            l_j = l_s[b, pl.ds(j, 1), :]
            x = out_ref[pl.ds(b, 1), :]
            y_j = jnp.sum(jnp.where(lane_v == j, y_s[pl.ds(b, 1), :], 0.0), axis=1, keepdims=True)
            l_jj = jnp.sum(jnp.where(lane_v == j, l_j, 0.0), axis=1, keepdims=True)
            known = jnp.sum(jnp.where(lane_v > j, l_j * x, 0.0), axis=1, keepdims=True)
            out_ref[pl.ds(b, 1), :] = jnp.where(lane_v == j, (y_j - known) / l_jj, x)
        return carry

    lax.fori_loop(0, n, back, 0)


def flip_bits(value, mask, bits):
    out = value - value % (1 << bits)
    for bit in range(bits):
        here = (value // (1 << bit)) % 2
        out = out + (1 << bit) * ((1 - here) if (mask >> bit) & 1 else here)
    return out


def doubling_kernel(
    n_rep, low_bits, rounds, x_ref, o_ref, full_recv, piece_recv, piece, gath,
    sem_a, sem_b, sem_c, sem_d, sem_e, sem_f,
):
    flat = lax.axis_index("ent") * n_rep + lax.axis_index("rep")
    group = 1 << low_bits
    rows = x_ref.shape[0] // group
    slot = flat % group

    def place(p):
        return (p // n_rep, p % n_rep)

    def flip(bit):
        step = 1 << bit
        upper = (flat // step) % 2
        return flat + step - 2 * step * upper

    members = [flip_bits(flat, k, low_bits) for k in range(1, group)]
    outer = [flip(bit) for bit in range(low_bits, rounds)]
    barrier = pltpu.get_barrier_semaphore()
    for p in members + outer:
        pl.semaphore_signal(barrier, inc=1, device_id=place(p), device_id_type=MESH_ID)
    pl.semaphore_wait(barrier, len(members) + len(outer))

    o_ref[...] = x_ref[...]
    for bit in range(low_bits):
        copy = pltpu.make_async_remote_copy(
            src_ref=o_ref, dst_ref=full_recv.at[bit], send_sem=sem_a.at[bit],
            recv_sem=sem_b.at[bit], device_id=place(flip(bit)), device_id_type=MESH_ID,
        )
        copy.start()
        copy.wait_recv()
        copy.wait_send()
        o_ref[...] = o_ref[...] + full_recv[bit]

    piece[...] = o_ref[pl.ds(pl.multiple_of(slot * rows, rows), rows), :]
    for index, p in enumerate(outer):
        copy = pltpu.make_async_remote_copy(
            src_ref=piece, dst_ref=piece_recv.at[index], send_sem=sem_c.at[index],
            recv_sem=sem_d.at[index], device_id=place(p), device_id_type=MESH_ID,
        )
        copy.start()
        copy.wait_recv()
        copy.wait_send()
        piece[...] = piece[...] + piece_recv[index]

    gath[slot] = piece[...]
    sends = []
    for index, p in enumerate(members):
        copy = pltpu.make_async_remote_copy(
            src_ref=piece, dst_ref=gath.at[slot], send_sem=sem_e.at[index],
            recv_sem=sem_f.at[slot], device_id=place(p), device_id_type=MESH_ID,
        )
        copy.start()
        sends.append(copy)
    for k in range(1, group):
        source = flip_bits(slot, k, low_bits)
        pltpu.make_async_remote_copy(
            src_ref=piece, dst_ref=gath.at[source], send_sem=sem_e.at[k - 1],
            recv_sem=sem_f.at[source], device_id=place(members[k - 1]), device_id_type=MESH_ID,
        ).wait_recv()
    for copy in sends:
        copy.wait_send()
    for part in range(group):
        o_ref[pl.ds(part * rows, rows), :] = gath[part]


def tree_sum(value, count):
    rounds = count.bit_length() - 1
    n_rep = lax.axis_size("rep")
    low_bits = (n_rep * 2).bit_length() - 1
    group = 1 << low_bits
    rows = value.shape[0] // group
    outer = rounds - low_bits
    return pl.pallas_call(
        functools.partial(doubling_kernel, n_rep, low_bits, rounds),
        out_shape=jax.ShapeDtypeStruct(value.shape, value.dtype),
        in_specs=[pl.BlockSpec(memory_space=pltpu.VMEM)],
        out_specs=pl.BlockSpec(memory_space=pltpu.VMEM),
        scratch_shapes=[
            pltpu.VMEM((low_bits,) + value.shape, value.dtype),
            pltpu.VMEM((outer, rows, value.shape[1]), value.dtype),
            pltpu.VMEM((rows, value.shape[1]), value.dtype),
            pltpu.VMEM((group, rows, value.shape[1]), value.dtype),
            pltpu.SemaphoreType.DMA((low_bits,)),
            pltpu.SemaphoreType.DMA((low_bits,)),
            pltpu.SemaphoreType.DMA((outer,)),
            pltpu.SemaphoreType.DMA((outer,)),
            pltpu.SemaphoreType.DMA((group - 1,)),
            pltpu.SemaphoreType.DMA((group,)),
        ],
        compiler_params=pltpu.CompilerParams(collective_id=0, has_side_effects=True),
    )(value)


def rep_peers(n_rep):
    me = lax.axis_index("rep")
    return me, [(me + shift) % n_rep for shift in range(1, n_rep)]


def owner_kernel(n_rep, blocks_ref, base_ref, out_ref, x_s, recv, a_s, l_s, y_s, fac, gath,
                 sem_a, sem_b, sem_c, sem_d):
    me, peers = rep_peers(n_rep)
    ent = lax.axis_index("ent")
    batch, n, _ = a_s.shape
    barrier = pltpu.get_barrier_semaphore()
    for peer in peers:
        pl.semaphore_signal(barrier, inc=1, device_id=(ent, peer), device_id_type=MESH_ID)
    pl.semaphore_wait(barrier, n_rep - 1)
    copies = []
    for index, peer in enumerate(peers):
        copy = pltpu.make_async_remote_copy(
            src_ref=blocks_ref.at[peer], dst_ref=recv.at[index], send_sem=sem_a.at[index],
            recv_sem=sem_b.at[index], device_id=(ent, peer), device_id_type=MESH_ID,
        )
        copy.start()
        copies.append(copy)
    total = blocks_ref[me]
    for index, copy in enumerate(copies):
        copy.wait_recv()
        total = total + recv[index]
    for copy in copies:
        copy.wait_send()
    base = base_ref[...]
    for b in range(batch):
        gram = total[b * n : (b + 1) * n] + base
        a_s[b] = (gram + gram.T) / 2
    y_s[...] = total[batch * n : batch * n + batch]
    cholesky_solve(a_s, l_s, y_s, x_s)
    fac[...] = x_s[...].astype(fac.dtype)
    gath[me] = fac[...]
    sends = []
    for index, peer in enumerate(peers):
        copy = pltpu.make_async_remote_copy(
            src_ref=fac, dst_ref=gath.at[me], send_sem=sem_c.at[index],
            recv_sem=sem_d.at[me], device_id=(ent, peer), device_id_type=MESH_ID,
        )
        copy.start()
        sends.append(copy)
    for index, source in enumerate(peers):
        pltpu.make_async_remote_copy(
            src_ref=fac, dst_ref=gath.at[source], send_sem=sem_c.at[index],
            recv_sem=sem_d.at[source], device_id=(ent, source), device_id_type=MESH_ID,
        ).wait_recv()
    for copy in sends:
        copy.wait_send()
    out_ref[...] = gath[...]


def solve_owned(blocks, base, n_rep, per_dev):
    n = blocks.shape[2]
    return pl.pallas_call(
        functools.partial(owner_kernel, n_rep),
        out_shape=(
            jax.ShapeDtypeStruct((n_rep, per_dev, n), jnp.bfloat16),
            jax.ShapeDtypeStruct((per_dev, n), jnp.float32),
        ),
        in_specs=[pl.BlockSpec(memory_space=pltpu.VMEM)] * 2,
        out_specs=(pl.BlockSpec(memory_space=pltpu.VMEM), pl.BlockSpec(memory_space=pltpu.VMEM)),
        scratch_shapes=[
            pltpu.VMEM((n_rep - 1,) + blocks.shape[1:], jnp.float32),
            pltpu.VMEM((per_dev, n, n), jnp.float32),
            pltpu.VMEM((per_dev, n, n), jnp.float32),
            pltpu.VMEM((per_dev, n), jnp.float32),
            pltpu.VMEM((per_dev, n), jnp.bfloat16),
            pltpu.VMEM((n_rep, per_dev, n), jnp.bfloat16),
            pltpu.SemaphoreType.DMA((n_rep - 1,)),
            pltpu.SemaphoreType.DMA((n_rep - 1,)),
            pltpu.SemaphoreType.DMA((n_rep - 1,)),
            pltpu.SemaphoreType.DMA((n_rep,)),
        ],
        compiler_params=pltpu.CompilerParams(collective_id=1, has_side_effects=True),
    )(blocks, base)


def gather_kernel(idx_ref, table_t_ref, out_ref):
    step = pl.program_id(0)
    idx = idx_ref[pl.ds(step, 1), :]
    picks = lax.broadcasted_iota(jnp.int32, (table_t_ref.shape[1], idx.shape[1]), 0) == idx
    rows_t = jnp.dot(table_t_ref[...], picks.astype(jnp.bfloat16), preferred_element_type=jnp.float32)
    out_ref[...] = rows_t.T.astype(out_ref.dtype)


def gather_rows(table, idx, chunk=2048):
    count = idx.shape[0]
    idx_lanes = idx.reshape(count // chunk, chunk)
    return pl.pallas_call(
        gather_kernel,
        out_shape=jax.ShapeDtypeStruct((count, table.shape[1]), table.dtype),
        grid=(count // chunk,),
        in_specs=[
            pl.BlockSpec(idx_lanes.shape, lambda i: (0, 0)),
            pl.BlockSpec((table.shape[1], table.shape[0]), lambda i: (0, 0)),
        ],
        out_specs=pl.BlockSpec((chunk, table.shape[1]), lambda i: (i, 0)),
        cost_estimate=pl.CostEstimate(
            flops=2 * count * table.shape[0] * table.shape[1],
            transcendentals=0,
            bytes_accessed=count * 4 + table.size * 2 + count * table.shape[1] * 2,
        ),
    )(idx_lanes, table.T)


def gram_kernel(n_user, per_dev, rows_ref, gw_ref, user_ref, rw_ref, out_ref):
    step = pl.program_id(0)
    width = rows_ref.shape[1]

    @pl.when(step == 0)
    def _():
        out_ref[...] = jnp.zeros_like(out_ref)

    rows = rows_ref[...]
    rows_t = rows.astype(jnp.float32).T
    weights_t = (rows_t * gw_ref[pl.ds(step, 1), :]).astype(jnp.bfloat16)
    users = user_ref[pl.ds(step, 1), :]
    zero = jnp.zeros((), jnp.bfloat16)
    for user in range(n_user):
        picked = jnp.where(users == user, weights_t, zero)
        block, spot = user // per_dev, (user % per_dev) * width
        out_ref[block, spot : spot + width, :] += jnp.dot(
            picked, rows, preferred_element_type=jnp.float32
        )
    slots = lax.broadcasted_iota(jnp.int32, (n_user, users.shape[1]), 0)
    per_user = jnp.where(users == slots, rw_ref[pl.ds(step, 1), :], 0.0)
    high = per_user.astype(jnp.bfloat16)
    low = (per_user - high.astype(jnp.float32)).astype(jnp.bfloat16)
    rhs = jnp.dot(high, rows, preferred_element_type=jnp.float32) + jnp.dot(
        low, rows, preferred_element_type=jnp.float32
    )
    base = per_dev * width
    for block in range(n_user // per_dev):
        out_ref[block, base : base + per_dev, :] += rhs[block * per_dev : (block + 1) * per_dev]


def user_grams(rows, gw_lanes, user_lanes, rw_lanes, n_user, per_dev):
    chunks, chunk = gw_lanes.shape
    width = rows.shape[1]
    n_block = n_user // per_dev
    block_rows = per_dev * width + per_dev
    return pl.pallas_call(
        functools.partial(gram_kernel, n_user, per_dev),
        out_shape=jax.ShapeDtypeStruct((n_block, block_rows, width), jnp.float32),
        grid=(chunks,),
        in_specs=[
            pl.BlockSpec((chunk, width), lambda i: (i, 0)),
            pl.BlockSpec((chunks, chunk), lambda i: (0, 0)),
            pl.BlockSpec((chunks, chunk), lambda i: (0, 0)),
            pl.BlockSpec((chunks, chunk), lambda i: (0, 0)),
        ],
        out_specs=pl.BlockSpec((n_block, block_rows, width), lambda i: (0, 0, 0)),
        cost_estimate=pl.CostEstimate(
            flops=2 * rows.shape[0] * width * width * (n_user + 2),
            transcendentals=0,
            bytes_accessed=rows.size * 2 + 12 * rows.shape[0] + n_user * width * (width + 1) * 4,
        ),
    )(rows, gw_lanes, user_lanes, rw_lanes)

def shards(item_factors, tile_items, send_tiles, tile_users, tile_counts, recv_tiles):
    highest = lax.Precision.HIGHEST
    rank_width = item_factors.shape[1]
    item_count = item_factors.shape[0]
    n_ent = lax.axis_size("ent")
    n_rep = lax.axis_size("rep")
    tile_slots = tile_items.shape[2]
    tile_rows = tile_items.shape[3]
    seg_count = tile_users.shape[3]
    seg_length = tile_rows // seg_count
    slot_cap = tile_slots // n_ent
    user_block = U_DEV * lax.axis_size("rep")
    item_ids = tile_items.reshape(tile_slots, tile_rows)
    slot_pos = jnp.arange(tile_slots, dtype=jnp.int32) % slot_cap
    live_send = slot_pos < jnp.repeat(send_tiles.reshape(n_ent), slot_cap)
    live_recv = slot_pos < jnp.repeat(recv_tiles.reshape(n_ent), slot_cap)
    partial_gram = lax.dot_general(
        item_factors, item_factors, (((0,), (0,)), ((), ())), preferred_element_type=jnp.float32
    )
    live_rows = jnp.repeat(live_send, tile_rows)
    picked = gather_rows(item_factors, jnp.where(live_rows, item_ids.reshape(-1), -1))
    incoming = lax.all_to_all(
        picked.reshape(n_ent, slot_cap * tile_rows, rank_width),
        "ent",
        split_axis=0,
        concat_axis=0,
        tiled=True,
    )
    counts_int = tile_counts.reshape(tile_slots, tile_rows)
    counts_f = counts_int.astype(jnp.float32)
    gram_weight = ALPHA * counts_f
    rhs_weight = jnp.where(
        live_recv[:, None] & (counts_int > 0), 1.0 + ALPHA * counts_f, jnp.float32(0.0)
    )
    owners = tile_users.reshape(tile_slots * seg_count)
    selector = owners[None, :] == jnp.arange(user_block, dtype=jnp.int32)[:, None]
    selector_f = selector.astype(jnp.float32)
    rows_all = incoming.reshape(tile_slots * tile_rows, rank_width)
    lane_chunk = 2048
    row_owner = jnp.repeat(owners, seg_length)
    gram_blocks = user_grams(
        rows_all,
        gram_weight.reshape(-1, lane_chunk),
        row_owner.reshape(-1, lane_chunk),
        rhs_weight.reshape(-1, lane_chunk),
        user_block,
        U_DEV,
    )
    identity_mat = jnp.eye(rank_width, dtype=jnp.float32)
    added_term = tree_sum(partial_gram, n_ent * n_rep) + RIDGE * identity_mat
    solved, own_factors = solve_owned(gram_blocks, added_term, n_rep, U_DEV)
    solved = solved.reshape(user_block, rank_width)
    run_factor = lax.dot_general(
        selector.astype(jnp.bfloat16),
        solved,
        (((0,), (0,)), ((), ())),
        preferred_element_type=jnp.float32,
    ).astype(jnp.bfloat16)
    back_load = jnp.concatenate(
        [
            run_factor.reshape(tile_slots, seg_count * rank_width),
            counts_int.astype(jnp.bfloat16),
        ],
        axis=1,
    )
    back_load = lax.all_to_all(
        back_load.reshape(n_ent, slot_cap, -1), "ent", split_axis=0, concat_axis=0, tiled=True
    ).reshape(tile_slots, -1)
    back_factor = back_load[:, : seg_count * rank_width]
    back_counts = back_load[:, seg_count * rank_width :].astype(jnp.float32)
    back_weight = jnp.where(
        live_send[:, None] & (back_counts > 0), 1.0 + ALPHA * back_counts, jnp.float32(0.0)
    )
    item_hot = item_ids[:, :, None] == jnp.arange(item_count, dtype=jnp.int32)[None, None, :]
    run_weight = back_weight.reshape(tile_slots * seg_count, seg_length)
    hot_runs = item_hot.reshape(tile_slots * seg_count, seg_length, item_count)
    spread_mat = jnp.sum(jnp.where(hot_runs, run_weight[:, :, None], 0.0), axis=1)
    item_rhs = lax.dot_general(
        spread_mat,
        back_factor.reshape(tile_slots * seg_count, rank_width).astype(jnp.float32),
        (((0,), (0,)), ((), ())),
        precision=highest,
        preferred_element_type=jnp.float32,
    )
    return (own_factors, item_rhs * RHS_SCALE)


def solution(mesh):
    in_specs = (
        P(("ent", "rep"), None),
        P("ent", "rep", None, None),
        P("ent", "rep", None),
        P("ent", "rep", None, None),
        P("ent", "rep", None, None),
        P("ent", "rep", None),
    )
    out_specs = (P(("ent", "rep"), None), P(("ent", "rep"), None))
    return jax.shard_map(shards, mesh=mesh, in_specs=in_specs, out_specs=out_specs, check_vma=False)
```

```python
import functools

import jax
import jax.numpy as jnp
from jax import lax
from jax.experimental import pallas as pl
from jax.experimental.pallas import tpu as pltpu
from jax.sharding import PartitionSpec as P

MESH_ID = pl.DeviceIdType.MESH

U_DEV = 2


ALPHA = 40.0
RIDGE = 1.0
RHS_SCALE = 1.0 / 640.0


def cholesky_solve(a_s, l_s, y_s, out_ref):
    batch, n, _ = a_s.shape
    out_ref[...] = jnp.zeros_like(out_ref)
    lane_v = lax.broadcasted_iota(jnp.int32, (1, n), 1)

    def factor(top, j, carry):
        span = n - top
        lane_m = lax.broadcasted_iota(jnp.int32, (span, n), 1)
        sub_m = lax.broadcasted_iota(jnp.int32, (span, n), 0) + top
        sub_v = lax.broadcasted_iota(jnp.int32, (span, 1), 0) + top
        for b in range(batch):
            a = a_s[b, top:, :]
            row = jnp.sum(jnp.where(sub_m == j, a, 0.0), axis=0, keepdims=True)
            col = jnp.sum(jnp.where(lane_m == j, a, 0.0), axis=1, keepdims=True)
            diag = jnp.sum(jnp.where(lane_v == j, row, 0.0), axis=1, keepdims=True)
            inv = 1.0 / jnp.sqrt(diag)
            l_row = jnp.where(lane_v >= j, row, 0.0) * inv
            l_col = jnp.where(sub_v >= j, col, 0.0) * inv
            a_s[b, top:, :] = a - l_col * l_row
            l_s[b, pl.ds(j, 1), :] = l_row
            y = y_s[pl.ds(b, 1), :]
            y_j = jnp.sum(jnp.where(lane_v == j, y, 0.0), axis=1, keepdims=True) * inv
            y_s[pl.ds(b, 1), :] = jnp.where(lane_v == j, y_j, y - y_j * l_row)
        return carry

    quarter = n // 4
    for part in range(4):
        top = part * quarter
        lax.fori_loop(top, top + quarter, functools.partial(factor, top), 0, unroll=2)

    def back(t, carry):
        j = n - 1 - t
        for b in range(batch):
            l_j = l_s[b, pl.ds(j, 1), :]
            x = out_ref[pl.ds(b, 1), :]
            y_j = jnp.sum(jnp.where(lane_v == j, y_s[pl.ds(b, 1), :], 0.0), axis=1, keepdims=True)
            l_jj = jnp.sum(jnp.where(lane_v == j, l_j, 0.0), axis=1, keepdims=True)
            known = jnp.sum(jnp.where(lane_v > j, l_j * x, 0.0), axis=1, keepdims=True)
            out_ref[pl.ds(b, 1), :] = jnp.where(lane_v == j, (y_j - known) / l_jj, x)
        return carry

    lax.fori_loop(0, n, back, 0, unroll=2)


def flip_bits(value, mask, bits):
    out = value - value % (1 << bits)
    for bit in range(bits):
        here = (value // (1 << bit)) % 2
        out = out + (1 << bit) * ((1 - here) if (mask >> bit) & 1 else here)
    return out


def doubling_kernel(
    n_rep, low_bits, rounds, x_ref, o_ref, full_recv, piece_recv, piece, gath,
    sem_a, sem_b, sem_c, sem_d, sem_e, sem_f,
):
    flat = lax.axis_index("ent") * n_rep + lax.axis_index("rep")
    group = 1 << low_bits
    rows = x_ref.shape[0] // group
    slot = flat % group

    def place(p):
        return (p // n_rep, p % n_rep)

    def flip(bit):
        step = 1 << bit
        upper = (flat // step) % 2
        return flat + step - 2 * step * upper

    members = [flip_bits(flat, k, low_bits) for k in range(1, group)]
    outer = [flip(bit) for bit in range(low_bits, rounds)]
    barrier = pltpu.get_barrier_semaphore()
    for p in members + outer:
        pl.semaphore_signal(barrier, inc=1, device_id=place(p), device_id_type=MESH_ID)
    pl.semaphore_wait(barrier, len(members) + len(outer))

    o_ref[...] = x_ref[...]
    for bit in range(low_bits):
        copy = pltpu.make_async_remote_copy(
            src_ref=o_ref, dst_ref=full_recv.at[bit], send_sem=sem_a.at[bit],
            recv_sem=sem_b.at[bit], device_id=place(flip(bit)), device_id_type=MESH_ID,
        )
        copy.start()
        copy.wait_recv()
        copy.wait_send()
        o_ref[...] = o_ref[...] + full_recv[bit]

    piece[...] = o_ref[pl.ds(pl.multiple_of(slot * rows, rows), rows), :]
    for index, p in enumerate(outer):
        copy = pltpu.make_async_remote_copy(
            src_ref=piece, dst_ref=piece_recv.at[index], send_sem=sem_c.at[index],
            recv_sem=sem_d.at[index], device_id=place(p), device_id_type=MESH_ID,
        )
        copy.start()
        copy.wait_recv()
        copy.wait_send()
        piece[...] = piece[...] + piece_recv[index]

    gath[slot] = piece[...]
    sends = []
    for index, p in enumerate(members):
        copy = pltpu.make_async_remote_copy(
            src_ref=piece, dst_ref=gath.at[slot], send_sem=sem_e.at[index],
            recv_sem=sem_f.at[slot], device_id=place(p), device_id_type=MESH_ID,
        )
        copy.start()
        sends.append(copy)
    for k in range(1, group):
        source = flip_bits(slot, k, low_bits)
        pltpu.make_async_remote_copy(
            src_ref=piece, dst_ref=gath.at[source], send_sem=sem_e.at[k - 1],
            recv_sem=sem_f.at[source], device_id=place(members[k - 1]), device_id_type=MESH_ID,
        ).wait_recv()
    for copy in sends:
        copy.wait_send()
    for part in range(group):
        o_ref[pl.ds(part * rows, rows), :] = gath[part]


def tree_sum(value, count):
    rounds = count.bit_length() - 1
    n_rep = lax.axis_size("rep")
    low_bits = (n_rep * 2).bit_length() - 1
    group = 1 << low_bits
    rows = value.shape[0] // group
    outer = rounds - low_bits
    return pl.pallas_call(
        functools.partial(doubling_kernel, n_rep, low_bits, rounds),
        out_shape=jax.ShapeDtypeStruct(value.shape, value.dtype),
        in_specs=[pl.BlockSpec(memory_space=pltpu.VMEM)],
        out_specs=pl.BlockSpec(memory_space=pltpu.VMEM),
        scratch_shapes=[
            pltpu.VMEM((low_bits,) + value.shape, value.dtype),
            pltpu.VMEM((outer, rows, value.shape[1]), value.dtype),
            pltpu.VMEM((rows, value.shape[1]), value.dtype),
            pltpu.VMEM((group, rows, value.shape[1]), value.dtype),
            pltpu.SemaphoreType.DMA((low_bits,)),
            pltpu.SemaphoreType.DMA((low_bits,)),
            pltpu.SemaphoreType.DMA((outer,)),
            pltpu.SemaphoreType.DMA((outer,)),
            pltpu.SemaphoreType.DMA((group - 1,)),
            pltpu.SemaphoreType.DMA((group,)),
        ],
        compiler_params=pltpu.CompilerParams(collective_id=0, has_side_effects=True),
    )(value)


def rep_peers(n_rep):
    me = lax.axis_index("rep")
    return me, [(me + shift) % n_rep for shift in range(1, n_rep)]


def owner_kernel(n_rep, blocks_ref, base_ref, out_ref, x_s, recv, a_s, l_s, y_s, fac, gath,
                 sem_a, sem_b, sem_c, sem_d):
    me, peers = rep_peers(n_rep)
    ent = lax.axis_index("ent")
    batch, n, _ = a_s.shape
    barrier = pltpu.get_barrier_semaphore()
    for peer in peers:
        pl.semaphore_signal(barrier, inc=1, device_id=(ent, peer), device_id_type=MESH_ID)
    pl.semaphore_wait(barrier, n_rep - 1)
    copies = []
    for index, peer in enumerate(peers):
        copy = pltpu.make_async_remote_copy(
            src_ref=blocks_ref.at[peer], dst_ref=recv.at[index], send_sem=sem_a.at[index],
            recv_sem=sem_b.at[index], device_id=(ent, peer), device_id_type=MESH_ID,
        )
        copy.start()
        copies.append(copy)
    total = blocks_ref[me]
    for index, copy in enumerate(copies):
        copy.wait_recv()
        total = total + recv[index]
    for copy in copies:
        copy.wait_send()
    base = base_ref[...]
    for b in range(batch):
        gram = total[b * n : (b + 1) * n] + base
        a_s[b] = (gram + gram.T) / 2
    y_s[...] = total[batch * n : batch * n + batch]
    cholesky_solve(a_s, l_s, y_s, x_s)
    fac[...] = x_s[...].astype(fac.dtype)
    gath[me] = fac[...]
    sends = []
    for index, peer in enumerate(peers):
        copy = pltpu.make_async_remote_copy(
            src_ref=fac, dst_ref=gath.at[me], send_sem=sem_c.at[index],
            recv_sem=sem_d.at[me], device_id=(ent, peer), device_id_type=MESH_ID,
        )
        copy.start()
        sends.append(copy)
    for index, source in enumerate(peers):
        pltpu.make_async_remote_copy(
            src_ref=fac, dst_ref=gath.at[source], send_sem=sem_c.at[index],
            recv_sem=sem_d.at[source], device_id=(ent, source), device_id_type=MESH_ID,
        ).wait_recv()
    for copy in sends:
        copy.wait_send()
    out_ref[...] = gath[...]


def solve_owned(blocks, base, n_rep, per_dev):
    n = blocks.shape[2]
    return pl.pallas_call(
        functools.partial(owner_kernel, n_rep),
        out_shape=(
            jax.ShapeDtypeStruct((n_rep, per_dev, n), jnp.bfloat16),
            jax.ShapeDtypeStruct((per_dev, n), jnp.float32),
        ),
        in_specs=[pl.BlockSpec(memory_space=pltpu.VMEM)] * 2,
        out_specs=(pl.BlockSpec(memory_space=pltpu.VMEM), pl.BlockSpec(memory_space=pltpu.VMEM)),
        scratch_shapes=[
            pltpu.VMEM((n_rep - 1,) + blocks.shape[1:], jnp.float32),
            pltpu.VMEM((per_dev, n, n), jnp.float32),
            pltpu.VMEM((per_dev, n, n), jnp.float32),
            pltpu.VMEM((per_dev, n), jnp.float32),
            pltpu.VMEM((per_dev, n), jnp.bfloat16),
            pltpu.VMEM((n_rep, per_dev, n), jnp.bfloat16),
            pltpu.SemaphoreType.DMA((n_rep - 1,)),
            pltpu.SemaphoreType.DMA((n_rep - 1,)),
            pltpu.SemaphoreType.DMA((n_rep - 1,)),
            pltpu.SemaphoreType.DMA((n_rep,)),
        ],
        compiler_params=pltpu.CompilerParams(collective_id=1, has_side_effects=True),
    )(blocks, base)


def gather_kernel(idx_ref, table_t_ref, out_ref):
    step = pl.program_id(0)
    idx = idx_ref[pl.ds(step, 1), :]
    picks = lax.broadcasted_iota(jnp.int32, (table_t_ref.shape[1], idx.shape[1]), 0) == idx
    rows_t = jnp.dot(table_t_ref[...], picks.astype(jnp.bfloat16), preferred_element_type=jnp.float32)
    out_ref[...] = rows_t.T.astype(out_ref.dtype)


def gather_rows(table, idx, chunk=2048):
    count = idx.shape[0]
    idx_lanes = idx.reshape(count // chunk, chunk)
    return pl.pallas_call(
        gather_kernel,
        out_shape=jax.ShapeDtypeStruct((count, table.shape[1]), table.dtype),
        grid=(count // chunk,),
        in_specs=[
            pl.BlockSpec(idx_lanes.shape, lambda i: (0, 0)),
            pl.BlockSpec((table.shape[1], table.shape[0]), lambda i: (0, 0)),
        ],
        out_specs=pl.BlockSpec((chunk, table.shape[1]), lambda i: (i, 0)),
        cost_estimate=pl.CostEstimate(
            flops=2 * count * table.shape[0] * table.shape[1],
            transcendentals=0,
            bytes_accessed=count * 4 + table.size * 2 + count * table.shape[1] * 2,
        ),
    )(idx_lanes, table.T)


def gram_kernel(n_user, per_dev, rows_ref, gw_ref, user_ref, rw_ref, out_ref):
    step = pl.program_id(0)
    width = rows_ref.shape[1]

    @pl.when(step == 0)
    def _():
        out_ref[...] = jnp.zeros_like(out_ref)

    rows = rows_ref[...]
    rows_t = rows.astype(jnp.float32).T
    weights_t = (rows_t * gw_ref[pl.ds(step, 1), :]).astype(jnp.bfloat16)
    users = user_ref[pl.ds(step, 1), :]
    zero = jnp.zeros((), jnp.bfloat16)
    for user in range(n_user):
        picked = jnp.where(users == user, weights_t, zero)
        block, spot = user // per_dev, (user % per_dev) * width
        out_ref[block, spot : spot + width, :] += jnp.dot(
            picked, rows, preferred_element_type=jnp.float32
        )
    slots = lax.broadcasted_iota(jnp.int32, (n_user, users.shape[1]), 0)
    per_user = jnp.where(users == slots, rw_ref[pl.ds(step, 1), :], 0.0)
    high = per_user.astype(jnp.bfloat16)
    low = (per_user - high.astype(jnp.float32)).astype(jnp.bfloat16)
    rhs = jnp.dot(high, rows, preferred_element_type=jnp.float32) + jnp.dot(
        low, rows, preferred_element_type=jnp.float32
    )
    base = per_dev * width
    for block in range(n_user // per_dev):
        out_ref[block, base : base + per_dev, :] += rhs[block * per_dev : (block + 1) * per_dev]


def user_grams(rows, gw_lanes, user_lanes, rw_lanes, n_user, per_dev):
    chunks, chunk = gw_lanes.shape
    width = rows.shape[1]
    n_block = n_user // per_dev
    block_rows = per_dev * width + per_dev
    return pl.pallas_call(
        functools.partial(gram_kernel, n_user, per_dev),
        out_shape=jax.ShapeDtypeStruct((n_block, block_rows, width), jnp.float32),
        grid=(chunks,),
        in_specs=[
            pl.BlockSpec((chunk, width), lambda i: (i, 0)),
            pl.BlockSpec((chunks, chunk), lambda i: (0, 0)),
            pl.BlockSpec((chunks, chunk), lambda i: (0, 0)),
            pl.BlockSpec((chunks, chunk), lambda i: (0, 0)),
        ],
        out_specs=pl.BlockSpec((n_block, block_rows, width), lambda i: (0, 0, 0)),
        cost_estimate=pl.CostEstimate(
            flops=2 * rows.shape[0] * width * width * (n_user + 2),
            transcendentals=0,
            bytes_accessed=rows.size * 2 + 12 * rows.shape[0] + n_user * width * (width + 1) * 4,
        ),
    )(rows, gw_lanes, user_lanes, rw_lanes)

def shards(item_factors, tile_items, send_tiles, tile_users, tile_counts, recv_tiles):
    highest = lax.Precision.HIGHEST
    rank_width = item_factors.shape[1]
    item_count = item_factors.shape[0]
    n_ent = lax.axis_size("ent")
    n_rep = lax.axis_size("rep")
    tile_slots = tile_items.shape[2]
    tile_rows = tile_items.shape[3]
    seg_count = tile_users.shape[3]
    seg_length = tile_rows // seg_count
    slot_cap = tile_slots // n_ent
    user_block = U_DEV * lax.axis_size("rep")
    item_ids = tile_items.reshape(tile_slots, tile_rows)
    slot_pos = jnp.arange(tile_slots, dtype=jnp.int32) % slot_cap
    live_send = slot_pos < jnp.repeat(send_tiles.reshape(n_ent), slot_cap)
    live_recv = slot_pos < jnp.repeat(recv_tiles.reshape(n_ent), slot_cap)
    partial_gram = lax.dot_general(
        item_factors, item_factors, (((0,), (0,)), ((), ())), preferred_element_type=jnp.float32
    )
    live_rows = jnp.repeat(live_send, tile_rows)
    picked = gather_rows(item_factors, jnp.where(live_rows, item_ids.reshape(-1), -1))
    incoming = lax.all_to_all(
        picked.reshape(n_ent, slot_cap * tile_rows, rank_width),
        "ent",
        split_axis=0,
        concat_axis=0,
        tiled=True,
    )
    counts_int = tile_counts.reshape(tile_slots, tile_rows)
    counts_f = counts_int.astype(jnp.float32)
    gram_weight = ALPHA * counts_f
    rhs_weight = jnp.where(
        live_recv[:, None] & (counts_int > 0), 1.0 + ALPHA * counts_f, jnp.float32(0.0)
    )
    owners = tile_users.reshape(tile_slots * seg_count)
    selector = owners[None, :] == jnp.arange(user_block, dtype=jnp.int32)[:, None]
    selector_f = selector.astype(jnp.float32)
    rows_all = incoming.reshape(tile_slots * tile_rows, rank_width)
    lane_chunk = 2048
    row_owner = jnp.repeat(owners, seg_length)
    gram_blocks = user_grams(
        rows_all,
        gram_weight.reshape(-1, lane_chunk),
        row_owner.reshape(-1, lane_chunk),
        rhs_weight.reshape(-1, lane_chunk),
        user_block,
        U_DEV,
    )
    identity_mat = jnp.eye(rank_width, dtype=jnp.float32)
    added_term = tree_sum(partial_gram, n_ent * n_rep) + RIDGE * identity_mat
    solved, own_factors = solve_owned(gram_blocks, added_term, n_rep, U_DEV)
    solved = solved.reshape(user_block, rank_width)
    run_factor = lax.dot_general(
        selector.astype(jnp.bfloat16),
        solved,
        (((0,), (0,)), ((), ())),
        preferred_element_type=jnp.float32,
    ).astype(jnp.bfloat16)
    back_load = jnp.concatenate(
        [
            run_factor.reshape(tile_slots, seg_count * rank_width),
            counts_int.astype(jnp.bfloat16),
        ],
        axis=1,
    )
    back_load = lax.all_to_all(
        back_load.reshape(n_ent, slot_cap, -1), "ent", split_axis=0, concat_axis=0, tiled=True
    ).reshape(tile_slots, -1)
    back_factor = back_load[:, : seg_count * rank_width]
    back_counts = back_load[:, seg_count * rank_width :].astype(jnp.float32)
    back_weight = jnp.where(
        live_send[:, None] & (back_counts > 0), 1.0 + ALPHA * back_counts, jnp.float32(0.0)
    )
    item_hot = item_ids[:, :, None] == jnp.arange(item_count, dtype=jnp.int32)[None, None, :]
    run_weight = back_weight.reshape(tile_slots * seg_count, seg_length)
    hot_runs = item_hot.reshape(tile_slots * seg_count, seg_length, item_count)
    spread_mat = jnp.sum(jnp.where(hot_runs, run_weight[:, :, None], 0.0), axis=1)
    item_rhs = lax.dot_general(
        spread_mat,
        back_factor.reshape(tile_slots * seg_count, rank_width).astype(jnp.float32),
        (((0,), (0,)), ((), ())),
        precision=highest,
        preferred_element_type=jnp.float32,
    )
    return (own_factors, item_rhs * RHS_SCALE)


def solution(mesh):
    in_specs = (
        P(("ent", "rep"), None),
        P("ent", "rep", None, None),
        P("ent", "rep", None),
        P("ent", "rep", None, None),
        P("ent", "rep", None, None),
        P("ent", "rep", None),
    )
    out_specs = (P(("ent", "rep"), None), P(("ent", "rep"), None))
    return jax.shard_map(shards, mesh=mesh, in_specs=in_specs, out_specs=out_specs, check_vma=False)
```

```python
import functools

import jax
import jax.numpy as jnp
from jax import lax
from jax.experimental import pallas as pl
from jax.experimental.pallas import tpu as pltpu
from jax.sharding import PartitionSpec as P

MESH_ID = pl.DeviceIdType.MESH

U_DEV = 2


ALPHA = 40.0
RIDGE = 1.0
RHS_SCALE = 1.0 / 640.0


def cholesky_solve(a_s, l_s, y_s, out_ref):
    batch, n, _ = a_s.shape
    out_ref[...] = jnp.zeros_like(out_ref)
    lane_v = lax.broadcasted_iota(jnp.int32, (1, n), 1)

    def factor(top, j, carry):
        span = n - top
        lane_m = lax.broadcasted_iota(jnp.int32, (span, n), 1)
        sub_m = lax.broadcasted_iota(jnp.int32, (span, n), 0) + top
        sub_v = lax.broadcasted_iota(jnp.int32, (span, 1), 0) + top
        for b in range(batch):
            a = a_s[b, top:, :]
            row = jnp.sum(jnp.where(sub_m == j, a, 0.0), axis=0, keepdims=True)
            col = jnp.sum(jnp.where(lane_m == j, a, 0.0), axis=1, keepdims=True)
            diag = jnp.sum(jnp.where(lane_v == j, row, 0.0), axis=1, keepdims=True)
            inv = 1.0 / jnp.sqrt(diag)
            l_row = jnp.where(lane_v >= j, row, 0.0) * inv
            l_col = jnp.where(sub_v >= j, col, 0.0) * inv
            a_s[b, top:, :] = a - l_col * l_row
            l_s[b, pl.ds(j, 1), :] = l_row
            y = y_s[pl.ds(b, 1), :]
            y_j = jnp.sum(jnp.where(lane_v == j, y, 0.0), axis=1, keepdims=True) * inv
            y_s[pl.ds(b, 1), :] = jnp.where(lane_v == j, y_j, y - y_j * l_row)
        return carry

    quarter = n // 4
    for part in range(4):
        top = part * quarter
        lax.fori_loop(top, top + quarter, functools.partial(factor, top), 0, unroll=4)

    def back(t, carry):
        j = n - 1 - t
        for b in range(batch):
            l_j = l_s[b, pl.ds(j, 1), :]
            x = out_ref[pl.ds(b, 1), :]
            y_j = jnp.sum(jnp.where(lane_v == j, y_s[pl.ds(b, 1), :], 0.0), axis=1, keepdims=True)
            l_jj = jnp.sum(jnp.where(lane_v == j, l_j, 0.0), axis=1, keepdims=True)
            known = jnp.sum(jnp.where(lane_v > j, l_j * x, 0.0), axis=1, keepdims=True)
            out_ref[pl.ds(b, 1), :] = jnp.where(lane_v == j, (y_j - known) / l_jj, x)
        return carry

    lax.fori_loop(0, n, back, 0, unroll=4)


def flip_bits(value, mask, bits):
    out = value - value % (1 << bits)
    for bit in range(bits):
        here = (value // (1 << bit)) % 2
        out = out + (1 << bit) * ((1 - here) if (mask >> bit) & 1 else here)
    return out


def doubling_kernel(
    n_rep, low_bits, rounds, x_ref, o_ref, full_recv, piece_recv, piece, gath,
    sem_a, sem_b, sem_c, sem_d, sem_e, sem_f,
):
    flat = lax.axis_index("ent") * n_rep + lax.axis_index("rep")
    group = 1 << low_bits
    rows = x_ref.shape[0] // group
    slot = flat % group

    def place(p):
        return (p // n_rep, p % n_rep)

    def flip(bit):
        step = 1 << bit
        upper = (flat // step) % 2
        return flat + step - 2 * step * upper

    members = [flip_bits(flat, k, low_bits) for k in range(1, group)]
    outer = [flip(bit) for bit in range(low_bits, rounds)]
    barrier = pltpu.get_barrier_semaphore()
    for p in members + outer:
        pl.semaphore_signal(barrier, inc=1, device_id=place(p), device_id_type=MESH_ID)
    pl.semaphore_wait(barrier, len(members) + len(outer))

    o_ref[...] = x_ref[...]
    for bit in range(low_bits):
        copy = pltpu.make_async_remote_copy(
            src_ref=o_ref, dst_ref=full_recv.at[bit], send_sem=sem_a.at[bit],
            recv_sem=sem_b.at[bit], device_id=place(flip(bit)), device_id_type=MESH_ID,
        )
        copy.start()
        copy.wait_recv()
        copy.wait_send()
        o_ref[...] = o_ref[...] + full_recv[bit]

    piece[...] = o_ref[pl.ds(pl.multiple_of(slot * rows, rows), rows), :]
    for index, p in enumerate(outer):
        copy = pltpu.make_async_remote_copy(
            src_ref=piece, dst_ref=piece_recv.at[index], send_sem=sem_c.at[index],
            recv_sem=sem_d.at[index], device_id=place(p), device_id_type=MESH_ID,
        )
        copy.start()
        copy.wait_recv()
        copy.wait_send()
        piece[...] = piece[...] + piece_recv[index]

    gath[slot] = piece[...]
    sends = []
    for index, p in enumerate(members):
        copy = pltpu.make_async_remote_copy(
            src_ref=piece, dst_ref=gath.at[slot], send_sem=sem_e.at[index],
            recv_sem=sem_f.at[slot], device_id=place(p), device_id_type=MESH_ID,
        )
        copy.start()
        sends.append(copy)
    for k in range(1, group):
        source = flip_bits(slot, k, low_bits)
        pltpu.make_async_remote_copy(
            src_ref=piece, dst_ref=gath.at[source], send_sem=sem_e.at[k - 1],
            recv_sem=sem_f.at[source], device_id=place(members[k - 1]), device_id_type=MESH_ID,
        ).wait_recv()
    for copy in sends:
        copy.wait_send()
    for part in range(group):
        o_ref[pl.ds(part * rows, rows), :] = gath[part]


def tree_sum(value, count):
    rounds = count.bit_length() - 1
    n_rep = lax.axis_size("rep")
    low_bits = (n_rep * 2).bit_length() - 1
    group = 1 << low_bits
    rows = value.shape[0] // group
    outer = rounds - low_bits
    return pl.pallas_call(
        functools.partial(doubling_kernel, n_rep, low_bits, rounds),
        out_shape=jax.ShapeDtypeStruct(value.shape, value.dtype),
        in_specs=[pl.BlockSpec(memory_space=pltpu.VMEM)],
        out_specs=pl.BlockSpec(memory_space=pltpu.VMEM),
        scratch_shapes=[
            pltpu.VMEM((low_bits,) + value.shape, value.dtype),
            pltpu.VMEM((outer, rows, value.shape[1]), value.dtype),
            pltpu.VMEM((rows, value.shape[1]), value.dtype),
            pltpu.VMEM((group, rows, value.shape[1]), value.dtype),
            pltpu.SemaphoreType.DMA((low_bits,)),
            pltpu.SemaphoreType.DMA((low_bits,)),
            pltpu.SemaphoreType.DMA((outer,)),
            pltpu.SemaphoreType.DMA((outer,)),
            pltpu.SemaphoreType.DMA((group - 1,)),
            pltpu.SemaphoreType.DMA((group,)),
        ],
        compiler_params=pltpu.CompilerParams(collective_id=0, has_side_effects=True),
    )(value)


def rep_peers(n_rep):
    me = lax.axis_index("rep")
    return me, [(me + shift) % n_rep for shift in range(1, n_rep)]


def owner_kernel(n_rep, blocks_ref, base_ref, out_ref, x_s, recv, a_s, l_s, y_s, fac, gath,
                 sem_a, sem_b, sem_c, sem_d):
    me, peers = rep_peers(n_rep)
    ent = lax.axis_index("ent")
    batch, n, _ = a_s.shape
    barrier = pltpu.get_barrier_semaphore()
    for peer in peers:
        pl.semaphore_signal(barrier, inc=1, device_id=(ent, peer), device_id_type=MESH_ID)
    pl.semaphore_wait(barrier, n_rep - 1)
    copies = []
    for index, peer in enumerate(peers):
        copy = pltpu.make_async_remote_copy(
            src_ref=blocks_ref.at[peer], dst_ref=recv.at[index], send_sem=sem_a.at[index],
            recv_sem=sem_b.at[index], device_id=(ent, peer), device_id_type=MESH_ID,
        )
        copy.start()
        copies.append(copy)
    total = blocks_ref[me]
    for index, copy in enumerate(copies):
        copy.wait_recv()
        total = total + recv[index]
    for copy in copies:
        copy.wait_send()
    base = base_ref[...]
    for b in range(batch):
        gram = total[b * n : (b + 1) * n] + base
        a_s[b] = (gram + gram.T) / 2
    y_s[...] = total[batch * n : batch * n + batch]
    cholesky_solve(a_s, l_s, y_s, x_s)
    fac[...] = x_s[...].astype(fac.dtype)
    gath[me] = fac[...]
    sends = []
    for index, peer in enumerate(peers):
        copy = pltpu.make_async_remote_copy(
            src_ref=fac, dst_ref=gath.at[me], send_sem=sem_c.at[index],
            recv_sem=sem_d.at[me], device_id=(ent, peer), device_id_type=MESH_ID,
        )
        copy.start()
        sends.append(copy)
    for index, source in enumerate(peers):
        pltpu.make_async_remote_copy(
            src_ref=fac, dst_ref=gath.at[source], send_sem=sem_c.at[index],
            recv_sem=sem_d.at[source], device_id=(ent, source), device_id_type=MESH_ID,
        ).wait_recv()
    for copy in sends:
        copy.wait_send()
    out_ref[...] = gath[...]


def solve_owned(blocks, base, n_rep, per_dev):
    n = blocks.shape[2]
    return pl.pallas_call(
        functools.partial(owner_kernel, n_rep),
        out_shape=(
            jax.ShapeDtypeStruct((n_rep, per_dev, n), jnp.bfloat16),
            jax.ShapeDtypeStruct((per_dev, n), jnp.float32),
        ),
        in_specs=[pl.BlockSpec(memory_space=pltpu.VMEM)] * 2,
        out_specs=(pl.BlockSpec(memory_space=pltpu.VMEM), pl.BlockSpec(memory_space=pltpu.VMEM)),
        scratch_shapes=[
            pltpu.VMEM((n_rep - 1,) + blocks.shape[1:], jnp.float32),
            pltpu.VMEM((per_dev, n, n), jnp.float32),
            pltpu.VMEM((per_dev, n, n), jnp.float32),
            pltpu.VMEM((per_dev, n), jnp.float32),
            pltpu.VMEM((per_dev, n), jnp.bfloat16),
            pltpu.VMEM((n_rep, per_dev, n), jnp.bfloat16),
            pltpu.SemaphoreType.DMA((n_rep - 1,)),
            pltpu.SemaphoreType.DMA((n_rep - 1,)),
            pltpu.SemaphoreType.DMA((n_rep - 1,)),
            pltpu.SemaphoreType.DMA((n_rep,)),
        ],
        compiler_params=pltpu.CompilerParams(collective_id=1, has_side_effects=True),
    )(blocks, base)


def gather_kernel(idx_ref, table_t_ref, out_ref):
    step = pl.program_id(0)
    idx = idx_ref[pl.ds(step, 1), :]
    picks = lax.broadcasted_iota(jnp.int32, (table_t_ref.shape[1], idx.shape[1]), 0) == idx
    rows_t = jnp.dot(table_t_ref[...], picks.astype(jnp.bfloat16), preferred_element_type=jnp.float32)
    out_ref[...] = rows_t.T.astype(out_ref.dtype)


def gather_rows(table, idx, chunk=2048):
    count = idx.shape[0]
    idx_lanes = idx.reshape(count // chunk, chunk)
    return pl.pallas_call(
        gather_kernel,
        out_shape=jax.ShapeDtypeStruct((count, table.shape[1]), table.dtype),
        grid=(count // chunk,),
        in_specs=[
            pl.BlockSpec(idx_lanes.shape, lambda i: (0, 0)),
            pl.BlockSpec((table.shape[1], table.shape[0]), lambda i: (0, 0)),
        ],
        out_specs=pl.BlockSpec((chunk, table.shape[1]), lambda i: (i, 0)),
        cost_estimate=pl.CostEstimate(
            flops=2 * count * table.shape[0] * table.shape[1],
            transcendentals=0,
            bytes_accessed=count * 4 + table.size * 2 + count * table.shape[1] * 2,
        ),
    )(idx_lanes, table.T)


def gram_kernel(n_user, per_dev, rows_ref, gw_ref, user_ref, rw_ref, out_ref):
    step = pl.program_id(0)
    width = rows_ref.shape[1]

    @pl.when(step == 0)
    def _():
        out_ref[...] = jnp.zeros_like(out_ref)

    rows = rows_ref[...]
    rows_t = rows.astype(jnp.float32).T
    weights_t = (rows_t * gw_ref[pl.ds(step, 1), :]).astype(jnp.bfloat16)
    users = user_ref[pl.ds(step, 1), :]
    zero = jnp.zeros((), jnp.bfloat16)
    for user in range(n_user):
        picked = jnp.where(users == user, weights_t, zero)
        block, spot = user // per_dev, (user % per_dev) * width
        out_ref[block, spot : spot + width, :] += jnp.dot(
            picked, rows, preferred_element_type=jnp.float32
        )
    slots = lax.broadcasted_iota(jnp.int32, (n_user, users.shape[1]), 0)
    per_user = jnp.where(users == slots, rw_ref[pl.ds(step, 1), :], 0.0)
    high = per_user.astype(jnp.bfloat16)
    low = (per_user - high.astype(jnp.float32)).astype(jnp.bfloat16)
    rhs = jnp.dot(high, rows, preferred_element_type=jnp.float32) + jnp.dot(
        low, rows, preferred_element_type=jnp.float32
    )
    base = per_dev * width
    for block in range(n_user // per_dev):
        out_ref[block, base : base + per_dev, :] += rhs[block * per_dev : (block + 1) * per_dev]


def user_grams(rows, gw_lanes, user_lanes, rw_lanes, n_user, per_dev):
    chunks, chunk = gw_lanes.shape
    width = rows.shape[1]
    n_block = n_user // per_dev
    block_rows = per_dev * width + per_dev
    return pl.pallas_call(
        functools.partial(gram_kernel, n_user, per_dev),
        out_shape=jax.ShapeDtypeStruct((n_block, block_rows, width), jnp.float32),
        grid=(chunks,),
        in_specs=[
            pl.BlockSpec((chunk, width), lambda i: (i, 0)),
            pl.BlockSpec((chunks, chunk), lambda i: (0, 0)),
            pl.BlockSpec((chunks, chunk), lambda i: (0, 0)),
            pl.BlockSpec((chunks, chunk), lambda i: (0, 0)),
        ],
        out_specs=pl.BlockSpec((n_block, block_rows, width), lambda i: (0, 0, 0)),
        cost_estimate=pl.CostEstimate(
            flops=2 * rows.shape[0] * width * width * (n_user + 2),
            transcendentals=0,
            bytes_accessed=rows.size * 2 + 12 * rows.shape[0] + n_user * width * (width + 1) * 4,
        ),
    )(rows, gw_lanes, user_lanes, rw_lanes)

def shards(item_factors, tile_items, send_tiles, tile_users, tile_counts, recv_tiles):
    highest = lax.Precision.HIGHEST
    rank_width = item_factors.shape[1]
    item_count = item_factors.shape[0]
    n_ent = lax.axis_size("ent")
    n_rep = lax.axis_size("rep")
    tile_slots = tile_items.shape[2]
    tile_rows = tile_items.shape[3]
    seg_count = tile_users.shape[3]
    seg_length = tile_rows // seg_count
    slot_cap = tile_slots // n_ent
    user_block = U_DEV * lax.axis_size("rep")
    item_ids = tile_items.reshape(tile_slots, tile_rows)
    slot_pos = jnp.arange(tile_slots, dtype=jnp.int32) % slot_cap
    live_send = slot_pos < jnp.repeat(send_tiles.reshape(n_ent), slot_cap)
    live_recv = slot_pos < jnp.repeat(recv_tiles.reshape(n_ent), slot_cap)
    partial_gram = lax.dot_general(
        item_factors, item_factors, (((0,), (0,)), ((), ())), preferred_element_type=jnp.float32
    )
    live_rows = jnp.repeat(live_send, tile_rows)
    picked = gather_rows(item_factors, jnp.where(live_rows, item_ids.reshape(-1), -1))
    incoming = lax.all_to_all(
        picked.reshape(n_ent, slot_cap * tile_rows, rank_width),
        "ent",
        split_axis=0,
        concat_axis=0,
        tiled=True,
    )
    counts_int = tile_counts.reshape(tile_slots, tile_rows)
    counts_f = counts_int.astype(jnp.float32)
    gram_weight = ALPHA * counts_f
    rhs_weight = jnp.where(
        live_recv[:, None] & (counts_int > 0), 1.0 + ALPHA * counts_f, jnp.float32(0.0)
    )
    owners = tile_users.reshape(tile_slots * seg_count)
    selector = owners[None, :] == jnp.arange(user_block, dtype=jnp.int32)[:, None]
    selector_f = selector.astype(jnp.float32)
    rows_all = incoming.reshape(tile_slots * tile_rows, rank_width)
    lane_chunk = 2048
    row_owner = jnp.repeat(owners, seg_length)
    gram_blocks = user_grams(
        rows_all,
        gram_weight.reshape(-1, lane_chunk),
        row_owner.reshape(-1, lane_chunk),
        rhs_weight.reshape(-1, lane_chunk),
        user_block,
        U_DEV,
    )
    identity_mat = jnp.eye(rank_width, dtype=jnp.float32)
    added_term = tree_sum(partial_gram, n_ent * n_rep) + RIDGE * identity_mat
    solved, own_factors = solve_owned(gram_blocks, added_term, n_rep, U_DEV)
    solved = solved.reshape(user_block, rank_width)
    run_factor = lax.dot_general(
        selector.astype(jnp.bfloat16),
        solved,
        (((0,), (0,)), ((), ())),
        preferred_element_type=jnp.float32,
    ).astype(jnp.bfloat16)
    back_load = jnp.concatenate(
        [
            run_factor.reshape(tile_slots, seg_count * rank_width),
            counts_int.astype(jnp.bfloat16),
        ],
        axis=1,
    )
    back_load = lax.all_to_all(
        back_load.reshape(n_ent, slot_cap, -1), "ent", split_axis=0, concat_axis=0, tiled=True
    ).reshape(tile_slots, -1)
    back_factor = back_load[:, : seg_count * rank_width]
    back_counts = back_load[:, seg_count * rank_width :].astype(jnp.float32)
    back_weight = jnp.where(
        live_send[:, None] & (back_counts > 0), 1.0 + ALPHA * back_counts, jnp.float32(0.0)
    )
    item_hot = item_ids[:, :, None] == jnp.arange(item_count, dtype=jnp.int32)[None, None, :]
    run_weight = back_weight.reshape(tile_slots * seg_count, seg_length)
    hot_runs = item_hot.reshape(tile_slots * seg_count, seg_length, item_count)
    spread_mat = jnp.sum(jnp.where(hot_runs, run_weight[:, :, None], 0.0), axis=1)
    item_rhs = lax.dot_general(
        spread_mat,
        back_factor.reshape(tile_slots * seg_count, rank_width).astype(jnp.float32),
        (((0,), (0,)), ((), ())),
        precision=highest,
        preferred_element_type=jnp.float32,
    )
    return (own_factors, item_rhs * RHS_SCALE)


def solution(mesh):
    in_specs = (
        P(("ent", "rep"), None),
        P("ent", "rep", None, None),
        P("ent", "rep", None),
        P("ent", "rep", None, None),
        P("ent", "rep", None, None),
        P("ent", "rep", None),
    )
    out_specs = (P(("ent", "rep"), None), P(("ent", "rep"), None))
    return jax.shard_map(shards, mesh=mesh, in_specs=in_specs, out_specs=out_specs, check_vma=False)
```

```python
import functools

import jax
import jax.numpy as jnp
from jax import lax
from jax.experimental import pallas as pl
from jax.experimental.pallas import tpu as pltpu
from jax.sharding import PartitionSpec as P

MESH_ID = pl.DeviceIdType.MESH

U_DEV = 2


ALPHA = 40.0
RIDGE = 1.0
RHS_SCALE = 1.0 / 640.0


def cholesky_solve(a_s, l_s, y_s, out_ref):
    batch, n, _ = a_s.shape
    out_ref[...] = jnp.zeros_like(out_ref)
    lane_v = lax.broadcasted_iota(jnp.int32, (1, n), 1)

    def factor(top, j, carry):
        span = n - top
        lane_m = lax.broadcasted_iota(jnp.int32, (span, n), 1)
        sub_m = lax.broadcasted_iota(jnp.int32, (span, n), 0) + top
        sub_v = lax.broadcasted_iota(jnp.int32, (span, 1), 0) + top
        for b in range(batch):
            a = a_s[b, top:, :]
            row = jnp.sum(jnp.where(sub_m == j, a, 0.0), axis=0, keepdims=True)
            col = jnp.sum(jnp.where(lane_m == j, a, 0.0), axis=1, keepdims=True)
            diag = jnp.sum(jnp.where(lane_v == j, row, 0.0), axis=1, keepdims=True)
            inv = 1.0 / jnp.sqrt(diag)
            l_row = jnp.where(lane_v >= j, row, 0.0) * inv
            l_col = jnp.where(sub_v >= j, col, 0.0) * inv
            a_s[b, top:, :] = a - l_col * l_row
            l_s[b, pl.ds(j, 1), :] = l_row
            y = y_s[pl.ds(b, 1), :]
            y_j = jnp.sum(jnp.where(lane_v == j, y, 0.0), axis=1, keepdims=True) * inv
            y_s[pl.ds(b, 1), :] = jnp.where(lane_v == j, y_j, y - y_j * l_row)
        return carry

    quarter = n // 4
    for part in range(4):
        top = part * quarter
        lax.fori_loop(top, top + quarter, functools.partial(factor, top), 0, unroll=2)

    def back(t, carry):
        j = n - 1 - t
        for b in range(batch):
            l_j = l_s[b, pl.ds(j, 1), :]
            x = out_ref[pl.ds(b, 1), :]
            y_j = jnp.sum(jnp.where(lane_v == j, y_s[pl.ds(b, 1), :], 0.0), axis=1, keepdims=True)
            l_jj = jnp.sum(jnp.where(lane_v == j, l_j, 0.0), axis=1, keepdims=True)
            known = jnp.sum(jnp.where(lane_v > j, l_j * x, 0.0), axis=1, keepdims=True)
            out_ref[pl.ds(b, 1), :] = jnp.where(lane_v == j, (y_j - known) / l_jj, x)
        return carry

    lax.fori_loop(0, n, back, 0, unroll=2)


def flip_bits(value, mask, bits):
    out = value - value % (1 << bits)
    for bit in range(bits):
        here = (value // (1 << bit)) % 2
        out = out + (1 << bit) * ((1 - here) if (mask >> bit) & 1 else here)
    return out


def doubling_kernel(
    n_rep, low_bits, rounds, x_ref, o_ref, full_recv, piece_recv, piece, gath,
    sem_a, sem_b, sem_c, sem_d, sem_e, sem_f,
):
    flat = lax.axis_index("ent") * n_rep + lax.axis_index("rep")
    group = 1 << low_bits
    rows = x_ref.shape[0] // group
    slot = flat % group

    def place(p):
        return (p // n_rep, p % n_rep)

    def flip(bit):
        step = 1 << bit
        upper = (flat // step) % 2
        return flat + step - 2 * step * upper

    members = [flip_bits(flat, k, low_bits) for k in range(1, group)]
    outer = [flip(bit) for bit in range(low_bits, rounds)]
    barrier = pltpu.get_barrier_semaphore()
    for p in members + outer:
        pl.semaphore_signal(barrier, inc=1, device_id=place(p), device_id_type=MESH_ID)
    pl.semaphore_wait(barrier, len(members) + len(outer))

    o_ref[...] = x_ref[...]
    for bit in range(low_bits):
        copy = pltpu.make_async_remote_copy(
            src_ref=o_ref, dst_ref=full_recv.at[bit], send_sem=sem_a.at[bit],
            recv_sem=sem_b.at[bit], device_id=place(flip(bit)), device_id_type=MESH_ID,
        )
        copy.start()
        copy.wait_recv()
        copy.wait_send()
        o_ref[...] = o_ref[...] + full_recv[bit]

    piece[...] = o_ref[pl.ds(pl.multiple_of(slot * rows, rows), rows), :]
    for index, p in enumerate(outer):
        copy = pltpu.make_async_remote_copy(
            src_ref=piece, dst_ref=piece_recv.at[index], send_sem=sem_c.at[index],
            recv_sem=sem_d.at[index], device_id=place(p), device_id_type=MESH_ID,
        )
        copy.start()
        copy.wait_recv()
        copy.wait_send()
        piece[...] = piece[...] + piece_recv[index]

    gath[slot] = piece[...]
    sends = []
    for index, p in enumerate(members):
        copy = pltpu.make_async_remote_copy(
            src_ref=piece, dst_ref=gath.at[slot], send_sem=sem_e.at[index],
            recv_sem=sem_f.at[slot], device_id=place(p), device_id_type=MESH_ID,
        )
        copy.start()
        sends.append(copy)
    for k in range(1, group):
        source = flip_bits(slot, k, low_bits)
        pltpu.make_async_remote_copy(
            src_ref=piece, dst_ref=gath.at[source], send_sem=sem_e.at[k - 1],
            recv_sem=sem_f.at[source], device_id=place(members[k - 1]), device_id_type=MESH_ID,
        ).wait_recv()
    for copy in sends:
        copy.wait_send()
    for part in range(group):
        o_ref[pl.ds(part * rows, rows), :] = gath[part]


def tree_sum(value, count):
    rounds = count.bit_length() - 1
    n_rep = lax.axis_size("rep")
    low_bits = (n_rep * 2).bit_length() - 1
    group = 1 << low_bits
    rows = value.shape[0] // group
    outer = rounds - low_bits
    return pl.pallas_call(
        functools.partial(doubling_kernel, n_rep, low_bits, rounds),
        out_shape=jax.ShapeDtypeStruct(value.shape, value.dtype),
        in_specs=[pl.BlockSpec(memory_space=pltpu.VMEM)],
        out_specs=pl.BlockSpec(memory_space=pltpu.VMEM),
        scratch_shapes=[
            pltpu.VMEM((low_bits,) + value.shape, value.dtype),
            pltpu.VMEM((outer, rows, value.shape[1]), value.dtype),
            pltpu.VMEM((rows, value.shape[1]), value.dtype),
            pltpu.VMEM((group, rows, value.shape[1]), value.dtype),
            pltpu.SemaphoreType.DMA((low_bits,)),
            pltpu.SemaphoreType.DMA((low_bits,)),
            pltpu.SemaphoreType.DMA((outer,)),
            pltpu.SemaphoreType.DMA((outer,)),
            pltpu.SemaphoreType.DMA((group - 1,)),
            pltpu.SemaphoreType.DMA((group,)),
        ],
        compiler_params=pltpu.CompilerParams(collective_id=0, has_side_effects=True),
    )(value)


def rep_peers(n_rep):
    me = lax.axis_index("rep")
    return me, [(me + shift) % n_rep for shift in range(1, n_rep)]


def owner_kernel(n_rep, blocks_ref, base_ref, out_ref, x_s, recv, a_s, l_s, y_s, fac, gath,
                 sem_a, sem_b, sem_c, sem_d):
    me, peers = rep_peers(n_rep)
    ent = lax.axis_index("ent")
    batch, n, _ = a_s.shape
    barrier = pltpu.get_barrier_semaphore()
    for peer in peers:
        pl.semaphore_signal(barrier, inc=1, device_id=(ent, peer), device_id_type=MESH_ID)
    pl.semaphore_wait(barrier, n_rep - 1)
    copies = []
    for index, peer in enumerate(peers):
        copy = pltpu.make_async_remote_copy(
            src_ref=blocks_ref.at[peer], dst_ref=recv.at[index], send_sem=sem_a.at[index],
            recv_sem=sem_b.at[index], device_id=(ent, peer), device_id_type=MESH_ID,
        )
        copy.start()
        copies.append(copy)
    total = blocks_ref[me]
    for index, copy in enumerate(copies):
        copy.wait_recv()
        total = total + recv[index]
    for copy in copies:
        copy.wait_send()
    base = base_ref[...]
    for b in range(batch):
        gram = total[b * n : (b + 1) * n] + base
        a_s[b] = (gram + gram.T) / 2
    y_s[...] = total[batch * n : batch * n + batch]
    cholesky_solve(a_s, l_s, y_s, x_s)
    fac[...] = x_s[...].astype(fac.dtype)
    gath[me] = fac[...]
    sends = []
    for index, peer in enumerate(peers):
        copy = pltpu.make_async_remote_copy(
            src_ref=fac, dst_ref=gath.at[me], send_sem=sem_c.at[index],
            recv_sem=sem_d.at[me], device_id=(ent, peer), device_id_type=MESH_ID,
        )
        copy.start()
        sends.append(copy)
    for index, source in enumerate(peers):
        pltpu.make_async_remote_copy(
            src_ref=fac, dst_ref=gath.at[source], send_sem=sem_c.at[index],
            recv_sem=sem_d.at[source], device_id=(ent, source), device_id_type=MESH_ID,
        ).wait_recv()
    for copy in sends:
        copy.wait_send()
    out_ref[...] = gath[...]


def solve_owned(blocks, base, n_rep, per_dev):
    n = blocks.shape[2]
    return pl.pallas_call(
        functools.partial(owner_kernel, n_rep),
        out_shape=(
            jax.ShapeDtypeStruct((n_rep, per_dev, n), jnp.bfloat16),
            jax.ShapeDtypeStruct((per_dev, n), jnp.float32),
        ),
        in_specs=[pl.BlockSpec(memory_space=pltpu.VMEM)] * 2,
        out_specs=(pl.BlockSpec(memory_space=pltpu.VMEM), pl.BlockSpec(memory_space=pltpu.VMEM)),
        scratch_shapes=[
            pltpu.VMEM((n_rep - 1,) + blocks.shape[1:], jnp.float32),
            pltpu.VMEM((per_dev, n, n), jnp.float32),
            pltpu.VMEM((per_dev, n, n), jnp.float32),
            pltpu.VMEM((per_dev, n), jnp.float32),
            pltpu.VMEM((per_dev, n), jnp.bfloat16),
            pltpu.VMEM((n_rep, per_dev, n), jnp.bfloat16),
            pltpu.SemaphoreType.DMA((n_rep - 1,)),
            pltpu.SemaphoreType.DMA((n_rep - 1,)),
            pltpu.SemaphoreType.DMA((n_rep - 1,)),
            pltpu.SemaphoreType.DMA((n_rep,)),
        ],
        compiler_params=pltpu.CompilerParams(collective_id=1, has_side_effects=True),
    )(blocks, base)


def gather_kernel(idx_ref, table_t_ref, out_ref):
    step = pl.program_id(0)
    idx = idx_ref[pl.ds(step, 1), :]
    picks = lax.broadcasted_iota(jnp.int32, (table_t_ref.shape[1], idx.shape[1]), 0) == idx
    rows_t = jnp.dot(table_t_ref[...], picks.astype(jnp.bfloat16), preferred_element_type=jnp.float32)
    out_ref[...] = rows_t.T.astype(out_ref.dtype)


def gather_rows(table, idx, chunk=2048):
    count = idx.shape[0]
    idx_lanes = idx.reshape(count // chunk, chunk)
    return pl.pallas_call(
        gather_kernel,
        out_shape=jax.ShapeDtypeStruct((count, table.shape[1]), table.dtype),
        grid=(count // chunk,),
        in_specs=[
            pl.BlockSpec(idx_lanes.shape, lambda i: (0, 0)),
            pl.BlockSpec((table.shape[1], table.shape[0]), lambda i: (0, 0)),
        ],
        out_specs=pl.BlockSpec((chunk, table.shape[1]), lambda i: (i, 0)),
        cost_estimate=pl.CostEstimate(
            flops=2 * count * table.shape[0] * table.shape[1],
            transcendentals=0,
            bytes_accessed=count * 4 + table.size * 2 + count * table.shape[1] * 2,
        ),
    )(idx_lanes, table.T)


def gram_kernel(n_user, per_dev, rows_ref, gw_ref, user_ref, rw_ref, out_ref):
    step = pl.program_id(0)
    width = rows_ref.shape[1]

    @pl.when(step == 0)
    def _():
        out_ref[...] = jnp.zeros_like(out_ref)

    rows = rows_ref[...]
    rows_t = rows.astype(jnp.float32).T
    weights_t = (rows_t * gw_ref[pl.ds(step, 1), :]).astype(jnp.bfloat16)
    users = user_ref[pl.ds(step, 1), :]
    zero = jnp.zeros((), jnp.bfloat16)
    for user in range(n_user):
        picked = jnp.where(users == user, weights_t, zero)
        block, spot = user // per_dev, (user % per_dev) * width
        out_ref[block, spot : spot + width, :] += jnp.dot(
            picked, rows, preferred_element_type=jnp.float32
        )
    slots = lax.broadcasted_iota(jnp.int32, (n_user, users.shape[1]), 0)
    per_user = jnp.where(users == slots, rw_ref[pl.ds(step, 1), :], 0.0)
    high = per_user.astype(jnp.bfloat16)
    low = (per_user - high.astype(jnp.float32)).astype(jnp.bfloat16)
    rhs = jnp.dot(high, rows, preferred_element_type=jnp.float32) + jnp.dot(
        low, rows, preferred_element_type=jnp.float32
    )
    base = per_dev * width
    for block in range(n_user // per_dev):
        out_ref[block, base : base + per_dev, :] += rhs[block * per_dev : (block + 1) * per_dev]


def user_grams(rows, gw_lanes, user_lanes, rw_lanes, n_user, per_dev):
    chunks, chunk = gw_lanes.shape
    width = rows.shape[1]
    n_block = n_user // per_dev
    block_rows = per_dev * width + per_dev
    return pl.pallas_call(
        functools.partial(gram_kernel, n_user, per_dev),
        out_shape=jax.ShapeDtypeStruct((n_block, block_rows, width), jnp.float32),
        grid=(chunks,),
        in_specs=[
            pl.BlockSpec((chunk, width), lambda i: (i, 0)),
            pl.BlockSpec((chunks, chunk), lambda i: (0, 0)),
            pl.BlockSpec((chunks, chunk), lambda i: (0, 0)),
            pl.BlockSpec((chunks, chunk), lambda i: (0, 0)),
        ],
        out_specs=pl.BlockSpec((n_block, block_rows, width), lambda i: (0, 0, 0)),
        cost_estimate=pl.CostEstimate(
            flops=2 * rows.shape[0] * width * width * (n_user + 2),
            transcendentals=0,
            bytes_accessed=rows.size * 2 + 12 * rows.shape[0] + n_user * width * (width + 1) * 4,
        ),
    )(rows, gw_lanes, user_lanes, rw_lanes)

def shards(item_factors, tile_items, send_tiles, tile_users, tile_counts, recv_tiles):
    highest = lax.Precision.HIGHEST
    rank_width = item_factors.shape[1]
    item_count = item_factors.shape[0]
    n_ent = lax.axis_size("ent")
    n_rep = lax.axis_size("rep")
    tile_slots = tile_items.shape[2]
    tile_rows = tile_items.shape[3]
    seg_count = tile_users.shape[3]
    seg_length = tile_rows // seg_count
    slot_cap = tile_slots // n_ent
    user_block = U_DEV * lax.axis_size("rep")
    item_ids = tile_items.reshape(tile_slots, tile_rows)
    slot_pos = jnp.arange(tile_slots, dtype=jnp.int32) % slot_cap
    live_send = slot_pos < jnp.repeat(send_tiles.reshape(n_ent), slot_cap)
    live_recv = slot_pos < jnp.repeat(recv_tiles.reshape(n_ent), slot_cap)
    partial_gram = lax.dot_general(
        item_factors, item_factors, (((0,), (0,)), ((), ())), preferred_element_type=jnp.float32
    )
    live_rows = jnp.repeat(live_send, tile_rows)
    picked = gather_rows(item_factors, jnp.where(live_rows, item_ids.reshape(-1), -1))
    incoming = lax.all_to_all(
        picked.reshape(n_ent, slot_cap * tile_rows, rank_width),
        "ent",
        split_axis=0,
        concat_axis=0,
        tiled=True,
    )
    counts_int = tile_counts.reshape(tile_slots, tile_rows)
    counts_f = counts_int.astype(jnp.float32)
    gram_weight = ALPHA * counts_f
    rhs_weight = jnp.where(
        live_recv[:, None] & (counts_int > 0), 1.0 + ALPHA * counts_f, jnp.float32(0.0)
    )
    owners = tile_users.reshape(tile_slots * seg_count)
    selector = owners[None, :] == jnp.arange(user_block, dtype=jnp.int32)[:, None]
    selector_f = selector.astype(jnp.float32)
    rows_all = incoming.reshape(tile_slots * tile_rows, rank_width)
    lane_chunk = 2048
    row_owner = jnp.repeat(owners, seg_length)
    gram_blocks = user_grams(
        rows_all,
        gram_weight.reshape(-1, lane_chunk),
        row_owner.reshape(-1, lane_chunk),
        rhs_weight.reshape(-1, lane_chunk),
        user_block,
        U_DEV,
    )
    identity_mat = jnp.eye(rank_width, dtype=jnp.float32)
    added_term = tree_sum(partial_gram, n_ent * n_rep) + RIDGE * identity_mat
    solved, own_factors = solve_owned(gram_blocks, added_term, n_rep, U_DEV)
    solved = solved.reshape(user_block, rank_width)
    run_factor = lax.dot_general(
        selector.astype(jnp.bfloat16),
        solved,
        (((0,), (0,)), ((), ())),
        preferred_element_type=jnp.float32,
    ).astype(jnp.bfloat16)
    back_counts = lax.all_to_all(
        counts_int.astype(jnp.bfloat16).reshape(n_ent, slot_cap, tile_rows),
        "ent",
        split_axis=0,
        concat_axis=0,
        tiled=True,
    ).reshape(tile_slots, tile_rows).astype(jnp.float32)
    back_weight = jnp.where(
        live_send[:, None] & (back_counts > 0), 1.0 + ALPHA * back_counts, jnp.float32(0.0)
    )
    back_factor = lax.all_to_all(
        run_factor.reshape(n_ent, slot_cap, seg_count * rank_width),
        "ent",
        split_axis=0,
        concat_axis=0,
        tiled=True,
    ).reshape(tile_slots, seg_count * rank_width)
    item_hot = item_ids[:, :, None] == jnp.arange(item_count, dtype=jnp.int32)[None, None, :]
    run_weight = back_weight.reshape(tile_slots * seg_count, seg_length)
    hot_runs = item_hot.reshape(tile_slots * seg_count, seg_length, item_count)
    spread_mat = jnp.sum(jnp.where(hot_runs, run_weight[:, :, None], 0.0), axis=1)
    item_rhs = lax.dot_general(
        spread_mat,
        back_factor.reshape(tile_slots * seg_count, rank_width).astype(jnp.float32),
        (((0,), (0,)), ((), ())),
        precision=highest,
        preferred_element_type=jnp.float32,
    )
    return (own_factors, item_rhs * RHS_SCALE)


def solution(mesh):
    in_specs = (
        P(("ent", "rep"), None),
        P("ent", "rep", None, None),
        P("ent", "rep", None),
        P("ent", "rep", None, None),
        P("ent", "rep", None, None),
        P("ent", "rep", None),
    )
    out_specs = (P(("ent", "rep"), None), P(("ent", "rep"), None))
    return jax.shard_map(shards, mesh=mesh, in_specs=in_specs, out_specs=out_specs, check_vma=False)
```

```python
import functools

import jax
import jax.numpy as jnp
from jax import lax
from jax.experimental import pallas as pl
from jax.experimental.pallas import tpu as pltpu
from jax.sharding import PartitionSpec as P

MESH_ID = pl.DeviceIdType.MESH

U_DEV = 2


ALPHA = 40.0
RIDGE = 1.0
RHS_SCALE = 1.0 / 640.0


def cholesky_solve(a_s, l_s, y_s, out_ref):
    batch, n, _ = a_s.shape
    out_ref[...] = jnp.zeros_like(out_ref)
    lane_v = lax.broadcasted_iota(jnp.int32, (1, n), 1)

    def factor(top, j, carry):
        span = n - top
        lane_m = lax.broadcasted_iota(jnp.int32, (span, n), 1)
        sub_m = lax.broadcasted_iota(jnp.int32, (span, n), 0) + top
        sub_v = lax.broadcasted_iota(jnp.int32, (span, 1), 0) + top
        for b in range(batch):
            a = a_s[b, top:, :]
            row = jnp.sum(jnp.where(sub_m == j, a, 0.0), axis=0, keepdims=True)
            col = jnp.sum(jnp.where(lane_m == j, a, 0.0), axis=1, keepdims=True)
            diag = jnp.sum(jnp.where(lane_v == j, row, 0.0), axis=1, keepdims=True)
            inv = 1.0 / jnp.sqrt(diag)
            l_row = jnp.where(lane_v >= j, row, 0.0) * inv
            l_col = jnp.where(sub_v >= j, col, 0.0) * inv
            a_s[b, top:, :] = a - l_col * l_row
            l_s[b, pl.ds(j, 1), :] = l_row
            y = y_s[pl.ds(b, 1), :]
            y_j = jnp.sum(jnp.where(lane_v == j, y, 0.0), axis=1, keepdims=True) * inv
            y_s[pl.ds(b, 1), :] = jnp.where(lane_v == j, y_j, y - y_j * l_row)
        return carry

    quarter = n // 4
    for part in range(4):
        top = part * quarter
        lax.fori_loop(top, top + quarter, functools.partial(factor, top), 0, unroll=2)

    def back(t, carry):
        j = n - 1 - t
        for b in range(batch):
            l_j = l_s[b, pl.ds(j, 1), :]
            x = out_ref[pl.ds(b, 1), :]
            y_j = jnp.sum(jnp.where(lane_v == j, y_s[pl.ds(b, 1), :], 0.0), axis=1, keepdims=True)
            l_jj = jnp.sum(jnp.where(lane_v == j, l_j, 0.0), axis=1, keepdims=True)
            known = jnp.sum(jnp.where(lane_v > j, l_j * x, 0.0), axis=1, keepdims=True)
            out_ref[pl.ds(b, 1), :] = jnp.where(lane_v == j, (y_j - known) / l_jj, x)
        return carry

    lax.fori_loop(0, n, back, 0, unroll=2)


def flip_bits(value, mask, bits):
    out = value - value % (1 << bits)
    for bit in range(bits):
        here = (value // (1 << bit)) % 2
        out = out + (1 << bit) * ((1 - here) if (mask >> bit) & 1 else here)
    return out


def doubling_kernel(
    n_rep, low_bits, rounds, x_ref, o_ref, full_recv, piece_recv, piece, gath,
    sem_a, sem_b, sem_c, sem_d, sem_e, sem_f,
):
    flat = lax.axis_index("ent") * n_rep + lax.axis_index("rep")
    group = 1 << low_bits
    rows = x_ref.shape[0] // group
    slot = flat % group

    def place(p):
        return (p // n_rep, p % n_rep)

    def flip(bit):
        step = 1 << bit
        upper = (flat // step) % 2
        return flat + step - 2 * step * upper

    members = [flip_bits(flat, k, low_bits) for k in range(1, group)]
    outer = [flip(bit) for bit in range(low_bits, rounds)]
    barrier = pltpu.get_barrier_semaphore()
    for p in members + outer:
        pl.semaphore_signal(barrier, inc=1, device_id=place(p), device_id_type=MESH_ID)
    pl.semaphore_wait(barrier, len(members) + len(outer))

    o_ref[...] = x_ref[...]
    for bit in range(low_bits):
        copy = pltpu.make_async_remote_copy(
            src_ref=o_ref, dst_ref=full_recv.at[bit], send_sem=sem_a.at[bit],
            recv_sem=sem_b.at[bit], device_id=place(flip(bit)), device_id_type=MESH_ID,
        )
        copy.start()
        copy.wait_recv()
        copy.wait_send()
        o_ref[...] = o_ref[...] + full_recv[bit]

    piece[...] = o_ref[pl.ds(pl.multiple_of(slot * rows, rows), rows), :]
    for index, p in enumerate(outer):
        copy = pltpu.make_async_remote_copy(
            src_ref=piece, dst_ref=piece_recv.at[index], send_sem=sem_c.at[index],
            recv_sem=sem_d.at[index], device_id=place(p), device_id_type=MESH_ID,
        )
        copy.start()
        copy.wait_recv()
        copy.wait_send()
        piece[...] = piece[...] + piece_recv[index]

    gath[slot] = piece[...]
    sends = []
    for index, p in enumerate(members):
        copy = pltpu.make_async_remote_copy(
            src_ref=piece, dst_ref=gath.at[slot], send_sem=sem_e.at[index],
            recv_sem=sem_f.at[slot], device_id=place(p), device_id_type=MESH_ID,
        )
        copy.start()
        sends.append(copy)
    for k in range(1, group):
        source = flip_bits(slot, k, low_bits)
        pltpu.make_async_remote_copy(
            src_ref=piece, dst_ref=gath.at[source], send_sem=sem_e.at[k - 1],
            recv_sem=sem_f.at[source], device_id=place(members[k - 1]), device_id_type=MESH_ID,
        ).wait_recv()
    for copy in sends:
        copy.wait_send()
    for part in range(group):
        o_ref[pl.ds(part * rows, rows), :] = gath[part]


def tree_sum(value, count):
    rounds = count.bit_length() - 1
    n_rep = lax.axis_size("rep")
    low_bits = (n_rep * 2).bit_length() - 1
    group = 1 << low_bits
    rows = value.shape[0] // group
    outer = rounds - low_bits
    return pl.pallas_call(
        functools.partial(doubling_kernel, n_rep, low_bits, rounds),
        out_shape=jax.ShapeDtypeStruct(value.shape, value.dtype),
        in_specs=[pl.BlockSpec(memory_space=pltpu.VMEM)],
        out_specs=pl.BlockSpec(memory_space=pltpu.VMEM),
        scratch_shapes=[
            pltpu.VMEM((low_bits,) + value.shape, value.dtype),
            pltpu.VMEM((outer, rows, value.shape[1]), value.dtype),
            pltpu.VMEM((rows, value.shape[1]), value.dtype),
            pltpu.VMEM((group, rows, value.shape[1]), value.dtype),
            pltpu.SemaphoreType.DMA((low_bits,)),
            pltpu.SemaphoreType.DMA((low_bits,)),
            pltpu.SemaphoreType.DMA((outer,)),
            pltpu.SemaphoreType.DMA((outer,)),
            pltpu.SemaphoreType.DMA((group - 1,)),
            pltpu.SemaphoreType.DMA((group,)),
        ],
        compiler_params=pltpu.CompilerParams(collective_id=0, has_side_effects=True),
    )(value)


def rep_peers(n_rep):
    me = lax.axis_index("rep")
    return me, [(me + shift) % n_rep for shift in range(1, n_rep)]


def owner_kernel(n_rep, blocks_ref, base_ref, out_ref, x_s, recv, a_s, l_s, y_s, fac, gath,
                 sem_a, sem_b, sem_c, sem_d):
    me, peers = rep_peers(n_rep)
    ent = lax.axis_index("ent")
    batch, n, _ = a_s.shape
    barrier = pltpu.get_barrier_semaphore()
    for peer in peers:
        pl.semaphore_signal(barrier, inc=1, device_id=(ent, peer), device_id_type=MESH_ID)
    pl.semaphore_wait(barrier, n_rep - 1)
    copies = []
    for index, peer in enumerate(peers):
        copy = pltpu.make_async_remote_copy(
            src_ref=blocks_ref.at[peer], dst_ref=recv.at[index], send_sem=sem_a.at[index],
            recv_sem=sem_b.at[index], device_id=(ent, peer), device_id_type=MESH_ID,
        )
        copy.start()
        copies.append(copy)
    total = blocks_ref[me]
    for index, copy in enumerate(copies):
        copy.wait_recv()
        total = total + recv[index]
    for copy in copies:
        copy.wait_send()
    base = base_ref[...]
    for b in range(batch):
        gram = total[b * n : (b + 1) * n] + base
        a_s[b] = (gram + gram.T) / 2
    y_s[...] = total[batch * n : batch * n + batch]
    cholesky_solve(a_s, l_s, y_s, x_s)
    fac[...] = x_s[...].astype(fac.dtype)
    gath[me] = fac[...]
    sends = []
    for index, peer in enumerate(peers):
        copy = pltpu.make_async_remote_copy(
            src_ref=fac, dst_ref=gath.at[me], send_sem=sem_c.at[index],
            recv_sem=sem_d.at[me], device_id=(ent, peer), device_id_type=MESH_ID,
        )
        copy.start()
        sends.append(copy)
    for index, source in enumerate(peers):
        pltpu.make_async_remote_copy(
            src_ref=fac, dst_ref=gath.at[source], send_sem=sem_c.at[index],
            recv_sem=sem_d.at[source], device_id=(ent, source), device_id_type=MESH_ID,
        ).wait_recv()
    for copy in sends:
        copy.wait_send()
    out_ref[...] = gath[...]


def solve_owned(blocks, base, n_rep, per_dev):
    n = blocks.shape[2]
    return pl.pallas_call(
        functools.partial(owner_kernel, n_rep),
        out_shape=(
            jax.ShapeDtypeStruct((n_rep, per_dev, n), jnp.bfloat16),
            jax.ShapeDtypeStruct((per_dev, n), jnp.float32),
        ),
        in_specs=[pl.BlockSpec(memory_space=pltpu.VMEM)] * 2,
        out_specs=(pl.BlockSpec(memory_space=pltpu.VMEM), pl.BlockSpec(memory_space=pltpu.VMEM)),
        scratch_shapes=[
            pltpu.VMEM((n_rep - 1,) + blocks.shape[1:], jnp.float32),
            pltpu.VMEM((per_dev, n, n), jnp.float32),
            pltpu.VMEM((per_dev, n, n), jnp.float32),
            pltpu.VMEM((per_dev, n), jnp.float32),
            pltpu.VMEM((per_dev, n), jnp.bfloat16),
            pltpu.VMEM((n_rep, per_dev, n), jnp.bfloat16),
            pltpu.SemaphoreType.DMA((n_rep - 1,)),
            pltpu.SemaphoreType.DMA((n_rep - 1,)),
            pltpu.SemaphoreType.DMA((n_rep - 1,)),
            pltpu.SemaphoreType.DMA((n_rep,)),
        ],
        compiler_params=pltpu.CompilerParams(collective_id=1, has_side_effects=True),
    )(blocks, base)


def gather_kernel(idx_ref, table_t_ref, out_ref):
    step = pl.program_id(0)
    idx = idx_ref[pl.ds(step, 1), :]
    picks = lax.broadcasted_iota(jnp.int32, (table_t_ref.shape[1], idx.shape[1]), 0) == idx
    rows_t = jnp.dot(table_t_ref[...], picks.astype(jnp.bfloat16), preferred_element_type=jnp.float32)
    out_ref[...] = rows_t.T.astype(out_ref.dtype)


def gather_rows(table, idx, chunk=4096):
    count = idx.shape[0]
    idx_lanes = idx.reshape(count // chunk, chunk)
    return pl.pallas_call(
        gather_kernel,
        out_shape=jax.ShapeDtypeStruct((count, table.shape[1]), table.dtype),
        grid=(count // chunk,),
        in_specs=[
            pl.BlockSpec(idx_lanes.shape, lambda i: (0, 0)),
            pl.BlockSpec((table.shape[1], table.shape[0]), lambda i: (0, 0)),
        ],
        out_specs=pl.BlockSpec((chunk, table.shape[1]), lambda i: (i, 0)),
        cost_estimate=pl.CostEstimate(
            flops=2 * count * table.shape[0] * table.shape[1],
            transcendentals=0,
            bytes_accessed=count * 4 + table.size * 2 + count * table.shape[1] * 2,
        ),
    )(idx_lanes, table.T)


def gram_kernel(n_user, per_dev, rows_ref, gw_ref, user_ref, rw_ref, out_ref):
    step = pl.program_id(0)
    width = rows_ref.shape[1]

    @pl.when(step == 0)
    def _():
        out_ref[...] = jnp.zeros_like(out_ref)

    rows = rows_ref[...]
    rows_t = rows.astype(jnp.float32).T
    weights_t = (rows_t * gw_ref[pl.ds(step, 1), :]).astype(jnp.bfloat16)
    users = user_ref[pl.ds(step, 1), :]
    zero = jnp.zeros((), jnp.bfloat16)
    for user in range(n_user):
        picked = jnp.where(users == user, weights_t, zero)
        block, spot = user // per_dev, (user % per_dev) * width
        out_ref[block, spot : spot + width, :] += jnp.dot(
            picked, rows, preferred_element_type=jnp.float32
        )
    slots = lax.broadcasted_iota(jnp.int32, (n_user, users.shape[1]), 0)
    per_user = jnp.where(users == slots, rw_ref[pl.ds(step, 1), :], 0.0)
    high = per_user.astype(jnp.bfloat16)
    low = (per_user - high.astype(jnp.float32)).astype(jnp.bfloat16)
    rhs = jnp.dot(high, rows, preferred_element_type=jnp.float32) + jnp.dot(
        low, rows, preferred_element_type=jnp.float32
    )
    base = per_dev * width
    for block in range(n_user // per_dev):
        out_ref[block, base : base + per_dev, :] += rhs[block * per_dev : (block + 1) * per_dev]


def user_grams(rows, gw_lanes, user_lanes, rw_lanes, n_user, per_dev):
    chunks, chunk = gw_lanes.shape
    width = rows.shape[1]
    n_block = n_user // per_dev
    block_rows = per_dev * width + per_dev
    return pl.pallas_call(
        functools.partial(gram_kernel, n_user, per_dev),
        out_shape=jax.ShapeDtypeStruct((n_block, block_rows, width), jnp.float32),
        grid=(chunks,),
        in_specs=[
            pl.BlockSpec((chunk, width), lambda i: (i, 0)),
            pl.BlockSpec((chunks, chunk), lambda i: (0, 0)),
            pl.BlockSpec((chunks, chunk), lambda i: (0, 0)),
            pl.BlockSpec((chunks, chunk), lambda i: (0, 0)),
        ],
        out_specs=pl.BlockSpec((n_block, block_rows, width), lambda i: (0, 0, 0)),
        cost_estimate=pl.CostEstimate(
            flops=2 * rows.shape[0] * width * width * (n_user + 2),
            transcendentals=0,
            bytes_accessed=rows.size * 2 + 12 * rows.shape[0] + n_user * width * (width + 1) * 4,
        ),
    )(rows, gw_lanes, user_lanes, rw_lanes)

def shards(item_factors, tile_items, send_tiles, tile_users, tile_counts, recv_tiles):
    highest = lax.Precision.HIGHEST
    rank_width = item_factors.shape[1]
    item_count = item_factors.shape[0]
    n_ent = lax.axis_size("ent")
    n_rep = lax.axis_size("rep")
    tile_slots = tile_items.shape[2]
    tile_rows = tile_items.shape[3]
    seg_count = tile_users.shape[3]
    seg_length = tile_rows // seg_count
    slot_cap = tile_slots // n_ent
    user_block = U_DEV * lax.axis_size("rep")
    item_ids = tile_items.reshape(tile_slots, tile_rows)
    slot_pos = jnp.arange(tile_slots, dtype=jnp.int32) % slot_cap
    live_send = slot_pos < jnp.repeat(send_tiles.reshape(n_ent), slot_cap)
    live_recv = slot_pos < jnp.repeat(recv_tiles.reshape(n_ent), slot_cap)
    partial_gram = lax.dot_general(
        item_factors, item_factors, (((0,), (0,)), ((), ())), preferred_element_type=jnp.float32
    )
    live_rows = jnp.repeat(live_send, tile_rows)
    picked = gather_rows(item_factors, jnp.where(live_rows, item_ids.reshape(-1), -1))
    incoming = lax.all_to_all(
        picked.reshape(n_ent, slot_cap * tile_rows, rank_width),
        "ent",
        split_axis=0,
        concat_axis=0,
        tiled=True,
    )
    counts_int = tile_counts.reshape(tile_slots, tile_rows)
    counts_f = counts_int.astype(jnp.float32)
    gram_weight = ALPHA * counts_f
    rhs_weight = jnp.where(
        live_recv[:, None] & (counts_int > 0), 1.0 + ALPHA * counts_f, jnp.float32(0.0)
    )
    owners = tile_users.reshape(tile_slots * seg_count)
    selector = owners[None, :] == jnp.arange(user_block, dtype=jnp.int32)[:, None]
    selector_f = selector.astype(jnp.float32)
    rows_all = incoming.reshape(tile_slots * tile_rows, rank_width)
    lane_chunk = 2048
    row_owner = jnp.repeat(owners, seg_length)
    gram_blocks = user_grams(
        rows_all,
        gram_weight.reshape(-1, lane_chunk),
        row_owner.reshape(-1, lane_chunk),
        rhs_weight.reshape(-1, lane_chunk),
        user_block,
        U_DEV,
    )
    identity_mat = jnp.eye(rank_width, dtype=jnp.float32)
    added_term = tree_sum(partial_gram, n_ent * n_rep) + RIDGE * identity_mat
    solved, own_factors = solve_owned(gram_blocks, added_term, n_rep, U_DEV)
    solved = solved.reshape(user_block, rank_width)
    run_factor = lax.dot_general(
        selector.astype(jnp.bfloat16),
        solved,
        (((0,), (0,)), ((), ())),
        preferred_element_type=jnp.float32,
    ).astype(jnp.bfloat16)
    back_load = jnp.concatenate(
        [
            run_factor.reshape(tile_slots, seg_count * rank_width),
            counts_int.astype(jnp.bfloat16),
        ],
        axis=1,
    )
    back_load = lax.all_to_all(
        back_load.reshape(n_ent, slot_cap, -1), "ent", split_axis=0, concat_axis=0, tiled=True
    ).reshape(tile_slots, -1)
    back_factor = back_load[:, : seg_count * rank_width]
    back_counts = back_load[:, seg_count * rank_width :].astype(jnp.float32)
    back_weight = jnp.where(
        live_send[:, None] & (back_counts > 0), 1.0 + ALPHA * back_counts, jnp.float32(0.0)
    )
    item_hot = item_ids[:, :, None] == jnp.arange(item_count, dtype=jnp.int32)[None, None, :]
    run_weight = back_weight.reshape(tile_slots * seg_count, seg_length)
    hot_runs = item_hot.reshape(tile_slots * seg_count, seg_length, item_count)
    spread_mat = jnp.sum(jnp.where(hot_runs, run_weight[:, :, None], 0.0), axis=1)
    item_rhs = lax.dot_general(
        spread_mat,
        back_factor.reshape(tile_slots * seg_count, rank_width).astype(jnp.float32),
        (((0,), (0,)), ((), ())),
        precision=highest,
        preferred_element_type=jnp.float32,
    )
    return (own_factors, item_rhs * RHS_SCALE)


def solution(mesh):
    in_specs = (
        P(("ent", "rep"), None),
        P("ent", "rep", None, None),
        P("ent", "rep", None),
        P("ent", "rep", None, None),
        P("ent", "rep", None, None),
        P("ent", "rep", None),
    )
    out_specs = (P(("ent", "rep"), None), P(("ent", "rep"), None))
    return jax.shard_map(shards, mesh=mesh, in_specs=in_specs, out_specs=out_specs, check_vma=False)
```

```python
import functools

import jax
import jax.numpy as jnp
from jax import lax
from jax.experimental import pallas as pl
from jax.experimental.pallas import tpu as pltpu
from jax.sharding import PartitionSpec as P

MESH_ID = pl.DeviceIdType.MESH

U_DEV = 2


ALPHA = 40.0
RIDGE = 1.0
RHS_SCALE = 1.0 / 640.0


def cholesky_solve(a_s, l_s, y_s, out_ref):
    batch, n, _ = a_s.shape
    out_ref[...] = jnp.zeros_like(out_ref)
    lane_v = lax.broadcasted_iota(jnp.int32, (1, n), 1)

    def factor(top, j, carry):
        span = n - top
        lane_m = lax.broadcasted_iota(jnp.int32, (span, n), 1)
        sub_m = lax.broadcasted_iota(jnp.int32, (span, n), 0) + top
        sub_v = lax.broadcasted_iota(jnp.int32, (span, 1), 0) + top
        for b in range(batch):
            a = a_s[b, top:, :]
            row = jnp.sum(jnp.where(sub_m == j, a, 0.0), axis=0, keepdims=True)
            col = jnp.sum(jnp.where(lane_m == j, a, 0.0), axis=1, keepdims=True)
            diag = jnp.sum(jnp.where(lane_v == j, row, 0.0), axis=1, keepdims=True)
            inv = 1.0 / jnp.sqrt(diag)
            l_row = jnp.where(lane_v >= j, row, 0.0) * inv
            l_col = jnp.where(sub_v >= j, col, 0.0) * inv
            a_s[b, top:, :] = a - l_col * l_row
            l_s[b, pl.ds(j, 1), :] = l_row
            y = y_s[pl.ds(b, 1), :]
            y_j = jnp.sum(jnp.where(lane_v == j, y, 0.0), axis=1, keepdims=True) * inv
            y_s[pl.ds(b, 1), :] = jnp.where(lane_v == j, y_j, y - y_j * l_row)
        return carry

    quarter = n // 4
    for part in range(4):
        top = part * quarter
        lax.fori_loop(top, top + quarter, functools.partial(factor, top), 0, unroll=2)

    def back(t, carry):
        j = n - 1 - t
        for b in range(batch):
            l_j = l_s[b, pl.ds(j, 1), :]
            x = out_ref[pl.ds(b, 1), :]
            y_j = jnp.sum(jnp.where(lane_v == j, y_s[pl.ds(b, 1), :], 0.0), axis=1, keepdims=True)
            l_jj = jnp.sum(jnp.where(lane_v == j, l_j, 0.0), axis=1, keepdims=True)
            known = jnp.sum(jnp.where(lane_v > j, l_j * x, 0.0), axis=1, keepdims=True)
            out_ref[pl.ds(b, 1), :] = jnp.where(lane_v == j, (y_j - known) / l_jj, x)
        return carry

    lax.fori_loop(0, n, back, 0, unroll=2)


def flip_bits(value, mask, bits):
    out = value - value % (1 << bits)
    for bit in range(bits):
        here = (value // (1 << bit)) % 2
        out = out + (1 << bit) * ((1 - here) if (mask >> bit) & 1 else here)
    return out


def doubling_kernel(
    n_rep, low_bits, rounds, x_ref, o_ref, full_recv, piece_recv, piece, gath,
    sem_a, sem_b, sem_c, sem_d, sem_e, sem_f,
):
    flat = lax.axis_index("ent") * n_rep + lax.axis_index("rep")
    group = 1 << low_bits
    rows = x_ref.shape[0] // group
    slot = flat % group

    def place(p):
        return (p // n_rep, p % n_rep)

    def flip(bit):
        step = 1 << bit
        upper = (flat // step) % 2
        return flat + step - 2 * step * upper

    members = [flip_bits(flat, k, low_bits) for k in range(1, group)]
    outer = [flip(bit) for bit in range(low_bits, rounds)]
    barrier = pltpu.get_barrier_semaphore()
    for p in members + outer:
        pl.semaphore_signal(barrier, inc=1, device_id=place(p), device_id_type=MESH_ID)
    pl.semaphore_wait(barrier, len(members) + len(outer))

    o_ref[...] = x_ref[...]
    for bit in range(low_bits):
        copy = pltpu.make_async_remote_copy(
            src_ref=o_ref, dst_ref=full_recv.at[bit], send_sem=sem_a.at[bit],
            recv_sem=sem_b.at[bit], device_id=place(flip(bit)), device_id_type=MESH_ID,
        )
        copy.start()
        copy.wait_recv()
        copy.wait_send()
        o_ref[...] = o_ref[...] + full_recv[bit]

    piece[...] = o_ref[pl.ds(pl.multiple_of(slot * rows, rows), rows), :]
    for index, p in enumerate(outer):
        copy = pltpu.make_async_remote_copy(
            src_ref=piece, dst_ref=piece_recv.at[index], send_sem=sem_c.at[index],
            recv_sem=sem_d.at[index], device_id=place(p), device_id_type=MESH_ID,
        )
        copy.start()
        copy.wait_recv()
        copy.wait_send()
        piece[...] = piece[...] + piece_recv[index]

    gath[slot] = piece[...]
    sends = []
    for index, p in enumerate(members):
        copy = pltpu.make_async_remote_copy(
            src_ref=piece, dst_ref=gath.at[slot], send_sem=sem_e.at[index],
            recv_sem=sem_f.at[slot], device_id=place(p), device_id_type=MESH_ID,
        )
        copy.start()
        sends.append(copy)
    for k in range(1, group):
        source = flip_bits(slot, k, low_bits)
        pltpu.make_async_remote_copy(
            src_ref=piece, dst_ref=gath.at[source], send_sem=sem_e.at[k - 1],
            recv_sem=sem_f.at[source], device_id=place(members[k - 1]), device_id_type=MESH_ID,
        ).wait_recv()
    for copy in sends:
        copy.wait_send()
    for part in range(group):
        o_ref[pl.ds(part * rows, rows), :] = gath[part]


def tree_sum(value, count):
    rounds = count.bit_length() - 1
    n_rep = lax.axis_size("rep")
    low_bits = (n_rep * 2).bit_length() - 1
    group = 1 << low_bits
    rows = value.shape[0] // group
    outer = rounds - low_bits
    return pl.pallas_call(
        functools.partial(doubling_kernel, n_rep, low_bits, rounds),
        out_shape=jax.ShapeDtypeStruct(value.shape, value.dtype),
        in_specs=[pl.BlockSpec(memory_space=pltpu.VMEM)],
        out_specs=pl.BlockSpec(memory_space=pltpu.VMEM),
        scratch_shapes=[
            pltpu.VMEM((low_bits,) + value.shape, value.dtype),
            pltpu.VMEM((outer, rows, value.shape[1]), value.dtype),
            pltpu.VMEM((rows, value.shape[1]), value.dtype),
            pltpu.VMEM((group, rows, value.shape[1]), value.dtype),
            pltpu.SemaphoreType.DMA((low_bits,)),
            pltpu.SemaphoreType.DMA((low_bits,)),
            pltpu.SemaphoreType.DMA((outer,)),
            pltpu.SemaphoreType.DMA((outer,)),
            pltpu.SemaphoreType.DMA((group - 1,)),
            pltpu.SemaphoreType.DMA((group,)),
        ],
        compiler_params=pltpu.CompilerParams(collective_id=0, has_side_effects=True),
    )(value)


def rep_peers(n_rep):
    me = lax.axis_index("rep")
    return me, [(me + shift) % n_rep for shift in range(1, n_rep)]


def owner_kernel(n_rep, blocks_ref, base_ref, out_ref, x_s, recv, a_s, l_s, y_s, fac, gath,
                 sem_a, sem_b, sem_c, sem_d):
    me, peers = rep_peers(n_rep)
    ent = lax.axis_index("ent")
    batch, n, _ = a_s.shape
    barrier = pltpu.get_barrier_semaphore()
    for peer in peers:
        pl.semaphore_signal(barrier, inc=1, device_id=(ent, peer), device_id_type=MESH_ID)
    pl.semaphore_wait(barrier, n_rep - 1)
    copies = []
    for index, peer in enumerate(peers):
        copy = pltpu.make_async_remote_copy(
            src_ref=blocks_ref.at[peer], dst_ref=recv.at[index], send_sem=sem_a.at[index],
            recv_sem=sem_b.at[index], device_id=(ent, peer), device_id_type=MESH_ID,
        )
        copy.start()
        copies.append(copy)
    total = blocks_ref[me]
    for index, copy in enumerate(copies):
        copy.wait_recv()
        total = total + recv[index]
    for copy in copies:
        copy.wait_send()
    base = base_ref[...]
    for b in range(batch):
        gram = total[b * n : (b + 1) * n] + base
        a_s[b] = (gram + gram.T) / 2
    y_s[...] = total[batch * n : batch * n + batch]
    cholesky_solve(a_s, l_s, y_s, x_s)
    fac[...] = x_s[...].astype(fac.dtype)
    gath[me] = fac[...]
    sends = []
    for index, peer in enumerate(peers):
        copy = pltpu.make_async_remote_copy(
            src_ref=fac, dst_ref=gath.at[me], send_sem=sem_c.at[index],
            recv_sem=sem_d.at[me], device_id=(ent, peer), device_id_type=MESH_ID,
        )
        copy.start()
        sends.append(copy)
    for index, source in enumerate(peers):
        pltpu.make_async_remote_copy(
            src_ref=fac, dst_ref=gath.at[source], send_sem=sem_c.at[index],
            recv_sem=sem_d.at[source], device_id=(ent, source), device_id_type=MESH_ID,
        ).wait_recv()
    for copy in sends:
        copy.wait_send()
    out_ref[...] = gath[...]


def solve_owned(blocks, base, n_rep, per_dev):
    n = blocks.shape[2]
    return pl.pallas_call(
        functools.partial(owner_kernel, n_rep),
        out_shape=(
            jax.ShapeDtypeStruct((n_rep, per_dev, n), jnp.bfloat16),
            jax.ShapeDtypeStruct((per_dev, n), jnp.float32),
        ),
        in_specs=[pl.BlockSpec(memory_space=pltpu.VMEM)] * 2,
        out_specs=(pl.BlockSpec(memory_space=pltpu.VMEM), pl.BlockSpec(memory_space=pltpu.VMEM)),
        scratch_shapes=[
            pltpu.VMEM((n_rep - 1,) + blocks.shape[1:], jnp.float32),
            pltpu.VMEM((per_dev, n, n), jnp.float32),
            pltpu.VMEM((per_dev, n, n), jnp.float32),
            pltpu.VMEM((per_dev, n), jnp.float32),
            pltpu.VMEM((per_dev, n), jnp.bfloat16),
            pltpu.VMEM((n_rep, per_dev, n), jnp.bfloat16),
            pltpu.SemaphoreType.DMA((n_rep - 1,)),
            pltpu.SemaphoreType.DMA((n_rep - 1,)),
            pltpu.SemaphoreType.DMA((n_rep - 1,)),
            pltpu.SemaphoreType.DMA((n_rep,)),
        ],
        compiler_params=pltpu.CompilerParams(collective_id=1, has_side_effects=True),
    )(blocks, base)


def gather_kernel(idx_ref, table_t_ref, out_ref):
    step = pl.program_id(0)
    idx = idx_ref[pl.ds(step, 1), :]
    picks = lax.broadcasted_iota(jnp.int32, (table_t_ref.shape[1], idx.shape[1]), 0) == idx
    rows_t = jnp.dot(table_t_ref[...], picks.astype(jnp.bfloat16), preferred_element_type=jnp.float32)
    out_ref[...] = rows_t.T.astype(out_ref.dtype)


def gather_rows(table, idx, chunk=4096):
    count = idx.shape[0]
    idx_lanes = idx.reshape(count // chunk, chunk)
    return pl.pallas_call(
        gather_kernel,
        out_shape=jax.ShapeDtypeStruct((count, table.shape[1]), table.dtype),
        grid=(count // chunk,),
        in_specs=[
            pl.BlockSpec(idx_lanes.shape, lambda i: (0, 0)),
            pl.BlockSpec((table.shape[1], table.shape[0]), lambda i: (0, 0)),
        ],
        out_specs=pl.BlockSpec((chunk, table.shape[1]), lambda i: (i, 0)),
        cost_estimate=pl.CostEstimate(
            flops=2 * count * table.shape[0] * table.shape[1],
            transcendentals=0,
            bytes_accessed=count * 4 + table.size * 2 + count * table.shape[1] * 2,
        ),
    )(idx_lanes, table.T)


def gram_kernel(n_user, per_dev, rows_ref, gw_ref, user_ref, rw_ref, out_ref):
    step = pl.program_id(0)
    width = rows_ref.shape[1]

    @pl.when(step == 0)
    def _():
        out_ref[...] = jnp.zeros_like(out_ref)

    rows = rows_ref[...]
    rows_t = rows.astype(jnp.float32).T
    weights_t = (rows_t * gw_ref[pl.ds(step, 1), :]).astype(jnp.bfloat16)
    users = user_ref[pl.ds(step, 1), :]
    zero = jnp.zeros((), jnp.bfloat16)
    for user in range(n_user):
        picked = jnp.where(users == user, weights_t, zero)
        block, spot = user // per_dev, (user % per_dev) * width
        out_ref[block, spot : spot + width, :] += jnp.dot(
            picked, rows, preferred_element_type=jnp.float32
        )
    slots = lax.broadcasted_iota(jnp.int32, (n_user, users.shape[1]), 0)
    per_user = jnp.where(users == slots, rw_ref[pl.ds(step, 1), :], 0.0)
    high = per_user.astype(jnp.bfloat16)
    low = (per_user - high.astype(jnp.float32)).astype(jnp.bfloat16)
    rhs = jnp.dot(high, rows, preferred_element_type=jnp.float32) + jnp.dot(
        low, rows, preferred_element_type=jnp.float32
    )
    base = per_dev * width
    for block in range(n_user // per_dev):
        out_ref[block, base : base + per_dev, :] += rhs[block * per_dev : (block + 1) * per_dev]


def user_grams(rows, gw_lanes, user_lanes, rw_lanes, n_user, per_dev):
    chunks, chunk = gw_lanes.shape
    width = rows.shape[1]
    n_block = n_user // per_dev
    block_rows = per_dev * width + per_dev
    return pl.pallas_call(
        functools.partial(gram_kernel, n_user, per_dev),
        out_shape=jax.ShapeDtypeStruct((n_block, block_rows, width), jnp.float32),
        grid=(chunks,),
        in_specs=[
            pl.BlockSpec((chunk, width), lambda i: (i, 0)),
            pl.BlockSpec((chunks, chunk), lambda i: (0, 0)),
            pl.BlockSpec((chunks, chunk), lambda i: (0, 0)),
            pl.BlockSpec((chunks, chunk), lambda i: (0, 0)),
        ],
        out_specs=pl.BlockSpec((n_block, block_rows, width), lambda i: (0, 0, 0)),
        cost_estimate=pl.CostEstimate(
            flops=2 * rows.shape[0] * width * width * (n_user + 2),
            transcendentals=0,
            bytes_accessed=rows.size * 2 + 12 * rows.shape[0] + n_user * width * (width + 1) * 4,
        ),
    )(rows, gw_lanes, user_lanes, rw_lanes)

def shards(item_factors, tile_items, send_tiles, tile_users, tile_counts, recv_tiles):
    highest = lax.Precision.HIGHEST
    rank_width = item_factors.shape[1]
    item_count = item_factors.shape[0]
    n_ent = lax.axis_size("ent")
    n_rep = lax.axis_size("rep")
    tile_slots = tile_items.shape[2]
    tile_rows = tile_items.shape[3]
    seg_count = tile_users.shape[3]
    seg_length = tile_rows // seg_count
    slot_cap = tile_slots // n_ent
    user_block = U_DEV * lax.axis_size("rep")
    item_ids = tile_items.reshape(tile_slots, tile_rows)
    slot_pos = jnp.arange(tile_slots, dtype=jnp.int32) % slot_cap
    live_send = slot_pos < jnp.repeat(send_tiles.reshape(n_ent), slot_cap)
    live_recv = slot_pos < jnp.repeat(recv_tiles.reshape(n_ent), slot_cap)
    partial_gram = lax.dot_general(
        item_factors, item_factors, (((0,), (0,)), ((), ())), preferred_element_type=jnp.float32
    )
    live_rows = jnp.repeat(live_send, tile_rows)
    picked = gather_rows(item_factors, jnp.where(live_rows, item_ids.reshape(-1), -1))
    incoming = lax.all_to_all(
        picked.reshape(n_ent, slot_cap * tile_rows, rank_width),
        "ent",
        split_axis=0,
        concat_axis=0,
        tiled=True,
    )
    counts_int = tile_counts.reshape(tile_slots, tile_rows)
    counts_f = counts_int.astype(jnp.float32)
    gram_weight = ALPHA * counts_f
    rhs_weight = jnp.where(
        live_recv[:, None] & (counts_int > 0), 1.0 + ALPHA * counts_f, jnp.float32(0.0)
    )
    owners = tile_users.reshape(tile_slots * seg_count)
    selector = owners[None, :] == jnp.arange(user_block, dtype=jnp.int32)[:, None]
    selector_f = selector.astype(jnp.float32)
    rows_all = incoming.reshape(tile_slots * tile_rows, rank_width)
    lane_chunk = 4096
    row_owner = jnp.repeat(owners, seg_length)
    gram_blocks = user_grams(
        rows_all,
        gram_weight.reshape(-1, lane_chunk),
        row_owner.reshape(-1, lane_chunk),
        rhs_weight.reshape(-1, lane_chunk),
        user_block,
        U_DEV,
    )
    identity_mat = jnp.eye(rank_width, dtype=jnp.float32)
    added_term = tree_sum(partial_gram, n_ent * n_rep) + RIDGE * identity_mat
    solved, own_factors = solve_owned(gram_blocks, added_term, n_rep, U_DEV)
    solved = solved.reshape(user_block, rank_width)
    run_factor = lax.dot_general(
        selector.astype(jnp.bfloat16),
        solved,
        (((0,), (0,)), ((), ())),
        preferred_element_type=jnp.float32,
    ).astype(jnp.bfloat16)
    back_load = jnp.concatenate(
        [
            run_factor.reshape(tile_slots, seg_count * rank_width),
            counts_int.astype(jnp.bfloat16),
        ],
        axis=1,
    )
    back_load = lax.all_to_all(
        back_load.reshape(n_ent, slot_cap, -1), "ent", split_axis=0, concat_axis=0, tiled=True
    ).reshape(tile_slots, -1)
    back_factor = back_load[:, : seg_count * rank_width]
    back_counts = back_load[:, seg_count * rank_width :].astype(jnp.float32)
    back_weight = jnp.where(
        live_send[:, None] & (back_counts > 0), 1.0 + ALPHA * back_counts, jnp.float32(0.0)
    )
    item_hot = item_ids[:, :, None] == jnp.arange(item_count, dtype=jnp.int32)[None, None, :]
    run_weight = back_weight.reshape(tile_slots * seg_count, seg_length)
    hot_runs = item_hot.reshape(tile_slots * seg_count, seg_length, item_count)
    spread_mat = jnp.sum(jnp.where(hot_runs, run_weight[:, :, None], 0.0), axis=1)
    item_rhs = lax.dot_general(
        spread_mat,
        back_factor.reshape(tile_slots * seg_count, rank_width).astype(jnp.float32),
        (((0,), (0,)), ((), ())),
        precision=highest,
        preferred_element_type=jnp.float32,
    )
    return (own_factors, item_rhs * RHS_SCALE)


def solution(mesh):
    in_specs = (
        P(("ent", "rep"), None),
        P("ent", "rep", None, None),
        P("ent", "rep", None),
        P("ent", "rep", None, None),
        P("ent", "rep", None, None),
        P("ent", "rep", None),
    )
    out_specs = (P(("ent", "rep"), None), P(("ent", "rep"), None))
    return jax.shard_map(shards, mesh=mesh, in_specs=in_specs, out_specs=out_specs, check_vma=False)
```

```python
import functools

import jax
import jax.numpy as jnp
from jax import lax
from jax.experimental import pallas as pl
from jax.experimental.pallas import tpu as pltpu
from jax.sharding import PartitionSpec as P

MESH_ID = pl.DeviceIdType.MESH

U_DEV = 2


ALPHA = 40.0
RIDGE = 1.0
RHS_SCALE = 1.0 / 640.0


def cholesky_solve(a_s, l_s, y_s, out_ref):
    batch, n, _ = a_s.shape
    out_ref[...] = jnp.zeros_like(out_ref)
    lane_v = lax.broadcasted_iota(jnp.int32, (1, n), 1)

    def factor(top, j, carry):
        span = n - top
        sub_m = lax.broadcasted_iota(jnp.int32, (span, n), 0) + top
        sub_v = lax.broadcasted_iota(jnp.int32, (span, 1), 0) + top
        for b in range(batch):
            a = a_s[b, top:, :]
            row = jnp.sum(jnp.where(sub_m == j, a, 0.0), axis=0, keepdims=True)
            col = jnp.transpose(jnp.broadcast_to(row, (8, n)))[top:, 0:1]
            diag = jnp.sum(jnp.where(lane_v == j, row, 0.0), axis=1, keepdims=True)
            inv = 1.0 / jnp.sqrt(diag)
            l_row = jnp.where(lane_v >= j, row, 0.0) * inv
            l_col = jnp.where(sub_v >= j, col, 0.0) * inv
            a_s[b, top:, :] = a - l_col * l_row
            l_s[b, pl.ds(j, 1), :] = l_row
            y = y_s[pl.ds(b, 1), :]
            y_j = jnp.sum(jnp.where(lane_v == j, y, 0.0), axis=1, keepdims=True) * inv
            y_s[pl.ds(b, 1), :] = jnp.where(lane_v == j, y_j, y - y_j * l_row)
        return carry

    quarter = n // 4
    for part in range(4):
        top = part * quarter
        lax.fori_loop(top, top + quarter, functools.partial(factor, top), 0, unroll=2)

    def back(t, carry):
        j = n - 1 - t
        for b in range(batch):
            l_j = l_s[b, pl.ds(j, 1), :]
            x = out_ref[pl.ds(b, 1), :]
            y_j = jnp.sum(jnp.where(lane_v == j, y_s[pl.ds(b, 1), :], 0.0), axis=1, keepdims=True)
            l_jj = jnp.sum(jnp.where(lane_v == j, l_j, 0.0), axis=1, keepdims=True)
            known = jnp.sum(jnp.where(lane_v > j, l_j * x, 0.0), axis=1, keepdims=True)
            out_ref[pl.ds(b, 1), :] = jnp.where(lane_v == j, (y_j - known) / l_jj, x)
        return carry

    lax.fori_loop(0, n, back, 0, unroll=2)


def flip_bits(value, mask, bits):
    out = value - value % (1 << bits)
    for bit in range(bits):
        here = (value // (1 << bit)) % 2
        out = out + (1 << bit) * ((1 - here) if (mask >> bit) & 1 else here)
    return out


def doubling_kernel(
    n_rep, low_bits, rounds, x_ref, o_ref, full_recv, piece_recv, piece, gath,
    sem_a, sem_b, sem_c, sem_d, sem_e, sem_f,
):
    flat = lax.axis_index("ent") * n_rep + lax.axis_index("rep")
    group = 1 << low_bits
    rows = x_ref.shape[0] // group
    slot = flat % group

    def place(p):
        return (p // n_rep, p % n_rep)

    def flip(bit):
        step = 1 << bit
        upper = (flat // step) % 2
        return flat + step - 2 * step * upper

    members = [flip_bits(flat, k, low_bits) for k in range(1, group)]
    outer = [flip(bit) for bit in range(low_bits, rounds)]
    barrier = pltpu.get_barrier_semaphore()
    for p in members + outer:
        pl.semaphore_signal(barrier, inc=1, device_id=place(p), device_id_type=MESH_ID)
    pl.semaphore_wait(barrier, len(members) + len(outer))

    o_ref[...] = x_ref[...]
    for bit in range(low_bits):
        copy = pltpu.make_async_remote_copy(
            src_ref=o_ref, dst_ref=full_recv.at[bit], send_sem=sem_a.at[bit],
            recv_sem=sem_b.at[bit], device_id=place(flip(bit)), device_id_type=MESH_ID,
        )
        copy.start()
        copy.wait_recv()
        copy.wait_send()
        o_ref[...] = o_ref[...] + full_recv[bit]

    piece[...] = o_ref[pl.ds(pl.multiple_of(slot * rows, rows), rows), :]
    for index, p in enumerate(outer):
        copy = pltpu.make_async_remote_copy(
            src_ref=piece, dst_ref=piece_recv.at[index], send_sem=sem_c.at[index],
            recv_sem=sem_d.at[index], device_id=place(p), device_id_type=MESH_ID,
        )
        copy.start()
        copy.wait_recv()
        copy.wait_send()
        piece[...] = piece[...] + piece_recv[index]

    gath[slot] = piece[...]
    sends = []
    for index, p in enumerate(members):
        copy = pltpu.make_async_remote_copy(
            src_ref=piece, dst_ref=gath.at[slot], send_sem=sem_e.at[index],
            recv_sem=sem_f.at[slot], device_id=place(p), device_id_type=MESH_ID,
        )
        copy.start()
        sends.append(copy)
    for k in range(1, group):
        source = flip_bits(slot, k, low_bits)
        pltpu.make_async_remote_copy(
            src_ref=piece, dst_ref=gath.at[source], send_sem=sem_e.at[k - 1],
            recv_sem=sem_f.at[source], device_id=place(members[k - 1]), device_id_type=MESH_ID,
        ).wait_recv()
    for copy in sends:
        copy.wait_send()
    for part in range(group):
        o_ref[pl.ds(part * rows, rows), :] = gath[part]


def tree_sum(value, count):
    rounds = count.bit_length() - 1
    n_rep = lax.axis_size("rep")
    low_bits = (n_rep * 2).bit_length() - 1
    group = 1 << low_bits
    rows = value.shape[0] // group
    outer = rounds - low_bits
    return pl.pallas_call(
        functools.partial(doubling_kernel, n_rep, low_bits, rounds),
        out_shape=jax.ShapeDtypeStruct(value.shape, value.dtype),
        in_specs=[pl.BlockSpec(memory_space=pltpu.VMEM)],
        out_specs=pl.BlockSpec(memory_space=pltpu.VMEM),
        scratch_shapes=[
            pltpu.VMEM((low_bits,) + value.shape, value.dtype),
            pltpu.VMEM((outer, rows, value.shape[1]), value.dtype),
            pltpu.VMEM((rows, value.shape[1]), value.dtype),
            pltpu.VMEM((group, rows, value.shape[1]), value.dtype),
            pltpu.SemaphoreType.DMA((low_bits,)),
            pltpu.SemaphoreType.DMA((low_bits,)),
            pltpu.SemaphoreType.DMA((outer,)),
            pltpu.SemaphoreType.DMA((outer,)),
            pltpu.SemaphoreType.DMA((group - 1,)),
            pltpu.SemaphoreType.DMA((group,)),
        ],
        compiler_params=pltpu.CompilerParams(collective_id=0, has_side_effects=True),
    )(value)


def rep_peers(n_rep):
    me = lax.axis_index("rep")
    return me, [(me + shift) % n_rep for shift in range(1, n_rep)]


def owner_kernel(n_rep, blocks_ref, base_ref, out_ref, x_s, recv, a_s, l_s, y_s, fac, gath,
                 sem_a, sem_b, sem_c, sem_d):
    me, peers = rep_peers(n_rep)
    ent = lax.axis_index("ent")
    batch, n, _ = a_s.shape
    barrier = pltpu.get_barrier_semaphore()
    for peer in peers:
        pl.semaphore_signal(barrier, inc=1, device_id=(ent, peer), device_id_type=MESH_ID)
    pl.semaphore_wait(barrier, n_rep - 1)
    copies = []
    for index, peer in enumerate(peers):
        copy = pltpu.make_async_remote_copy(
            src_ref=blocks_ref.at[peer], dst_ref=recv.at[index], send_sem=sem_a.at[index],
            recv_sem=sem_b.at[index], device_id=(ent, peer), device_id_type=MESH_ID,
        )
        copy.start()
        copies.append(copy)
    total = blocks_ref[me]
    for index, copy in enumerate(copies):
        copy.wait_recv()
        total = total + recv[index]
    for copy in copies:
        copy.wait_send()
    base = base_ref[...]
    for b in range(batch):
        gram = total[b * n : (b + 1) * n] + base
        a_s[b] = (gram + gram.T) / 2
    y_s[...] = total[batch * n : batch * n + batch]
    cholesky_solve(a_s, l_s, y_s, x_s)
    fac[...] = x_s[...].astype(fac.dtype)
    gath[me] = fac[...]
    sends = []
    for index, peer in enumerate(peers):
        copy = pltpu.make_async_remote_copy(
            src_ref=fac, dst_ref=gath.at[me], send_sem=sem_c.at[index],
            recv_sem=sem_d.at[me], device_id=(ent, peer), device_id_type=MESH_ID,
        )
        copy.start()
        sends.append(copy)
    for index, source in enumerate(peers):
        pltpu.make_async_remote_copy(
            src_ref=fac, dst_ref=gath.at[source], send_sem=sem_c.at[index],
            recv_sem=sem_d.at[source], device_id=(ent, source), device_id_type=MESH_ID,
        ).wait_recv()
    for copy in sends:
        copy.wait_send()
    out_ref[...] = gath[...]


def solve_owned(blocks, base, n_rep, per_dev):
    n = blocks.shape[2]
    return pl.pallas_call(
        functools.partial(owner_kernel, n_rep),
        out_shape=(
            jax.ShapeDtypeStruct((n_rep, per_dev, n), jnp.bfloat16),
            jax.ShapeDtypeStruct((per_dev, n), jnp.float32),
        ),
        in_specs=[pl.BlockSpec(memory_space=pltpu.VMEM)] * 2,
        out_specs=(pl.BlockSpec(memory_space=pltpu.VMEM), pl.BlockSpec(memory_space=pltpu.VMEM)),
        scratch_shapes=[
            pltpu.VMEM((n_rep - 1,) + blocks.shape[1:], jnp.float32),
            pltpu.VMEM((per_dev, n, n), jnp.float32),
            pltpu.VMEM((per_dev, n, n), jnp.float32),
            pltpu.VMEM((per_dev, n), jnp.float32),
            pltpu.VMEM((per_dev, n), jnp.bfloat16),
            pltpu.VMEM((n_rep, per_dev, n), jnp.bfloat16),
            pltpu.SemaphoreType.DMA((n_rep - 1,)),
            pltpu.SemaphoreType.DMA((n_rep - 1,)),
            pltpu.SemaphoreType.DMA((n_rep - 1,)),
            pltpu.SemaphoreType.DMA((n_rep,)),
        ],
        compiler_params=pltpu.CompilerParams(collective_id=1, has_side_effects=True),
    )(blocks, base)


def gather_kernel(idx_ref, table_t_ref, out_ref):
    step = pl.program_id(0)
    idx = idx_ref[pl.ds(step, 1), :]
    picks = lax.broadcasted_iota(jnp.int32, (table_t_ref.shape[1], idx.shape[1]), 0) == idx
    rows_t = jnp.dot(table_t_ref[...], picks.astype(jnp.bfloat16), preferred_element_type=jnp.float32)
    out_ref[...] = rows_t.T.astype(out_ref.dtype)


def gather_rows(table, idx, chunk=4096):
    count = idx.shape[0]
    idx_lanes = idx.reshape(count // chunk, chunk)
    return pl.pallas_call(
        gather_kernel,
        out_shape=jax.ShapeDtypeStruct((count, table.shape[1]), table.dtype),
        grid=(count // chunk,),
        in_specs=[
            pl.BlockSpec(idx_lanes.shape, lambda i: (0, 0)),
            pl.BlockSpec((table.shape[1], table.shape[0]), lambda i: (0, 0)),
        ],
        out_specs=pl.BlockSpec((chunk, table.shape[1]), lambda i: (i, 0)),
        cost_estimate=pl.CostEstimate(
            flops=2 * count * table.shape[0] * table.shape[1],
            transcendentals=0,
            bytes_accessed=count * 4 + table.size * 2 + count * table.shape[1] * 2,
        ),
    )(idx_lanes, table.T)


def gram_kernel(n_user, per_dev, rows_ref, gw_ref, user_ref, rw_ref, out_ref):
    step = pl.program_id(0)
    width = rows_ref.shape[1]

    @pl.when(step == 0)
    def _():
        out_ref[...] = jnp.zeros_like(out_ref)

    rows = rows_ref[...]
    rows_t = rows.astype(jnp.float32).T
    weights_t = (rows_t * gw_ref[pl.ds(step, 1), :]).astype(jnp.bfloat16)
    users = user_ref[pl.ds(step, 1), :]
    zero = jnp.zeros((), jnp.bfloat16)
    for user in range(n_user):
        picked = jnp.where(users == user, weights_t, zero)
        block, spot = user // per_dev, (user % per_dev) * width
        out_ref[block, spot : spot + width, :] += jnp.dot(
            picked, rows, preferred_element_type=jnp.float32
        )
    slots = lax.broadcasted_iota(jnp.int32, (n_user, users.shape[1]), 0)
    per_user = jnp.where(users == slots, rw_ref[pl.ds(step, 1), :], 0.0)
    high = per_user.astype(jnp.bfloat16)
    low = (per_user - high.astype(jnp.float32)).astype(jnp.bfloat16)
    rhs = jnp.dot(high, rows, preferred_element_type=jnp.float32) + jnp.dot(
        low, rows, preferred_element_type=jnp.float32
    )
    base = per_dev * width
    for block in range(n_user // per_dev):
        out_ref[block, base : base + per_dev, :] += rhs[block * per_dev : (block + 1) * per_dev]


def user_grams(rows, gw_lanes, user_lanes, rw_lanes, n_user, per_dev):
    chunks, chunk = gw_lanes.shape
    width = rows.shape[1]
    n_block = n_user // per_dev
    block_rows = per_dev * width + per_dev
    return pl.pallas_call(
        functools.partial(gram_kernel, n_user, per_dev),
        out_shape=jax.ShapeDtypeStruct((n_block, block_rows, width), jnp.float32),
        grid=(chunks,),
        in_specs=[
            pl.BlockSpec((chunk, width), lambda i: (i, 0)),
            pl.BlockSpec((chunks, chunk), lambda i: (0, 0)),
            pl.BlockSpec((chunks, chunk), lambda i: (0, 0)),
            pl.BlockSpec((chunks, chunk), lambda i: (0, 0)),
        ],
        out_specs=pl.BlockSpec((n_block, block_rows, width), lambda i: (0, 0, 0)),
        cost_estimate=pl.CostEstimate(
            flops=2 * rows.shape[0] * width * width * (n_user + 2),
            transcendentals=0,
            bytes_accessed=rows.size * 2 + 12 * rows.shape[0] + n_user * width * (width + 1) * 4,
        ),
    )(rows, gw_lanes, user_lanes, rw_lanes)

def shards(item_factors, tile_items, send_tiles, tile_users, tile_counts, recv_tiles):
    highest = lax.Precision.HIGHEST
    rank_width = item_factors.shape[1]
    item_count = item_factors.shape[0]
    n_ent = lax.axis_size("ent")
    n_rep = lax.axis_size("rep")
    tile_slots = tile_items.shape[2]
    tile_rows = tile_items.shape[3]
    seg_count = tile_users.shape[3]
    seg_length = tile_rows // seg_count
    slot_cap = tile_slots // n_ent
    user_block = U_DEV * lax.axis_size("rep")
    item_ids = tile_items.reshape(tile_slots, tile_rows)
    slot_pos = jnp.arange(tile_slots, dtype=jnp.int32) % slot_cap
    live_send = slot_pos < jnp.repeat(send_tiles.reshape(n_ent), slot_cap)
    live_recv = slot_pos < jnp.repeat(recv_tiles.reshape(n_ent), slot_cap)
    partial_gram = lax.dot_general(
        item_factors, item_factors, (((0,), (0,)), ((), ())), preferred_element_type=jnp.float32
    )
    live_rows = jnp.repeat(live_send, tile_rows)
    picked = gather_rows(item_factors, jnp.where(live_rows, item_ids.reshape(-1), -1))
    incoming = lax.all_to_all(
        picked.reshape(n_ent, slot_cap * tile_rows, rank_width),
        "ent",
        split_axis=0,
        concat_axis=0,
        tiled=True,
    )
    counts_int = tile_counts.reshape(tile_slots, tile_rows)
    counts_f = counts_int.astype(jnp.float32)
    gram_weight = ALPHA * counts_f
    rhs_weight = jnp.where(
        live_recv[:, None] & (counts_int > 0), 1.0 + ALPHA * counts_f, jnp.float32(0.0)
    )
    owners = tile_users.reshape(tile_slots * seg_count)
    selector = owners[None, :] == jnp.arange(user_block, dtype=jnp.int32)[:, None]
    selector_f = selector.astype(jnp.float32)
    rows_all = incoming.reshape(tile_slots * tile_rows, rank_width)
    lane_chunk = 2048
    row_owner = jnp.repeat(owners, seg_length)
    gram_blocks = user_grams(
        rows_all,
        gram_weight.reshape(-1, lane_chunk),
        row_owner.reshape(-1, lane_chunk),
        rhs_weight.reshape(-1, lane_chunk),
        user_block,
        U_DEV,
    )
    identity_mat = jnp.eye(rank_width, dtype=jnp.float32)
    added_term = tree_sum(partial_gram, n_ent * n_rep) + RIDGE * identity_mat
    solved, own_factors = solve_owned(gram_blocks, added_term, n_rep, U_DEV)
    solved = solved.reshape(user_block, rank_width)
    run_factor = lax.dot_general(
        selector.astype(jnp.bfloat16),
        solved,
        (((0,), (0,)), ((), ())),
        preferred_element_type=jnp.float32,
    ).astype(jnp.bfloat16)
    back_load = jnp.concatenate(
        [
            run_factor.reshape(tile_slots, seg_count * rank_width),
            counts_int.astype(jnp.bfloat16),
        ],
        axis=1,
    )
    back_load = lax.all_to_all(
        back_load.reshape(n_ent, slot_cap, -1), "ent", split_axis=0, concat_axis=0, tiled=True
    ).reshape(tile_slots, -1)
    back_factor = back_load[:, : seg_count * rank_width]
    back_counts = back_load[:, seg_count * rank_width :].astype(jnp.float32)
    back_weight = jnp.where(
        live_send[:, None] & (back_counts > 0), 1.0 + ALPHA * back_counts, jnp.float32(0.0)
    )
    item_hot = item_ids[:, :, None] == jnp.arange(item_count, dtype=jnp.int32)[None, None, :]
    run_weight = back_weight.reshape(tile_slots * seg_count, seg_length)
    hot_runs = item_hot.reshape(tile_slots * seg_count, seg_length, item_count)
    spread_mat = jnp.sum(jnp.where(hot_runs, run_weight[:, :, None], 0.0), axis=1)
    item_rhs = lax.dot_general(
        spread_mat,
        back_factor.reshape(tile_slots * seg_count, rank_width).astype(jnp.float32),
        (((0,), (0,)), ((), ())),
        precision=highest,
        preferred_element_type=jnp.float32,
    )
    return (own_factors, item_rhs * RHS_SCALE)


def solution(mesh):
    in_specs = (
        P(("ent", "rep"), None),
        P("ent", "rep", None, None),
        P("ent", "rep", None),
        P("ent", "rep", None, None),
        P("ent", "rep", None, None),
        P("ent", "rep", None),
    )
    out_specs = (P(("ent", "rep"), None), P(("ent", "rep"), None))
    return jax.shard_map(shards, mesh=mesh, in_specs=in_specs, out_specs=out_specs, check_vma=False)
```

```python
import functools

import jax
import jax.numpy as jnp
from jax import lax
from jax.experimental import pallas as pl
from jax.experimental.pallas import tpu as pltpu
from jax.sharding import PartitionSpec as P

MESH_ID = pl.DeviceIdType.MESH

U_DEV = 2


ALPHA = 40.0
RIDGE = 1.0
RHS_SCALE = 1.0 / 640.0


def cholesky_solve(a_s, l_s, y_s, out_ref):
    batch, n, _ = a_s.shape
    out_ref[...] = jnp.zeros_like(out_ref)
    lane_v = lax.broadcasted_iota(jnp.int32, (1, n), 1)

    def factor(top, j, carry):
        span = n - top
        lane_m = lax.broadcasted_iota(jnp.int32, (span, n), 1)
        sub_m = lax.broadcasted_iota(jnp.int32, (span, n), 0) + top
        sub_v = lax.broadcasted_iota(jnp.int32, (span, 1), 0) + top
        for b in range(batch):
            a = a_s[b, top:, :]
            row = jnp.sum(jnp.where(sub_m == j, a, 0.0), axis=0, keepdims=True)
            col = jnp.sum(jnp.where(lane_m == j, a, 0.0), axis=1, keepdims=True)
            diag = jnp.sum(jnp.where(lane_v == j, row, 0.0), axis=1, keepdims=True)
            inv = 1.0 / jnp.sqrt(diag)
            l_row = jnp.where(lane_v >= j, row, 0.0) * inv
            l_col = jnp.where(sub_v >= j, col, 0.0) * inv
            a_s[b, top:, :] = a - l_col * l_row
            l_s[b, pl.ds(j, 1), :] = l_row
            y = y_s[pl.ds(b, 1), :]
            y_j = jnp.sum(jnp.where(lane_v == j, y, 0.0), axis=1, keepdims=True) * inv
            y_s[pl.ds(b, 1), :] = jnp.where(lane_v == j, y_j, y - y_j * l_row)
        return carry

    parts = 8
    quarter = n // parts
    for part in range(parts):
        top = part * quarter
        lax.fori_loop(top, top + quarter, functools.partial(factor, top), 0, unroll=2)

    def back(t, carry):
        j = n - 1 - t
        for b in range(batch):
            l_j = l_s[b, pl.ds(j, 1), :]
            x = out_ref[pl.ds(b, 1), :]
            y_j = jnp.sum(jnp.where(lane_v == j, y_s[pl.ds(b, 1), :], 0.0), axis=1, keepdims=True)
            l_jj = jnp.sum(jnp.where(lane_v == j, l_j, 0.0), axis=1, keepdims=True)
            known = jnp.sum(jnp.where(lane_v > j, l_j * x, 0.0), axis=1, keepdims=True)
            out_ref[pl.ds(b, 1), :] = jnp.where(lane_v == j, (y_j - known) / l_jj, x)
        return carry

    lax.fori_loop(0, n, back, 0, unroll=2)


def flip_bits(value, mask, bits):
    out = value - value % (1 << bits)
    for bit in range(bits):
        here = (value // (1 << bit)) % 2
        out = out + (1 << bit) * ((1 - here) if (mask >> bit) & 1 else here)
    return out


def doubling_kernel(
    n_rep, low_bits, rounds, x_ref, o_ref, full_recv, piece_recv, piece, gath,
    sem_a, sem_b, sem_c, sem_d, sem_e, sem_f,
):
    flat = lax.axis_index("ent") * n_rep + lax.axis_index("rep")
    group = 1 << low_bits
    rows = x_ref.shape[0] // group
    slot = flat % group

    def place(p):
        return (p // n_rep, p % n_rep)

    def flip(bit):
        step = 1 << bit
        upper = (flat // step) % 2
        return flat + step - 2 * step * upper

    members = [flip_bits(flat, k, low_bits) for k in range(1, group)]
    outer = [flip(bit) for bit in range(low_bits, rounds)]
    barrier = pltpu.get_barrier_semaphore()
    for p in members + outer:
        pl.semaphore_signal(barrier, inc=1, device_id=place(p), device_id_type=MESH_ID)
    pl.semaphore_wait(barrier, len(members) + len(outer))

    o_ref[...] = x_ref[...]
    for bit in range(low_bits):
        copy = pltpu.make_async_remote_copy(
            src_ref=o_ref, dst_ref=full_recv.at[bit], send_sem=sem_a.at[bit],
            recv_sem=sem_b.at[bit], device_id=place(flip(bit)), device_id_type=MESH_ID,
        )
        copy.start()
        copy.wait_recv()
        copy.wait_send()
        o_ref[...] = o_ref[...] + full_recv[bit]

    piece[...] = o_ref[pl.ds(pl.multiple_of(slot * rows, rows), rows), :]
    for index, p in enumerate(outer):
        copy = pltpu.make_async_remote_copy(
            src_ref=piece, dst_ref=piece_recv.at[index], send_sem=sem_c.at[index],
            recv_sem=sem_d.at[index], device_id=place(p), device_id_type=MESH_ID,
        )
        copy.start()
        copy.wait_recv()
        copy.wait_send()
        piece[...] = piece[...] + piece_recv[index]

    gath[slot] = piece[...]
    sends = []
    for index, p in enumerate(members):
        copy = pltpu.make_async_remote_copy(
            src_ref=piece, dst_ref=gath.at[slot], send_sem=sem_e.at[index],
            recv_sem=sem_f.at[slot], device_id=place(p), device_id_type=MESH_ID,
        )
        copy.start()
        sends.append(copy)
    for k in range(1, group):
        source = flip_bits(slot, k, low_bits)
        pltpu.make_async_remote_copy(
            src_ref=piece, dst_ref=gath.at[source], send_sem=sem_e.at[k - 1],
            recv_sem=sem_f.at[source], device_id=place(members[k - 1]), device_id_type=MESH_ID,
        ).wait_recv()
    for copy in sends:
        copy.wait_send()
    for part in range(group):
        o_ref[pl.ds(part * rows, rows), :] = gath[part]


def tree_sum(value, count):
    rounds = count.bit_length() - 1
    n_rep = lax.axis_size("rep")
    low_bits = (n_rep * 2).bit_length() - 1
    group = 1 << low_bits
    rows = value.shape[0] // group
    outer = rounds - low_bits
    return pl.pallas_call(
        functools.partial(doubling_kernel, n_rep, low_bits, rounds),
        out_shape=jax.ShapeDtypeStruct(value.shape, value.dtype),
        in_specs=[pl.BlockSpec(memory_space=pltpu.VMEM)],
        out_specs=pl.BlockSpec(memory_space=pltpu.VMEM),
        scratch_shapes=[
            pltpu.VMEM((low_bits,) + value.shape, value.dtype),
            pltpu.VMEM((outer, rows, value.shape[1]), value.dtype),
            pltpu.VMEM((rows, value.shape[1]), value.dtype),
            pltpu.VMEM((group, rows, value.shape[1]), value.dtype),
            pltpu.SemaphoreType.DMA((low_bits,)),
            pltpu.SemaphoreType.DMA((low_bits,)),
            pltpu.SemaphoreType.DMA((outer,)),
            pltpu.SemaphoreType.DMA((outer,)),
            pltpu.SemaphoreType.DMA((group - 1,)),
            pltpu.SemaphoreType.DMA((group,)),
        ],
        compiler_params=pltpu.CompilerParams(collective_id=0, has_side_effects=True),
    )(value)


def rep_peers(n_rep):
    me = lax.axis_index("rep")
    return me, [(me + shift) % n_rep for shift in range(1, n_rep)]


def owner_kernel(n_rep, blocks_ref, base_ref, out_ref, x_s, recv, a_s, l_s, y_s, fac, gath,
                 sem_a, sem_b, sem_c, sem_d):
    me, peers = rep_peers(n_rep)
    ent = lax.axis_index("ent")
    batch, n, _ = a_s.shape
    barrier = pltpu.get_barrier_semaphore()
    for peer in peers:
        pl.semaphore_signal(barrier, inc=1, device_id=(ent, peer), device_id_type=MESH_ID)
    pl.semaphore_wait(barrier, n_rep - 1)
    copies = []
    for index, peer in enumerate(peers):
        copy = pltpu.make_async_remote_copy(
            src_ref=blocks_ref.at[peer], dst_ref=recv.at[index], send_sem=sem_a.at[index],
            recv_sem=sem_b.at[index], device_id=(ent, peer), device_id_type=MESH_ID,
        )
        copy.start()
        copies.append(copy)
    total = blocks_ref[me]
    for index, copy in enumerate(copies):
        copy.wait_recv()
        total = total + recv[index]
    for copy in copies:
        copy.wait_send()
    base = base_ref[...]
    for b in range(batch):
        gram = total[b * n : (b + 1) * n] + base
        a_s[b] = (gram + gram.T) / 2
    y_s[...] = total[batch * n : batch * n + batch]
    cholesky_solve(a_s, l_s, y_s, x_s)
    fac[...] = x_s[...].astype(fac.dtype)
    gath[me] = fac[...]
    sends = []
    for index, peer in enumerate(peers):
        copy = pltpu.make_async_remote_copy(
            src_ref=fac, dst_ref=gath.at[me], send_sem=sem_c.at[index],
            recv_sem=sem_d.at[me], device_id=(ent, peer), device_id_type=MESH_ID,
        )
        copy.start()
        sends.append(copy)
    for index, source in enumerate(peers):
        pltpu.make_async_remote_copy(
            src_ref=fac, dst_ref=gath.at[source], send_sem=sem_c.at[index],
            recv_sem=sem_d.at[source], device_id=(ent, source), device_id_type=MESH_ID,
        ).wait_recv()
    for copy in sends:
        copy.wait_send()
    out_ref[...] = gath[...]


def solve_owned(blocks, base, n_rep, per_dev):
    n = blocks.shape[2]
    return pl.pallas_call(
        functools.partial(owner_kernel, n_rep),
        out_shape=(
            jax.ShapeDtypeStruct((n_rep, per_dev, n), jnp.bfloat16),
            jax.ShapeDtypeStruct((per_dev, n), jnp.float32),
        ),
        in_specs=[pl.BlockSpec(memory_space=pltpu.VMEM)] * 2,
        out_specs=(pl.BlockSpec(memory_space=pltpu.VMEM), pl.BlockSpec(memory_space=pltpu.VMEM)),
        scratch_shapes=[
            pltpu.VMEM((n_rep - 1,) + blocks.shape[1:], jnp.float32),
            pltpu.VMEM((per_dev, n, n), jnp.float32),
            pltpu.VMEM((per_dev, n, n), jnp.float32),
            pltpu.VMEM((per_dev, n), jnp.float32),
            pltpu.VMEM((per_dev, n), jnp.bfloat16),
            pltpu.VMEM((n_rep, per_dev, n), jnp.bfloat16),
            pltpu.SemaphoreType.DMA((n_rep - 1,)),
            pltpu.SemaphoreType.DMA((n_rep - 1,)),
            pltpu.SemaphoreType.DMA((n_rep - 1,)),
            pltpu.SemaphoreType.DMA((n_rep,)),
        ],
        compiler_params=pltpu.CompilerParams(collective_id=1, has_side_effects=True),
    )(blocks, base)


def gather_kernel(idx_ref, table_t_ref, out_ref):
    step = pl.program_id(0)
    idx = idx_ref[pl.ds(step, 1), :]
    picks = lax.broadcasted_iota(jnp.int32, (table_t_ref.shape[1], idx.shape[1]), 0) == idx
    rows_t = jnp.dot(table_t_ref[...], picks.astype(jnp.bfloat16), preferred_element_type=jnp.float32)
    out_ref[...] = rows_t.T.astype(out_ref.dtype)


def gather_rows(table, idx, chunk=4096):
    count = idx.shape[0]
    idx_lanes = idx.reshape(count // chunk, chunk)
    return pl.pallas_call(
        gather_kernel,
        out_shape=jax.ShapeDtypeStruct((count, table.shape[1]), table.dtype),
        grid=(count // chunk,),
        in_specs=[
            pl.BlockSpec(idx_lanes.shape, lambda i: (0, 0)),
            pl.BlockSpec((table.shape[1], table.shape[0]), lambda i: (0, 0)),
        ],
        out_specs=pl.BlockSpec((chunk, table.shape[1]), lambda i: (i, 0)),
        cost_estimate=pl.CostEstimate(
            flops=2 * count * table.shape[0] * table.shape[1],
            transcendentals=0,
            bytes_accessed=count * 4 + table.size * 2 + count * table.shape[1] * 2,
        ),
    )(idx_lanes, table.T)


def gram_kernel(n_user, per_dev, rows_ref, gw_ref, user_ref, rw_ref, out_ref):
    step = pl.program_id(0)
    width = rows_ref.shape[1]

    @pl.when(step == 0)
    def _():
        out_ref[...] = jnp.zeros_like(out_ref)

    rows = rows_ref[...]
    rows_t = rows.astype(jnp.float32).T
    weights_t = (rows_t * gw_ref[pl.ds(step, 1), :]).astype(jnp.bfloat16)
    users = user_ref[pl.ds(step, 1), :]
    zero = jnp.zeros((), jnp.bfloat16)
    for user in range(n_user):
        picked = jnp.where(users == user, weights_t, zero)
        block, spot = user // per_dev, (user % per_dev) * width
        out_ref[block, spot : spot + width, :] += jnp.dot(
            picked, rows, preferred_element_type=jnp.float32
        )
    slots = lax.broadcasted_iota(jnp.int32, (n_user, users.shape[1]), 0)
    per_user = jnp.where(users == slots, rw_ref[pl.ds(step, 1), :], 0.0)
    high = per_user.astype(jnp.bfloat16)
    low = (per_user - high.astype(jnp.float32)).astype(jnp.bfloat16)
    rhs = jnp.dot(high, rows, preferred_element_type=jnp.float32) + jnp.dot(
        low, rows, preferred_element_type=jnp.float32
    )
    base = per_dev * width
    for block in range(n_user // per_dev):
        out_ref[block, base : base + per_dev, :] += rhs[block * per_dev : (block + 1) * per_dev]


def user_grams(rows, gw_lanes, user_lanes, rw_lanes, n_user, per_dev):
    chunks, chunk = gw_lanes.shape
    width = rows.shape[1]
    n_block = n_user // per_dev
    block_rows = per_dev * width + per_dev
    return pl.pallas_call(
        functools.partial(gram_kernel, n_user, per_dev),
        out_shape=jax.ShapeDtypeStruct((n_block, block_rows, width), jnp.float32),
        grid=(chunks,),
        in_specs=[
            pl.BlockSpec((chunk, width), lambda i: (i, 0)),
            pl.BlockSpec((chunks, chunk), lambda i: (0, 0)),
            pl.BlockSpec((chunks, chunk), lambda i: (0, 0)),
            pl.BlockSpec((chunks, chunk), lambda i: (0, 0)),
        ],
        out_specs=pl.BlockSpec((n_block, block_rows, width), lambda i: (0, 0, 0)),
        cost_estimate=pl.CostEstimate(
            flops=2 * rows.shape[0] * width * width * (n_user + 2),
            transcendentals=0,
            bytes_accessed=rows.size * 2 + 12 * rows.shape[0] + n_user * width * (width + 1) * 4,
        ),
    )(rows, gw_lanes, user_lanes, rw_lanes)

def shards(item_factors, tile_items, send_tiles, tile_users, tile_counts, recv_tiles):
    highest = lax.Precision.HIGHEST
    rank_width = item_factors.shape[1]
    item_count = item_factors.shape[0]
    n_ent = lax.axis_size("ent")
    n_rep = lax.axis_size("rep")
    tile_slots = tile_items.shape[2]
    tile_rows = tile_items.shape[3]
    seg_count = tile_users.shape[3]
    seg_length = tile_rows // seg_count
    slot_cap = tile_slots // n_ent
    user_block = U_DEV * lax.axis_size("rep")
    item_ids = tile_items.reshape(tile_slots, tile_rows)
    slot_pos = jnp.arange(tile_slots, dtype=jnp.int32) % slot_cap
    live_send = slot_pos < jnp.repeat(send_tiles.reshape(n_ent), slot_cap)
    live_recv = slot_pos < jnp.repeat(recv_tiles.reshape(n_ent), slot_cap)
    partial_gram = lax.dot_general(
        item_factors, item_factors, (((0,), (0,)), ((), ())), preferred_element_type=jnp.float32
    )
    live_rows = jnp.repeat(live_send, tile_rows)
    picked = gather_rows(item_factors, jnp.where(live_rows, item_ids.reshape(-1), -1))
    incoming = lax.all_to_all(
        picked.reshape(n_ent, slot_cap * tile_rows, rank_width),
        "ent",
        split_axis=0,
        concat_axis=0,
        tiled=True,
    )
    counts_int = tile_counts.reshape(tile_slots, tile_rows)
    counts_f = counts_int.astype(jnp.float32)
    gram_weight = ALPHA * counts_f
    rhs_weight = jnp.where(
        live_recv[:, None] & (counts_int > 0), 1.0 + ALPHA * counts_f, jnp.float32(0.0)
    )
    owners = tile_users.reshape(tile_slots * seg_count)
    selector = owners[None, :] == jnp.arange(user_block, dtype=jnp.int32)[:, None]
    selector_f = selector.astype(jnp.float32)
    rows_all = incoming.reshape(tile_slots * tile_rows, rank_width)
    lane_chunk = 2048
    row_owner = jnp.repeat(owners, seg_length)
    gram_blocks = user_grams(
        rows_all,
        gram_weight.reshape(-1, lane_chunk),
        row_owner.reshape(-1, lane_chunk),
        rhs_weight.reshape(-1, lane_chunk),
        user_block,
        U_DEV,
    )
    identity_mat = jnp.eye(rank_width, dtype=jnp.float32)
    added_term = tree_sum(partial_gram, n_ent * n_rep) + RIDGE * identity_mat
    solved, own_factors = solve_owned(gram_blocks, added_term, n_rep, U_DEV)
    solved = solved.reshape(user_block, rank_width)
    run_factor = lax.dot_general(
        selector.astype(jnp.bfloat16),
        solved,
        (((0,), (0,)), ((), ())),
        preferred_element_type=jnp.float32,
    ).astype(jnp.bfloat16)
    back_load = jnp.concatenate(
        [
            run_factor.reshape(tile_slots, seg_count * rank_width),
            counts_int.astype(jnp.bfloat16),
        ],
        axis=1,
    )
    back_load = lax.all_to_all(
        back_load.reshape(n_ent, slot_cap, -1), "ent", split_axis=0, concat_axis=0, tiled=True
    ).reshape(tile_slots, -1)
    back_factor = back_load[:, : seg_count * rank_width]
    back_counts = back_load[:, seg_count * rank_width :].astype(jnp.float32)
    back_weight = jnp.where(
        live_send[:, None] & (back_counts > 0), 1.0 + ALPHA * back_counts, jnp.float32(0.0)
    )
    item_hot = item_ids[:, :, None] == jnp.arange(item_count, dtype=jnp.int32)[None, None, :]
    run_weight = back_weight.reshape(tile_slots * seg_count, seg_length)
    hot_runs = item_hot.reshape(tile_slots * seg_count, seg_length, item_count)
    spread_mat = jnp.sum(jnp.where(hot_runs, run_weight[:, :, None], 0.0), axis=1)
    item_rhs = lax.dot_general(
        spread_mat,
        back_factor.reshape(tile_slots * seg_count, rank_width).astype(jnp.float32),
        (((0,), (0,)), ((), ())),
        precision=highest,
        preferred_element_type=jnp.float32,
    )
    return (own_factors, item_rhs * RHS_SCALE)


def solution(mesh):
    in_specs = (
        P(("ent", "rep"), None),
        P("ent", "rep", None, None),
        P("ent", "rep", None),
        P("ent", "rep", None, None),
        P("ent", "rep", None, None),
        P("ent", "rep", None),
    )
    out_specs = (P(("ent", "rep"), None), P(("ent", "rep"), None))
    return jax.shard_map(shards, mesh=mesh, in_specs=in_specs, out_specs=out_specs, check_vma=False)
```

```python
import functools

import jax
import jax.numpy as jnp
from jax import lax
from jax.experimental import pallas as pl
from jax.experimental.pallas import tpu as pltpu
from jax.sharding import PartitionSpec as P

MESH_ID = pl.DeviceIdType.MESH

U_DEV = 2


ALPHA = 40.0
RIDGE = 1.0
RHS_SCALE = 1.0 / 640.0


def cholesky_solve(a_s, l_s, y_s, out_ref):
    batch, n, _ = a_s.shape
    out_ref[...] = jnp.zeros_like(out_ref)
    lane_v = lax.broadcasted_iota(jnp.int32, (1, n), 1)

    def factor(top, j, carry):
        span = n - top
        lane_m = lax.broadcasted_iota(jnp.int32, (span, n), 1)
        sub_m = lax.broadcasted_iota(jnp.int32, (span, n), 0) + top
        sub_v = lax.broadcasted_iota(jnp.int32, (span, 1), 0) + top
        for b in range(batch):
            a = a_s[b, top:, :]
            row = jnp.sum(jnp.where(sub_m == j, a, 0.0), axis=0, keepdims=True)
            col = jnp.sum(jnp.where(lane_m == j, a, 0.0), axis=1, keepdims=True)
            diag = jnp.sum(jnp.where(lane_v == j, row, 0.0), axis=1, keepdims=True)
            inv = 1.0 / jnp.sqrt(diag)
            l_row = jnp.where(lane_v >= j, row, 0.0) * inv
            l_col = jnp.where(sub_v >= j, col, 0.0) * inv
            a_s[b, top:, :] = a - l_col * l_row
            l_s[b, pl.ds(j, 1), :] = l_row
            y = y_s[pl.ds(b, 1), :]
            y_j = jnp.sum(jnp.where(lane_v == j, y, 0.0), axis=1, keepdims=True) * inv
            y_s[pl.ds(b, 1), :] = jnp.where(lane_v == j, y_j, y - y_j * l_row)
        return carry

    quarter = n // 4
    for part in range(4):
        top = part * quarter
        lax.fori_loop(top, top + quarter, functools.partial(factor, top), 0, unroll=2)

    def back(t, carry):
        j = n - 1 - t
        for b in range(batch):
            l_j = l_s[b, pl.ds(j, 1), :]
            x = out_ref[pl.ds(b, 1), :]
            y_j = jnp.sum(jnp.where(lane_v == j, y_s[pl.ds(b, 1), :], 0.0), axis=1, keepdims=True)
            l_jj = jnp.sum(jnp.where(lane_v == j, l_j, 0.0), axis=1, keepdims=True)
            known = jnp.sum(jnp.where(lane_v > j, l_j * x, 0.0), axis=1, keepdims=True)
            out_ref[pl.ds(b, 1), :] = jnp.where(lane_v == j, (y_j - known) / l_jj, x)
        return carry

    lax.fori_loop(0, n, back, 0, unroll=2)


def flip_bits(value, mask, bits):
    out = value - value % (1 << bits)
    for bit in range(bits):
        here = (value // (1 << bit)) % 2
        out = out + (1 << bit) * ((1 - here) if (mask >> bit) & 1 else here)
    return out


def doubling_kernel(
    n_rep, low_bits, rounds, x_ref, o_ref, full_recv, piece_recv, piece, gath,
    sem_a, sem_b, sem_c, sem_d, sem_e, sem_f,
):
    flat = lax.axis_index("ent") * n_rep + lax.axis_index("rep")
    group = 1 << low_bits
    rows = x_ref.shape[0] // group
    slot = flat % group

    def place(p):
        return (p // n_rep, p % n_rep)

    def flip(bit):
        step = 1 << bit
        upper = (flat // step) % 2
        return flat + step - 2 * step * upper

    members = [flip_bits(flat, k, low_bits) for k in range(1, group)]
    outer = [flip(bit) for bit in range(low_bits, rounds)]
    barrier = pltpu.get_barrier_semaphore()
    for p in members + outer:
        pl.semaphore_signal(barrier, inc=1, device_id=place(p), device_id_type=MESH_ID)
    pl.semaphore_wait(barrier, len(members) + len(outer))

    o_ref[...] = x_ref[...]
    for bit in range(low_bits):
        copy = pltpu.make_async_remote_copy(
            src_ref=o_ref, dst_ref=full_recv.at[bit], send_sem=sem_a.at[bit],
            recv_sem=sem_b.at[bit], device_id=place(flip(bit)), device_id_type=MESH_ID,
        )
        copy.start()
        copy.wait_recv()
        copy.wait_send()
        o_ref[...] = o_ref[...] + full_recv[bit]

    piece[...] = o_ref[pl.ds(pl.multiple_of(slot * rows, rows), rows), :]
    for index, p in enumerate(outer):
        copy = pltpu.make_async_remote_copy(
            src_ref=piece, dst_ref=piece_recv.at[index], send_sem=sem_c.at[index],
            recv_sem=sem_d.at[index], device_id=place(p), device_id_type=MESH_ID,
        )
        copy.start()
        copy.wait_recv()
        copy.wait_send()
        piece[...] = piece[...] + piece_recv[index]

    gath[slot] = piece[...]
    sends = []
    for index, p in enumerate(members):
        copy = pltpu.make_async_remote_copy(
            src_ref=piece, dst_ref=gath.at[slot], send_sem=sem_e.at[index],
            recv_sem=sem_f.at[slot], device_id=place(p), device_id_type=MESH_ID,
        )
        copy.start()
        sends.append(copy)
    for k in range(1, group):
        source = flip_bits(slot, k, low_bits)
        pltpu.make_async_remote_copy(
            src_ref=piece, dst_ref=gath.at[source], send_sem=sem_e.at[k - 1],
            recv_sem=sem_f.at[source], device_id=place(members[k - 1]), device_id_type=MESH_ID,
        ).wait_recv()
    for copy in sends:
        copy.wait_send()
    for part in range(group):
        o_ref[pl.ds(part * rows, rows), :] = gath[part]


def tree_sum(value, count):
    rounds = count.bit_length() - 1
    n_rep = lax.axis_size("rep")
    low_bits = (n_rep * 2).bit_length() - 1
    group = 1 << low_bits
    rows = value.shape[0] // group
    outer = rounds - low_bits
    return pl.pallas_call(
        functools.partial(doubling_kernel, n_rep, low_bits, rounds),
        out_shape=jax.ShapeDtypeStruct(value.shape, value.dtype),
        in_specs=[pl.BlockSpec(memory_space=pltpu.VMEM)],
        out_specs=pl.BlockSpec(memory_space=pltpu.VMEM),
        scratch_shapes=[
            pltpu.VMEM((low_bits,) + value.shape, value.dtype),
            pltpu.VMEM((outer, rows, value.shape[1]), value.dtype),
            pltpu.VMEM((rows, value.shape[1]), value.dtype),
            pltpu.VMEM((group, rows, value.shape[1]), value.dtype),
            pltpu.SemaphoreType.DMA((low_bits,)),
            pltpu.SemaphoreType.DMA((low_bits,)),
            pltpu.SemaphoreType.DMA((outer,)),
            pltpu.SemaphoreType.DMA((outer,)),
            pltpu.SemaphoreType.DMA((group - 1,)),
            pltpu.SemaphoreType.DMA((group,)),
        ],
        compiler_params=pltpu.CompilerParams(collective_id=0, has_side_effects=True),
    )(value)


def rep_peers(n_rep):
    me = lax.axis_index("rep")
    return me, [(me + shift) % n_rep for shift in range(1, n_rep)]


def owner_kernel(n_rep, blocks_ref, base_ref, out_ref, x_s, recv, a_s, l_s, y_s, fac, gath,
                 sem_a, sem_b, sem_c, sem_d):
    me, peers = rep_peers(n_rep)
    ent = lax.axis_index("ent")
    batch, n, _ = a_s.shape
    barrier = pltpu.get_barrier_semaphore()
    for peer in peers:
        pl.semaphore_signal(barrier, inc=1, device_id=(ent, peer), device_id_type=MESH_ID)
    pl.semaphore_wait(barrier, n_rep - 1)
    copies = []
    for index, peer in enumerate(peers):
        copy = pltpu.make_async_remote_copy(
            src_ref=blocks_ref.at[peer], dst_ref=recv.at[index], send_sem=sem_a.at[index],
            recv_sem=sem_b.at[index], device_id=(ent, peer), device_id_type=MESH_ID,
        )
        copy.start()
        copies.append(copy)
    total = blocks_ref[me]
    for index, copy in enumerate(copies):
        copy.wait_recv()
        total = total + recv[index]
    for copy in copies:
        copy.wait_send()
    base = base_ref[...]
    for b in range(batch):
        gram = total[b * n : (b + 1) * n] + base
        a_s[b] = (gram + gram.T) / 2
    y_s[...] = total[batch * n : batch * n + batch]
    cholesky_solve(a_s, l_s, y_s, x_s)
    fac[...] = x_s[...].astype(fac.dtype)
    gath[me] = fac[...]
    sends = []
    for index, peer in enumerate(peers):
        copy = pltpu.make_async_remote_copy(
            src_ref=fac, dst_ref=gath.at[me], send_sem=sem_c.at[index],
            recv_sem=sem_d.at[me], device_id=(ent, peer), device_id_type=MESH_ID,
        )
        copy.start()
        sends.append(copy)
    for index, source in enumerate(peers):
        pltpu.make_async_remote_copy(
            src_ref=fac, dst_ref=gath.at[source], send_sem=sem_c.at[index],
            recv_sem=sem_d.at[source], device_id=(ent, source), device_id_type=MESH_ID,
        ).wait_recv()
    for copy in sends:
        copy.wait_send()
    out_ref[...] = gath[...]


def solve_owned(blocks, base, n_rep, per_dev):
    n = blocks.shape[2]
    return pl.pallas_call(
        functools.partial(owner_kernel, n_rep),
        out_shape=(
            jax.ShapeDtypeStruct((n_rep, per_dev, n), jnp.bfloat16),
            jax.ShapeDtypeStruct((per_dev, n), jnp.float32),
        ),
        in_specs=[pl.BlockSpec(memory_space=pltpu.VMEM)] * 2,
        out_specs=(pl.BlockSpec(memory_space=pltpu.VMEM), pl.BlockSpec(memory_space=pltpu.VMEM)),
        scratch_shapes=[
            pltpu.VMEM((n_rep - 1,) + blocks.shape[1:], jnp.float32),
            pltpu.VMEM((per_dev, n, n), jnp.float32),
            pltpu.VMEM((per_dev, n, n), jnp.float32),
            pltpu.VMEM((per_dev, n), jnp.float32),
            pltpu.VMEM((per_dev, n), jnp.bfloat16),
            pltpu.VMEM((n_rep, per_dev, n), jnp.bfloat16),
            pltpu.SemaphoreType.DMA((n_rep - 1,)),
            pltpu.SemaphoreType.DMA((n_rep - 1,)),
            pltpu.SemaphoreType.DMA((n_rep - 1,)),
            pltpu.SemaphoreType.DMA((n_rep,)),
        ],
        compiler_params=pltpu.CompilerParams(collective_id=1, has_side_effects=True),
    )(blocks, base)


def gather_kernel(idx_ref, table_t_ref, out_ref):
    step = pl.program_id(0)
    idx = idx_ref[pl.ds(step, 1), :]
    picks = lax.broadcasted_iota(jnp.int32, (table_t_ref.shape[1], idx.shape[1]), 0) == idx
    rows_t = jnp.dot(table_t_ref[...], picks.astype(jnp.bfloat16), preferred_element_type=jnp.float32)
    out_ref[...] = rows_t.T.astype(out_ref.dtype)


def gather_rows(table, idx, chunk=4096):
    count = idx.shape[0]
    idx_lanes = idx.reshape(count // chunk, chunk)
    return pl.pallas_call(
        gather_kernel,
        out_shape=jax.ShapeDtypeStruct((count, table.shape[1]), table.dtype),
        grid=(count // chunk,),
        in_specs=[
            pl.BlockSpec(idx_lanes.shape, lambda i: (0, 0)),
            pl.BlockSpec((table.shape[1], table.shape[0]), lambda i: (0, 0)),
        ],
        out_specs=pl.BlockSpec((chunk, table.shape[1]), lambda i: (i, 0)),
        cost_estimate=pl.CostEstimate(
            flops=2 * count * table.shape[0] * table.shape[1],
            transcendentals=0,
            bytes_accessed=count * 4 + table.size * 2 + count * table.shape[1] * 2,
        ),
    )(idx_lanes, table.T)


def gram_kernel(n_user, per_dev, rows_ref, gw_ref, user_ref, rw_ref, out_ref):
    step = pl.program_id(0)
    width = rows_ref.shape[1]

    @pl.when(step == 0)
    def _():
        out_ref[...] = jnp.zeros_like(out_ref)

    rows = rows_ref[...]
    rows_t = rows.astype(jnp.float32).T
    weights_t = (rows_t * gw_ref[pl.ds(step, 1), :]).astype(jnp.bfloat16)
    users = user_ref[pl.ds(step, 1), :]
    zero = jnp.zeros((), jnp.bfloat16)
    picked = jnp.concatenate(
        [jnp.where(users == user, weights_t, zero) for user in range(n_user)], axis=0
    )
    grams = jnp.dot(picked, rows, preferred_element_type=jnp.float32)
    for user in range(n_user):
        block, spot = user // per_dev, (user % per_dev) * width
        out_ref[block, spot : spot + width, :] += grams[user * width : (user + 1) * width]
    slots = lax.broadcasted_iota(jnp.int32, (n_user, users.shape[1]), 0)
    per_user = jnp.where(users == slots, rw_ref[pl.ds(step, 1), :], 0.0)
    high = per_user.astype(jnp.bfloat16)
    low = (per_user - high.astype(jnp.float32)).astype(jnp.bfloat16)
    rhs = jnp.dot(high, rows, preferred_element_type=jnp.float32) + jnp.dot(
        low, rows, preferred_element_type=jnp.float32
    )
    base = per_dev * width
    for block in range(n_user // per_dev):
        out_ref[block, base : base + per_dev, :] += rhs[block * per_dev : (block + 1) * per_dev]


def user_grams(rows, gw_lanes, user_lanes, rw_lanes, n_user, per_dev):
    chunks, chunk = gw_lanes.shape
    width = rows.shape[1]
    n_block = n_user // per_dev
    block_rows = per_dev * width + per_dev
    return pl.pallas_call(
        functools.partial(gram_kernel, n_user, per_dev),
        out_shape=jax.ShapeDtypeStruct((n_block, block_rows, width), jnp.float32),
        grid=(chunks,),
        in_specs=[
            pl.BlockSpec((chunk, width), lambda i: (i, 0)),
            pl.BlockSpec((chunks, chunk), lambda i: (0, 0)),
            pl.BlockSpec((chunks, chunk), lambda i: (0, 0)),
            pl.BlockSpec((chunks, chunk), lambda i: (0, 0)),
        ],
        out_specs=pl.BlockSpec((n_block, block_rows, width), lambda i: (0, 0, 0)),
        cost_estimate=pl.CostEstimate(
            flops=2 * rows.shape[0] * width * width * (n_user + 2),
            transcendentals=0,
            bytes_accessed=rows.size * 2 + 12 * rows.shape[0] + n_user * width * (width + 1) * 4,
        ),
    )(rows, gw_lanes, user_lanes, rw_lanes)

def shards(item_factors, tile_items, send_tiles, tile_users, tile_counts, recv_tiles):
    highest = lax.Precision.HIGHEST
    rank_width = item_factors.shape[1]
    item_count = item_factors.shape[0]
    n_ent = lax.axis_size("ent")
    n_rep = lax.axis_size("rep")
    tile_slots = tile_items.shape[2]
    tile_rows = tile_items.shape[3]
    seg_count = tile_users.shape[3]
    seg_length = tile_rows // seg_count
    slot_cap = tile_slots // n_ent
    user_block = U_DEV * lax.axis_size("rep")
    item_ids = tile_items.reshape(tile_slots, tile_rows)
    slot_pos = jnp.arange(tile_slots, dtype=jnp.int32) % slot_cap
    live_send = slot_pos < jnp.repeat(send_tiles.reshape(n_ent), slot_cap)
    live_recv = slot_pos < jnp.repeat(recv_tiles.reshape(n_ent), slot_cap)
    partial_gram = lax.dot_general(
        item_factors, item_factors, (((0,), (0,)), ((), ())), preferred_element_type=jnp.float32
    )
    live_rows = jnp.repeat(live_send, tile_rows)
    picked = gather_rows(item_factors, jnp.where(live_rows, item_ids.reshape(-1), -1))
    incoming = lax.all_to_all(
        picked.reshape(n_ent, slot_cap * tile_rows, rank_width),
        "ent",
        split_axis=0,
        concat_axis=0,
        tiled=True,
    )
    counts_int = tile_counts.reshape(tile_slots, tile_rows)
    counts_f = counts_int.astype(jnp.float32)
    gram_weight = ALPHA * counts_f
    rhs_weight = jnp.where(
        live_recv[:, None] & (counts_int > 0), 1.0 + ALPHA * counts_f, jnp.float32(0.0)
    )
    owners = tile_users.reshape(tile_slots * seg_count)
    selector = owners[None, :] == jnp.arange(user_block, dtype=jnp.int32)[:, None]
    selector_f = selector.astype(jnp.float32)
    rows_all = incoming.reshape(tile_slots * tile_rows, rank_width)
    lane_chunk = 2048
    row_owner = jnp.repeat(owners, seg_length)
    gram_blocks = user_grams(
        rows_all,
        gram_weight.reshape(-1, lane_chunk),
        row_owner.reshape(-1, lane_chunk),
        rhs_weight.reshape(-1, lane_chunk),
        user_block,
        U_DEV,
    )
    identity_mat = jnp.eye(rank_width, dtype=jnp.float32)
    added_term = tree_sum(partial_gram, n_ent * n_rep) + RIDGE * identity_mat
    solved, own_factors = solve_owned(gram_blocks, added_term, n_rep, U_DEV)
    solved = solved.reshape(user_block, rank_width)
    run_factor = lax.dot_general(
        selector.astype(jnp.bfloat16),
        solved,
        (((0,), (0,)), ((), ())),
        preferred_element_type=jnp.float32,
    ).astype(jnp.bfloat16)
    back_load = jnp.concatenate(
        [
            run_factor.reshape(tile_slots, seg_count * rank_width),
            counts_int.astype(jnp.bfloat16),
        ],
        axis=1,
    )
    back_load = lax.all_to_all(
        back_load.reshape(n_ent, slot_cap, -1), "ent", split_axis=0, concat_axis=0, tiled=True
    ).reshape(tile_slots, -1)
    back_factor = back_load[:, : seg_count * rank_width]
    back_counts = back_load[:, seg_count * rank_width :].astype(jnp.float32)
    back_weight = jnp.where(
        live_send[:, None] & (back_counts > 0), 1.0 + ALPHA * back_counts, jnp.float32(0.0)
    )
    item_hot = item_ids[:, :, None] == jnp.arange(item_count, dtype=jnp.int32)[None, None, :]
    run_weight = back_weight.reshape(tile_slots * seg_count, seg_length)
    hot_runs = item_hot.reshape(tile_slots * seg_count, seg_length, item_count)
    spread_mat = jnp.sum(jnp.where(hot_runs, run_weight[:, :, None], 0.0), axis=1)
    item_rhs = lax.dot_general(
        spread_mat,
        back_factor.reshape(tile_slots * seg_count, rank_width).astype(jnp.float32),
        (((0,), (0,)), ((), ())),
        precision=highest,
        preferred_element_type=jnp.float32,
    )
    return (own_factors, item_rhs * RHS_SCALE)


def solution(mesh):
    in_specs = (
        P(("ent", "rep"), None),
        P("ent", "rep", None, None),
        P("ent", "rep", None),
        P("ent", "rep", None, None),
        P("ent", "rep", None, None),
        P("ent", "rep", None),
    )
    out_specs = (P(("ent", "rep"), None), P(("ent", "rep"), None))
    return jax.shard_map(shards, mesh=mesh, in_specs=in_specs, out_specs=out_specs, check_vma=False)
```

```python
import functools

import jax
import jax.numpy as jnp
from jax import lax
from jax.experimental import pallas as pl
from jax.experimental.pallas import tpu as pltpu
from jax.sharding import PartitionSpec as P

MESH_ID = pl.DeviceIdType.MESH

U_DEV = 2


ALPHA = 40.0
RIDGE = 1.0
RHS_SCALE = 1.0 / 640.0


def cholesky_solve(a_s, l_s, y_s, out_ref):
    batch, n, _ = a_s.shape
    out_ref[...] = jnp.zeros_like(out_ref)
    lane_v = lax.broadcasted_iota(jnp.int32, (1, n), 1)

    def factor(top, j, carry):
        span = n - top
        lane_m = lax.broadcasted_iota(jnp.int32, (span, n), 1)
        sub_m = lax.broadcasted_iota(jnp.int32, (span, n), 0) + top
        sub_v = lax.broadcasted_iota(jnp.int32, (span, 1), 0) + top
        for b in range(batch):
            a = a_s[b, top:, :]
            row = jnp.sum(jnp.where(sub_m == j, a, 0.0), axis=0, keepdims=True)
            col = jnp.sum(jnp.where(lane_m == j, a, 0.0), axis=1, keepdims=True)
            diag = jnp.sum(jnp.where(lane_v == j, row, 0.0), axis=1, keepdims=True)
            inv = 1.0 / jnp.sqrt(diag)
            l_row = jnp.where(lane_v >= j, row, 0.0) * inv
            l_col = jnp.where(sub_v >= j, col, 0.0) * inv
            a_s[b, top:, :] = a - l_col * l_row
            l_s[b, pl.ds(j, 1), :] = l_row
            y = y_s[pl.ds(b, 1), :]
            y_j = jnp.sum(jnp.where(lane_v == j, y, 0.0), axis=1, keepdims=True) * inv
            y_s[pl.ds(b, 1), :] = jnp.where(lane_v == j, y_j, y - y_j * l_row)
        return carry

    quarter = n // 4
    for part in range(4):
        top = part * quarter
        lax.fori_loop(top, top + quarter, functools.partial(factor, top), 0, unroll=2)

    def back(t, carry):
        j = n - 1 - t
        for b in range(batch):
            l_j = l_s[b, pl.ds(j, 1), :]
            x = out_ref[pl.ds(b, 1), :]
            y_j = jnp.sum(jnp.where(lane_v == j, y_s[pl.ds(b, 1), :], 0.0), axis=1, keepdims=True)
            l_jj = jnp.sum(jnp.where(lane_v == j, l_j, 0.0), axis=1, keepdims=True)
            known = jnp.sum(jnp.where(lane_v > j, l_j * x, 0.0), axis=1, keepdims=True)
            out_ref[pl.ds(b, 1), :] = jnp.where(lane_v == j, (y_j - known) / l_jj, x)
        return carry

    lax.fori_loop(0, n, back, 0, unroll=2)


def flip_bits(value, mask, bits):
    out = value - value % (1 << bits)
    for bit in range(bits):
        here = (value // (1 << bit)) % 2
        out = out + (1 << bit) * ((1 - here) if (mask >> bit) & 1 else here)
    return out


def doubling_kernel(
    n_rep, low_bits, rounds, x_ref, o_ref, full_recv, piece_recv, piece, gath,
    sem_a, sem_b, sem_c, sem_d, sem_e, sem_f,
):
    flat = lax.axis_index("ent") * n_rep + lax.axis_index("rep")
    group = 1 << low_bits
    rows = x_ref.shape[0] // group
    slot = flat % group

    def place(p):
        return (p // n_rep, p % n_rep)

    def flip(bit):
        step = 1 << bit
        upper = (flat // step) % 2
        return flat + step - 2 * step * upper

    members = [flip_bits(flat, k, low_bits) for k in range(1, group)]
    outer = [flip(bit) for bit in range(low_bits, rounds)]
    barrier = pltpu.get_barrier_semaphore()
    for p in members + outer:
        pl.semaphore_signal(barrier, inc=1, device_id=place(p), device_id_type=MESH_ID)
    pl.semaphore_wait(barrier, len(members) + len(outer))

    o_ref[...] = x_ref[...]
    for bit in range(low_bits):
        copy = pltpu.make_async_remote_copy(
            src_ref=o_ref, dst_ref=full_recv.at[bit], send_sem=sem_a.at[bit],
            recv_sem=sem_b.at[bit], device_id=place(flip(bit)), device_id_type=MESH_ID,
        )
        copy.start()
        copy.wait_recv()
        copy.wait_send()
        o_ref[...] = o_ref[...] + full_recv[bit]

    piece[...] = o_ref[pl.ds(pl.multiple_of(slot * rows, rows), rows), :]
    for index, p in enumerate(outer):
        copy = pltpu.make_async_remote_copy(
            src_ref=piece, dst_ref=piece_recv.at[index], send_sem=sem_c.at[index],
            recv_sem=sem_d.at[index], device_id=place(p), device_id_type=MESH_ID,
        )
        copy.start()
        copy.wait_recv()
        copy.wait_send()
        piece[...] = piece[...] + piece_recv[index]

    gath[slot] = piece[...]
    sends = []
    for index, p in enumerate(members):
        copy = pltpu.make_async_remote_copy(
            src_ref=piece, dst_ref=gath.at[slot], send_sem=sem_e.at[index],
            recv_sem=sem_f.at[slot], device_id=place(p), device_id_type=MESH_ID,
        )
        copy.start()
        sends.append(copy)
    for k in range(1, group):
        source = flip_bits(slot, k, low_bits)
        pltpu.make_async_remote_copy(
            src_ref=piece, dst_ref=gath.at[source], send_sem=sem_e.at[k - 1],
            recv_sem=sem_f.at[source], device_id=place(members[k - 1]), device_id_type=MESH_ID,
        ).wait_recv()
    for copy in sends:
        copy.wait_send()
    for part in range(group):
        o_ref[pl.ds(part * rows, rows), :] = gath[part]


def tree_sum(value, count):
    rounds = count.bit_length() - 1
    n_rep = lax.axis_size("rep")
    low_bits = (n_rep * 2).bit_length() - 1
    group = 1 << low_bits
    rows = value.shape[0] // group
    outer = rounds - low_bits
    return pl.pallas_call(
        functools.partial(doubling_kernel, n_rep, low_bits, rounds),
        out_shape=jax.ShapeDtypeStruct(value.shape, value.dtype),
        in_specs=[pl.BlockSpec(memory_space=pltpu.VMEM)],
        out_specs=pl.BlockSpec(memory_space=pltpu.VMEM),
        scratch_shapes=[
            pltpu.VMEM((low_bits,) + value.shape, value.dtype),
            pltpu.VMEM((outer, rows, value.shape[1]), value.dtype),
            pltpu.VMEM((rows, value.shape[1]), value.dtype),
            pltpu.VMEM((group, rows, value.shape[1]), value.dtype),
            pltpu.SemaphoreType.DMA((low_bits,)),
            pltpu.SemaphoreType.DMA((low_bits,)),
            pltpu.SemaphoreType.DMA((outer,)),
            pltpu.SemaphoreType.DMA((outer,)),
            pltpu.SemaphoreType.DMA((group - 1,)),
            pltpu.SemaphoreType.DMA((group,)),
        ],
        compiler_params=pltpu.CompilerParams(collective_id=0, has_side_effects=True),
    )(value)


def rep_peers(n_rep):
    me = lax.axis_index("rep")
    return me, [(me + shift) % n_rep for shift in range(1, n_rep)]


def owner_kernel(n_rep, blocks_ref, base_ref, out_ref, x_s, recv, a_s, l_s, y_s, fac, gath,
                 sem_a, sem_b, sem_c, sem_d):
    me, peers = rep_peers(n_rep)
    ent = lax.axis_index("ent")
    batch, n, _ = a_s.shape
    barrier = pltpu.get_barrier_semaphore()
    for peer in peers:
        pl.semaphore_signal(barrier, inc=1, device_id=(ent, peer), device_id_type=MESH_ID)
    pl.semaphore_wait(barrier, n_rep - 1)
    copies = []
    for index, peer in enumerate(peers):
        copy = pltpu.make_async_remote_copy(
            src_ref=blocks_ref.at[peer], dst_ref=recv.at[index], send_sem=sem_a.at[index],
            recv_sem=sem_b.at[index], device_id=(ent, peer), device_id_type=MESH_ID,
        )
        copy.start()
        copies.append(copy)
    total = blocks_ref[me]
    for index, copy in enumerate(copies):
        copy.wait_recv()
        total = total + recv[index]
    for copy in copies:
        copy.wait_send()
    base = base_ref[...]
    for b in range(batch):
        gram = total[b * n : (b + 1) * n] + base
        a_s[b] = (gram + gram.T) / 2
    y_s[...] = total[batch * n : batch * n + batch]
    cholesky_solve(a_s, l_s, y_s, x_s)
    fac[...] = x_s[...].astype(fac.dtype)
    gath[me] = fac[...]
    sends = []
    for index, peer in enumerate(peers):
        copy = pltpu.make_async_remote_copy(
            src_ref=fac, dst_ref=gath.at[me], send_sem=sem_c.at[index],
            recv_sem=sem_d.at[me], device_id=(ent, peer), device_id_type=MESH_ID,
        )
        copy.start()
        sends.append(copy)
    for index, source in enumerate(peers):
        pltpu.make_async_remote_copy(
            src_ref=fac, dst_ref=gath.at[source], send_sem=sem_c.at[index],
            recv_sem=sem_d.at[source], device_id=(ent, source), device_id_type=MESH_ID,
        ).wait_recv()
    for copy in sends:
        copy.wait_send()
    out_ref[...] = gath[...]


def solve_owned(blocks, base, n_rep, per_dev):
    n = blocks.shape[2]
    return pl.pallas_call(
        functools.partial(owner_kernel, n_rep),
        out_shape=(
            jax.ShapeDtypeStruct((n_rep, per_dev, n), jnp.bfloat16),
            jax.ShapeDtypeStruct((per_dev, n), jnp.float32),
        ),
        in_specs=[pl.BlockSpec(memory_space=pltpu.VMEM)] * 2,
        out_specs=(pl.BlockSpec(memory_space=pltpu.VMEM), pl.BlockSpec(memory_space=pltpu.VMEM)),
        scratch_shapes=[
            pltpu.VMEM((n_rep - 1,) + blocks.shape[1:], jnp.float32),
            pltpu.VMEM((per_dev, n, n), jnp.float32),
            pltpu.VMEM((per_dev, n, n), jnp.float32),
            pltpu.VMEM((per_dev, n), jnp.float32),
            pltpu.VMEM((per_dev, n), jnp.bfloat16),
            pltpu.VMEM((n_rep, per_dev, n), jnp.bfloat16),
            pltpu.SemaphoreType.DMA((n_rep - 1,)),
            pltpu.SemaphoreType.DMA((n_rep - 1,)),
            pltpu.SemaphoreType.DMA((n_rep - 1,)),
            pltpu.SemaphoreType.DMA((n_rep,)),
        ],
        compiler_params=pltpu.CompilerParams(collective_id=1, has_side_effects=True),
    )(blocks, base)


def gather_kernel(idx_ref, table_t_ref, out_ref):
    step = pl.program_id(0)
    idx = idx_ref[pl.ds(step, 1), :]
    picks = lax.broadcasted_iota(jnp.int32, (table_t_ref.shape[1], idx.shape[1]), 0) == idx
    rows_t = jnp.dot(table_t_ref[...], picks.astype(jnp.bfloat16), preferred_element_type=jnp.float32)
    out_ref[...] = rows_t.T.astype(out_ref.dtype)


def gather_rows(table, idx, chunk=8192):
    count = idx.shape[0]
    idx_lanes = idx.reshape(count // chunk, chunk)
    return pl.pallas_call(
        gather_kernel,
        out_shape=jax.ShapeDtypeStruct((count, table.shape[1]), table.dtype),
        grid=(count // chunk,),
        in_specs=[
            pl.BlockSpec(idx_lanes.shape, lambda i: (0, 0)),
            pl.BlockSpec((table.shape[1], table.shape[0]), lambda i: (0, 0)),
        ],
        out_specs=pl.BlockSpec((chunk, table.shape[1]), lambda i: (i, 0)),
        cost_estimate=pl.CostEstimate(
            flops=2 * count * table.shape[0] * table.shape[1],
            transcendentals=0,
            bytes_accessed=count * 4 + table.size * 2 + count * table.shape[1] * 2,
        ),
    )(idx_lanes, table.T)


def gram_kernel(n_user, per_dev, rows_ref, gw_ref, user_ref, rw_ref, out_ref):
    step = pl.program_id(0)
    width = rows_ref.shape[1]

    @pl.when(step == 0)
    def _():
        out_ref[...] = jnp.zeros_like(out_ref)

    rows = rows_ref[...]
    rows_t = rows.astype(jnp.float32).T
    weights_t = (rows_t * gw_ref[pl.ds(step, 1), :]).astype(jnp.bfloat16)
    users = user_ref[pl.ds(step, 1), :]
    zero = jnp.zeros((), jnp.bfloat16)
    for user in range(n_user):
        picked = jnp.where(users == user, weights_t, zero)
        block, spot = user // per_dev, (user % per_dev) * width
        out_ref[block, spot : spot + width, :] += jnp.dot(
            picked, rows, preferred_element_type=jnp.float32
        )
    slots = lax.broadcasted_iota(jnp.int32, (n_user, users.shape[1]), 0)
    per_user = jnp.where(users == slots, rw_ref[pl.ds(step, 1), :], 0.0)
    high = per_user.astype(jnp.bfloat16)
    low = (per_user - high.astype(jnp.float32)).astype(jnp.bfloat16)
    rhs = jnp.dot(high, rows, preferred_element_type=jnp.float32) + jnp.dot(
        low, rows, preferred_element_type=jnp.float32
    )
    base = per_dev * width
    for block in range(n_user // per_dev):
        out_ref[block, base : base + per_dev, :] += rhs[block * per_dev : (block + 1) * per_dev]


def user_grams(rows, gw_lanes, user_lanes, rw_lanes, n_user, per_dev):
    chunks, chunk = gw_lanes.shape
    width = rows.shape[1]
    n_block = n_user // per_dev
    block_rows = per_dev * width + per_dev
    return pl.pallas_call(
        functools.partial(gram_kernel, n_user, per_dev),
        out_shape=jax.ShapeDtypeStruct((n_block, block_rows, width), jnp.float32),
        grid=(chunks,),
        in_specs=[
            pl.BlockSpec((chunk, width), lambda i: (i, 0)),
            pl.BlockSpec((chunks, chunk), lambda i: (0, 0)),
            pl.BlockSpec((chunks, chunk), lambda i: (0, 0)),
            pl.BlockSpec((chunks, chunk), lambda i: (0, 0)),
        ],
        out_specs=pl.BlockSpec((n_block, block_rows, width), lambda i: (0, 0, 0)),
        cost_estimate=pl.CostEstimate(
            flops=2 * rows.shape[0] * width * width * (n_user + 2),
            transcendentals=0,
            bytes_accessed=rows.size * 2 + 12 * rows.shape[0] + n_user * width * (width + 1) * 4,
        ),
    )(rows, gw_lanes, user_lanes, rw_lanes)

def shards(item_factors, tile_items, send_tiles, tile_users, tile_counts, recv_tiles):
    highest = lax.Precision.HIGHEST
    rank_width = item_factors.shape[1]
    item_count = item_factors.shape[0]
    n_ent = lax.axis_size("ent")
    n_rep = lax.axis_size("rep")
    tile_slots = tile_items.shape[2]
    tile_rows = tile_items.shape[3]
    seg_count = tile_users.shape[3]
    seg_length = tile_rows // seg_count
    slot_cap = tile_slots // n_ent
    user_block = U_DEV * lax.axis_size("rep")
    item_ids = tile_items.reshape(tile_slots, tile_rows)
    slot_pos = jnp.arange(tile_slots, dtype=jnp.int32) % slot_cap
    live_send = slot_pos < jnp.repeat(send_tiles.reshape(n_ent), slot_cap)
    live_recv = slot_pos < jnp.repeat(recv_tiles.reshape(n_ent), slot_cap)
    partial_gram = lax.dot_general(
        item_factors, item_factors, (((0,), (0,)), ((), ())), preferred_element_type=jnp.float32
    )
    live_rows = jnp.repeat(live_send, tile_rows)
    picked = gather_rows(item_factors, jnp.where(live_rows, item_ids.reshape(-1), -1))
    incoming = lax.all_to_all(
        picked.reshape(n_ent, slot_cap * tile_rows, rank_width),
        "ent",
        split_axis=0,
        concat_axis=0,
        tiled=True,
    )
    counts_int = tile_counts.reshape(tile_slots, tile_rows)
    counts_f = counts_int.astype(jnp.float32)
    gram_weight = ALPHA * counts_f
    rhs_weight = jnp.where(
        live_recv[:, None] & (counts_int > 0), 1.0 + ALPHA * counts_f, jnp.float32(0.0)
    )
    owners = tile_users.reshape(tile_slots * seg_count)
    selector = owners[None, :] == jnp.arange(user_block, dtype=jnp.int32)[:, None]
    selector_f = selector.astype(jnp.float32)
    rows_all = incoming.reshape(tile_slots * tile_rows, rank_width)
    lane_chunk = 2048
    row_owner = jnp.repeat(owners, seg_length)
    gram_blocks = user_grams(
        rows_all,
        gram_weight.reshape(-1, lane_chunk),
        row_owner.reshape(-1, lane_chunk),
        rhs_weight.reshape(-1, lane_chunk),
        user_block,
        U_DEV,
    )
    identity_mat = jnp.eye(rank_width, dtype=jnp.float32)
    added_term = tree_sum(partial_gram, n_ent * n_rep) + RIDGE * identity_mat
    solved, own_factors = solve_owned(gram_blocks, added_term, n_rep, U_DEV)
    solved = solved.reshape(user_block, rank_width)
    run_factor = lax.dot_general(
        selector.astype(jnp.bfloat16),
        solved,
        (((0,), (0,)), ((), ())),
        preferred_element_type=jnp.float32,
    ).astype(jnp.bfloat16)
    back_load = jnp.concatenate(
        [
            run_factor.reshape(tile_slots, seg_count * rank_width),
            counts_int.astype(jnp.bfloat16),
        ],
        axis=1,
    )
    back_load = lax.all_to_all(
        back_load.reshape(n_ent, slot_cap, -1), "ent", split_axis=0, concat_axis=0, tiled=True
    ).reshape(tile_slots, -1)
    back_factor = back_load[:, : seg_count * rank_width]
    back_counts = back_load[:, seg_count * rank_width :].astype(jnp.float32)
    back_weight = jnp.where(
        live_send[:, None] & (back_counts > 0), 1.0 + ALPHA * back_counts, jnp.float32(0.0)
    )
    item_hot = item_ids[:, :, None] == jnp.arange(item_count, dtype=jnp.int32)[None, None, :]
    run_weight = back_weight.reshape(tile_slots * seg_count, seg_length)
    hot_runs = item_hot.reshape(tile_slots * seg_count, seg_length, item_count)
    spread_mat = jnp.sum(jnp.where(hot_runs, run_weight[:, :, None], 0.0), axis=1)
    item_rhs = lax.dot_general(
        spread_mat,
        back_factor.reshape(tile_slots * seg_count, rank_width).astype(jnp.float32),
        (((0,), (0,)), ((), ())),
        precision=highest,
        preferred_element_type=jnp.float32,
    )
    return (own_factors, item_rhs * RHS_SCALE)


def solution(mesh):
    in_specs = (
        P(("ent", "rep"), None),
        P("ent", "rep", None, None),
        P("ent", "rep", None),
        P("ent", "rep", None, None),
        P("ent", "rep", None, None),
        P("ent", "rep", None),
    )
    out_specs = (P(("ent", "rep"), None), P(("ent", "rep"), None))
    return jax.shard_map(shards, mesh=mesh, in_specs=in_specs, out_specs=out_specs, check_vma=False)
```

```python
import functools

import jax
import jax.numpy as jnp
from jax import lax
from jax.experimental import pallas as pl
from jax.experimental.pallas import tpu as pltpu
from jax.sharding import PartitionSpec as P

MESH_ID = pl.DeviceIdType.MESH

U_DEV = 2


ALPHA = 40.0
RIDGE = 1.0
RHS_SCALE = 1.0 / 640.0


def cholesky_solve(a_s, l_s, y_s, out_ref):
    batch, n, _ = a_s.shape
    out_ref[...] = jnp.zeros_like(out_ref)
    lane_v = lax.broadcasted_iota(jnp.int32, (1, n), 1)

    def factor(top, j, carry):
        span = n - top
        lane_m = lax.broadcasted_iota(jnp.int32, (span, n), 1)
        sub_m = lax.broadcasted_iota(jnp.int32, (span, n), 0) + top
        sub_v = lax.broadcasted_iota(jnp.int32, (span, 1), 0) + top
        for b in range(batch):
            a = a_s[b, top:, :]
            row = jnp.sum(jnp.where(sub_m == j, a, 0.0), axis=0, keepdims=True)
            col = jnp.sum(jnp.where(lane_m == j, a, 0.0), axis=1, keepdims=True)
            diag = jnp.sum(jnp.where(lane_v == j, row, 0.0), axis=1, keepdims=True)
            inv = 1.0 / jnp.sqrt(diag)
            l_row = jnp.where(lane_v >= j, row, 0.0) * inv
            l_col = jnp.where(sub_v >= j, col, 0.0) * inv
            a_s[b, top:, :] = a - l_col * l_row
            l_s[b, pl.ds(j, 1), :] = l_row
            y = y_s[pl.ds(b, 1), :]
            y_j = jnp.sum(jnp.where(lane_v == j, y, 0.0), axis=1, keepdims=True) * inv
            y_s[pl.ds(b, 1), :] = jnp.where(lane_v == j, y_j, y - y_j * l_row)
        return carry

    quarter = n // 4
    for part in range(4):
        top = part * quarter
        lax.fori_loop(top, top + quarter, functools.partial(factor, top), 0, unroll=2)

    def back(t, carry):
        j = n - 1 - t
        for b in range(batch):
            l_j = l_s[b, pl.ds(j, 1), :]
            x = out_ref[pl.ds(b, 1), :]
            y_j = jnp.sum(jnp.where(lane_v == j, y_s[pl.ds(b, 1), :], 0.0), axis=1, keepdims=True)
            l_jj = jnp.sum(jnp.where(lane_v == j, l_j, 0.0), axis=1, keepdims=True)
            known = jnp.sum(jnp.where(lane_v > j, l_j * x, 0.0), axis=1, keepdims=True)
            out_ref[pl.ds(b, 1), :] = jnp.where(lane_v == j, (y_j - known) / l_jj, x)
        return carry

    lax.fori_loop(0, n, back, 0, unroll=2)


def flip_bits(value, mask, bits):
    out = value - value % (1 << bits)
    for bit in range(bits):
        here = (value // (1 << bit)) % 2
        out = out + (1 << bit) * ((1 - here) if (mask >> bit) & 1 else here)
    return out


def doubling_kernel(
    n_rep, low_bits, rounds, x_ref, o_ref, full_recv, piece_recv, piece, gath,
    sem_a, sem_b, sem_c, sem_d, sem_e, sem_f,
):
    flat = lax.axis_index("ent") * n_rep + lax.axis_index("rep")
    group = 1 << low_bits
    rows = x_ref.shape[0] // group
    slot = flat % group

    def place(p):
        return (p // n_rep, p % n_rep)

    def flip(bit):
        step = 1 << bit
        upper = (flat // step) % 2
        return flat + step - 2 * step * upper

    members = [flip_bits(flat, k, low_bits) for k in range(1, group)]
    outer = [flip(bit) for bit in range(low_bits, rounds)]
    barrier = pltpu.get_barrier_semaphore()
    for p in members + outer:
        pl.semaphore_signal(barrier, inc=1, device_id=place(p), device_id_type=MESH_ID)
    pl.semaphore_wait(barrier, len(members) + len(outer))

    o_ref[...] = x_ref[...]
    for bit in range(low_bits):
        copy = pltpu.make_async_remote_copy(
            src_ref=o_ref, dst_ref=full_recv.at[bit], send_sem=sem_a.at[bit],
            recv_sem=sem_b.at[bit], device_id=place(flip(bit)), device_id_type=MESH_ID,
        )
        copy.start()
        copy.wait_recv()
        copy.wait_send()
        o_ref[...] = o_ref[...] + full_recv[bit]

    piece[...] = o_ref[pl.ds(pl.multiple_of(slot * rows, rows), rows), :]
    for index, p in enumerate(outer):
        copy = pltpu.make_async_remote_copy(
            src_ref=piece, dst_ref=piece_recv.at[index], send_sem=sem_c.at[index],
            recv_sem=sem_d.at[index], device_id=place(p), device_id_type=MESH_ID,
        )
        copy.start()
        copy.wait_recv()
        copy.wait_send()
        piece[...] = piece[...] + piece_recv[index]

    gath[slot] = piece[...]
    sends = []
    for index, p in enumerate(members):
        copy = pltpu.make_async_remote_copy(
            src_ref=piece, dst_ref=gath.at[slot], send_sem=sem_e.at[index],
            recv_sem=sem_f.at[slot], device_id=place(p), device_id_type=MESH_ID,
        )
        copy.start()
        sends.append(copy)
    for k in range(1, group):
        source = flip_bits(slot, k, low_bits)
        pltpu.make_async_remote_copy(
            src_ref=piece, dst_ref=gath.at[source], send_sem=sem_e.at[k - 1],
            recv_sem=sem_f.at[source], device_id=place(members[k - 1]), device_id_type=MESH_ID,
        ).wait_recv()
    for copy in sends:
        copy.wait_send()
    for part in range(group):
        o_ref[pl.ds(part * rows, rows), :] = gath[part]


def tree_sum(value, count):
    rounds = count.bit_length() - 1
    n_rep = lax.axis_size("rep")
    low_bits = (n_rep * 2).bit_length() - 1
    group = 1 << low_bits
    rows = value.shape[0] // group
    outer = rounds - low_bits
    return pl.pallas_call(
        functools.partial(doubling_kernel, n_rep, low_bits, rounds),
        out_shape=jax.ShapeDtypeStruct(value.shape, value.dtype),
        in_specs=[pl.BlockSpec(memory_space=pltpu.VMEM)],
        out_specs=pl.BlockSpec(memory_space=pltpu.VMEM),
        scratch_shapes=[
            pltpu.VMEM((low_bits,) + value.shape, value.dtype),
            pltpu.VMEM((outer, rows, value.shape[1]), value.dtype),
            pltpu.VMEM((rows, value.shape[1]), value.dtype),
            pltpu.VMEM((group, rows, value.shape[1]), value.dtype),
            pltpu.SemaphoreType.DMA((low_bits,)),
            pltpu.SemaphoreType.DMA((low_bits,)),
            pltpu.SemaphoreType.DMA((outer,)),
            pltpu.SemaphoreType.DMA((outer,)),
            pltpu.SemaphoreType.DMA((group - 1,)),
            pltpu.SemaphoreType.DMA((group,)),
        ],
        compiler_params=pltpu.CompilerParams(collective_id=0, has_side_effects=True),
    )(value)


def rep_peers(n_rep):
    me = lax.axis_index("rep")
    return me, [(me + shift) % n_rep for shift in range(1, n_rep)]


def owner_kernel(n_rep, blocks_ref, base_ref, out_ref, x_s, recv, a_s, l_s, y_s, fac, gath,
                 sem_a, sem_b, sem_c, sem_d):
    me, peers = rep_peers(n_rep)
    ent = lax.axis_index("ent")
    batch, n, _ = a_s.shape
    barrier = pltpu.get_barrier_semaphore()
    for peer in peers:
        pl.semaphore_signal(barrier, inc=1, device_id=(ent, peer), device_id_type=MESH_ID)
    pl.semaphore_wait(barrier, n_rep - 1)
    copies = []
    for index, peer in enumerate(peers):
        copy = pltpu.make_async_remote_copy(
            src_ref=blocks_ref.at[peer], dst_ref=recv.at[index], send_sem=sem_a.at[index],
            recv_sem=sem_b.at[index], device_id=(ent, peer), device_id_type=MESH_ID,
        )
        copy.start()
        copies.append(copy)
    total = blocks_ref[me]
    for index, copy in enumerate(copies):
        copy.wait_recv()
        total = total + recv[index]
    for copy in copies:
        copy.wait_send()
    base = base_ref[...]
    for b in range(batch):
        gram = total[b * n : (b + 1) * n] + base
        a_s[b] = (gram + gram.T) / 2
    y_s[...] = total[batch * n : batch * n + batch]
    cholesky_solve(a_s, l_s, y_s, x_s)
    fac[...] = x_s[...].astype(fac.dtype)
    gath[me] = fac[...]
    sends = []
    for index, peer in enumerate(peers):
        copy = pltpu.make_async_remote_copy(
            src_ref=fac, dst_ref=gath.at[me], send_sem=sem_c.at[index],
            recv_sem=sem_d.at[me], device_id=(ent, peer), device_id_type=MESH_ID,
        )
        copy.start()
        sends.append(copy)
    for index, source in enumerate(peers):
        pltpu.make_async_remote_copy(
            src_ref=fac, dst_ref=gath.at[source], send_sem=sem_c.at[index],
            recv_sem=sem_d.at[source], device_id=(ent, source), device_id_type=MESH_ID,
        ).wait_recv()
    for copy in sends:
        copy.wait_send()
    out_ref[...] = gath[...]


def solve_owned(blocks, base, n_rep, per_dev):
    n = blocks.shape[2]
    return pl.pallas_call(
        functools.partial(owner_kernel, n_rep),
        out_shape=(
            jax.ShapeDtypeStruct((n_rep, per_dev, n), jnp.bfloat16),
            jax.ShapeDtypeStruct((per_dev, n), jnp.float32),
        ),
        in_specs=[pl.BlockSpec(memory_space=pltpu.VMEM)] * 2,
        out_specs=(pl.BlockSpec(memory_space=pltpu.VMEM), pl.BlockSpec(memory_space=pltpu.VMEM)),
        scratch_shapes=[
            pltpu.VMEM((n_rep - 1,) + blocks.shape[1:], jnp.float32),
            pltpu.VMEM((per_dev, n, n), jnp.float32),
            pltpu.VMEM((per_dev, n, n), jnp.float32),
            pltpu.VMEM((per_dev, n), jnp.float32),
            pltpu.VMEM((per_dev, n), jnp.bfloat16),
            pltpu.VMEM((n_rep, per_dev, n), jnp.bfloat16),
            pltpu.SemaphoreType.DMA((n_rep - 1,)),
            pltpu.SemaphoreType.DMA((n_rep - 1,)),
            pltpu.SemaphoreType.DMA((n_rep - 1,)),
            pltpu.SemaphoreType.DMA((n_rep,)),
        ],
        compiler_params=pltpu.CompilerParams(collective_id=1, has_side_effects=True),
    )(blocks, base)


def gather_kernel(idx_ref, table_t_ref, out_ref):
    step = pl.program_id(0)
    idx = idx_ref[pl.ds(step, 1), :]
    picks = lax.broadcasted_iota(jnp.int32, (table_t_ref.shape[1], idx.shape[1]), 0) == idx
    rows_t = jnp.dot(table_t_ref[...], picks.astype(jnp.bfloat16), preferred_element_type=jnp.float32)
    out_ref[...] = rows_t.T.astype(out_ref.dtype)


def gather_rows(table, idx, chunk=8192):
    count = idx.shape[0]
    idx_lanes = idx.reshape(count // chunk, chunk)
    return pl.pallas_call(
        gather_kernel,
        out_shape=jax.ShapeDtypeStruct((count, table.shape[1]), table.dtype),
        grid=(count // chunk,),
        in_specs=[
            pl.BlockSpec(idx_lanes.shape, lambda i: (0, 0)),
            pl.BlockSpec((table.shape[1], table.shape[0]), lambda i: (0, 0)),
        ],
        out_specs=pl.BlockSpec((chunk, table.shape[1]), lambda i: (i, 0)),
        cost_estimate=pl.CostEstimate(
            flops=2 * count * table.shape[0] * table.shape[1],
            transcendentals=0,
            bytes_accessed=count * 4 + table.size * 2 + count * table.shape[1] * 2,
        ),
    )(idx_lanes, table.T)


def gram_kernel(n_user, per_dev, rows_ref, gw_ref, user_ref, rw_ref, out_ref):
    step = pl.program_id(0)
    width = rows_ref.shape[1]

    @pl.when(step == 0)
    def _():
        out_ref[...] = jnp.zeros_like(out_ref)

    rows = rows_ref[...]
    rows_t = rows.astype(jnp.float32).T
    weights_t = (rows_t * gw_ref[pl.ds(step, 1), :]).astype(jnp.bfloat16)
    users = user_ref[pl.ds(step, 1), :]
    zero = jnp.zeros((), jnp.bfloat16)
    for user in range(n_user):
        picked = jnp.where(users == user, weights_t, zero)
        block, spot = user // per_dev, (user % per_dev) * width
        out_ref[block, spot : spot + width, :] += jnp.dot(
            picked, rows, preferred_element_type=jnp.float32
        )
    slots = lax.broadcasted_iota(jnp.int32, (n_user, users.shape[1]), 0)
    per_user = jnp.where(users == slots, rw_ref[pl.ds(step, 1), :], 0.0)
    high = per_user.astype(jnp.bfloat16)
    low = (per_user - high.astype(jnp.float32)).astype(jnp.bfloat16)
    rhs = jnp.dot(high, rows, preferred_element_type=jnp.float32) + jnp.dot(
        low, rows, preferred_element_type=jnp.float32
    )
    base = per_dev * width
    for block in range(n_user // per_dev):
        out_ref[block, base : base + per_dev, :] += rhs[block * per_dev : (block + 1) * per_dev]


def user_grams(rows, gw_lanes, user_lanes, rw_lanes, n_user, per_dev):
    chunks, chunk = gw_lanes.shape
    width = rows.shape[1]
    n_block = n_user // per_dev
    block_rows = per_dev * width + per_dev
    return pl.pallas_call(
        functools.partial(gram_kernel, n_user, per_dev),
        out_shape=jax.ShapeDtypeStruct((n_block, block_rows, width), jnp.float32),
        grid=(chunks,),
        in_specs=[
            pl.BlockSpec((chunk, width), lambda i: (i, 0)),
            pl.BlockSpec((chunks, chunk), lambda i: (0, 0)),
            pl.BlockSpec((chunks, chunk), lambda i: (0, 0)),
            pl.BlockSpec((chunks, chunk), lambda i: (0, 0)),
        ],
        out_specs=pl.BlockSpec((n_block, block_rows, width), lambda i: (0, 0, 0)),
        cost_estimate=pl.CostEstimate(
            flops=2 * rows.shape[0] * width * width * (n_user + 2),
            transcendentals=0,
            bytes_accessed=rows.size * 2 + 12 * rows.shape[0] + n_user * width * (width + 1) * 4,
        ),
    )(rows, gw_lanes, user_lanes, rw_lanes)

def shards(item_factors, tile_items, send_tiles, tile_users, tile_counts, recv_tiles):
    highest = lax.Precision.HIGHEST
    rank_width = item_factors.shape[1]
    item_count = item_factors.shape[0]
    n_ent = lax.axis_size("ent")
    n_rep = lax.axis_size("rep")
    tile_slots = tile_items.shape[2]
    tile_rows = tile_items.shape[3]
    seg_count = tile_users.shape[3]
    seg_length = tile_rows // seg_count
    slot_cap = tile_slots // n_ent
    user_block = U_DEV * lax.axis_size("rep")
    item_ids = tile_items.reshape(tile_slots, tile_rows)
    slot_pos = jnp.arange(tile_slots, dtype=jnp.int32) % slot_cap
    live_send = slot_pos < jnp.repeat(send_tiles.reshape(n_ent), slot_cap)
    live_recv = slot_pos < jnp.repeat(recv_tiles.reshape(n_ent), slot_cap)
    partial_gram = lax.dot_general(
        item_factors, item_factors, (((0,), (0,)), ((), ())), preferred_element_type=jnp.float32
    )
    live_rows = jnp.repeat(live_send, tile_rows)
    picked = gather_rows(item_factors, jnp.where(live_rows, item_ids.reshape(-1), -1))
    incoming = lax.all_to_all(
        picked.reshape(n_ent, slot_cap * tile_rows, rank_width),
        "ent",
        split_axis=0,
        concat_axis=0,
        tiled=True,
    )
    counts_int = tile_counts.reshape(tile_slots, tile_rows)
    counts_f = counts_int.astype(jnp.float32)
    gram_weight = ALPHA * counts_f
    rhs_weight = jnp.where(
        live_recv[:, None] & (counts_int > 0), 1.0 + ALPHA * counts_f, jnp.float32(0.0)
    )
    owners = tile_users.reshape(tile_slots * seg_count)
    selector = owners[None, :] == jnp.arange(user_block, dtype=jnp.int32)[:, None]
    selector_f = selector.astype(jnp.float32)
    rows_all = incoming.reshape(tile_slots * tile_rows, rank_width)
    lane_chunk = 8192
    row_owner = jnp.repeat(owners, seg_length)
    gram_blocks = user_grams(
        rows_all,
        gram_weight.reshape(-1, lane_chunk),
        row_owner.reshape(-1, lane_chunk),
        rhs_weight.reshape(-1, lane_chunk),
        user_block,
        U_DEV,
    )
    identity_mat = jnp.eye(rank_width, dtype=jnp.float32)
    added_term = tree_sum(partial_gram, n_ent * n_rep) + RIDGE * identity_mat
    solved, own_factors = solve_owned(gram_blocks, added_term, n_rep, U_DEV)
    solved = solved.reshape(user_block, rank_width)
    run_factor = lax.dot_general(
        selector.astype(jnp.bfloat16),
        solved,
        (((0,), (0,)), ((), ())),
        preferred_element_type=jnp.float32,
    ).astype(jnp.bfloat16)
    back_load = jnp.concatenate(
        [
            run_factor.reshape(tile_slots, seg_count * rank_width),
            counts_int.astype(jnp.bfloat16),
        ],
        axis=1,
    )
    back_load = lax.all_to_all(
        back_load.reshape(n_ent, slot_cap, -1), "ent", split_axis=0, concat_axis=0, tiled=True
    ).reshape(tile_slots, -1)
    back_factor = back_load[:, : seg_count * rank_width]
    back_counts = back_load[:, seg_count * rank_width :].astype(jnp.float32)
    back_weight = jnp.where(
        live_send[:, None] & (back_counts > 0), 1.0 + ALPHA * back_counts, jnp.float32(0.0)
    )
    item_hot = item_ids[:, :, None] == jnp.arange(item_count, dtype=jnp.int32)[None, None, :]
    run_weight = back_weight.reshape(tile_slots * seg_count, seg_length)
    hot_runs = item_hot.reshape(tile_slots * seg_count, seg_length, item_count)
    spread_mat = jnp.sum(jnp.where(hot_runs, run_weight[:, :, None], 0.0), axis=1)
    item_rhs = lax.dot_general(
        spread_mat,
        back_factor.reshape(tile_slots * seg_count, rank_width).astype(jnp.float32),
        (((0,), (0,)), ((), ())),
        precision=highest,
        preferred_element_type=jnp.float32,
    )
    return (own_factors, item_rhs * RHS_SCALE)


def solution(mesh):
    in_specs = (
        P(("ent", "rep"), None),
        P("ent", "rep", None, None),
        P("ent", "rep", None),
        P("ent", "rep", None, None),
        P("ent", "rep", None, None),
        P("ent", "rep", None),
    )
    out_specs = (P(("ent", "rep"), None), P(("ent", "rep"), None))
    return jax.shard_map(shards, mesh=mesh, in_specs=in_specs, out_specs=out_specs, check_vma=False)
```
